32 devices in a mesh: page: 8 (over z, y), seq: 4 (over x, core).
Axes of the slice: x: 2, y: 2, z: 4, core: 2. Of those that a mesh axis runs over, the one named last changes fastest.
Arguments:
- tokens: float32 [8, 512, 1024], P('page', 'seq'), may hold values from -6 to 6
- valid_len: int32 [8], P('page'), may hold values from 128 to 512, as said below
- query_weight: float32 [1024, 1024], P(('page', 'seq')), may hold values from -0.1875 to 0.1875
- query_bias: float32 [1024], P(('page', 'seq')), may hold values from -3 to 3
- key_weight: float32 [1024, 1024], P(('page', 'seq')), may hold values from -0.1875 to 0.1875
- value_weight: float32 [1024, 1024], P(('page', 'seq')), may hold values from -0.1875 to 0.1875
- value_bias: float32 [1024], P(('page', 'seq')), may hold values from -3 to 3
- output_weight: float32 [1024, 1024], P(('page', 'seq')), may hold values from -0.75 to 0.75
- output_bias: float32 [1024], P(('page', 'seq')), may hold values from -3 to 3
- attn_gain: float32 [1024], P(('page', 'seq')), may hold values from 0.25 to 1.75
- attn_shift: float32 [1024], P(('page', 'seq')), may hold values from -3 to 3
- inner_weight: float32 [1024, 4096], P(('page', 'seq')), may hold values from -0.1875 to 0.1875
- inner_bias: float32 [4096], P(('page', 'seq')), may hold values from -3 to 3
- outer_weight: float32 [4096, 1024], P(('page', 'seq')), may hold values from -0.09375 to 0.09375
- outer_bias: float32 [1024], P(('page', 'seq')), may hold values from -3 to 3
- final_gain: float32 [1024], P(('page', 'seq')), may hold values from 0.25 to 1.75
- final_shift: float32 [1024], P(('page', 'seq')), may hold values from -3 to 3
- out_grad: float32 [8, 512, 1024], P('page', 'seq'), may hold values from -6 to 6
Outputs:
- layer_out: float32 [8, 512, 1024], P('page', 'seq')
- input_grad: float32 [8, 512, 1024], P('page', 'seq')
- query_weight_grad: float32 [1024, 1024], P(('page', 'seq'))
- query_bias_grad: float32 [1024], P(('page', 'seq'))
- key_weight_grad: float32 [1024, 1024], P(('page', 'seq'))
- value_weight_grad: float32 [1024, 1024], P(('page', 'seq'))
- value_bias_grad: float32 [1024], P(('page', 'seq'))
- output_weight_grad: float32 [1024, 1024], P(('page', 'seq'))
- output_bias_grad: float32 [1024], P(('page', 'seq'))
- attn_gain_grad: float32 [1024], P(('page', 'seq'))
- attn_shift_grad: float32 [1024], P(('page', 'seq'))
- inner_weight_grad: float32 [1024, 4096], P(('page', 'seq'))
- inner_bias_grad: float32 [4096], P(('page', 'seq'))
- outer_weight_grad: float32 [4096, 1024], P(('page', 'seq'))
- outer_bias_grad: float32 [1024], P(('page', 'seq'))
- final_gain_grad: float32 [1024], P(('page', 'seq'))
- final_shift_grad: float32 [1024], P(('page', 'seq'))
The draws below stay inside these ranges and needn't reach their ends.
Inputs may be any that keep to these rules, and one draw needn't show every extreme that they name: `valid_len`: keys at or beyond a page's valid length are padding; some page is full and some page has only 128 valid tokens.
All inputs are finite; a program needn't handle non-finite values.
Results may differ from the reference program's by a relative error of at most 0.015.
The reference program's roundings to bfloat16 on the way count: a program that leaves them out, or rounds other values in their place, can miss the bound.
Values may be sent and summed in bfloat16 or wider, within the bound.
A program may use at most 192 MiB of HBM per device.

```python
import math
import jax
import jax.numpy as jnp
from jax import lax

D = 1024
HEADS = 16
HEAD_DIM = 64
FF = 4096
SEQ = 512
PAGES = 8


def draw_valid_len(key, part):
    key_lengths, key_longest, key_shortest = jax.random.split(jax.random.fold_in(key, 17), 3)
    lengths = jax.random.randint(key_lengths, (PAGES,), SEQ // 4, SEQ + 1)
    longest = jax.random.randint(key_longest, (), 0, PAGES)
    shortest = (longest + 1 + jax.random.randint(key_shortest, (), 0, PAGES - 1)) % PAGES
    positions = jnp.arange(PAGES)
    lengths = jnp.where(positions == longest, SEQ, lengths)
    lengths = jnp.where(positions == shortest, SEQ // 4, lengths)
    return lengths.astype(jnp.int32)


def with_spikes(array, stream_key, source, target, parts, factor):
    owner, partner = [(jnp.arange(array.shape[position]) // (array.shape[position] // parts)).reshape([-1 if axis == position else 1 for axis in range(array.ndim)]) for position in (source, target)]
    chosen = jax.random.permutation(stream_key, parts)[partner]
    strong = (owner == chosen) | (owner == (partner + parts // 2) % parts)
    return jnp.where(strong, factor * array, array)


def block_levels(key, dims, pieces, low, largest):
    def one(position, blocks):
        heights = jax.random.uniform(jax.random.fold_in(jax.random.fold_in(key, 6), position), (blocks,), jnp.float32, low / len(pieces), largest / len(pieces))
        return jnp.repeat(jnp.exp(heights), dims[position] // blocks).reshape((-1,) + (1,) * (len(dims) - position - 1))

    loudness = one(*pieces[0])
    for cut in pieces[1:]:
        loudness = loudness * one(*cut)
    return loudness


def scatter_about(rng, shape, width, reach, cuts=(), kind=jnp.bfloat16):
    values = jax.random.normal(rng, shape, jnp.float32) * width
    if len(cuts) > 0:
        values = block_levels(rng, shape, cuts, -0.22, 0.18) * values
    return jnp.clip(values, min=-reach, max=reach).astype(kind)


def heavy_noise(rng, dims, deviation, bound, shards, heavy, held_as=jnp.bfloat16):
    array = deviation * jax.random.normal(rng, dims, jnp.float32)
    if shards:
        array = array * block_levels(rng, dims, shards, -0.22, 0.18)
    return jnp.clip(with_spikes(array, jax.random.fold_in(rng, 3), *heavy), -bound, bound).astype(held_as)


def setup_inputs(seed: int = 0) -> dict:
    seeds = jax.random.split(jax.random.key(seed), 19)
    return {
        "tokens": scatter_about(seeds[0], (PAGES, SEQ, D), 1.0, 6.0, ((0, 8), (1, 4)), jnp.float32),
        "valid_len": draw_valid_len(jax.random.fold_in(seeds[18], 71), 0),
        "query_weight": scatter_about(seeds[2], (D, D), D ** -0.5, 0.1875, ((0, 32),), jnp.float32),
        "query_bias": scatter_about(seeds[3], (D,), 0.5, 3.0, ((0, 32),), jnp.float32),
        "key_weight": scatter_about(seeds[4], (D, D), D ** -0.5, 0.1875, ((0, 32),), jnp.float32),
        "value_weight": scatter_about(seeds[5], (D, D), D ** -0.5, 0.1875, ((0, 32),), jnp.float32),
        "value_bias": scatter_about(seeds[6], (D,), 0.5, 3.0, ((0, 32),), jnp.float32),
        "output_weight": scatter_about(seeds[7], (D, D), (D // 16) ** -0.5, 0.75, ((0, 32),), jnp.float32),
        "output_bias": scatter_about(seeds[8], (D,), 0.5, 3.0, ((0, 32),), jnp.float32),
        "attn_gain": jnp.clip(1.0 + 0.15 * jax.random.normal(seeds[9], (D,), jnp.float32), 0.25, 1.75),
        "attn_shift": scatter_about(seeds[10], (D,), 0.5, 3.0, ((0, 32),), jnp.float32),
        "inner_weight": scatter_about(seeds[11], (D, FF), D ** -0.5, 0.1875, ((0, 32),), jnp.float32),
        "inner_bias": scatter_about(seeds[12], (FF,), 0.5, 3.0, ((0, 32),), jnp.float32),
        "outer_weight": scatter_about(seeds[13], (FF, D), FF ** -0.5, 0.09375, ((0, 32),), jnp.float32),
        "outer_bias": scatter_about(seeds[14], (D,), 0.5, 3.0, ((0, 32),), jnp.float32),
        "final_gain": jnp.clip(1.0 + 0.15 * jax.random.normal(seeds[15], (D,), jnp.float32), 0.25, 1.75),
        "final_shift": scatter_about(seeds[16], (D,), 0.5, 3.0, ((0, 32),), jnp.float32),
        "out_grad": heavy_noise(seeds[17], (PAGES, SEQ, D), 1.0, 6.0, ((0, 8), (1, 4)), (0, 2, 8, 2.0), jnp.float32),
    }


@jax.custom_vjp
def low(v):
    return lax.optimization_barrier(v.astype(jnp.bfloat16)).astype(jnp.float32)

@jax.custom_vjp
def low_back(v):
    return v

def low_keep(v):
    return (low(v), None)

def low_pass(kept, grad):
    return (grad,)

def back_keep(v):
    return (v, None)

def back_low(kept, grad):
    return (low(grad),)
low.defvjp(low_keep, low_pass)
low_back.defvjp(back_keep, back_low)
EPSILON = 1e-05
HIGHEST = lax.Precision.HIGHEST

def product(left, right):
    return jnp.dot(left, right, precision=HIGHEST, preferred_element_type=jnp.float32)

def layer_norm(values, gain, shift):
    center = values - lax.optimization_barrier(jnp.mean(values, axis=-1, keepdims=True))
    spread = lax.optimization_barrier(jnp.mean(center * center, axis=-1, keepdims=True))
    return center * lax.rsqrt(spread + EPSILON) * gain + shift

def forward(params, block_tokens, block_lengths):
    w_query, b_query, w_key, w_value, b_value, w_out, b_out, g_attn, s_attn, w_inner, b_inner, w_outer, b_outer, g_final, s_final = [low(piece) for piece in params]
    block_pages = block_tokens.shape[0]
    tok_rows = block_tokens.reshape(block_pages * SEQ, D)
    tok_low = low(tok_rows)
    queries = low(low_back(product(tok_low, w_query) + b_query))
    keys = low(low_back(product(tok_low, w_key)))
    values = low(low_back(product(tok_low, w_value) + b_value))
    q_heads = queries.reshape(block_pages, SEQ, HEADS, HEAD_DIM)
    k_heads = keys.reshape(block_pages, SEQ, HEADS, HEAD_DIM)
    v_heads = values.reshape(block_pages, SEQ, HEADS, HEAD_DIM)
    scores = low_back(jnp.einsum('pqhe,pkhe->phqk', q_heads, k_heads, precision=HIGHEST) * HEAD_DIM ** (-0.5))
    key_mask = jnp.arange(SEQ, dtype=jnp.int32)[None, :] < block_lengths[:, None]
    scores = jnp.where(key_mask[:, None, None, :], scores, -1000000000.0)
    probs = low(jax.nn.softmax(scores, axis=-1))
    context = jnp.einsum('phqk,pkhe->pqhe', probs, v_heads, precision=HIGHEST).reshape(block_pages * SEQ, D)
    context = low(low_back(context))
    attended = low_back(product(context, w_out) + b_out)
    hidden = layer_norm(tok_rows + attended, g_attn, s_attn)
    inner = low_back(product(low(hidden), w_inner) + b_inner)
    active = low(jax.nn.gelu(inner, approximate=False))
    outer = low_back(product(active, w_outer) + b_outer)
    result = layer_norm(hidden + outer, g_final, s_final)
    return result.reshape(block_tokens.shape)

def reference(tokens, valid_len, query_weight, query_bias, key_weight, value_weight, value_bias, output_weight, output_bias, attn_gain, attn_shift, inner_weight, inner_bias, outer_weight, outer_bias, final_gain, final_shift, out_grad):
    params = (query_weight, query_bias, key_weight, value_weight, value_bias, output_weight, output_bias, attn_gain, attn_shift, inner_weight, inner_bias, outer_weight, outer_bias, final_gain, final_shift)
    group = math.gcd(PAGES, max(1, 4096 // SEQ))
    blocks = PAGES // group
    tok_blocks = tokens.reshape(blocks, group, SEQ, D)
    len_blocks = valid_len.reshape(blocks, group)
    cot_blocks = out_grad.reshape(blocks, group, SEQ, D)

    def step(totals, block):
        block_tokens, block_lengths, block_cot = block
        result, pullback = jax.vjp(lambda params_in, tokens_in: forward(params_in, tokens_in, block_lengths), params, block_tokens)
        param_grads, token_grads = pullback(block_cot)
        totals = jax.tree.map(jnp.add, totals, param_grads)
        return (totals, (result, token_grads))
    initial = tuple((jnp.zeros_like(piece, dtype=jnp.float32) for piece in params))
    totals, (results, token_grads) = lax.scan(step, initial, (tok_blocks, len_blocks, cot_blocks))
    return (results.reshape(PAGES, SEQ, D), token_grads.reshape(PAGES, SEQ, D), totals[0], totals[1], totals[2], totals[3], totals[4], totals[5], totals[6], totals[7], totals[8], totals[9], totals[10], totals[11], totals[12], totals[13], totals[14])
```

```python
import functools
import math
import types

import jax
import jax.numpy as jnp
from jax import lax
from jax.experimental import pallas as pl
from jax.experimental.pallas import tpu as pltpu
from jax.sharding import PartitionSpec as P

HEAD_DIM = 64


EPSILON = 1e-05
INV_ROOT_TWO = 1.0 / math.sqrt(2.0)
INV_ROOT_TWO_PI = 1.0 / math.sqrt(2.0 * math.pi)


def product(left, right):
    return jnp.dot(left, right, preferred_element_type=jnp.float32)


def product_tn(left, right):
    return lax.dot_general(
        left, right, (((0,), (0,)), ((), ())), preferred_element_type=jnp.float32
    )


def product_nt(left, right):
    return lax.dot_general(
        left, right, (((1,), (1,)), ((), ())), preferred_element_type=jnp.float32
    )


def norm_parts(values):
    center = values - jnp.mean(values, axis=-1, keepdims=True)
    inverse = lax.rsqrt(jnp.mean(center * center, axis=-1, keepdims=True) + EPSILON)
    return (center * inverse, inverse)


def norm_backward(grad_out, normed, inverse, gain):
    scaled = grad_out * gain
    return inverse * (
        scaled
        - jnp.mean(scaled, axis=-1, keepdims=True)
        - normed * jnp.mean(scaled * normed, axis=-1, keepdims=True)
    )


def gelu_parts(values):
    cumulative = 0.5 * (1.0 + lax.erf(values * INV_ROOT_TWO))
    return (
        values * cumulative,
        cumulative + values * jnp.exp(-0.5 * values * values) * INV_ROOT_TWO_PI,
    )


def sequence_layer(tokens, valid_len, lowered, out_grad):
    fetched = (
        lax.all_gather(lowered[0], ("page", "seq"), axis=0, tiled=True),
        lax.all_gather(lowered[1], ("page", "seq"), axis=0, tiled=True),
        lax.all_gather(lowered[2], ("page", "seq"), axis=0, tiled=True),
        lax.all_gather(lowered[3], ("page", "seq"), axis=0, tiled=True),
        lax.all_gather(lowered[4], ("page", "seq"), axis=0, tiled=True),
        lax.all_gather(lowered[5], ("page", "seq"), axis=0, tiled=True),
        lax.all_gather(lowered[6], ("page", "seq"), axis=0, tiled=True),
        lax.all_gather(lowered[7], ("page", "seq"), axis=0, tiled=True),
        lax.all_gather(lowered[8], ("page", "seq"), axis=0, tiled=True),
        lax.all_gather(lowered[9], ("page", "seq"), axis=0, tiled=True),
        lax.all_gather(lowered[10], ("page", "seq"), axis=0, tiled=True),
        lax.all_gather(lowered[11], ("page", "seq"), axis=0, tiled=True),
        lax.all_gather(lowered[12], ("page", "seq"), axis=0, tiled=True),
        lax.all_gather(lowered[13], ("page", "seq"), axis=0, tiled=True),
        lax.all_gather(lowered[14], ("page", "seq"), axis=0, tiled=True),
    )
    (
        w_query,
        b_query,
        w_key,
        w_value,
        b_value,
        w_out,
        b_out,
        g_attn,
        s_attn,
        w_inner,
        b_inner,
        w_outer,
        b_outer,
        g_final,
        s_final,
    ) = fetched
    f32 = jnp.float32
    bf16 = jnp.bfloat16
    scale = HEAD_DIM ** (-0.5)
    page_count, span_len, width = tokens.shape
    heads = width // HEAD_DIM
    row_count = page_count * span_len
    tok_rows = tokens.reshape(row_count, width)
    tok_low = tok_rows.astype(bf16)
    q_low = (product(tok_low, w_query) + b_query.astype(f32)).astype(bf16)
    k_low = product(tok_low, w_key).astype(bf16)
    v_low = (product(tok_low, w_value) + b_value.astype(f32)).astype(bf16)
    k_full, v_full = (
        lax.all_gather(k_low.reshape(page_count, span_len, width), "seq", axis=1, tiled=True),
        lax.all_gather(v_low.reshape(page_count, span_len, width), "seq", axis=1, tiled=True),
    )
    seq_len = k_full.shape[1]
    q_heads = q_low.reshape(page_count, span_len, heads, HEAD_DIM)
    k_heads = k_full.reshape(page_count, seq_len, heads, HEAD_DIM)
    v_heads = v_full.reshape(page_count, seq_len, heads, HEAD_DIM)
    key_mask = (lax.broadcasted_iota(jnp.int32, (page_count, seq_len), 1) < valid_len[:, None])[
        :, None, None, :
    ]

    def masked_scores():
        raw = jnp.einsum("pqhe,pkhe->phqk", q_heads, k_heads, preferred_element_type=f32) * scale
        return jnp.where(key_mask, raw, -1000000000.0)

    scores = masked_scores()
    top_score = jnp.max(scores, axis=-1, keepdims=True)
    log_total = top_score + jnp.log(jnp.sum(jnp.exp(scores - top_score), axis=-1, keepdims=True))
    probs_low = jnp.exp(scores - log_total).astype(bf16)
    context = jnp.einsum("phqk,pkhe->pqhe", probs_low, v_heads, preferred_element_type=f32)
    ctx_low = context.reshape(row_count, width).astype(bf16)
    attended = product(ctx_low, w_out) + b_out.astype(f32)
    norm_one, inv_one = norm_parts(tok_rows + attended)
    hidden = norm_one * g_attn.astype(f32) + s_attn.astype(f32)
    hid_low = hidden.astype(bf16)
    inner = product(hid_low, w_inner) + b_inner.astype(f32)
    active, slope = gelu_parts(inner)
    act_low = active.astype(bf16)
    outer = product(act_low, w_outer) + b_outer.astype(f32)
    norm_two, inv_two = norm_parts(hidden + outer)
    result = norm_two * g_final.astype(f32) + s_final.astype(f32)
    (
        w_query,
        b_query,
        w_key,
        w_value,
        b_value,
        w_out,
        b_out,
        g_attn,
        s_attn,
        w_inner,
        b_inner,
        w_outer,
        b_outer,
        g_final,
        s_final,
    ) = (
        lax.all_gather(lowered[0], ("page", "seq"), axis=0, tiled=True),
        lax.all_gather(lowered[1], ("page", "seq"), axis=0, tiled=True),
        lax.all_gather(lowered[2], ("page", "seq"), axis=0, tiled=True),
        lax.all_gather(lowered[3], ("page", "seq"), axis=0, tiled=True),
        lax.all_gather(lowered[4], ("page", "seq"), axis=0, tiled=True),
        lax.all_gather(lowered[5], ("page", "seq"), axis=0, tiled=True),
        lax.all_gather(lowered[6], ("page", "seq"), axis=0, tiled=True),
        lax.all_gather(lowered[7], ("page", "seq"), axis=0, tiled=True),
        lax.all_gather(lowered[8], ("page", "seq"), axis=0, tiled=True),
        lax.all_gather(lowered[9], ("page", "seq"), axis=0, tiled=True),
        lax.all_gather(lowered[10], ("page", "seq"), axis=0, tiled=True),
        lax.all_gather(lowered[11], ("page", "seq"), axis=0, tiled=True),
        lax.all_gather(lowered[12], ("page", "seq"), axis=0, tiled=True),
        lax.all_gather(lowered[13], ("page", "seq"), axis=0, tiled=True),
        lax.all_gather(lowered[14], ("page", "seq"), axis=0, tiled=True),
    )
    grad_rows = out_grad.reshape(row_count, width)
    grad_gfinal = jnp.sum(grad_rows * norm_two, axis=0)
    grad_sfinal = jnp.sum(grad_rows, axis=0)
    grad_sum = norm_backward(grad_rows, norm_two, inv_two, g_final.astype(f32))
    grad_f_low = grad_sum.astype(bf16)
    grad_bouter = jnp.sum(grad_f_low.astype(f32), axis=0)
    grad_wouter = product_tn(act_low, grad_f_low)
    grad_active = product_nt(grad_f_low, w_outer)
    grad_in_low = (grad_active * slope).astype(bf16)
    grad_binner = jnp.sum(grad_in_low.astype(f32), axis=0)
    grad_winner = product_tn(hid_low, grad_in_low)
    grad_hidden = grad_sum + product_nt(grad_in_low, w_inner)
    grad_gattn = jnp.sum(grad_hidden * norm_one, axis=0)
    grad_sattn = jnp.sum(grad_hidden, axis=0)
    grad_mixed = norm_backward(grad_hidden, norm_one, inv_one, g_attn.astype(f32))
    grad_att_low = grad_mixed.astype(bf16)
    grad_bout = jnp.sum(grad_att_low.astype(f32), axis=0)
    grad_wout = product_tn(ctx_low, grad_att_low)
    grad_ctx = (
        product_nt(grad_att_low, w_out).astype(bf16).reshape(page_count, span_len, heads, HEAD_DIM)
    )
    probs = jnp.exp(masked_scores() - log_total)
    probs_low = probs.astype(bf16)
    grad_probs = jnp.einsum("pqhe,pkhe->phqk", grad_ctx, v_heads, preferred_element_type=f32)
    grad_vfull = jnp.einsum("phqk,pqhe->pkhe", probs_low, grad_ctx, preferred_element_type=f32)
    grad_scores = (
        probs * (grad_probs - jnp.sum(grad_probs * probs, axis=-1, keepdims=True))
    ).astype(bf16)
    grad_q_low = (
        (jnp.einsum("phqk,pkhe->pqhe", grad_scores, k_heads, preferred_element_type=f32) * scale)
        .astype(bf16)
        .reshape(row_count, width)
    )
    grad_kfull = (
        jnp.einsum("phqk,pqhe->pkhe", grad_scores, q_heads, preferred_element_type=f32) * scale
    )
    grad_keys, grad_values = (
        lax.psum_scatter(
            grad_kfull.reshape(page_count, seq_len, width).astype(jnp.bfloat16),
            "seq",
            scatter_dimension=1,
            tiled=True,
        ).astype(jnp.float32),
        lax.psum_scatter(
            grad_vfull.reshape(page_count, seq_len, width).astype(jnp.bfloat16),
            "seq",
            scatter_dimension=1,
            tiled=True,
        ).astype(jnp.float32),
    )
    grad_k_low = grad_keys.reshape(row_count, width).astype(bf16)
    grad_v_low = grad_values.reshape(row_count, width).astype(bf16)
    grad_tokens = (
        grad_mixed
        + product_nt(grad_q_low, w_query)
        + product_nt(grad_k_low, w_key)
        + product_nt(grad_v_low, w_value)
    )
    grad_wquery = product_tn(tok_low, grad_q_low)
    grad_bquery = jnp.sum(grad_q_low.astype(f32), axis=0)
    grad_wkey = product_tn(tok_low, grad_k_low)
    grad_wvalue = product_tn(tok_low, grad_v_low)
    grad_bvalue = jnp.sum(grad_v_low.astype(f32), axis=0)
    owned = (
        lax.psum_scatter(grad_wquery, ("page", "seq"), scatter_dimension=0, tiled=True),
        lax.psum_scatter(grad_bquery, ("page", "seq"), scatter_dimension=0, tiled=True),
        lax.psum_scatter(grad_wkey, ("page", "seq"), scatter_dimension=0, tiled=True),
        lax.psum_scatter(grad_wvalue, ("page", "seq"), scatter_dimension=0, tiled=True),
        lax.psum_scatter(grad_bvalue, ("page", "seq"), scatter_dimension=0, tiled=True),
        lax.psum_scatter(grad_wout, ("page", "seq"), scatter_dimension=0, tiled=True),
        lax.psum_scatter(grad_bout, ("page", "seq"), scatter_dimension=0, tiled=True),
        lax.psum_scatter(grad_gattn, ("page", "seq"), scatter_dimension=0, tiled=True),
        lax.psum_scatter(grad_sattn, ("page", "seq"), scatter_dimension=0, tiled=True),
        lax.psum_scatter(grad_winner, ("page", "seq"), scatter_dimension=0, tiled=True),
        lax.psum_scatter(grad_binner, ("page", "seq"), scatter_dimension=0, tiled=True),
        lax.psum_scatter(grad_wouter, ("page", "seq"), scatter_dimension=0, tiled=True),
        lax.psum_scatter(grad_bouter, ("page", "seq"), scatter_dimension=0, tiled=True),
        lax.psum_scatter(grad_gfinal, ("page", "seq"), scatter_dimension=0, tiled=True),
        lax.psum_scatter(grad_sfinal, ("page", "seq"), scatter_dimension=0, tiled=True),
    )
    return (
        result.reshape(tokens.shape),
        grad_tokens.reshape(tokens.shape),
        owned[0],
        owned[1],
        owned[2],
        owned[3],
        owned[4],
        owned[5],
        owned[6],
        owned[7],
        owned[8],
        owned[9],
        owned[10],
        owned[11],
        owned[12],
        owned[13],
        owned[14],
    )


MESH = pl.DeviceIdType.MESH
BF16 = jnp.bfloat16
F32 = jnp.float32
VECTORS = 8
SLAB = 16
NEGATIVE = -1000000000.0


def dot_nn(left, right):
    return lax.dot_general(left, right, (((1,), (0,)), ((), ())), preferred_element_type=F32)


def dot_nt(left, right):
    return lax.dot_general(left, right, (((1,), (1,)), ((), ())), preferred_element_type=F32)


def dot_tn(left, right):
    return lax.dot_general(left, right, (((0,), (0,)), ((), ())), preferred_element_type=F32)


class Sizes:
    def __init__(self, mesh, width, units, span):
        self.pages = mesh.shape["page"]
        self.parts = mesh.shape["seq"]
        self.half = self.pages // 2
        self.width = width
        self.units = units
        self.span = span
        self.length = span * self.parts
        self.row = width // (self.pages * self.parts)
        self.rows = self.row * self.parts
        self.unit = units // (self.pages * self.parts)
        self.mine = self.unit * self.pages
        self.cols = width // self.parts
        self.heads = self.cols // HEAD_DIM


def supported(mesh, token_shape, width, units):
    pages, parts = mesh.shape["page"], mesh.shape["seq"]
    return (
        parts == 4
        and pages % 2 == 0
        and pages >= 4
        and token_shape[0] == pages
        and token_shape[1] % (parts * 128) == 0
        and width % (pages * parts * 32) == 0
        and width // pages == 128
        and units % (pages * parts * 128) == 0
        and (width // parts) % 128 == 0
    )


def layer_kernel(z, names, *refs):
    r = types.SimpleNamespace(**dict(zip(names, refs)))
    send_sem, recv_sem = r.send_sem, r.recv_sem
    page = lax.axis_index("page")
    part = lax.axis_index("seq")
    counter = [0]
    sent = []

    def slots(count):
        first = counter[0]
        counter[0] += count
        return first

    odd = page % 2
    place = odd * (z.pages - 1 - page // 2) + (1 - odd) * (page // 2)

    def page_at(index):
        index = (index + 2 * z.pages) % z.pages
        late = index // z.half
        return (1 - late) * (2 * index) + late * (2 * z.pages - 1 - 2 * index)

    def peer(j):
        return ((part // 2 + j // 2) % 2) * 2 + (part % 2 + j % 2) % 2

    rank = page * z.parts + part
    hold_page, hold_part = rank % z.pages, rank // z.pages
    flat = part * z.pages + page
    own_page, own_part = flat // z.parts, flat % z.parts
    moves = 1 - (1 - jnp.minimum(1, (hold_page - page) * (hold_page - page))) * (
        1 - jnp.minimum(1, (hold_part - part) * (hold_part - part))
    )

    def copy(src, dst, index, device):
        return pltpu.make_async_remote_copy(
            src_ref=src,
            dst_ref=dst,
            send_sem=send_sem.at[index],
            recv_sem=recv_sem.at[index],
            device_id=device,
            device_id_type=MESH,
        )

    def block(ref, index, size):
        return ref.at[pl.ds(pl.multiple_of(index * size, size), size)]

    barrier = pltpu.get_barrier_semaphore()

    def greet(device):
        pl.semaphore_signal(barrier, inc=1, device_id=device, device_id_type=MESH)

    for j in (1, 2, 3):
        greet((page, peer(j)))
    greet((page_at(place + 1), part))
    greet((page_at(place - 1), part))

    @pl.when(moves == 1)
    def _():
        greet((hold_page, hold_part))
        greet((own_page, own_part))

    class Share:
        def __init__(self, ref, size):
            self.ref, self.size, self.first = ref, size, slots(4)

        def copy(self, j, owner):
            piece = block(self.ref, owner, self.size)
            return copy(piece, piece, self.first + j, (page, peer(j)))

        def start(self):
            for j in (2, 3, 1):
                self.copy(j, part).start()
            sent.append(lambda: [self.copy(j, part).wait_send() for j in (1, 2, 3)])

        def wait(self, j):
            self.copy(j, peer(j)).wait_recv()

        def wait_all(self):
            for j in (1, 2, 3):
                self.wait(j)

    class Spread:
        def __init__(self, src, dst, size):
            self.src, self.dst, self.size, self.first = src, dst, size, slots(4)

        def copy(self, j):
            return copy(
                block(self.src, peer(j), self.size),
                self.dst.at[j],
                self.first + j,
                (page, peer(j)),
            )

        def start(self, j):
            self.copy(j).start()

        def start_all(self):
            for j in (2, 3, 1):
                self.start(j)

        def finish(self):
            sent.append(lambda: [self.copy(j).wait_send() for j in (1, 2, 3)])

        def wait(self, j):
            self.copy(j).wait_recv()

    class Place:
        def __init__(self, src, dst, size, base):
            self.src, self.dst, self.size, self.base, self.first = src, dst, size, base, slots(4)

        def copy(self, j, owner):
            return copy(
                block(self.src, peer(j), self.size),
                block(self.dst, self.base + owner, self.size),
                self.first + j,
                (page, peer(j)),
            )

        def start(self):
            for j in (2, 3, 1):
                self.copy(j, part).start()
            sent.append(lambda: [self.copy(j, part).wait_send() for j in (1, 2, 3)])

        def wait(self):
            for j in (1, 2, 3):
                self.copy(j, peer(j)).wait_recv()

    class Gather:
        def __init__(self, ref, size):
            self.ref, self.size = ref, size
            self.first = slots(2 * z.half)

        def copy(self, t, d, index):
            piece = block(self.ref, page_at(index), self.size)
            if t == z.half - 1:
                h = self.size // 2
                piece = piece.at[pl.ds(d * h, h)]
            return copy(
                piece, piece, self.first + 2 * t + d, (page_at(place + 1 - 2 * d), part)
            )

        def wait(self, t):
            for d in (0, 1):
                self.copy(t, d, place - (1 - 2 * d) * (1 + t)).wait_recv()

        def step(self, t):
            if t > 0:
                self.wait(t - 1)
            for d in (0, 1):
                self.copy(t, d, place - (1 - 2 * d) * t).start()
                sent.append(
                    functools.partial(
                        lambda t, d: self.copy(t, d, place - (1 - 2 * d) * t).wait_send(), t, d
                    )
                )

        def done(self):
            self.wait(z.half - 1)

    class Reduce:
        def __init__(self, slot, stage, local, shape, kind):
            self.slot, self.stage, self.local = slot, stage, local
            self.size, self.kind = shape[0], kind
            self.first = slots(2 * z.half)

        def copy(self, t, d):
            h = self.size // 2
            if t == 0:
                src = self.stage.at[pl.ds(d * h, h)]
                dst = self.slot.at[d, 0, pl.ds(d * h, h)]
            else:
                src = self.slot.at[d, t - 1]
                dst = self.slot.at[d, t]
            return copy(src, dst, self.first + 2 * t + d, (page_at(place + 1 - 2 * d), part))

        def step(self, t):
            h = self.size // 2
            if t == 0:
                self.stage[...] = self.local(page_at(place + z.half)).astype(self.kind)
                for d in (0, 1):
                    self.copy(0, d).start()
            else:
                for d in (0, 1):
                    term = self.local(page_at(place + (1 - 2 * d) * (z.half - t)))
                    self.copy(t - 1, d).wait_recv()
                    held = self.slot.at[d, t - 1]
                    if t == 1:
                        near, far = pl.ds(d * h, h), pl.ds((1 - d) * h, h)
                        part_near = term[d * h : (d + 1) * h]
                        part_far = term[(1 - d) * h : (2 - d) * h]
                        held[near] = (held[near].astype(F32) + part_near).astype(self.kind)
                        held[far] = part_far.astype(self.kind)
                    else:
                        held[...] = (held[...].astype(F32) + term).astype(self.kind)
                    self.copy(t, d).start()
            for d in (0, 1):
                sent.append(functools.partial(lambda t, d: self.copy(t, d).wait_send(), t, d))

        def total(self):
            term = self.local(page)
            for d in (0, 1):
                self.copy(z.half - 1, d).wait_recv()
            last = z.half - 1
            return term + self.slot[0, last].astype(F32) + self.slot[1, last].astype(F32)

    c, w, n = z.cols, z.width, z.span
    for q in range(z.parts):
        rows = pl.ds(q * z.row, z.row)
        for i, weight in enumerate((r.w_query, r.w_key, r.w_value)):
            r.cut_qkv[rows, i * c : (i + 1) * c] = weight[:, q * c : (q + 1) * c].astype(BF16)
        for g in range(z.pages):
            at = (z.parts * g + q) * z.unit
            r.cut_inner[rows, g * z.unit : (g + 1) * z.unit] = r.w_inner[
                :, at : at + z.unit
            ].astype(BF16)
    r.own_out[...] = r.w_out[...].astype(BF16)
    r.tok_all[pl.ds(pl.multiple_of(part * n, n), n), :] = r.tokens[...].astype(BF16)
    base = pl.multiple_of(rank * SLAB, SLAB)
    for i, small in enumerate(
        (r.b_query, r.b_value, r.b_out, r.g_attn, r.s_attn, r.b_outer, r.g_final, r.s_final)
    ):
        r.vec_all[pl.ds(base + i, 1), 0 : z.row] = small[...]
    r.vec_all[pl.ds(base + VECTORS, 1), :] = r.b_inner[...]

    cut_qkv = Place(r.cut_qkv, r.qkv_w, z.row, page * z.parts)
    cut_inner = Place(r.cut_inner, r.inner_w, z.row, page * z.parts)
    share_tok = Share(r.tok_all, n)

    class ShareVec:
        first = slots(4)

        def copy(self, j, owner):
            piece = block(r.vec_all, page * z.parts + owner, SLAB)
            return copy(piece, piece, self.first + j, (page, peer(j)))

    vec_share = ShareVec()
    hold = slots(1)

    def hold_copy():
        return copy(
            r.own_out, block(r.out_w, own_slot_page, z.row), hold, (hold_page, hold_part)
        )

    own_slot_page = hold_page
    pl.semaphore_wait(barrier, 5 + 2 * moves)
    cut_qkv.start()
    for j in (2, 3, 1):
        vec_share.copy(j, part).start()
    sent.append(lambda: [vec_share.copy(j, part).wait_send() for j in (1, 2, 3)])
    share_tok.start()

    @pl.when(moves == 1)
    def _():
        hold_copy().start()

    @pl.when(moves == 0)
    def _():
        r.out_w[pl.ds(pl.multiple_of(page * z.row, z.row), z.row), :] = r.own_out[...]

    cut_inner.start()
    own_rows = pl.ds(pl.multiple_of(rank * z.row, z.row), z.row)
    cut_rows = pl.ds(pl.multiple_of(part * z.row, z.row), z.row)
    r.qkv_w[own_rows, :] = r.cut_qkv[cut_rows, :]
    r.inner_w[own_rows, :] = r.cut_inner[cut_rows, :]
    r.outer_w[pl.ds(pl.multiple_of(page * z.unit, z.unit), z.unit), :] = r.w_outer[
        ...
    ].astype(BF16)

    ring_qkv = Gather(r.qkv_w, z.rows)
    ring_vec = Gather(r.vec_all, z.parts * SLAB)
    ring_inner = Gather(r.inner_w, z.rows)
    ring_out = Gather(r.out_w, z.row)
    ring_outer = Gather(r.outer_w, z.unit)

    cut_qkv.wait()
    ring_qkv.step(0)
    for j in (1, 2, 3):
        vec_share.copy(j, peer(j)).wait_recv()
    ring_vec.step(0)
    for t in range(1, z.half):
        ring_qkv.step(t)
        ring_vec.step(t)

    @pl.when(moves == 1)
    def _():
        copy(
            r.own_out, block(r.out_w, page, z.row), hold, (hold_page, hold_part)
        ).wait_recv()

    ring_out.step(0)
    cut_inner.wait()
    ring_inner.step(0)
    ring_qkv.done()
    ring_vec.done()

    lane = lax.broadcasted_iota(jnp.int32, (VECTORS, 128), 1)
    for g in range(z.pages):
        total = jnp.zeros((VECTORS, 128), F32)
        for q in range(z.parts):
            tile = r.vec_all[pl.ds((g * z.parts + q) * SLAB, VECTORS), :]
            if q:
                tile = pltpu.roll(tile, q * z.row, 1)
            total = total + jnp.where(lane // z.row == q, tile, 0.0)
        r.vecs[:, g * 128 : (g + 1) * 128] = total.astype(BF16).astype(F32)
        at = pl.multiple_of((g * z.parts + part) * SLAB + VECTORS, VECTORS)
        tile = r.vec_all[pl.ds(at, 8), :]
        r.b_mine[:, g * z.unit : (g + 1) * z.unit] = tile[0:1].astype(BF16).astype(F32)

    def vector(i):
        return r.vecs[i : i + 1, :]

    my_cols = pl.ds(pl.multiple_of(part * c, c), c)

    share_tok.wait_all()

    def make_qkv(b, carry):
        rows = pl.ds(pl.multiple_of(b * n, n), n)
        out = dot_nn(r.tok_all[rows, :], r.qkv_w[...])
        r.qkv[rows, 0:c] = (out[:, 0:c] + r.vecs[0:1, my_cols]).astype(BF16)
        r.qkv[rows, c : 2 * c] = out[:, c : 2 * c].astype(BF16)
        r.qkv[rows, 2 * c :] = (out[:, 2 * c :] + r.vecs[1:2, my_cols]).astype(BF16)
        return carry

    lax.fori_loop(0, z.parts, make_qkv, 0)
    ring_out.step(1)
    ring_inner.step(1)

    scale = HEAD_DIM ** (-0.5)
    first_head = lax.broadcasted_iota(jnp.int32, (n, 128), 1) < HEAD_DIM
    key_place = lax.broadcasted_iota(jnp.int32, (n, z.length), 1)
    valid = r.valid[0]

    def pair_cols(kind, pair):
        return pl.ds(kind * c + pair * 128, 128)

    def attend(pair):
        def body(b, carry):
            rows = pl.ds(pl.multiple_of(b * n, n), n)
            queries = r.qkv[rows, pair_cols(0, pair)]
            keys = r.qkv[:, pair_cols(1, pair)]
            values = r.qkv[:, pair_cols(2, pair)]
            outs = []
            for h in range(2):
                mine = first_head if h == 0 else ~first_head
                scores = dot_nt(jnp.where(mine, queries, jnp.zeros_like(queries)), keys) * scale
                scores = jnp.where(key_place < valid, scores, NEGATIVE)
                top = jnp.max(scores, axis=-1, keepdims=True)
                weight = jnp.exp(scores - top)
                probs = weight * (1.0 / jnp.sum(weight, axis=-1, keepdims=True))
                r.probs[2 * pair + h, rows, :] = probs
                outs.append(dot_nn(probs.astype(BF16), values))
            r.ctx[rows, pl.ds(pair * 128, 128)] = jnp.where(first_head, outs[0], outs[1]).astype(
                BF16
            )
            return carry

        lax.fori_loop(0, z.parts, body, 0)

    attend(0)
    ring_out.step(2)
    ring_inner.step(2)
    ring_outer.step(0)
    attend(1)
    ring_out.step(3)
    ring_inner.step(3)
    ring_outer.step(1)
    ring_out.done()

    def partial_rows(phase, make):
        spread = Spread(r.part_out.at[phase], r.part_in.at[phase], n)

        def body(i, carry):
            j = (i + 1) % 4
            b = peer(j)
            rows = pl.ds(pl.multiple_of(b * n, n), n)
            term = make(rows, j)

            @pl.when(j > 0)
            def _():
                r.part_out[phase, rows, :] = term.astype(BF16)
                spread.start(j)

            @pl.when(j == 0)
            def _():
                r.part_own[...] = term

            return carry

        lax.fori_loop(0, z.parts, body, 0)
        spread.finish()
        return spread

    def row_sum(phase, rows):
        total = r.part_own[rows, :]
        for j in (1, 2, 3):
            total = total + r.part_in[phase, j, rows, :].astype(F32)
        return total

    def by_rows(fn):
        size = 32

        def body(i, carry):
            fn(pl.ds(pl.multiple_of(i * size, size), size), pl.multiple_of(i * size, size))
            return carry

        lax.fori_loop(0, n // size, body, 0)

    def add_column_sum(i, values):
        r.sums[i : i + 1, :] += jnp.sum(values, axis=0, keepdims=True)

    r.sums[...] = jnp.zeros_like(r.sums)

    spread = partial_rows(0, lambda rows, j: dot_nn(r.ctx[rows, :], r.out_w[...]))
    ring_outer.step(2)
    for j in (1, 2, 3):
        spread.wait(j)

    share_hid = Share(r.hid_all, n)

    def first_norm(rows, at):
        mixed = r.tokens[rows, :] + (row_sum(0, rows) + vector(2))
        normed, inverse = norm_parts(mixed)
        hidden = normed * vector(3) + vector(4)
        r.norm_one[rows, :] = normed
        r.inv_one[rows, :] = inverse
        r.hidden[rows, :] = hidden
        r.hid_all[pl.ds(pl.multiple_of(part * n + at, 32), 32), :] = hidden.astype(BF16)

    by_rows(first_norm)
    share_hid.start()
    ring_outer.step(3)
    ring_inner.done()

    def make_inner(j, carry):
        @pl.when(j > 0)
        def _():
            share_hid.copy(j, peer(j)).wait_recv()

        rows = pl.ds(pl.multiple_of(peer(j) * n, n), n)
        tile = 256

        def columns(i, carry):
            cols = pl.ds(pl.multiple_of(i * tile, tile), tile)
            inner = dot_nn(r.hid_all[rows, :], r.inner_w[:, cols]) + r.b_mine[:, cols]
            active, slope = gelu_parts(inner)
            r.active[rows, cols] = active.astype(BF16)
            r.slope[rows, cols] = slope
            return carry

        return lax.fori_loop(0, z.mine // tile, columns, carry)

    lax.fori_loop(0, z.parts, make_inner, 0)
    ring_outer.done()
    spread = partial_rows(1, lambda rows, j: dot_nn(r.active[rows, :], r.outer_w[...]))
    for j in (1, 2, 3):
        spread.wait(j)

    share_gf = Share(r.gf_all, n)

    def second_norm(rows, at):
        outer = row_sum(1, rows) + vector(5)
        normed, inverse = norm_parts(r.hidden[rows, :] + outer)
        r.o_out[rows, :] = normed * vector(6) + vector(7)
        grad = r.out_grad[rows, :]
        add_column_sum(6, grad * normed)
        add_column_sum(7, grad)
        grad_sum = norm_backward(grad, normed, inverse, vector(6))
        low = grad_sum.astype(BF16)
        add_column_sum(5, low.astype(F32))
        r.grad_sum[rows, :] = grad_sum
        r.gf_all[pl.ds(pl.multiple_of(part * n + at, 32), 32), :] = low

    by_rows(second_norm)
    share_gf.start()

    def chunk_term(left, right, size):
        def local(g):
            cols = pl.ds(pl.multiple_of(g * size, size), size)
            return dot_tn(left[:, cols], right[...])

        return local

    reduce_outer = Reduce(
        r.slot_outer, r.stage_outer, chunk_term(r.active, r.gf_all, z.unit), (z.unit, w), BF16
    )
    reduce_inner = Reduce(
        r.slot_inner, r.stage_inner, chunk_term(r.hid_all, r.grad_inner, z.rows),
        (z.rows, z.mine), BF16,
    )
    reduce_qkv = Reduce(
        r.slot_qkv, r.stage_qkv, chunk_term(r.tok_all, r.grad_qkv, z.rows),
        (z.rows, 3 * c), BF16,
    )
    reduce_out = Reduce(
        r.slot_out, r.stage_out,
        lambda g: r.term_out[pl.ds(pl.multiple_of(g * z.row, z.row), z.row), :], (z.row, w), BF16,
    )
    reduce_vec = Reduce(
        r.slot_vec, r.stage_vec,
        lambda g: r.term_vec[pl.ds(pl.multiple_of(g * SLAB, SLAB), SLAB), :], (SLAB, 128), F32,
    )

    r.b_sum[...] = jnp.zeros_like(r.b_sum)

    def make_grad_inner(rows, j):
        @pl.when(j > 0)
        def _():
            share_gf.copy(j, peer(j)).wait_recv()

        tile = 256

        def columns(i, carry):
            cols = pl.ds(pl.multiple_of(i * tile, tile), tile)
            grad = dot_nt(r.gf_all[rows, :], r.outer_w[cols, :]) * r.slope[rows, cols]
            low = grad.astype(BF16)
            r.grad_inner[rows, cols] = low
            r.b_sum[:, cols] += jnp.sum(low.astype(F32), axis=0, keepdims=True)
            return carry

        lax.fori_loop(0, z.mine // tile, columns, 0)
        return dot_nt(r.grad_inner[rows, :], r.inner_w[...])

    spread = partial_rows(2, make_grad_inner)
    reduce_outer.step(0)
    reduce_inner.step(0)
    for j in (1, 2, 3):
        spread.wait(j)

    share_ga = Share(r.ga_all, n)

    def first_norm_back(rows, at):
        grad = r.grad_sum[rows, :] + row_sum(2, rows)
        normed = r.norm_one[rows, :]
        add_column_sum(3, grad * normed)
        add_column_sum(4, grad)
        mixed = norm_backward(grad, normed, r.inv_one[rows, :], vector(3))
        low = mixed.astype(BF16)
        add_column_sum(2, low.astype(F32))
        r.grad_mixed[rows, :] = mixed
        r.ga_all[pl.ds(pl.multiple_of(part * n + at, 32), 32), :] = low

    by_rows(first_norm_back)
    share_ga.start()
    reduce_outer.step(1)
    reduce_inner.step(1)

    def make_grad_ctx(j, carry):
        @pl.when(j > 0)
        def _():
            share_ga.copy(j, peer(j)).wait_recv()

        rows = pl.ds(pl.multiple_of(peer(j) * n, n), n)
        r.grad_ctx[rows, :] = dot_nt(r.ga_all[rows, :], r.out_w[...]).astype(BF16)
        return carry

    lax.fori_loop(0, z.parts, make_grad_ctx, 0)
    r.term_out[...] = dot_tn(r.ctx[...], r.ga_all[...])
    reduce_out.step(0)

    def attend_back(pair):
        r.grad_kv[...] = jnp.zeros_like(r.grad_kv)

        def body(b, carry):
            rows = pl.ds(pl.multiple_of(b * n, n), n)
            queries = r.qkv[rows, pair_cols(0, pair)]
            keys = r.qkv[:, pair_cols(1, pair)]
            values = r.qkv[:, pair_cols(2, pair)]
            grad = r.grad_ctx[rows, pl.ds(pair * 128, 128)]
            outs = []
            for h in range(2):
                mine = first_head if h == 0 else ~first_head
                grad_mine = jnp.where(mine, grad, jnp.zeros_like(grad))
                query_mine = jnp.where(mine, queries, jnp.zeros_like(queries))
                probs = r.probs[2 * pair + h, rows, :]
                grad_probs = dot_nt(grad_mine, values)
                r.grad_kv[1] += dot_tn(probs.astype(BF16), grad_mine)
                inside = jnp.sum(grad_probs * probs, axis=-1, keepdims=True)
                grad_scores = (probs * (grad_probs - inside)).astype(BF16)
                outs.append(dot_nn(grad_scores, keys))
                r.grad_kv[0] += dot_tn(grad_scores, query_mine)
            r.grad_qkv[rows, pair_cols(0, pair)] = (
                jnp.where(first_head, outs[0], outs[1]) * scale
            ).astype(BF16)
            return carry

        lax.fori_loop(0, z.parts, body, 0)
        r.grad_qkv[:, pair_cols(1, pair)] = (r.grad_kv[0] * scale).astype(BF16)
        r.grad_qkv[:, pair_cols(2, pair)] = r.grad_kv[1].astype(BF16)

    attend_back(0)
    reduce_outer.step(2)
    reduce_inner.step(2)
    reduce_out.step(1)
    attend_back(1)
    reduce_outer.step(3)
    reduce_inner.step(3)
    reduce_out.step(2)
    reduce_qkv.step(0)

    r.sums[0:1, my_cols] = jnp.sum(r.grad_qkv[:, 0:c].astype(F32), axis=0, keepdims=True)
    r.sums[1:2, my_cols] = jnp.sum(r.grad_qkv[:, 2 * c :].astype(F32), axis=0, keepdims=True)
    r.term_vec[...] = jnp.zeros_like(r.term_vec)
    for g in range(z.pages):
        r.term_vec[g * SLAB : g * SLAB + VECTORS, :] = r.sums[:, g * 128 : (g + 1) * 128]
        r.term_vec[g * SLAB + VECTORS : g * SLAB + VECTORS + 1, :] = r.b_sum[
            :, g * z.unit : (g + 1) * z.unit
        ]
    reduce_vec.step(0)

    spread = partial_rows(3, lambda rows, j: dot_nt(r.grad_qkv[rows, :], r.qkv_w[...]))
    reduce_out.step(3)
    reduce_qkv.step(1)
    reduce_vec.step(1)

    r.o_outer[...] = reduce_outer.total()
    r.fin_inner[...] = reduce_inner.total().astype(BF16)
    fin_inner = Spread(r.fin_inner, r.got_inner, z.row)
    fin_inner.start_all()
    fin_inner.finish()
    reduce_qkv.step(2)
    reduce_vec.step(2)
    for j in (1, 2, 3):
        spread.wait(j)

    def input_rows(rows, at):
        r.o_grad[rows, :] = r.grad_mixed[rows, :] + row_sum(3, rows)

    by_rows(input_rows)
    r.fin_out[...] = reduce_out.total().astype(BF16)
    home = slots(1)

    def home_copy():
        return copy(r.fin_out, r.got_out, home, (own_page, own_part))

    @pl.when(moves == 1)
    def _():
        home_copy().start()

    @pl.when(moves == 0)
    def _():
        r.got_out[...] = r.fin_out[...]

    reduce_qkv.step(3)
    reduce_vec.step(3)
    r.fin_vec[...] = reduce_vec.total()

    class VecAll:
        first = slots(4)

        def copy(self, j):
            return copy(r.fin_vec, r.got_vec.at[j], self.first + j, (page, peer(j)))

    fin_vec = VecAll()
    for j in (2, 3, 1):
        fin_vec.copy(j).start()
    sent.append(lambda: [fin_vec.copy(j).wait_send() for j in (1, 2, 3)])
    r.fin_qkv[...] = reduce_qkv.total().astype(BF16)
    fin_qkv = Spread(r.fin_qkv, r.got_qkv, z.row)
    fin_qkv.start_all()
    fin_qkv.finish()

    my_rows = pl.ds(pl.multiple_of(part * z.row, z.row), z.row)

    def deliver(spread, mine, got, out):
        for j in range(4):
            if j:
                spread.wait(j)
            value = got[j] if j else mine[my_rows, :]
            out[peer(j)] = value

    deliver(fin_inner, r.fin_inner, r.got_inner, r.o_inner)

    @pl.when(moves == 1)
    def _():
        home_copy().wait_recv()

    r.o_wout[...] = r.got_out[...]
    summed = r.fin_vec[0:VECTORS, :]
    for j in (1, 2, 3):
        fin_vec.copy(j).wait_recv()
        summed = summed + r.got_vec[j, 0:VECTORS, :]
    r.o_vec[0:VECTORS, :] = pltpu.roll(summed, (128 - part * z.row) % 128, 1)
    r.o_vec[VECTORS:, :] = r.fin_vec[VECTORS:, :]
    deliver(fin_qkv, r.fin_qkv, r.got_qkv, r.o_qkv)

    for wait in sent:
        wait()

    @pl.when(moves == 1)
    def _():
        hold_copy().wait_send()
        home_copy().wait_send()

    assert counter[0] <= z.sems, counter[0]


def finish_kernel(z, out, grad, outer, inner, qkv, wout, vec, *outs):
    (o_out, o_grad, o_wq, o_bq, o_wk, o_wv, o_bv, o_wo, o_bo, o_ga, o_sa, o_wi, o_bi, o_wu, o_bu, o_gf, o_sf) = outs
    o_out[...] = out[...]
    o_grad[...] = grad[...]
    o_wu[...] = outer[...]
    o_wo[...] = wout[...].astype(F32)
    c = z.cols
    for q in range(z.parts):
        for i, ref in enumerate((o_wq, o_wk, o_wv)):
            ref[:, q * c : (q + 1) * c] = qkv[q, :, i * c : (i + 1) * c].astype(F32)
        for g in range(z.pages):
            at = (z.parts * g + q) * z.unit
            o_wi[:, at : at + z.unit] = inner[q, :, g * z.unit : (g + 1) * z.unit].astype(F32)
    for i, ref in enumerate((o_bq, o_bv, o_bo, o_ga, o_sa, o_bu, o_gf, o_sf)):
        ref[...] = vec[i : i + 1, 0 : z.row]
    o_bi[...] = vec[VECTORS : VECTORS + 1, :]


def paged_layer(z, tokens, valid_len, params, out_grad):
    (
        w_query, b_query, w_key, w_value, b_value, w_out, b_out, g_attn, s_attn,
        w_inner, b_inner, w_outer, b_outer, g_final, s_final,
    ) = params
    flat = lambda v: v.reshape(1, v.shape[0])
    c, w, n, ln, half = z.cols, z.width, z.span, z.length, z.half
    ins = dict(
        valid=valid_len,
        tokens=tokens.reshape(n, w),
        out_grad=out_grad.reshape(n, w),
        w_query=w_query, w_key=w_key, w_value=w_value, w_out=w_out,
        w_inner=w_inner, w_outer=w_outer,
        b_query=flat(b_query), b_value=flat(b_value), b_out=flat(b_out),
        g_attn=flat(g_attn), s_attn=flat(s_attn), b_inner=flat(b_inner),
        b_outer=flat(b_outer), g_final=flat(g_final), s_final=flat(s_final),
    )
    outs = dict(
        o_out=((n, w), F32),
        o_grad=((n, w), F32),
        o_outer=((z.unit, w), F32),
        o_inner=((z.parts, z.row, z.mine), BF16),
        o_qkv=((z.parts, z.row, 3 * c), BF16),
        o_wout=((z.row, w), BF16),
        o_vec=((SLAB, 128), F32),
    )
    scratch = dict(
        qkv_w=((w, 3 * c), BF16),
        inner_w=((w, z.mine), BF16),
        out_w=((c, w), BF16),
        outer_w=((z.mine, w), BF16),
        vec_all=((z.pages * z.parts * SLAB, 128), F32),
        cut_qkv=((z.rows, 3 * c), BF16),
        cut_inner=((z.rows, z.mine), BF16),
        own_out=((z.row, w), BF16),
        vecs=((VECTORS, w), F32),
        b_mine=((1, z.mine), F32),
        tok_all=((ln, w), BF16),
        hid_all=((ln, w), BF16),
        gf_all=((ln, w), BF16),
        ga_all=((ln, w), BF16),
        qkv=((ln, 3 * c), BF16),
        grad_qkv=((ln, 3 * c), BF16),
        probs=((z.heads, ln, ln), F32),
        ctx=((ln, c), BF16),
        grad_ctx=((ln, c), BF16),
        grad_kv=((2, ln, 128), F32),
        part_out=((4, ln, w), BF16),
        part_in=((4, 4, n, w), BF16),
        part_own=((n, w), F32),
        norm_one=((n, w), F32),
        inv_one=((n, 1), F32),
        hidden=((n, w), F32),
        grad_sum=((n, w), F32),
        grad_mixed=((n, w), F32),
        active=((ln, z.mine), BF16),
        slope=((ln, z.mine), F32),
        grad_inner=((ln, z.mine), BF16),
        sums=((VECTORS, w), F32),
        b_sum=((1, z.mine), F32),
        term_out=((c, w), F32),
        term_vec=((z.pages * SLAB, 128), F32),
        slot_outer=((2, half, z.unit, w), BF16), stage_outer=((z.unit, w), BF16),
        slot_inner=((2, half, z.rows, z.mine), BF16), stage_inner=((z.rows, z.mine), BF16),
        slot_qkv=((2, half, z.rows, 3 * c), BF16), stage_qkv=((z.rows, 3 * c), BF16),
        slot_out=((2, half, z.row, w), BF16), stage_out=((z.row, w), BF16),
        slot_vec=((2, half, SLAB, 128), F32), stage_vec=((SLAB, 128), F32),
        fin_inner=((z.rows, z.mine), BF16), got_inner=((4, z.row, z.mine), BF16),
        fin_qkv=((z.rows, 3 * c), BF16), got_qkv=((4, z.row, 3 * c), BF16),
        fin_out=((z.row, w), BF16), got_out=((z.row, w), BF16),
        fin_vec=((SLAB, 128), F32), got_vec=((4, SLAB, 128), F32),
    )
    z.sems = 192
    sems = pltpu.SemaphoreType.DMA((z.sems,))
    names = list(ins) + list(outs) + list(scratch) + list(dict(send_sem=0, recv_sem=0))
    vmem = pl.BlockSpec(memory_space=pltpu.VMEM)
    parts = pl.pallas_call(
        functools.partial(layer_kernel, z, names),
        out_shape=[jax.ShapeDtypeStruct(*v) for v in outs.values()],
        in_specs=[
            pl.BlockSpec(memory_space=pltpu.SMEM) if v is valid_len else vmem for v in ins.values()
        ],
        out_specs=[vmem] * len(outs),
        scratch_shapes=[pltpu.VMEM(*v) for v in scratch.values()]
        + [sems, sems],
        compiler_params=pltpu.CompilerParams(
            collective_id=0, has_side_effects=True, vmem_limit_bytes=67043328
        ),
        name="layer",
    )(*ins.values())
    row, big = z.row, jax.ShapeDtypeStruct((n, w), F32)
    mat = jax.ShapeDtypeStruct((row, w), F32)
    vec = jax.ShapeDtypeStruct((1, row), F32)
    shapes = [
        big, big, mat, vec, mat, mat, vec, mat, vec, vec, vec,
        jax.ShapeDtypeStruct((row, z.units), F32), jax.ShapeDtypeStruct((1, z.unit), F32),
        jax.ShapeDtypeStruct((z.unit, w), F32), vec, vec, vec,
    ]
    results = pl.pallas_call(
        functools.partial(finish_kernel, z),
        out_shape=shapes,
        in_specs=[vmem] * 7,
        out_specs=[vmem] * len(shapes),
        name="finish",
    )(*parts)
    results = list(results)
    for i in (0, 1):
        results[i] = results[i].reshape(tokens.shape)
    for i in range(2, 17):
        if results[i].shape[0] == 1:
            results[i] = results[i].reshape(results[i].shape[1])
    return tuple(results)


def body(
    tokens,
    valid_len,
    query_weight,
    query_bias,
    key_weight,
    value_weight,
    value_bias,
    output_weight,
    output_bias,
    attn_gain,
    attn_shift,
    inner_weight,
    inner_bias,
    outer_weight,
    outer_bias,
    final_gain,
    final_shift,
    out_grad,
):
    lowered = [
        piece.astype(jnp.bfloat16)
        for piece in (
            query_weight,
            query_bias,
            key_weight,
            value_weight,
            value_bias,
            output_weight,
            output_bias,
            attn_gain,
            attn_shift,
            inner_weight,
            inner_bias,
            outer_weight,
            outer_bias,
            final_gain,
            final_shift,
        )
    ]
    outputs = sequence_layer(tokens, valid_len, lowered, out_grad)
    return outputs


def solution(mesh):
    in_specs = (
        P("page", "seq", None),
        P("page"),
        P(("page", "seq"), None),
        P(("page", "seq")),
        P(("page", "seq"), None),
        P(("page", "seq"), None),
        P(("page", "seq")),
        P(("page", "seq"), None),
        P(("page", "seq")),
        P(("page", "seq")),
        P(("page", "seq")),
        P(("page", "seq"), None),
        P(("page", "seq")),
        P(("page", "seq"), None),
        P(("page", "seq")),
        P(("page", "seq")),
        P(("page", "seq")),
        P("page", "seq", None),
    )
    out_specs = (
        P("page", "seq", None),
        P("page", "seq", None),
        P(("page", "seq"), None),
        P(("page", "seq")),
        P(("page", "seq"), None),
        P(("page", "seq"), None),
        P(("page", "seq")),
        P(("page", "seq"), None),
        P(("page", "seq")),
        P(("page", "seq")),
        P(("page", "seq")),
        P(("page", "seq"), None),
        P(("page", "seq")),
        P(("page", "seq"), None),
        P(("page", "seq")),
        P(("page", "seq")),
        P(("page", "seq")),
    )

    def layer(*arrays):
        width, units = arrays[11].shape
        if supported(mesh, arrays[0].shape, width, units):
            z = Sizes(mesh, width, units, arrays[0].shape[1] // mesh.shape["seq"])

            def run(tokens, valid_len, *rest):
                return paged_layer(z, tokens, valid_len, rest[:-1], rest[-1])

            chosen = run
        else:
            chosen = body
        return jax.shard_map(
            chosen, mesh=mesh, in_specs=in_specs, out_specs=out_specs, check_vma=False
        )(*arrays)

    return layer
```

```python
import functools
import math
import types

import jax
import jax.numpy as jnp
from jax import lax
from jax.experimental import pallas as pl
from jax.experimental.pallas import tpu as pltpu
from jax.sharding import PartitionSpec as P

HEAD_DIM = 64


EPSILON = 1e-05
INV_ROOT_TWO = 1.0 / math.sqrt(2.0)
INV_ROOT_TWO_PI = 1.0 / math.sqrt(2.0 * math.pi)


def product(left, right):
    return jnp.dot(left, right, preferred_element_type=jnp.float32)


def product_tn(left, right):
    return lax.dot_general(
        left, right, (((0,), (0,)), ((), ())), preferred_element_type=jnp.float32
    )


def product_nt(left, right):
    return lax.dot_general(
        left, right, (((1,), (1,)), ((), ())), preferred_element_type=jnp.float32
    )


def norm_parts(values):
    center = values - jnp.mean(values, axis=-1, keepdims=True)
    inverse = lax.rsqrt(jnp.mean(center * center, axis=-1, keepdims=True) + EPSILON)
    return (center * inverse, inverse)


def norm_backward(grad_out, normed, inverse, gain):
    scaled = grad_out * gain
    return inverse * (
        scaled
        - jnp.mean(scaled, axis=-1, keepdims=True)
        - normed * jnp.mean(scaled * normed, axis=-1, keepdims=True)
    )


def gelu_parts(values):
    cumulative = 0.5 * (1.0 + lax.erf(values * INV_ROOT_TWO))
    return (
        values * cumulative,
        cumulative + values * jnp.exp(-0.5 * values * values) * INV_ROOT_TWO_PI,
    )


def sequence_layer(tokens, valid_len, lowered, out_grad):
    fetched = (
        lax.all_gather(lowered[0], ("page", "seq"), axis=0, tiled=True),
        lax.all_gather(lowered[1], ("page", "seq"), axis=0, tiled=True),
        lax.all_gather(lowered[2], ("page", "seq"), axis=0, tiled=True),
        lax.all_gather(lowered[3], ("page", "seq"), axis=0, tiled=True),
        lax.all_gather(lowered[4], ("page", "seq"), axis=0, tiled=True),
        lax.all_gather(lowered[5], ("page", "seq"), axis=0, tiled=True),
        lax.all_gather(lowered[6], ("page", "seq"), axis=0, tiled=True),
        lax.all_gather(lowered[7], ("page", "seq"), axis=0, tiled=True),
        lax.all_gather(lowered[8], ("page", "seq"), axis=0, tiled=True),
        lax.all_gather(lowered[9], ("page", "seq"), axis=0, tiled=True),
        lax.all_gather(lowered[10], ("page", "seq"), axis=0, tiled=True),
        lax.all_gather(lowered[11], ("page", "seq"), axis=0, tiled=True),
        lax.all_gather(lowered[12], ("page", "seq"), axis=0, tiled=True),
        lax.all_gather(lowered[13], ("page", "seq"), axis=0, tiled=True),
        lax.all_gather(lowered[14], ("page", "seq"), axis=0, tiled=True),
    )
    (
        w_query,
        b_query,
        w_key,
        w_value,
        b_value,
        w_out,
        b_out,
        g_attn,
        s_attn,
        w_inner,
        b_inner,
        w_outer,
        b_outer,
        g_final,
        s_final,
    ) = fetched
    f32 = jnp.float32
    bf16 = jnp.bfloat16
    scale = HEAD_DIM ** (-0.5)
    page_count, span_len, width = tokens.shape
    heads = width // HEAD_DIM
    row_count = page_count * span_len
    tok_rows = tokens.reshape(row_count, width)
    tok_low = tok_rows.astype(bf16)
    q_low = (product(tok_low, w_query) + b_query.astype(f32)).astype(bf16)
    k_low = product(tok_low, w_key).astype(bf16)
    v_low = (product(tok_low, w_value) + b_value.astype(f32)).astype(bf16)
    k_full, v_full = (
        lax.all_gather(k_low.reshape(page_count, span_len, width), "seq", axis=1, tiled=True),
        lax.all_gather(v_low.reshape(page_count, span_len, width), "seq", axis=1, tiled=True),
    )
    seq_len = k_full.shape[1]
    q_heads = q_low.reshape(page_count, span_len, heads, HEAD_DIM)
    k_heads = k_full.reshape(page_count, seq_len, heads, HEAD_DIM)
    v_heads = v_full.reshape(page_count, seq_len, heads, HEAD_DIM)
    key_mask = (lax.broadcasted_iota(jnp.int32, (page_count, seq_len), 1) < valid_len[:, None])[
        :, None, None, :
    ]

    def masked_scores():
        raw = jnp.einsum("pqhe,pkhe->phqk", q_heads, k_heads, preferred_element_type=f32) * scale
        return jnp.where(key_mask, raw, -1000000000.0)

    scores = masked_scores()
    top_score = jnp.max(scores, axis=-1, keepdims=True)
    log_total = top_score + jnp.log(jnp.sum(jnp.exp(scores - top_score), axis=-1, keepdims=True))
    probs_low = jnp.exp(scores - log_total).astype(bf16)
    context = jnp.einsum("phqk,pkhe->pqhe", probs_low, v_heads, preferred_element_type=f32)
    ctx_low = context.reshape(row_count, width).astype(bf16)
    attended = product(ctx_low, w_out) + b_out.astype(f32)
    norm_one, inv_one = norm_parts(tok_rows + attended)
    hidden = norm_one * g_attn.astype(f32) + s_attn.astype(f32)
    hid_low = hidden.astype(bf16)
    inner = product(hid_low, w_inner) + b_inner.astype(f32)
    active, slope = gelu_parts(inner)
    act_low = active.astype(bf16)
    outer = product(act_low, w_outer) + b_outer.astype(f32)
    norm_two, inv_two = norm_parts(hidden + outer)
    result = norm_two * g_final.astype(f32) + s_final.astype(f32)
    (
        w_query,
        b_query,
        w_key,
        w_value,
        b_value,
        w_out,
        b_out,
        g_attn,
        s_attn,
        w_inner,
        b_inner,
        w_outer,
        b_outer,
        g_final,
        s_final,
    ) = (
        lax.all_gather(lowered[0], ("page", "seq"), axis=0, tiled=True),
        lax.all_gather(lowered[1], ("page", "seq"), axis=0, tiled=True),
        lax.all_gather(lowered[2], ("page", "seq"), axis=0, tiled=True),
        lax.all_gather(lowered[3], ("page", "seq"), axis=0, tiled=True),
        lax.all_gather(lowered[4], ("page", "seq"), axis=0, tiled=True),
        lax.all_gather(lowered[5], ("page", "seq"), axis=0, tiled=True),
        lax.all_gather(lowered[6], ("page", "seq"), axis=0, tiled=True),
        lax.all_gather(lowered[7], ("page", "seq"), axis=0, tiled=True),
        lax.all_gather(lowered[8], ("page", "seq"), axis=0, tiled=True),
        lax.all_gather(lowered[9], ("page", "seq"), axis=0, tiled=True),
        lax.all_gather(lowered[10], ("page", "seq"), axis=0, tiled=True),
        lax.all_gather(lowered[11], ("page", "seq"), axis=0, tiled=True),
        lax.all_gather(lowered[12], ("page", "seq"), axis=0, tiled=True),
        lax.all_gather(lowered[13], ("page", "seq"), axis=0, tiled=True),
        lax.all_gather(lowered[14], ("page", "seq"), axis=0, tiled=True),
    )
    grad_rows = out_grad.reshape(row_count, width)
    grad_gfinal = jnp.sum(grad_rows * norm_two, axis=0)
    grad_sfinal = jnp.sum(grad_rows, axis=0)
    grad_sum = norm_backward(grad_rows, norm_two, inv_two, g_final.astype(f32))
    grad_f_low = grad_sum.astype(bf16)
    grad_bouter = jnp.sum(grad_f_low.astype(f32), axis=0)
    grad_wouter = product_tn(act_low, grad_f_low)
    grad_active = product_nt(grad_f_low, w_outer)
    grad_in_low = (grad_active * slope).astype(bf16)
    grad_binner = jnp.sum(grad_in_low.astype(f32), axis=0)
    grad_winner = product_tn(hid_low, grad_in_low)
    grad_hidden = grad_sum + product_nt(grad_in_low, w_inner)
    grad_gattn = jnp.sum(grad_hidden * norm_one, axis=0)
    grad_sattn = jnp.sum(grad_hidden, axis=0)
    grad_mixed = norm_backward(grad_hidden, norm_one, inv_one, g_attn.astype(f32))
    grad_att_low = grad_mixed.astype(bf16)
    grad_bout = jnp.sum(grad_att_low.astype(f32), axis=0)
    grad_wout = product_tn(ctx_low, grad_att_low)
    grad_ctx = (
        product_nt(grad_att_low, w_out).astype(bf16).reshape(page_count, span_len, heads, HEAD_DIM)
    )
    probs = jnp.exp(masked_scores() - log_total)
    probs_low = probs.astype(bf16)
    grad_probs = jnp.einsum("pqhe,pkhe->phqk", grad_ctx, v_heads, preferred_element_type=f32)
    grad_vfull = jnp.einsum("phqk,pqhe->pkhe", probs_low, grad_ctx, preferred_element_type=f32)
    grad_scores = (
        probs * (grad_probs - jnp.sum(grad_probs * probs, axis=-1, keepdims=True))
    ).astype(bf16)
    grad_q_low = (
        (jnp.einsum("phqk,pkhe->pqhe", grad_scores, k_heads, preferred_element_type=f32) * scale)
        .astype(bf16)
        .reshape(row_count, width)
    )
    grad_kfull = (
        jnp.einsum("phqk,pqhe->pkhe", grad_scores, q_heads, preferred_element_type=f32) * scale
    )
    grad_keys, grad_values = (
        lax.psum_scatter(
            grad_kfull.reshape(page_count, seq_len, width).astype(jnp.bfloat16),
            "seq",
            scatter_dimension=1,
            tiled=True,
        ).astype(jnp.float32),
        lax.psum_scatter(
            grad_vfull.reshape(page_count, seq_len, width).astype(jnp.bfloat16),
            "seq",
            scatter_dimension=1,
            tiled=True,
        ).astype(jnp.float32),
    )
    grad_k_low = grad_keys.reshape(row_count, width).astype(bf16)
    grad_v_low = grad_values.reshape(row_count, width).astype(bf16)
    grad_tokens = (
        grad_mixed
        + product_nt(grad_q_low, w_query)
        + product_nt(grad_k_low, w_key)
        + product_nt(grad_v_low, w_value)
    )
    grad_wquery = product_tn(tok_low, grad_q_low)
    grad_bquery = jnp.sum(grad_q_low.astype(f32), axis=0)
    grad_wkey = product_tn(tok_low, grad_k_low)
    grad_wvalue = product_tn(tok_low, grad_v_low)
    grad_bvalue = jnp.sum(grad_v_low.astype(f32), axis=0)
    owned = (
        lax.psum_scatter(grad_wquery, ("page", "seq"), scatter_dimension=0, tiled=True),
        lax.psum_scatter(grad_bquery, ("page", "seq"), scatter_dimension=0, tiled=True),
        lax.psum_scatter(grad_wkey, ("page", "seq"), scatter_dimension=0, tiled=True),
        lax.psum_scatter(grad_wvalue, ("page", "seq"), scatter_dimension=0, tiled=True),
        lax.psum_scatter(grad_bvalue, ("page", "seq"), scatter_dimension=0, tiled=True),
        lax.psum_scatter(grad_wout, ("page", "seq"), scatter_dimension=0, tiled=True),
        lax.psum_scatter(grad_bout, ("page", "seq"), scatter_dimension=0, tiled=True),
        lax.psum_scatter(grad_gattn, ("page", "seq"), scatter_dimension=0, tiled=True),
        lax.psum_scatter(grad_sattn, ("page", "seq"), scatter_dimension=0, tiled=True),
        lax.psum_scatter(grad_winner, ("page", "seq"), scatter_dimension=0, tiled=True),
        lax.psum_scatter(grad_binner, ("page", "seq"), scatter_dimension=0, tiled=True),
        lax.psum_scatter(grad_wouter, ("page", "seq"), scatter_dimension=0, tiled=True),
        lax.psum_scatter(grad_bouter, ("page", "seq"), scatter_dimension=0, tiled=True),
        lax.psum_scatter(grad_gfinal, ("page", "seq"), scatter_dimension=0, tiled=True),
        lax.psum_scatter(grad_sfinal, ("page", "seq"), scatter_dimension=0, tiled=True),
    )
    return (
        result.reshape(tokens.shape),
        grad_tokens.reshape(tokens.shape),
        owned[0],
        owned[1],
        owned[2],
        owned[3],
        owned[4],
        owned[5],
        owned[6],
        owned[7],
        owned[8],
        owned[9],
        owned[10],
        owned[11],
        owned[12],
        owned[13],
        owned[14],
    )


MESH = pl.DeviceIdType.MESH
BF16 = jnp.bfloat16
F32 = jnp.float32
VECTORS = 8
SLAB = 16
NEGATIVE = -1000000000.0


def dot_nn(left, right):
    return lax.dot_general(left, right, (((1,), (0,)), ((), ())), preferred_element_type=F32)


def dot_nt(left, right):
    return lax.dot_general(left, right, (((1,), (1,)), ((), ())), preferred_element_type=F32)


def dot_tn(left, right):
    return lax.dot_general(left, right, (((0,), (0,)), ((), ())), preferred_element_type=F32)


class Sizes:
    def __init__(self, mesh, width, units, span):
        self.pages = mesh.shape["page"]
        self.parts = mesh.shape["seq"]
        self.half = self.pages // 2
        self.width = width
        self.units = units
        self.span = span
        self.length = span * self.parts
        self.row = width // (self.pages * self.parts)
        self.rows = self.row * self.parts
        self.unit = units // (self.pages * self.parts)
        self.mine = self.unit * self.pages
        self.cols = width // self.parts
        self.heads = self.cols // HEAD_DIM


def supported(mesh, token_shape, width, units):
    pages, parts = mesh.shape["page"], mesh.shape["seq"]
    return (
        parts == 4
        and pages % 2 == 0
        and pages >= 4
        and token_shape[0] == pages
        and token_shape[1] % (parts * 128) == 0
        and width % (pages * parts * 32) == 0
        and width // pages == 128
        and units % (pages * parts * 128) == 0
        and (width // parts) % 128 == 0
    )


def layer_kernel(z, names, *refs):
    r = types.SimpleNamespace(**dict(zip(names, refs)))
    send_sem, recv_sem = r.send_sem, r.recv_sem
    page = lax.axis_index("page")
    part = lax.axis_index("seq")
    counter = [0]
    sent = []

    def slots(count):
        first = counter[0]
        counter[0] += count
        return first

    odd = page % 2
    place = odd * (z.pages - 1 - page // 2) + (1 - odd) * (page // 2)

    def page_at(index):
        index = (index + 2 * z.pages) % z.pages
        late = index // z.half
        return (1 - late) * (2 * index) + late * (2 * z.pages - 1 - 2 * index)

    def peer(j):
        return ((part // 2 + j // 2) % 2) * 2 + (part % 2 + j % 2) % 2

    rank = page * z.parts + part
    hold_page, hold_part = rank % z.pages, rank // z.pages
    flat = part * z.pages + page
    own_page, own_part = flat // z.parts, flat % z.parts
    moves = 1 - (1 - jnp.minimum(1, (hold_page - page) * (hold_page - page))) * (
        1 - jnp.minimum(1, (hold_part - part) * (hold_part - part))
    )

    def copy(src, dst, index, device):
        return pltpu.make_async_remote_copy(
            src_ref=src,
            dst_ref=dst,
            send_sem=send_sem.at[index],
            recv_sem=recv_sem.at[index],
            device_id=device,
            device_id_type=MESH,
        )

    def block(ref, index, size):
        return ref.at[pl.ds(pl.multiple_of(index * size, size), size)]

    barrier = pltpu.get_barrier_semaphore()

    def greet(device):
        pl.semaphore_signal(barrier, inc=1, device_id=device, device_id_type=MESH)

    for j in (1, 2, 3):
        greet((page, peer(j)))
    greet((page_at(place + 1), part))
    greet((page_at(place - 1), part))

    @pl.when(moves == 1)
    def _():
        greet((hold_page, hold_part))
        greet((own_page, own_part))

    class Share:
        def __init__(self, ref, size):
            self.ref, self.size, self.first = ref, size, slots(4)

        def copy(self, j, owner):
            piece = block(self.ref, owner, self.size)
            return copy(piece, piece, self.first + j, (page, peer(1 if j == 3 else j)))

        def start(self):
            self.copy(2, part).start()
            self.copy(1, part).start()

        def forward(self):
            self.copy(2, peer(2)).wait_recv()
            self.copy(3, peer(2)).start()

            def leave():
                self.copy(1, part).wait_send()
                self.copy(2, part).wait_send()
                self.copy(3, peer(2)).wait_send()

            sent.append(leave)

        def wait(self, j):
            self.copy(j, peer(j)).wait_recv()

    class Combine:
        def __init__(self, phase, make):
            self.phase, self.make, self.first = phase, make, slots(4)

        def rows(self, j):
            return pl.ds(pl.multiple_of(peer(j) * n, n), n)

        def copy(self, j):
            return copy(
                r.part_out.at[self.phase, self.rows(j)],
                r.part_in.at[self.phase, j],
                self.first + j,
                (page, peer(2 if j == 2 else 1)),
            )

        def term(self, j):
            value = self.make(self.rows(j))
            if j == 0:
                r.part_own[...] = value
                return
            if j == 2:
                self.copy(3).wait_recv()
                value = value + r.part_in[self.phase, 3].astype(F32)
            r.part_out[self.phase, self.rows(j), :] = value.astype(BF16)
            self.copy(j).start()
            sent.append(lambda: self.copy(j).wait_send())

        def wait(self):
            for j in (1, 2):
                self.copy(j).wait_recv()

        def total(self, rows):
            total = r.part_own[rows, :]
            for j in (1, 2):
                total = total + r.part_in[self.phase, j, rows, :].astype(F32)
            return total

    class Spread:
        def __init__(self, src, dst, size):
            self.src, self.dst, self.size, self.first = src, dst, size, slots(4)

        def copy(self, j):
            return copy(
                block(self.src, peer(j), self.size),
                self.dst.at[j],
                self.first + j,
                (page, peer(j)),
            )

        def start(self):
            for j in (2, 3, 1):
                self.copy(j).start()
            sent.append(lambda: [self.copy(j).wait_send() for j in (1, 2, 3)])

        def wait(self, j):
            self.copy(j).wait_recv()

    class Place:
        def __init__(self, src, dst, size, base):
            self.src, self.dst, self.size, self.base, self.first = src, dst, size, base, slots(4)

        def copy(self, j, owner):
            return copy(
                block(self.src, peer(j), self.size),
                block(self.dst, self.base + owner, self.size),
                self.first + j,
                (page, peer(j)),
            )

        def start(self):
            for j in (2, 3, 1):
                self.copy(j, part).start()
            sent.append(lambda: [self.copy(j, part).wait_send() for j in (1, 2, 3)])

        def wait(self):
            for j in (1, 2, 3):
                self.copy(j, peer(j)).wait_recv()

    class Gather:
        def __init__(self, ref, size, pieces=1):
            self.ref, self.size, self.pieces = ref, size, pieces
            self.first = slots(2 * z.half * pieces)

        def copy(self, t, d, k, index):
            height = self.size // self.pieces
            start = k * height
            if t == z.half - 1:
                height = height // 2
                start = start + d * height
            piece = block(self.ref, page_at(index), self.size).at[pl.ds(start, height)]
            return copy(
                piece,
                piece,
                self.first + (t * self.pieces + k) * 2 + d,
                (page_at(place + 1 - 2 * d), part),
            )

        def wait(self, t, k, d):
            self.copy(t, d, k, place - (1 - 2 * d) * (1 + t)).wait_recv()

        def step(self, t):
            for k in range(self.pieces):
                for d in (0, 1):
                    if t > 0:
                        self.wait(t - 1, k, d)
                    self.copy(t, d, k, place - (1 - 2 * d) * t).start()
                    sent.append(functools.partial(self.leave, t, k, d))

        def leave(self, t, k, d):
            self.copy(t, d, k, place - (1 - 2 * d) * t).wait_send()

        def done(self):
            for k in range(self.pieces):
                for d in (0, 1):
                    self.wait(z.half - 1, k, d)

    class Reduce:
        def __init__(self, slot, stage, local, shape, kind, pieces=1):
            self.slot, self.stage, self.local = slot, stage, local
            self.size, self.kind, self.pieces = shape[0], kind, pieces
            self.wide = shape[1] // pieces
            self.first = slots(2 * z.half * pieces)

        def copy(self, t, d, k):
            h = self.size // 2
            if t == 0:
                src = self.stage.at[k, pl.ds(d * h, h)]
                dst = self.slot.at[k, d, 0, pl.ds(d * h, h)]
            else:
                src = self.slot.at[k, d, t - 1]
                dst = self.slot.at[k, d, t]
            return copy(
                src,
                dst,
                self.first + (t * self.pieces + k) * 2 + d,
                (page_at(place + 1 - 2 * d), part),
            )

        def leave(self, t, d, k):
            self.copy(t, d, k).wait_send()

        def step(self, t):
            h = self.size // 2
            wide = self.wide
            if t == 0:
                term = self.local(page_at(place + z.half)).astype(self.kind)
                for k in range(self.pieces):
                    self.stage[k] = term[:, k * wide : (k + 1) * wide]
            else:
                terms = [
                    self.local(page_at(place + (1 - 2 * d) * (z.half - t))) for d in (0, 1)
                ]
            for k in range(self.pieces):
                for d in (0, 1):
                    if t > 0:
                        term = terms[d][:, k * wide : (k + 1) * wide]
                        self.copy(t - 1, d, k).wait_recv()
                        held = self.slot.at[k, d, t - 1]
                        if t == 1:
                            near, far = pl.ds(d * h, h), pl.ds((1 - d) * h, h)
                            term_near = term[d * h : (d + 1) * h]
                            term_far = term[(1 - d) * h : (2 - d) * h]
                            held[near] = (held[near].astype(F32) + term_near).astype(self.kind)
                            held[far] = term_far.astype(self.kind)
                        else:
                            held[...] = (held[...].astype(F32) + term).astype(self.kind)
                    self.copy(t, d, k).start()
                    sent.append(functools.partial(self.leave, t, d, k))

        def total(self, out):
            term = self.local(page)
            last = z.half - 1
            for k in range(self.pieces):
                for d in (0, 1):
                    self.copy(last, d, k).wait_recv()
                at = slice(k * self.wide, (k + 1) * self.wide)
                out[:, at] = (
                    term[:, at] + self.slot[k, 0, last].astype(F32) + self.slot[k, 1, last].astype(F32)
                ).astype(out.dtype)

    c, w, n = z.cols, z.width, z.span
    for q in range(z.parts):
        rows = pl.ds(q * z.row, z.row)
        for i, weight in enumerate((r.w_query, r.w_key, r.w_value)):
            r.cut_qkv[rows, i * c : (i + 1) * c] = weight[:, q * c : (q + 1) * c].astype(BF16)
    base = pl.multiple_of(rank * SLAB, SLAB)
    for i, small in enumerate(
        (r.b_query, r.b_value, r.b_out, r.g_attn, r.s_attn, r.b_outer, r.g_final, r.s_final)
    ):
        r.vec_all[pl.ds(base + i, 1), 0 : z.row] = small[...]
    r.vec_all[pl.ds(base + VECTORS, 1), :] = r.b_inner[...]
    r.outer_w[pl.ds(pl.multiple_of(page * z.unit, z.unit), z.unit), :] = r.w_outer[...].astype(
        BF16
    )

    ring_qkv = Gather(r.qkv_w, z.rows, 2)
    ring_vec = Gather(r.vec_all, z.parts * SLAB)
    ring_inner = Gather(r.inner_w, z.rows, 2)
    ring_out = Gather(r.out_w, z.row)
    ring_outer = Gather(r.outer_w, z.unit, 2)
    cut_qkv = Place(r.cut_qkv, r.qkv_w, z.row, page * z.parts)
    cut_inner = Place(r.cut_inner, r.inner_w, z.row, page * z.parts)
    share_tok = Share(r.tok_all, n)

    class ShareVec:
        first = slots(4)

        def copy(self, j, owner):
            piece = block(r.vec_all, page * z.parts + owner, SLAB)
            return copy(piece, piece, self.first + j, (page, peer(j)))

    vec_share = ShareVec()
    hold = slots(1)

    def hold_copy(slot):
        return copy(r.own_out, block(r.out_w, slot, z.row), hold, (hold_page, hold_part))

    pl.semaphore_wait(barrier, 5 + 2 * moves)
    cut_qkv.start()
    for j in (2, 3, 1):
        vec_share.copy(j, part).start()
    sent.append(lambda: [vec_share.copy(j, part).wait_send() for j in (1, 2, 3)])
    ring_outer.step(0)
    r.own_out[...] = r.w_out[...].astype(BF16)

    @pl.when(moves == 1)
    def _():
        hold_copy(hold_page).start()

    @pl.when(moves == 0)
    def _():
        r.out_w[pl.ds(pl.multiple_of(page * z.row, z.row), z.row), :] = r.own_out[...]

    r.tok_all[pl.ds(pl.multiple_of(part * n, n), n), :] = r.tokens[...].astype(BF16)
    share_tok.start()
    for q in range(z.parts):
        rows = pl.ds(q * z.row, z.row)
        for g in range(z.pages):
            at = (z.parts * g + q) * z.unit
            r.cut_inner[rows, g * z.unit : (g + 1) * z.unit] = r.w_inner[
                :, at : at + z.unit
            ].astype(BF16)
    cut_inner.start()
    own_rows = pl.ds(pl.multiple_of(rank * z.row, z.row), z.row)
    cut_rows = pl.ds(pl.multiple_of(part * z.row, z.row), z.row)
    r.qkv_w[own_rows, :] = r.cut_qkv[cut_rows, :]
    r.inner_w[own_rows, :] = r.cut_inner[cut_rows, :]

    cut_qkv.wait()
    ring_qkv.step(0)
    for j in (1, 2, 3):
        vec_share.copy(j, peer(j)).wait_recv()
    ring_vec.step(0)

    @pl.when(moves == 1)
    def _():
        hold_copy(page).wait_recv()

    ring_out.step(0)
    for t in range(1, z.half):
        ring_qkv.step(t)
        ring_vec.step(t)
        ring_out.step(t)
        if t == 1:
            share_tok.forward()
    cut_inner.wait()
    ring_inner.step(0)
    ring_vec.done()

    lane = lax.broadcasted_iota(jnp.int32, (VECTORS, 128), 1)
    for g in range(z.pages):
        total = jnp.zeros((VECTORS, 128), F32)
        for q in range(z.parts):
            tile = r.vec_all[pl.ds((g * z.parts + q) * SLAB, VECTORS), :]
            if q:
                tile = pltpu.roll(tile, q * z.row, 1)
            total = total + jnp.where(lane // z.row == q, tile, 0.0)
        r.vecs[:, g * 128 : (g + 1) * 128] = total.astype(BF16).astype(F32)
        at = pl.multiple_of((g * z.parts + part) * SLAB + VECTORS, VECTORS)
        tile = r.vec_all[pl.ds(at, 8), :]
        r.b_mine[:, g * z.unit : (g + 1) * z.unit] = tile[0:1].astype(BF16).astype(F32)

    def vector(i):
        return r.vecs[i : i + 1, :]

    my_cols = pl.ds(pl.multiple_of(part * c, c), c)

    share_tok.wait(1)
    share_tok.wait(3)
    ring_qkv.done()

    def make_qkv(b, carry):
        rows = pl.ds(pl.multiple_of(b * n, n), n)
        out = dot_nn(r.tok_all[rows, :], r.qkv_w[...])
        r.qkv[rows, 0:c] = (out[:, 0:c] + r.vecs[0:1, my_cols]).astype(BF16)
        r.qkv[rows, c : 2 * c] = out[:, c : 2 * c].astype(BF16)
        r.qkv[rows, 2 * c :] = (out[:, 2 * c :] + r.vecs[1:2, my_cols]).astype(BF16)
        return carry

    lax.fori_loop(0, z.parts, make_qkv, 0)
    ring_inner.step(1)

    scale = HEAD_DIM ** (-0.5)
    first_head = lax.broadcasted_iota(jnp.int32, (n, 128), 1) < HEAD_DIM
    key_place = lax.broadcasted_iota(jnp.int32, (n, z.length), 1)
    valid = r.valid[0]

    def pair_cols(kind, pair):
        return pl.ds(kind * c + pair * 128, 128)

    def attend(pair):
        def body(b, carry):
            rows = pl.ds(pl.multiple_of(b * n, n), n)
            queries = r.qkv[rows, pair_cols(0, pair)]
            keys = r.qkv[:, pair_cols(1, pair)]
            values = r.qkv[:, pair_cols(2, pair)]
            outs = []
            for h in range(2):
                mine = first_head if h == 0 else ~first_head
                scores = dot_nt(jnp.where(mine, queries, jnp.zeros_like(queries)), keys) * scale
                scores = jnp.where(key_place < valid, scores, NEGATIVE)
                top = jnp.max(scores, axis=-1, keepdims=True)
                weight = jnp.exp(scores - top)
                probs = weight * (1.0 / jnp.sum(weight, axis=-1, keepdims=True))
                r.probs[2 * pair + h, rows, :] = probs
                outs.append(dot_nn(probs.astype(BF16), values))
            r.ctx[rows, pl.ds(pair * 128, 128)] = jnp.where(first_head, outs[0], outs[1]).astype(
                BF16
            )
            return carry

        lax.fori_loop(0, z.parts, body, 0)

    attend(0)
    ring_inner.step(2)
    ring_outer.step(1)
    attend(1)
    ring_out.done()

    combine = Combine(0, lambda rows: dot_nn(r.ctx[rows, :], r.out_w[...]))
    combine.term(3)
    combine.term(2)
    ring_inner.step(3)
    ring_outer.step(2)
    combine.term(1)
    combine.term(0)

    def by_rows(fn):
        size = 32

        def body(i, carry):
            fn(pl.ds(pl.multiple_of(i * size, size), size), pl.multiple_of(i * size, size))
            return carry

        lax.fori_loop(0, n // size, body, 0)

    def add_column_sum(i, values):
        r.sums[i : i + 1, :] += jnp.sum(values, axis=0, keepdims=True)

    r.sums[...] = jnp.zeros_like(r.sums)

    combine.wait()

    share_hid = Share(r.hid_all, n)

    def first_norm(rows, at):
        mixed = r.tokens[rows, :] + (combine.total(rows) + vector(2))
        normed, inverse = norm_parts(mixed)
        hidden = normed * vector(3) + vector(4)
        r.norm_one[rows, :] = normed
        r.inv_one[rows, :] = inverse
        r.hidden[rows, :] = hidden
        r.hid_all[pl.ds(pl.multiple_of(part * n + at, 32), 32), :] = hidden.astype(BF16)

    by_rows(first_norm)
    share_hid.start()
    ring_outer.step(3)
    ring_inner.done()

    tile = 256

    def make_inner(j):
        rows = pl.ds(pl.multiple_of(peer(j) * n, n), n)

        def columns(i, carry):
            cols = pl.ds(pl.multiple_of(i * tile, tile), tile)
            inner = dot_nn(r.hid_all[rows, :], r.inner_w[:, cols]) + r.b_mine[:, cols]
            active, slope = gelu_parts(inner)
            r.active[rows, cols] = active.astype(BF16)
            r.slope[rows, cols] = slope
            return carry

        lax.fori_loop(0, z.mine // tile, columns, 0)

    make_inner(0)
    share_hid.wait(1)
    make_inner(1)
    share_hid.forward()
    make_inner(2)
    share_hid.wait(3)
    make_inner(3)
    ring_outer.done()
    combine_two = Combine(1, lambda rows: dot_nn(r.active[rows, :], r.outer_w[...]))
    for j in (3, 2, 1, 0):
        combine_two.term(j)
    combine_two.wait()

    share_gf = Share(r.gf_all, n)

    def second_norm(rows, at):
        outer = combine_two.total(rows) + vector(5)
        normed, inverse = norm_parts(r.hidden[rows, :] + outer)
        r.o_out[rows, :] = normed * vector(6) + vector(7)
        grad = r.out_grad[rows, :]
        add_column_sum(6, grad * normed)
        add_column_sum(7, grad)
        grad_sum = norm_backward(grad, normed, inverse, vector(6))
        low = grad_sum.astype(BF16)
        add_column_sum(5, low.astype(F32))
        r.grad_sum[rows, :] = grad_sum
        r.gf_all[pl.ds(pl.multiple_of(part * n + at, 32), 32), :] = low

    by_rows(second_norm)
    share_gf.start()

    def chunk_term(left, right, size):
        def local(g):
            cols = pl.ds(pl.multiple_of(g * size, size), size)
            return dot_tn(left[:, cols], right[...])

        return local

    reduce_outer = Reduce(
        r.slot_outer, r.stage_outer, chunk_term(r.active, r.gf_all, z.unit), (z.unit, w), BF16, 2
    )
    reduce_inner = Reduce(
        r.slot_inner, r.stage_inner, chunk_term(r.hid_all, r.grad_inner, z.rows),
        (z.rows, z.mine), BF16, 2
    )
    reduce_qkv = Reduce(
        r.slot_qkv, r.stage_qkv, chunk_term(r.tok_all, r.grad_qkv, z.rows),
        (z.rows, 3 * c), BF16, 2
    )
    reduce_out = Reduce(
        r.slot_out, r.stage_out,
        lambda g: r.term_out[pl.ds(pl.multiple_of(g * z.row, z.row), z.row), :], (z.row, w), BF16,
    )
    reduce_vec = Reduce(
        r.slot_vec, r.stage_vec,
        lambda g: r.term_vec[pl.ds(pl.multiple_of(g * SLAB, SLAB), SLAB), :], (SLAB, 128), F32,
    )

    r.b_sum[...] = jnp.zeros_like(r.b_sum)

    def make_grad_inner(j):
        rows = pl.ds(pl.multiple_of(peer(j) * n, n), n)

        def columns(i, carry):
            cols = pl.ds(pl.multiple_of(i * tile, tile), tile)
            grad = dot_nt(r.gf_all[rows, :], r.outer_w[cols, :]) * r.slope[rows, cols]
            low = grad.astype(BF16)
            r.grad_inner[rows, cols] = low
            r.b_sum[:, cols] += jnp.sum(low.astype(F32), axis=0, keepdims=True)
            return carry

        lax.fori_loop(0, z.mine // tile, columns, 0)

    make_grad_inner(0)
    share_gf.wait(1)
    make_grad_inner(1)
    share_gf.forward()
    share_gf.wait(3)
    reduce_outer.step(0)
    make_grad_inner(2)
    make_grad_inner(3)
    combine_three = Combine(2, lambda rows: dot_nt(r.grad_inner[rows, :], r.inner_w[...]))
    combine_three.term(3)
    combine_three.term(2)
    reduce_outer.step(1)
    reduce_inner.step(0)
    combine_three.term(1)
    combine_three.term(0)
    reduce_outer.step(2)
    reduce_inner.step(1)
    combine_three.wait()

    share_ga = Share(r.ga_all, n)

    def first_norm_back(rows, at):
        grad = r.grad_sum[rows, :] + combine_three.total(rows)
        normed = r.norm_one[rows, :]
        add_column_sum(3, grad * normed)
        add_column_sum(4, grad)
        mixed = norm_backward(grad, normed, r.inv_one[rows, :], vector(3))
        low = mixed.astype(BF16)
        add_column_sum(2, low.astype(F32))
        r.grad_mixed[rows, :] = mixed
        r.ga_all[pl.ds(pl.multiple_of(part * n + at, 32), 32), :] = low

    by_rows(first_norm_back)
    share_ga.start()

    def make_grad_ctx(j):
        rows = pl.ds(pl.multiple_of(peer(j) * n, n), n)
        r.grad_ctx[rows, :] = dot_nt(r.ga_all[rows, :], r.out_w[...]).astype(BF16)

    make_grad_ctx(0)
    share_ga.wait(1)
    make_grad_ctx(1)
    reduce_outer.step(3)
    reduce_inner.step(2)
    share_ga.forward()
    make_grad_ctx(2)
    share_ga.wait(3)
    make_grad_ctx(3)
    r.term_out[...] = dot_tn(r.ctx[...], r.ga_all[...])
    reduce_out.step(0)

    def attend_back(pair):
        r.grad_kv[...] = jnp.zeros_like(r.grad_kv)

        def body(b, carry):
            rows = pl.ds(pl.multiple_of(b * n, n), n)
            queries = r.qkv[rows, pair_cols(0, pair)]
            keys = r.qkv[:, pair_cols(1, pair)]
            values = r.qkv[:, pair_cols(2, pair)]
            grad = r.grad_ctx[rows, pl.ds(pair * 128, 128)]
            outs = []
            for h in range(2):
                mine = first_head if h == 0 else ~first_head
                grad_mine = jnp.where(mine, grad, jnp.zeros_like(grad))
                query_mine = jnp.where(mine, queries, jnp.zeros_like(queries))
                probs = r.probs[2 * pair + h, rows, :]
                grad_probs = dot_nt(grad_mine, values)
                r.grad_kv[1] += dot_tn(probs.astype(BF16), grad_mine)
                inside = jnp.sum(grad_probs * probs, axis=-1, keepdims=True)
                grad_scores = (probs * (grad_probs - inside)).astype(BF16)
                outs.append(dot_nn(grad_scores, keys))
                r.grad_kv[0] += dot_tn(grad_scores, query_mine)
            r.grad_qkv[rows, pair_cols(0, pair)] = (
                jnp.where(first_head, outs[0], outs[1]) * scale
            ).astype(BF16)
            return carry

        lax.fori_loop(0, z.parts, body, 0)
        r.grad_qkv[:, pair_cols(1, pair)] = (r.grad_kv[0] * scale).astype(BF16)
        r.grad_qkv[:, pair_cols(2, pair)] = r.grad_kv[1].astype(BF16)

    attend_back(0)
    reduce_inner.step(3)
    reduce_out.step(1)
    attend_back(1)
    reduce_qkv.step(0)
    reduce_out.step(2)

    r.sums[0:1, my_cols] = jnp.sum(r.grad_qkv[:, 0:c].astype(F32), axis=0, keepdims=True)
    r.sums[1:2, my_cols] = jnp.sum(r.grad_qkv[:, 2 * c :].astype(F32), axis=0, keepdims=True)
    r.term_vec[...] = jnp.zeros_like(r.term_vec)
    for g in range(z.pages):
        r.term_vec[g * SLAB : g * SLAB + VECTORS, :] = r.sums[:, g * 128 : (g + 1) * 128]
        r.term_vec[g * SLAB + VECTORS : g * SLAB + VECTORS + 1, :] = r.b_sum[
            :, g * z.unit : (g + 1) * z.unit
        ]
    reduce_vec.step(0)

    combine_four = Combine(3, lambda rows: dot_nt(r.grad_qkv[rows, :], r.qkv_w[...]))
    combine_four.term(3)
    combine_four.term(2)
    reduce_qkv.step(1)
    reduce_vec.step(1)
    reduce_out.step(3)
    combine_four.term(1)
    combine_four.term(0)

    reduce_outer.total(r.o_outer)
    reduce_inner.total(r.fin_inner)
    fin_inner = Spread(r.fin_inner, r.got_inner, z.row)
    fin_inner.start()
    reduce_qkv.step(2)
    reduce_vec.step(2)
    combine_four.wait()

    def input_rows(rows, at):
        r.o_grad[rows, :] = r.grad_mixed[rows, :] + combine_four.total(rows)

    by_rows(input_rows)
    reduce_out.total(r.fin_out)
    home = slots(1)

    def home_copy():
        return copy(r.fin_out, r.got_out, home, (own_page, own_part))

    @pl.when(moves == 1)
    def _():
        home_copy().start()

    @pl.when(moves == 0)
    def _():
        r.got_out[...] = r.fin_out[...]

    reduce_qkv.step(3)
    reduce_vec.step(3)
    reduce_vec.total(r.fin_vec)

    class VecAll:
        first = slots(4)

        def copy(self, j):
            return copy(r.fin_vec, r.got_vec.at[j], self.first + j, (page, peer(j)))

    fin_vec = VecAll()
    for j in (2, 3, 1):
        fin_vec.copy(j).start()
    sent.append(lambda: [fin_vec.copy(j).wait_send() for j in (1, 2, 3)])
    reduce_qkv.total(r.fin_qkv)
    fin_qkv = Spread(r.fin_qkv, r.got_qkv, z.row)
    fin_qkv.start()

    my_rows = pl.ds(pl.multiple_of(part * z.row, z.row), z.row)

    def deliver(spread, mine, got, out):
        for j in range(4):
            if j:
                spread.wait(j)
            value = got[j] if j else mine[my_rows, :]
            out[peer(j)] = value

    deliver(fin_inner, r.fin_inner, r.got_inner, r.o_inner)

    @pl.when(moves == 1)
    def _():
        home_copy().wait_recv()

    r.o_wout[...] = r.got_out[...]
    summed = r.fin_vec[0:VECTORS, :]
    for j in (1, 2, 3):
        fin_vec.copy(j).wait_recv()
        summed = summed + r.got_vec[j, 0:VECTORS, :]
    r.o_vec[0:VECTORS, :] = pltpu.roll(summed, (128 - part * z.row) % 128, 1)
    r.o_vec[VECTORS:, :] = r.fin_vec[VECTORS:, :]
    deliver(fin_qkv, r.fin_qkv, r.got_qkv, r.o_qkv)

    for wait in sent:
        wait()

    @pl.when(moves == 1)
    def _():
        hold_copy(hold_page).wait_send()
        home_copy().wait_send()

    assert counter[0] <= z.sems, counter[0]


def finish_kernel(z, out, grad, outer, inner, qkv, wout, vec, *outs):
    (o_out, o_grad, o_wq, o_bq, o_wk, o_wv, o_bv, o_wo, o_bo, o_ga, o_sa, o_wi, o_bi, o_wu, o_bu, o_gf, o_sf) = outs
    o_out[...] = out[...]
    o_grad[...] = grad[...]
    o_wu[...] = outer[...]
    o_wo[...] = wout[...].astype(F32)
    c = z.cols
    for q in range(z.parts):
        for i, ref in enumerate((o_wq, o_wk, o_wv)):
            ref[:, q * c : (q + 1) * c] = qkv[q, :, i * c : (i + 1) * c].astype(F32)
        for g in range(z.pages):
            at = (z.parts * g + q) * z.unit
            o_wi[:, at : at + z.unit] = inner[q, :, g * z.unit : (g + 1) * z.unit].astype(F32)
    for i, ref in enumerate((o_bq, o_bv, o_bo, o_ga, o_sa, o_bu, o_gf, o_sf)):
        ref[...] = vec[i : i + 1, 0 : z.row]
    o_bi[...] = vec[VECTORS : VECTORS + 1, :]


def paged_layer(z, tokens, valid_len, params, out_grad):
    (
        w_query, b_query, w_key, w_value, b_value, w_out, b_out, g_attn, s_attn,
        w_inner, b_inner, w_outer, b_outer, g_final, s_final,
    ) = params
    flat = lambda v: v.reshape(1, v.shape[0])
    c, w, n, ln, half = z.cols, z.width, z.span, z.length, z.half
    ins = dict(
        valid=valid_len,
        tokens=tokens.reshape(n, w),
        out_grad=out_grad.reshape(n, w),
        w_query=w_query, w_key=w_key, w_value=w_value, w_out=w_out,
        w_inner=w_inner, w_outer=w_outer,
        b_query=flat(b_query), b_value=flat(b_value), b_out=flat(b_out),
        g_attn=flat(g_attn), s_attn=flat(s_attn), b_inner=flat(b_inner),
        b_outer=flat(b_outer), g_final=flat(g_final), s_final=flat(s_final),
    )
    outs = dict(
        o_out=((n, w), F32),
        o_grad=((n, w), F32),
        o_outer=((z.unit, w), F32),
        o_inner=((z.parts, z.row, z.mine), BF16),
        o_qkv=((z.parts, z.row, 3 * c), BF16),
        o_wout=((z.row, w), BF16),
        o_vec=((SLAB, 128), F32),
    )
    scratch = dict(
        qkv_w=((w, 3 * c), BF16),
        inner_w=((w, z.mine), BF16),
        out_w=((c, w), BF16),
        outer_w=((z.mine, w), BF16),
        vec_all=((z.pages * z.parts * SLAB, 128), F32),
        cut_qkv=((z.rows, 3 * c), BF16),
        cut_inner=((z.rows, z.mine), BF16),
        own_out=((z.row, w), BF16),
        vecs=((VECTORS, w), F32),
        b_mine=((1, z.mine), F32),
        tok_all=((ln, w), BF16),
        hid_all=((ln, w), BF16),
        gf_all=((ln, w), BF16),
        ga_all=((ln, w), BF16),
        qkv=((ln, 3 * c), BF16),
        grad_qkv=((ln, 3 * c), BF16),
        probs=((z.heads, ln, ln), F32),
        ctx=((ln, c), BF16),
        grad_ctx=((ln, c), BF16),
        grad_kv=((2, ln, 128), F32),
        part_out=((4, ln, w), BF16),
        part_in=((4, 4, n, w), BF16),
        part_own=((n, w), F32),
        norm_one=((n, w), F32),
        inv_one=((n, 1), F32),
        hidden=((n, w), F32),
        grad_sum=((n, w), F32),
        grad_mixed=((n, w), F32),
        active=((ln, z.mine), BF16),
        slope=((ln, z.mine), F32),
        grad_inner=((ln, z.mine), BF16),
        sums=((VECTORS, w), F32),
        b_sum=((1, z.mine), F32),
        term_out=((c, w), F32),
        term_vec=((z.pages * SLAB, 128), F32),
        slot_outer=((2, 2, half, z.unit, w // 2), BF16), stage_outer=((2, z.unit, w // 2), BF16),
        slot_inner=((2, 2, half, z.rows, z.mine // 2), BF16), stage_inner=((2, z.rows, z.mine // 2), BF16),
        slot_qkv=((2, 2, half, z.rows, 3 * c // 2), BF16), stage_qkv=((2, z.rows, 3 * c // 2), BF16),
        slot_out=((1, 2, half, z.row, w // 1), BF16), stage_out=((1, z.row, w // 1), BF16),
        slot_vec=((1, 2, half, SLAB, 128 // 1), F32), stage_vec=((1, SLAB, 128 // 1), F32),
        fin_inner=((z.rows, z.mine), BF16), got_inner=((4, z.row, z.mine), BF16),
        fin_qkv=((z.rows, 3 * c), BF16), got_qkv=((4, z.row, 3 * c), BF16),
        fin_out=((z.row, w), BF16), got_out=((z.row, w), BF16),
        fin_vec=((SLAB, 128), F32), got_vec=((4, SLAB, 128), F32),
    )
    z.sems = 192
    sems = pltpu.SemaphoreType.DMA((z.sems,))
    names = list(ins) + list(outs) + list(scratch) + list(dict(send_sem=0, recv_sem=0))
    vmem = pl.BlockSpec(memory_space=pltpu.VMEM)
    parts = pl.pallas_call(
        functools.partial(layer_kernel, z, names),
        out_shape=[jax.ShapeDtypeStruct(*v) for v in outs.values()],
        in_specs=[
            pl.BlockSpec(memory_space=pltpu.SMEM) if v is valid_len else vmem for v in ins.values()
        ],
        out_specs=[vmem] * len(outs),
        scratch_shapes=[pltpu.VMEM(*v) for v in scratch.values()]
        + [sems, sems],
        compiler_params=pltpu.CompilerParams(
            collective_id=0, has_side_effects=True, vmem_limit_bytes=67043328
        ),
        name="layer",
    )(*ins.values())
    row, big = z.row, jax.ShapeDtypeStruct((n, w), F32)
    mat = jax.ShapeDtypeStruct((row, w), F32)
    vec = jax.ShapeDtypeStruct((1, row), F32)
    shapes = [
        big, big, mat, vec, mat, mat, vec, mat, vec, vec, vec,
        jax.ShapeDtypeStruct((row, z.units), F32), jax.ShapeDtypeStruct((1, z.unit), F32),
        jax.ShapeDtypeStruct((z.unit, w), F32), vec, vec, vec,
    ]
    results = pl.pallas_call(
        functools.partial(finish_kernel, z),
        out_shape=shapes,
        in_specs=[vmem] * 7,
        out_specs=[vmem] * len(shapes),
        name="finish",
    )(*parts)
    results = list(results)
    for i in (0, 1):
        results[i] = results[i].reshape(tokens.shape)
    for i in range(2, 17):
        if results[i].shape[0] == 1:
            results[i] = results[i].reshape(results[i].shape[1])
    return tuple(results)


def body(
    tokens,
    valid_len,
    query_weight,
    query_bias,
    key_weight,
    value_weight,
    value_bias,
    output_weight,
    output_bias,
    attn_gain,
    attn_shift,
    inner_weight,
    inner_bias,
    outer_weight,
    outer_bias,
    final_gain,
    final_shift,
    out_grad,
):
    lowered = [
        piece.astype(jnp.bfloat16)
        for piece in (
            query_weight,
            query_bias,
            key_weight,
            value_weight,
            value_bias,
            output_weight,
            output_bias,
            attn_gain,
            attn_shift,
            inner_weight,
            inner_bias,
            outer_weight,
            outer_bias,
            final_gain,
            final_shift,
        )
    ]
    outputs = sequence_layer(tokens, valid_len, lowered, out_grad)
    return outputs


def solution(mesh):
    in_specs = (
        P("page", "seq", None),
        P("page"),
        P(("page", "seq"), None),
        P(("page", "seq")),
        P(("page", "seq"), None),
        P(("page", "seq"), None),
        P(("page", "seq")),
        P(("page", "seq"), None),
        P(("page", "seq")),
        P(("page", "seq")),
        P(("page", "seq")),
        P(("page", "seq"), None),
        P(("page", "seq")),
        P(("page", "seq"), None),
        P(("page", "seq")),
        P(("page", "seq")),
        P(("page", "seq")),
        P("page", "seq", None),
    )
    out_specs = (
        P("page", "seq", None),
        P("page", "seq", None),
        P(("page", "seq"), None),
        P(("page", "seq")),
        P(("page", "seq"), None),
        P(("page", "seq"), None),
        P(("page", "seq")),
        P(("page", "seq"), None),
        P(("page", "seq")),
        P(("page", "seq")),
        P(("page", "seq")),
        P(("page", "seq"), None),
        P(("page", "seq")),
        P(("page", "seq"), None),
        P(("page", "seq")),
        P(("page", "seq")),
        P(("page", "seq")),
    )

    def layer(*arrays):
        width, units = arrays[11].shape
        if supported(mesh, arrays[0].shape, width, units):
            z = Sizes(mesh, width, units, arrays[0].shape[1] // mesh.shape["seq"])

            def run(tokens, valid_len, *rest):
                return paged_layer(z, tokens, valid_len, rest[:-1], rest[-1])

            chosen = run
        else:
            chosen = body
        return jax.shard_map(
            chosen, mesh=mesh, in_specs=in_specs, out_specs=out_specs, check_vma=False
        )(*arrays)

    return layer
```

```python
import functools
import math
import types

import jax
import jax.numpy as jnp
from jax import lax
from jax.experimental import pallas as pl
from jax.experimental.pallas import tpu as pltpu
from jax.sharding import PartitionSpec as P

HEAD_DIM = 64


EPSILON = 1e-05
INV_ROOT_TWO = 1.0 / math.sqrt(2.0)
INV_ROOT_TWO_PI = 1.0 / math.sqrt(2.0 * math.pi)


def product(left, right):
    return jnp.dot(left, right, preferred_element_type=jnp.float32)


def product_tn(left, right):
    return lax.dot_general(
        left, right, (((0,), (0,)), ((), ())), preferred_element_type=jnp.float32
    )


def product_nt(left, right):
    return lax.dot_general(
        left, right, (((1,), (1,)), ((), ())), preferred_element_type=jnp.float32
    )


def norm_parts(values):
    center = values - jnp.mean(values, axis=-1, keepdims=True)
    inverse = lax.rsqrt(jnp.mean(center * center, axis=-1, keepdims=True) + EPSILON)
    return (center * inverse, inverse)


def norm_backward(grad_out, normed, inverse, gain):
    scaled = grad_out * gain
    return inverse * (
        scaled
        - jnp.mean(scaled, axis=-1, keepdims=True)
        - normed * jnp.mean(scaled * normed, axis=-1, keepdims=True)
    )


def gelu_parts(values):
    cumulative = 0.5 * (1.0 + lax.erf(values * INV_ROOT_TWO))
    return (
        values * cumulative,
        cumulative + values * jnp.exp(-0.5 * values * values) * INV_ROOT_TWO_PI,
    )


def sequence_layer(tokens, valid_len, lowered, out_grad):
    fetched = (
        lax.all_gather(lowered[0], ("page", "seq"), axis=0, tiled=True),
        lax.all_gather(lowered[1], ("page", "seq"), axis=0, tiled=True),
        lax.all_gather(lowered[2], ("page", "seq"), axis=0, tiled=True),
        lax.all_gather(lowered[3], ("page", "seq"), axis=0, tiled=True),
        lax.all_gather(lowered[4], ("page", "seq"), axis=0, tiled=True),
        lax.all_gather(lowered[5], ("page", "seq"), axis=0, tiled=True),
        lax.all_gather(lowered[6], ("page", "seq"), axis=0, tiled=True),
        lax.all_gather(lowered[7], ("page", "seq"), axis=0, tiled=True),
        lax.all_gather(lowered[8], ("page", "seq"), axis=0, tiled=True),
        lax.all_gather(lowered[9], ("page", "seq"), axis=0, tiled=True),
        lax.all_gather(lowered[10], ("page", "seq"), axis=0, tiled=True),
        lax.all_gather(lowered[11], ("page", "seq"), axis=0, tiled=True),
        lax.all_gather(lowered[12], ("page", "seq"), axis=0, tiled=True),
        lax.all_gather(lowered[13], ("page", "seq"), axis=0, tiled=True),
        lax.all_gather(lowered[14], ("page", "seq"), axis=0, tiled=True),
    )
    (
        w_query,
        b_query,
        w_key,
        w_value,
        b_value,
        w_out,
        b_out,
        g_attn,
        s_attn,
        w_inner,
        b_inner,
        w_outer,
        b_outer,
        g_final,
        s_final,
    ) = fetched
    f32 = jnp.float32
    bf16 = jnp.bfloat16
    scale = HEAD_DIM ** (-0.5)
    page_count, span_len, width = tokens.shape
    heads = width // HEAD_DIM
    row_count = page_count * span_len
    tok_rows = tokens.reshape(row_count, width)
    tok_low = tok_rows.astype(bf16)
    q_low = (product(tok_low, w_query) + b_query.astype(f32)).astype(bf16)
    k_low = product(tok_low, w_key).astype(bf16)
    v_low = (product(tok_low, w_value) + b_value.astype(f32)).astype(bf16)
    k_full, v_full = (
        lax.all_gather(k_low.reshape(page_count, span_len, width), "seq", axis=1, tiled=True),
        lax.all_gather(v_low.reshape(page_count, span_len, width), "seq", axis=1, tiled=True),
    )
    seq_len = k_full.shape[1]
    q_heads = q_low.reshape(page_count, span_len, heads, HEAD_DIM)
    k_heads = k_full.reshape(page_count, seq_len, heads, HEAD_DIM)
    v_heads = v_full.reshape(page_count, seq_len, heads, HEAD_DIM)
    key_mask = (lax.broadcasted_iota(jnp.int32, (page_count, seq_len), 1) < valid_len[:, None])[
        :, None, None, :
    ]

    def masked_scores():
        raw = jnp.einsum("pqhe,pkhe->phqk", q_heads, k_heads, preferred_element_type=f32) * scale
        return jnp.where(key_mask, raw, -1000000000.0)

    scores = masked_scores()
    top_score = jnp.max(scores, axis=-1, keepdims=True)
    log_total = top_score + jnp.log(jnp.sum(jnp.exp(scores - top_score), axis=-1, keepdims=True))
    probs_low = jnp.exp(scores - log_total).astype(bf16)
    context = jnp.einsum("phqk,pkhe->pqhe", probs_low, v_heads, preferred_element_type=f32)
    ctx_low = context.reshape(row_count, width).astype(bf16)
    attended = product(ctx_low, w_out) + b_out.astype(f32)
    norm_one, inv_one = norm_parts(tok_rows + attended)
    hidden = norm_one * g_attn.astype(f32) + s_attn.astype(f32)
    hid_low = hidden.astype(bf16)
    inner = product(hid_low, w_inner) + b_inner.astype(f32)
    active, slope = gelu_parts(inner)
    act_low = active.astype(bf16)
    outer = product(act_low, w_outer) + b_outer.astype(f32)
    norm_two, inv_two = norm_parts(hidden + outer)
    result = norm_two * g_final.astype(f32) + s_final.astype(f32)
    (
        w_query,
        b_query,
        w_key,
        w_value,
        b_value,
        w_out,
        b_out,
        g_attn,
        s_attn,
        w_inner,
        b_inner,
        w_outer,
        b_outer,
        g_final,
        s_final,
    ) = (
        lax.all_gather(lowered[0], ("page", "seq"), axis=0, tiled=True),
        lax.all_gather(lowered[1], ("page", "seq"), axis=0, tiled=True),
        lax.all_gather(lowered[2], ("page", "seq"), axis=0, tiled=True),
        lax.all_gather(lowered[3], ("page", "seq"), axis=0, tiled=True),
        lax.all_gather(lowered[4], ("page", "seq"), axis=0, tiled=True),
        lax.all_gather(lowered[5], ("page", "seq"), axis=0, tiled=True),
        lax.all_gather(lowered[6], ("page", "seq"), axis=0, tiled=True),
        lax.all_gather(lowered[7], ("page", "seq"), axis=0, tiled=True),
        lax.all_gather(lowered[8], ("page", "seq"), axis=0, tiled=True),
        lax.all_gather(lowered[9], ("page", "seq"), axis=0, tiled=True),
        lax.all_gather(lowered[10], ("page", "seq"), axis=0, tiled=True),
        lax.all_gather(lowered[11], ("page", "seq"), axis=0, tiled=True),
        lax.all_gather(lowered[12], ("page", "seq"), axis=0, tiled=True),
        lax.all_gather(lowered[13], ("page", "seq"), axis=0, tiled=True),
        lax.all_gather(lowered[14], ("page", "seq"), axis=0, tiled=True),
    )
    grad_rows = out_grad.reshape(row_count, width)
    grad_gfinal = jnp.sum(grad_rows * norm_two, axis=0)
    grad_sfinal = jnp.sum(grad_rows, axis=0)
    grad_sum = norm_backward(grad_rows, norm_two, inv_two, g_final.astype(f32))
    grad_f_low = grad_sum.astype(bf16)
    grad_bouter = jnp.sum(grad_f_low.astype(f32), axis=0)
    grad_wouter = product_tn(act_low, grad_f_low)
    grad_active = product_nt(grad_f_low, w_outer)
    grad_in_low = (grad_active * slope).astype(bf16)
    grad_binner = jnp.sum(grad_in_low.astype(f32), axis=0)
    grad_winner = product_tn(hid_low, grad_in_low)
    grad_hidden = grad_sum + product_nt(grad_in_low, w_inner)
    grad_gattn = jnp.sum(grad_hidden * norm_one, axis=0)
    grad_sattn = jnp.sum(grad_hidden, axis=0)
    grad_mixed = norm_backward(grad_hidden, norm_one, inv_one, g_attn.astype(f32))
    grad_att_low = grad_mixed.astype(bf16)
    grad_bout = jnp.sum(grad_att_low.astype(f32), axis=0)
    grad_wout = product_tn(ctx_low, grad_att_low)
    grad_ctx = (
        product_nt(grad_att_low, w_out).astype(bf16).reshape(page_count, span_len, heads, HEAD_DIM)
    )
    probs = jnp.exp(masked_scores() - log_total)
    probs_low = probs.astype(bf16)
    grad_probs = jnp.einsum("pqhe,pkhe->phqk", grad_ctx, v_heads, preferred_element_type=f32)
    grad_vfull = jnp.einsum("phqk,pqhe->pkhe", probs_low, grad_ctx, preferred_element_type=f32)
    grad_scores = (
        probs * (grad_probs - jnp.sum(grad_probs * probs, axis=-1, keepdims=True))
    ).astype(bf16)
    grad_q_low = (
        (jnp.einsum("phqk,pkhe->pqhe", grad_scores, k_heads, preferred_element_type=f32) * scale)
        .astype(bf16)
        .reshape(row_count, width)
    )
    grad_kfull = (
        jnp.einsum("phqk,pqhe->pkhe", grad_scores, q_heads, preferred_element_type=f32) * scale
    )
    grad_keys, grad_values = (
        lax.psum_scatter(
            grad_kfull.reshape(page_count, seq_len, width).astype(jnp.bfloat16),
            "seq",
            scatter_dimension=1,
            tiled=True,
        ).astype(jnp.float32),
        lax.psum_scatter(
            grad_vfull.reshape(page_count, seq_len, width).astype(jnp.bfloat16),
            "seq",
            scatter_dimension=1,
            tiled=True,
        ).astype(jnp.float32),
    )
    grad_k_low = grad_keys.reshape(row_count, width).astype(bf16)
    grad_v_low = grad_values.reshape(row_count, width).astype(bf16)
    grad_tokens = (
        grad_mixed
        + product_nt(grad_q_low, w_query)
        + product_nt(grad_k_low, w_key)
        + product_nt(grad_v_low, w_value)
    )
    grad_wquery = product_tn(tok_low, grad_q_low)
    grad_bquery = jnp.sum(grad_q_low.astype(f32), axis=0)
    grad_wkey = product_tn(tok_low, grad_k_low)
    grad_wvalue = product_tn(tok_low, grad_v_low)
    grad_bvalue = jnp.sum(grad_v_low.astype(f32), axis=0)
    owned = (
        lax.psum_scatter(grad_wquery, ("page", "seq"), scatter_dimension=0, tiled=True),
        lax.psum_scatter(grad_bquery, ("page", "seq"), scatter_dimension=0, tiled=True),
        lax.psum_scatter(grad_wkey, ("page", "seq"), scatter_dimension=0, tiled=True),
        lax.psum_scatter(grad_wvalue, ("page", "seq"), scatter_dimension=0, tiled=True),
        lax.psum_scatter(grad_bvalue, ("page", "seq"), scatter_dimension=0, tiled=True),
        lax.psum_scatter(grad_wout, ("page", "seq"), scatter_dimension=0, tiled=True),
        lax.psum_scatter(grad_bout, ("page", "seq"), scatter_dimension=0, tiled=True),
        lax.psum_scatter(grad_gattn, ("page", "seq"), scatter_dimension=0, tiled=True),
        lax.psum_scatter(grad_sattn, ("page", "seq"), scatter_dimension=0, tiled=True),
        lax.psum_scatter(grad_winner, ("page", "seq"), scatter_dimension=0, tiled=True),
        lax.psum_scatter(grad_binner, ("page", "seq"), scatter_dimension=0, tiled=True),
        lax.psum_scatter(grad_wouter, ("page", "seq"), scatter_dimension=0, tiled=True),
        lax.psum_scatter(grad_bouter, ("page", "seq"), scatter_dimension=0, tiled=True),
        lax.psum_scatter(grad_gfinal, ("page", "seq"), scatter_dimension=0, tiled=True),
        lax.psum_scatter(grad_sfinal, ("page", "seq"), scatter_dimension=0, tiled=True),
    )
    return (
        result.reshape(tokens.shape),
        grad_tokens.reshape(tokens.shape),
        owned[0],
        owned[1],
        owned[2],
        owned[3],
        owned[4],
        owned[5],
        owned[6],
        owned[7],
        owned[8],
        owned[9],
        owned[10],
        owned[11],
        owned[12],
        owned[13],
        owned[14],
    )


MESH = pl.DeviceIdType.MESH
BF16 = jnp.bfloat16
F32 = jnp.float32
VECTORS = 8
SLAB = 16
NEGATIVE = -1000000000.0


def dot_nn(left, right):
    return lax.dot_general(left, right, (((1,), (0,)), ((), ())), preferred_element_type=F32)


def dot_nt(left, right):
    return lax.dot_general(left, right, (((1,), (1,)), ((), ())), preferred_element_type=F32)


def dot_tn(left, right):
    return lax.dot_general(left, right, (((0,), (0,)), ((), ())), preferred_element_type=F32)


class Sizes:
    def __init__(self, mesh, width, units, span):
        self.pages = mesh.shape["page"]
        self.parts = mesh.shape["seq"]
        self.half = self.pages // 2
        self.width = width
        self.units = units
        self.span = span
        self.length = span * self.parts
        self.row = width // (self.pages * self.parts)
        self.rows = self.row * self.parts
        self.unit = units // (self.pages * self.parts)
        self.mine = self.unit * self.pages
        self.cols = width // self.parts
        self.heads = self.cols // HEAD_DIM


def supported(mesh, token_shape, width, units):
    pages, parts = mesh.shape["page"], mesh.shape["seq"]
    return (
        parts == 4
        and pages % 2 == 0
        and pages >= 4
        and token_shape[0] == pages
        and token_shape[1] % (parts * 128) == 0
        and width % (pages * parts * 32) == 0
        and width // pages == 128
        and units % (pages * parts * 128) == 0
        and (width // parts) % 128 == 0
    )


def layer_kernel(z, names, *refs):
    r = types.SimpleNamespace(**dict(zip(names, refs)))
    send_sem, recv_sem, load_sem = r.send_sem, r.recv_sem, r.load_sem
    page = lax.axis_index("page")
    part = lax.axis_index("seq")
    counter = [0]

    def slots(count):
        first = counter[0]
        counter[0] += count
        return first

    odd = page % 2
    place = odd * (z.pages - 1 - page // 2) + (1 - odd) * (page // 2)

    def page_at(index):
        index = (index + z.pages) % z.pages
        late = index // z.half
        return (1 - late) * (2 * index) + late * (2 * z.pages - 1 - 2 * index)

    ring = [page] + [page_at(place + step) for step in range(1, z.pages)]
    peers = [part] + [
        ((part // 2 + j // 2) % 2) * 2 + (part % 2 + j % 2) % 2 for j in range(1, 4)
    ]

    def around(step):
        return ring[step % z.pages]

    def peer(j):
        return peers[j]

    rank = page * z.parts + part
    hold_page, hold_part = rank % z.pages, rank // z.pages
    flat = part * z.pages + page
    own_page, own_part = flat // z.parts, flat % z.parts
    moves = 1 - (1 - jnp.minimum(1, (hold_page - page) * (hold_page - page))) * (
        1 - jnp.minimum(1, (hold_part - part) * (hold_part - part))
    )

    class Copy:
        def __init__(self, src, dst, index, device, group=None):
            self.args = src, dst, index, device
            self.group = group

        def made(self, group):
            src, dst, index, device = self.args
            return pltpu.make_async_remote_copy(
                src_ref=src,
                dst_ref=dst,
                send_sem=send_sem.at[group],
                recv_sem=recv_sem.at[index],
                device_id=device,
                device_id_type=MESH,
            )

        def start(self):
            group = self.group
            if group is None:
                src = self.args[0]
                size = math.prod(src.shape) * jnp.dtype(src.dtype).itemsize
                if groups[-1] + size > z.group_bytes:
                    groups.append(0)
                groups[-1] += size
                group = 2 + len(groups) - 1
            self.made(group).start()

        def wait_recv(self):
            self.made(0).wait_recv()

        def wait_send(self):
            self.made(self.group).wait_send()

    groups = [0]
    copy = Copy

    def block(ref, index, size):
        return ref.at[pl.ds(pl.multiple_of(index * size, size), size)]

    barrier = pltpu.get_barrier_semaphore()

    def greet(device):
        pl.semaphore_signal(barrier, inc=1, device_id=device, device_id_type=MESH)

    for j in (1, 2, 3):
        greet((page, peer(j)))
    greet((around(1), part))
    greet((around(-1), part))

    @pl.when(moves == 1)
    def _():
        greet((hold_page, hold_part))
        greet((own_page, own_part))

    class Share:
        def __init__(self, ref, size, pieces=2):
            self.ref, self.size, self.pieces = ref, size, pieces
            self.first = slots(3 * pieces) - 1

        def copy(self, j, owner, k):
            height = self.size // self.pieces
            piece = block(self.ref, owner, self.size).at[pl.ds(k * height, height)]
            return copy(piece, piece, self.first + 3 * k + j, (page, peer(1 if j == 3 else j)))

        def start(self, k):
            self.copy(2, part, k).start()
            self.copy(1, part, k).start()

        def forward(self):
            for k in range(self.pieces):
                self.copy(2, peer(2), k).wait_recv()
                self.copy(3, peer(2), k).start()


        def wait(self, j):
            for k in range(self.pieces):
                self.copy(j, peer(j), k).wait_recv()

    class Combine:
        def __init__(self, phase, make, pieces=2):
            self.phase, self.make, self.pieces = phase, make, pieces
            self.first = slots(3 * pieces) - 1

        def copy(self, j, k):
            height = n // self.pieces
            at = pl.multiple_of(peer(j) * n + k * height, height)
            return copy(
                r.part_out.at[self.phase, pl.ds(at, height)],
                r.part_in.at[self.phase, j, pl.ds(k * height, height)],
                self.first + 3 * k + j,
                (page, peer(2 if j == 2 else 1)),
            )

        def term(self, j):
            value = self.make(pl.ds(pl.multiple_of(peer(j) * n, n), n))
            if j == 0:
                r.part_own[...] = value
                return
            height = n // self.pieces
            for k in range(self.pieces):
                rows = slice(k * height, (k + 1) * height)
                mine = value[rows]
                if j == 2:
                    self.copy(3, k).wait_recv()
                    mine = mine + r.part_in[self.phase, 3, rows, :].astype(F32)
                at = pl.multiple_of(peer(j) * n + k * height, height)
                r.part_out[self.phase, pl.ds(at, height), :] = mine.astype(BF16)
                self.copy(j, k).start()


        def finish(self, fn, after=None):
            height, size = n // self.pieces, 32
            for k in range(self.pieces):
                for j in (1, 2):
                    self.copy(j, k).wait_recv()

                def body(i, carry):
                    at = pl.multiple_of(k * height + i * size, size)
                    rows = pl.ds(at, size)
                    total = r.part_own[rows, :]
                    for j in (1, 2):
                        total = total + r.part_in[self.phase, j, rows, :].astype(F32)
                    fn(rows, at, total)
                    return carry

                lax.fori_loop(0, height // size, body, 0)
                if after is not None:
                    after(k)

    class Spread:
        def __init__(self, src, dst, size):
            self.src, self.dst, self.size, self.first = src, dst, size, slots(3) - 1

        def copy(self, j):
            return copy(
                block(self.src, peer(j), self.size),
                self.dst.at[j],
                self.first + j,
                (page, peer(j)),
            )

        def start(self):
            for j in (2, 3, 1):
                self.copy(j).start()

        def wait(self, j):
            self.copy(j).wait_recv()

    class Place:
        def __init__(self, src, dst, size, base):
            self.src, self.dst, self.size, self.base, self.first = src, dst, size, base, slots(3) - 1

        def copy(self, j, owner):
            return copy(
                block(self.src, peer(j), self.size),
                block(self.dst, self.base + owner, self.size),
                self.first + j,
                (page, peer(j)),
            )

        def start(self):
            for j in (2, 3, 1):
                self.copy(j, part).start()

        def wait(self):
            for j in (1, 2, 3):
                self.copy(j, peer(j)).wait_recv()

    class Gather:
        def __init__(self, ref, size, pieces=1):
            self.ref, self.size, self.pieces = ref, size, pieces
            self.first = slots(2 * z.half * pieces)

        def copy(self, t, d, k, step):
            height = self.size // self.pieces
            start = k * height
            if t == z.half - 1:
                height = height // 2
                start = start + d * height
            piece = block(self.ref, around(step), self.size).at[pl.ds(start, height)]
            return copy(
                piece,
                piece,
                self.first + (t * self.pieces + k) * 2 + d,
                (around(1 - 2 * d), part),
            )

        def wait(self, t, k, d):
            self.copy(t, d, k, -(1 - 2 * d) * (1 + t)).wait_recv()

        def step(self, t):
            for k in range(self.pieces):
                for d in (0, 1):
                    if t > 0:
                        self.wait(t - 1, k, d)
                    self.copy(t, d, k, -(1 - 2 * d) * t).start()


        def done(self):
            for k in range(self.pieces):
                for d in (0, 1):
                    self.wait(z.half - 1, k, d)

    class Reduce:
        def __init__(self, slot, stage, local, shape, kind, pieces=1):
            self.slot, self.stage, self.local = slot, stage, local
            self.size, self.kind, self.pieces = shape[0], kind, pieces
            self.wide = shape[1] // pieces
            self.first = slots(2 * z.half * pieces)

        def copy(self, t, d, k):
            h = self.size // 2
            if t == 0:
                src = self.stage.at[k, pl.ds(d * h, h)]
                dst = self.slot.at[k, d, 0, pl.ds(d * h, h)]
            else:
                src = self.slot.at[k, d, t - 1]
                dst = self.slot.at[k, d, t]
            return copy(
                src,
                dst,
                self.first + (t * self.pieces + k) * 2 + d,
                (around(1 - 2 * d), part),
            )


        def step(self, t):
            h = self.size // 2
            wide = self.wide
            if t == 0:
                term = self.local(around(z.half)).astype(self.kind)
                for k in range(self.pieces):
                    self.stage[k] = term[:, k * wide : (k + 1) * wide]
            else:
                terms = [
                    self.local(around((1 - 2 * d) * (z.half - t))) for d in (0, 1)
                ]
            for k in range(self.pieces):
                for d in (0, 1):
                    if t > 0:
                        term = terms[d][:, k * wide : (k + 1) * wide]
                        self.copy(t - 1, d, k).wait_recv()
                        held = self.slot.at[k, d, t - 1]
                        if t == 1:
                            near, far = pl.ds(d * h, h), pl.ds((1 - d) * h, h)
                            term_near = term[d * h : (d + 1) * h]
                            term_far = term[(1 - d) * h : (2 - d) * h]
                            held[near] = (held[near].astype(F32) + term_near).astype(self.kind)
                            held[far] = term_far.astype(self.kind)
                        else:
                            held[...] = (held[...].astype(F32) + term).astype(self.kind)
                    self.copy(t, d, k).start()

        def total(self, out):
            term = self.local(page)
            last = z.half - 1
            for k in range(self.pieces):
                for d in (0, 1):
                    self.copy(last, d, k).wait_recv()
                at = slice(k * self.wide, (k + 1) * self.wide)
                out[:, at] = (
                    term[:, at] + self.slot[k, 0, last].astype(F32) + self.slot[k, 1, last].astype(F32)
                ).astype(out.dtype)

    c, w, n = z.cols, z.width, z.span

    def fetch(i, name):
        return pltpu.make_async_copy(getattr(r, name), getattr(r, z.held + name), load_sem.at[i])

    for i, name in enumerate(z.fetched):
        fetch(i, name).start()
    hbm = r
    r = types.SimpleNamespace(**vars(hbm))
    for name in z.fetched:
        setattr(r, name, getattr(hbm, z.held + name))
    fetches = iter(range(len(z.fetched)))

    def arrive(count):
        for _ in range(count):
            i = next(fetches)
            pltpu.make_async_copy(
                getattr(hbm, z.fetched[i]), getattr(r, z.fetched[i]), load_sem.at[i]
            ).wait()

    arrive(3)
    for q in range(z.parts):
        rows = pl.ds(q * z.row, z.row)
        for i, weight in enumerate((r.w_query, r.w_key, r.w_value)):
            r.cut_qkv[rows, i * c : (i + 1) * c] = weight[:, q * c : (q + 1) * c].astype(BF16)
    mine = pl.multiple_of(part * SLAB, SLAB)
    for i, small in enumerate(
        (r.b_query, r.b_value, r.b_out, r.g_attn, r.s_attn, r.b_outer, r.g_final, r.s_final)
    ):
        r.vec_raw[pl.ds(mine + i, 1), 0 : z.row] = small[...]
    at_page = pl.multiple_of(page * SLAB, SLAB)
    r.vec_all[pl.ds(at_page + VECTORS, 1), :] = r.b_inner[...]
    arrive(1)
    r.outer_w[pl.ds(pl.multiple_of(page * z.unit, z.unit), z.unit), :] = r.w_outer[...].astype(
        BF16
    )

    ring_qkv = Gather(r.qkv_w, z.rows, 2)
    ring_vec = Gather(r.vec_all, SLAB)
    ring_inner = Gather(r.inner_w, z.rows, 2)
    ring_out = Gather(r.out_w, z.row)
    ring_outer = Gather(r.outer_w, z.unit, 2)
    cut_qkv = Place(r.cut_qkv, r.qkv_w, z.row, page * z.parts)
    cut_inner = Place(r.cut_inner, r.inner_w, z.row, page * z.parts)
    share_tok = Share(r.tok_all, n)

    class ShareVec:
        first = slots(3) - 1

        def copy(self, j, owner):
            piece = block(r.vec_raw, owner, SLAB).at[pl.ds(0, VECTORS)]
            return copy(piece, piece, self.first + j, (page, peer(j)))

    vec_share = ShareVec()
    hold = slots(1)

    def hold_copy(slot):
        return copy(r.own_out, block(r.out_w, slot, z.row), hold, (hold_page, hold_part), 0)

    pl.semaphore_wait(barrier, 5 + 2 * moves)
    cut_qkv.start()
    for j in (2, 3, 1):
        vec_share.copy(j, part).start()
    ring_outer.step(0)
    arrive(1)
    r.own_out[...] = r.w_out[...].astype(BF16)
    arrive(1)

    @pl.when(moves == 1)
    def _():
        hold_copy(hold_page).start()

    @pl.when(moves == 0)
    def _():
        r.out_w[pl.ds(pl.multiple_of(page * z.row, z.row), z.row), :] = r.own_out[...]

    r.tok_all[pl.ds(pl.multiple_of(part * n, n), n), :] = r.tokens[...].astype(BF16)
    share_tok.start(0)
    share_tok.start(1)
    arrive(1)
    for q in range(z.parts):
        rows = pl.ds(q * z.row, z.row)
        for g in range(z.pages):
            at = (z.parts * g + q) * z.unit
            r.cut_inner[rows, g * z.unit : (g + 1) * z.unit] = r.w_inner[
                :, at : at + z.unit
            ].astype(BF16)
    cut_inner.start()
    own_rows = pl.ds(pl.multiple_of(rank * z.row, z.row), z.row)
    cut_rows = pl.ds(pl.multiple_of(part * z.row, z.row), z.row)
    r.qkv_w[own_rows, :] = r.cut_qkv[cut_rows, :]
    r.inner_w[own_rows, :] = r.cut_inner[cut_rows, :]

    cut_qkv.wait()
    ring_qkv.step(0)
    for j in (1, 2, 3):
        vec_share.copy(j, peer(j)).wait_recv()
    lane = lax.broadcasted_iota(jnp.int32, (VECTORS, 128), 1)
    total = jnp.zeros((VECTORS, 128), F32)
    for q in range(z.parts):
        tile = r.vec_raw[q * SLAB : q * SLAB + VECTORS, :]
        if q:
            tile = pltpu.roll(tile, q * z.row, 1)
        total = total + jnp.where(lane // z.row == q, tile, 0.0)
    r.vec_all[pl.ds(at_page, VECTORS), :] = total
    ring_vec.step(0)
    ring_qkv.step(1)
    ring_vec.step(1)

    @pl.when(moves == 1)
    def _():
        hold_copy(page).wait_recv()

    ring_out.step(0)
    ring_qkv.step(2)
    ring_vec.step(2)
    ring_out.step(1)
    share_tok.forward()
    ring_qkv.step(3)
    ring_vec.step(3)
    ring_out.step(2)
    cut_inner.wait()
    ring_inner.step(0)
    ring_vec.done()

    for g in range(z.pages):
        tile = r.vec_all[g * SLAB : (g + 1) * SLAB, :].astype(BF16).astype(F32)
        r.vecs[:, g * 128 : (g + 1) * 128] = tile[0:VECTORS]
        r.b_mine[:, g * z.unit : (g + 1) * z.unit] = tile[VECTORS : VECTORS + 1]

    def vector(i):
        return r.vecs[i : i + 1, :]

    my_cols = pl.ds(pl.multiple_of(part * c, c), c)

    share_tok.wait(1)
    share_tok.wait(3)
    ring_qkv.done()

    def make_qkv(b, carry):
        rows = pl.ds(pl.multiple_of(b * n, n), n)
        out = dot_nn(r.tok_all[rows, :], r.qkv_w[...])
        r.qkv[rows, 0:c] = (out[:, 0:c] + r.vecs[0:1, my_cols]).astype(BF16)
        r.qkv[rows, c : 2 * c] = out[:, c : 2 * c].astype(BF16)
        r.qkv[rows, 2 * c :] = (out[:, 2 * c :] + r.vecs[1:2, my_cols]).astype(BF16)
        return carry

    lax.fori_loop(0, z.parts, make_qkv, 0)
    ring_inner.step(1)
    ring_out.step(3)
    ring_outer.step(1)

    scale = HEAD_DIM ** (-0.5)
    first_head = lax.broadcasted_iota(jnp.int32, (n, 128), 1) < HEAD_DIM
    key_place = lax.broadcasted_iota(jnp.int32, (n, z.length), 1)
    valid = r.valid[0]

    def pair_cols(kind, pair):
        return pl.ds(kind * c + pair * 128, 128)

    def attend(pair):
        def body(b, carry):
            rows = pl.ds(pl.multiple_of(b * n, n), n)
            queries = r.qkv[rows, pair_cols(0, pair)]
            keys = r.qkv[:, pair_cols(1, pair)]
            values = r.qkv[:, pair_cols(2, pair)]
            outs = []
            for h in range(2):
                mine = first_head if h == 0 else ~first_head
                scores = dot_nt(jnp.where(mine, queries, jnp.zeros_like(queries)), keys) * scale
                scores = jnp.where(key_place < valid, scores, NEGATIVE)
                top = jnp.max(scores, axis=-1, keepdims=True)
                weight = jnp.exp(scores - top)
                probs = weight * (1.0 / jnp.sum(weight, axis=-1, keepdims=True))
                r.probs[2 * pair + h, rows, :] = probs
                outs.append(dot_nn(probs.astype(BF16), values))
            r.ctx[rows, pl.ds(pair * 128, 128)] = jnp.where(first_head, outs[0], outs[1]).astype(
                BF16
            )
            return carry

        lax.fori_loop(0, z.parts, body, 0)

    attend(0)
    attend(1)
    ring_out.done()

    combine = Combine(0, lambda rows: dot_nn(r.ctx[rows, :], r.out_w[...]))
    combine.term(3)
    combine.term(2)
    ring_inner.step(2)
    combine.term(1)
    combine.term(0)
    ring_outer.step(2)

    def add_column_sum(i, values):
        r.sums[i : i + 1, :] += jnp.sum(values, axis=0, keepdims=True)

    r.sums[...] = jnp.zeros_like(r.sums)

    share_hid = Share(r.hid_all, n)

    def first_norm(rows, at, total):
        mixed = r.tokens[rows, :] + (total + vector(2))
        normed, inverse = norm_parts(mixed)
        hidden = normed * vector(3) + vector(4)
        r.norm_one[rows, :] = normed
        r.inv_one[rows, :] = inverse
        r.hidden[rows, :] = hidden
        r.hid_all[pl.ds(pl.multiple_of(part * n + at, 32), 32), :] = hidden.astype(BF16)

    combine.finish(first_norm, share_hid.start)
    ring_inner.step(3)
    ring_outer.step(3)
    ring_inner.done()

    tile = 256

    def make_inner(j):
        rows = pl.ds(pl.multiple_of(peer(j) * n, n), n)

        def columns(i, carry):
            cols = pl.ds(pl.multiple_of(i * tile, tile), tile)
            inner = dot_nn(r.hid_all[rows, :], r.inner_w[:, cols]) + r.b_mine[:, cols]
            active, slope = gelu_parts(inner)
            r.active[rows, cols] = active.astype(BF16)
            r.slope[rows, cols] = slope
            return carry

        lax.fori_loop(0, z.mine // tile, columns, 0)

    make_inner(0)
    share_hid.wait(1)
    make_inner(1)
    share_hid.forward()
    make_inner(2)
    share_hid.wait(3)
    make_inner(3)
    ring_outer.done()
    combine_two = Combine(1, lambda rows: dot_nn(r.active[rows, :], r.outer_w[...]))
    for j in (3, 2, 1, 0):
        combine_two.term(j)
    share_gf = Share(r.gf_all, n)

    arrive(1)

    def second_norm(rows, at, total):
        outer = total + vector(5)
        normed, inverse = norm_parts(r.hidden[rows, :] + outer)
        r.o_out[rows, :] = normed * vector(6) + vector(7)
        grad = r.out_grad[rows, :]
        add_column_sum(6, grad * normed)
        add_column_sum(7, grad)
        grad_sum = norm_backward(grad, normed, inverse, vector(6))
        low = grad_sum.astype(BF16)
        add_column_sum(5, low.astype(F32))
        r.grad_sum[rows, :] = grad_sum
        r.gf_all[pl.ds(pl.multiple_of(part * n + at, 32), 32), :] = low

    combine_two.finish(second_norm, share_gf.start)

    def chunk_term(left, right, size):
        def local(g):
            cols = pl.ds(pl.multiple_of(g * size, size), size)
            return dot_tn(left[:, cols], right[...])

        return local

    reduce_outer_a = Reduce(
        r.slot_outer_a, r.stage_outer_a,
        chunk_term(r.active, r.gf_all.at[:, 0 : w // 2], z.unit), (z.unit, w // 2), BF16,
    )
    reduce_outer_b = Reduce(
        r.slot_outer_b, r.stage_outer_b,
        chunk_term(r.active, r.gf_all.at[:, w // 2 :], z.unit), (z.unit, w // 2), BF16,
    )
    reduce_inner = Reduce(
        r.slot_inner, r.stage_inner, chunk_term(r.hid_all, r.grad_inner, z.rows),
        (z.rows, z.mine), BF16, 2
    )
    reduce_qkv = Reduce(
        r.slot_qkv, r.stage_qkv, chunk_term(r.tok_all, r.grad_qkv, z.rows),
        (z.rows, 3 * c), BF16, 2
    )
    reduce_out = Reduce(
        r.slot_out, r.stage_out,
        lambda g: r.term_out[pl.ds(pl.multiple_of(g * z.row, z.row), z.row), :], (z.row, w), BF16,
    )
    reduce_vec = Reduce(
        r.slot_vec, r.stage_vec,
        lambda g: r.term_vec[pl.ds(pl.multiple_of(g * SLAB, SLAB), SLAB), :], (SLAB, 128), F32,
    )

    r.b_sum[...] = jnp.zeros_like(r.b_sum)

    def make_grad_inner(j):
        rows = pl.ds(pl.multiple_of(peer(j) * n, n), n)

        def columns(i, carry):
            cols = pl.ds(pl.multiple_of(i * tile, tile), tile)
            grad = dot_nt(r.gf_all[rows, :], r.outer_w[cols, :]) * r.slope[rows, cols]
            low = grad.astype(BF16)
            r.grad_inner[rows, cols] = low
            r.b_sum[:, cols] += jnp.sum(low.astype(F32), axis=0, keepdims=True)
            return carry

        lax.fori_loop(0, z.mine // tile, columns, 0)

    make_grad_inner(0)
    share_gf.wait(1)
    make_grad_inner(1)
    share_gf.forward()
    make_grad_inner(2)
    share_gf.wait(3)
    reduce_outer_a.step(0)
    make_grad_inner(3)
    combine_three = Combine(2, lambda rows: dot_nt(r.grad_inner[rows, :], r.inner_w[...]))
    combine_three.term(3)
    combine_three.term(2)
    reduce_inner.step(0)
    reduce_outer_a.step(1)
    combine_three.term(1)
    combine_three.term(0)
    reduce_inner.step(1)

    share_ga = Share(r.ga_all, n)

    def first_norm_back(rows, at, total):
        grad = r.grad_sum[rows, :] + total
        normed = r.norm_one[rows, :]
        add_column_sum(3, grad * normed)
        add_column_sum(4, grad)
        mixed = norm_backward(grad, normed, r.inv_one[rows, :], vector(3))
        low = mixed.astype(BF16)
        add_column_sum(2, low.astype(F32))
        r.grad_mixed[rows, :] = mixed
        r.ga_all[pl.ds(pl.multiple_of(part * n + at, 32), 32), :] = low

    combine_three.finish(first_norm_back, share_ga.start)

    def make_grad_ctx(j):
        rows = pl.ds(pl.multiple_of(peer(j) * n, n), n)
        r.grad_ctx[rows, :] = dot_nt(r.ga_all[rows, :], r.out_w[...]).astype(BF16)

    make_grad_ctx(0)
    share_ga.wait(1)
    make_grad_ctx(1)
    reduce_outer_a.step(2)
    reduce_inner.step(2)
    share_ga.forward()
    make_grad_ctx(2)
    share_ga.wait(3)
    make_grad_ctx(3)
    r.term_out[...] = dot_tn(r.ctx[...], r.ga_all[...])
    reduce_out.step(0)
    reduce_outer_a.step(3)

    def attend_back(pair):
        r.grad_kv[...] = jnp.zeros_like(r.grad_kv)

        def body(b, carry):
            rows = pl.ds(pl.multiple_of(b * n, n), n)
            queries = r.qkv[rows, pair_cols(0, pair)]
            keys = r.qkv[:, pair_cols(1, pair)]
            values = r.qkv[:, pair_cols(2, pair)]
            grad = r.grad_ctx[rows, pl.ds(pair * 128, 128)]
            outs = []
            for h in range(2):
                mine = first_head if h == 0 else ~first_head
                grad_mine = jnp.where(mine, grad, jnp.zeros_like(grad))
                query_mine = jnp.where(mine, queries, jnp.zeros_like(queries))
                probs = r.probs[2 * pair + h, rows, :]
                grad_probs = dot_nt(grad_mine, values)
                r.grad_kv[1] += dot_tn(probs.astype(BF16), grad_mine)
                inside = jnp.sum(grad_probs * probs, axis=-1, keepdims=True)
                grad_scores = (probs * (grad_probs - inside)).astype(BF16)
                outs.append(dot_nn(grad_scores, keys))
                r.grad_kv[0] += dot_tn(grad_scores, query_mine)
            r.grad_qkv[rows, pair_cols(0, pair)] = (
                jnp.where(first_head, outs[0], outs[1]) * scale
            ).astype(BF16)
            return carry

        lax.fori_loop(0, z.parts, body, 0)
        r.grad_qkv[:, pair_cols(1, pair)] = (r.grad_kv[0] * scale).astype(BF16)
        r.grad_qkv[:, pair_cols(2, pair)] = r.grad_kv[1].astype(BF16)

    attend_back(0)
    reduce_inner.step(3)
    reduce_out.step(1)
    attend_back(1)
    reduce_qkv.step(0)
    reduce_outer_b.step(0)
    reduce_out.step(2)

    r.sums[0:1, my_cols] = jnp.sum(r.grad_qkv[:, 0:c].astype(F32), axis=0, keepdims=True)
    r.sums[1:2, my_cols] = jnp.sum(r.grad_qkv[:, 2 * c :].astype(F32), axis=0, keepdims=True)
    r.term_vec[...] = jnp.zeros_like(r.term_vec)
    for g in range(z.pages):
        r.term_vec[g * SLAB : g * SLAB + VECTORS, :] = r.sums[:, g * 128 : (g + 1) * 128]
        r.term_vec[g * SLAB + VECTORS : g * SLAB + VECTORS + 1, :] = r.b_sum[
            :, g * z.unit : (g + 1) * z.unit
        ]
    reduce_vec.step(0)

    combine_four = Combine(3, lambda rows: dot_nt(r.grad_qkv[rows, :], r.qkv_w[...]))
    combine_four.term(3)
    combine_four.term(2)
    reduce_qkv.step(1)
    reduce_outer_b.step(1)
    reduce_vec.step(1)
    reduce_out.step(3)
    combine_four.term(1)
    combine_four.term(0)

    reduce_inner.total(r.fin_inner)
    fin_inner = Spread(r.fin_inner, r.got_inner, z.row)
    fin_inner.start()
    reduce_qkv.step(2)
    reduce_outer_b.step(2)
    reduce_vec.step(2)

    def input_rows(rows, at, total):
        r.o_grad[rows, :] = r.grad_mixed[rows, :] + total

    combine_four.finish(input_rows)
    reduce_outer_a.total(r.o_outer.at[:, 0 : w // 2])
    reduce_out.total(r.fin_out)
    home = slots(1)

    def home_copy():
        return copy(r.fin_out, r.got_out, home, (own_page, own_part), 1)

    @pl.when(moves == 1)
    def _():
        home_copy().start()

    @pl.when(moves == 0)
    def _():
        r.got_out[...] = r.fin_out[...]

    reduce_qkv.step(3)
    reduce_vec.step(3)
    reduce_outer_b.step(3)
    reduce_vec.total(r.fin_vec)

    class VecAll:
        first = slots(3) - 1

        def copy(self, j):
            return copy(r.fin_vec, r.got_vec.at[j], self.first + j, (page, peer(j)))

    fin_vec = VecAll()
    for j in (2, 3, 1):
        fin_vec.copy(j).start()
    reduce_qkv.total(r.fin_qkv)
    fin_qkv = Spread(r.fin_qkv, r.got_qkv, z.row)
    fin_qkv.start()

    my_rows = pl.ds(pl.multiple_of(part * z.row, z.row), z.row)

    def deliver(spread, mine, got, out):
        for j in range(4):
            if j:
                spread.wait(j)
            value = got[j] if j else mine[my_rows, :]
            out[peer(j)] = value

    deliver(fin_inner, r.fin_inner, r.got_inner, r.o_inner)

    @pl.when(moves == 1)
    def _():
        home_copy().wait_recv()

    r.o_wout[...] = r.got_out[...]
    summed = r.fin_vec[0:VECTORS, :]
    for j in (1, 2, 3):
        fin_vec.copy(j).wait_recv()
        summed = summed + r.got_vec[j, 0:VECTORS, :]
    r.o_vec[0:VECTORS, :] = pltpu.roll(summed, (128 - part * z.row) % 128, 1)
    r.o_vec[VECTORS:, :] = r.fin_vec[VECTORS:, :]
    reduce_outer_b.total(r.o_outer.at[:, w // 2 :])
    deliver(fin_qkv, r.fin_qkv, r.got_qkv, r.o_qkv)

    for group, size in enumerate(groups):
        rows = r.measure.at[pl.ds(0, size // 512)]
        copy(rows, rows, 0, (page, part), 2 + group).wait_send()

    @pl.when(moves == 1)
    def _():
        hold_copy(hold_page).wait_send()
        home_copy().wait_send()

    assert counter[0] == z.sems and 2 + len(groups) <= z.groups, (counter, groups)


def finish_kernel(z, out, grad, outer, inner, qkv, wout, vec, *outs):
    (o_out, o_grad, o_wq, o_bq, o_wk, o_wv, o_bv, o_wo, o_bo, o_ga, o_sa, o_wi, o_bi, o_wu, o_bu, o_gf, o_sf) = outs
    o_out[...] = out[...]
    o_grad[...] = grad[...]
    o_wu[...] = outer[...]
    o_wo[...] = wout[...].astype(F32)
    c = z.cols
    for q in range(z.parts):
        for i, ref in enumerate((o_wq, o_wk, o_wv)):
            ref[:, q * c : (q + 1) * c] = qkv[q, :, i * c : (i + 1) * c].astype(F32)
        for g in range(z.pages):
            at = (z.parts * g + q) * z.unit
            o_wi[:, at : at + z.unit] = inner[q, :, g * z.unit : (g + 1) * z.unit].astype(F32)
    for i, ref in enumerate((o_bq, o_bv, o_bo, o_ga, o_sa, o_bu, o_gf, o_sf)):
        ref[...] = vec[i : i + 1, 0 : z.row]
    o_bi[...] = vec[VECTORS : VECTORS + 1, :]


def paged_layer(z, tokens, valid_len, params, out_grad):
    (
        w_query, b_query, w_key, w_value, b_value, w_out, b_out, g_attn, s_attn,
        w_inner, b_inner, w_outer, b_outer, g_final, s_final,
    ) = params
    flat = lambda v: v.reshape(1, v.shape[0])
    c, w, n, ln, half = z.cols, z.width, z.span, z.length, z.half
    ins = dict(
        valid=valid_len,
        tokens=tokens.reshape(n, w),
        out_grad=out_grad.reshape(n, w),
        w_query=w_query, w_key=w_key, w_value=w_value, w_out=w_out,
        w_inner=w_inner, w_outer=w_outer,
        b_query=flat(b_query), b_value=flat(b_value), b_out=flat(b_out),
        g_attn=flat(g_attn), s_attn=flat(s_attn), b_inner=flat(b_inner),
        b_outer=flat(b_outer), g_final=flat(g_final), s_final=flat(s_final),
    )
    outs = dict(
        o_out=((n, w), F32),
        o_grad=((n, w), F32),
        o_outer=((z.unit, w), F32),
        o_inner=((z.parts, z.row, z.mine), BF16),
        o_qkv=((z.parts, z.row, 3 * c), BF16),
        o_wout=((z.row, w), BF16),
        o_vec=((SLAB, 128), F32),
    )
    scratch = dict(
        qkv_w=((w, 3 * c), BF16),
        inner_w=((w, z.mine), BF16),
        out_w=((c, w), BF16),
        outer_w=((z.mine, w), BF16),
        vec_all=((z.pages * SLAB, 128), F32),
        vec_raw=((z.parts * SLAB, 128), F32),
        cut_qkv=((z.rows, 3 * c), BF16),
        cut_inner=((z.rows, z.mine), BF16),
        own_out=((z.row, w), BF16),
        vecs=((VECTORS, w), F32),
        b_mine=((1, z.mine), F32),
        tok_all=((ln, w), BF16),
        hid_all=((ln, w), BF16),
        gf_all=((ln, w), BF16),
        ga_all=((ln, w), BF16),
        qkv=((ln, 3 * c), BF16),
        grad_qkv=((ln, 3 * c), BF16),
        probs=((z.heads, ln, ln), F32),
        measure=((8192, 128), F32),
        ctx=((ln, c), BF16),
        grad_ctx=((ln, c), BF16),
        grad_kv=((2, ln, 128), F32),
        part_out=((4, ln, w), BF16),
        part_in=((4, 4, n, w), BF16),
        part_own=((n, w), F32),
        norm_one=((n, w), F32),
        inv_one=((n, 1), F32),
        hidden=((n, w), F32),
        grad_sum=((n, w), F32),
        grad_mixed=((n, w), F32),
        active=((ln, z.mine), BF16),
        slope=((ln, z.mine), F32),
        grad_inner=((ln, z.mine), BF16),
        sums=((VECTORS, w), F32),
        b_sum=((1, z.mine), F32),
        term_out=((c, w), F32),
        term_vec=((z.pages * SLAB, 128), F32),
        slot_outer_a=((1, 2, half, z.unit, w // 2), BF16), stage_outer_a=((1, z.unit, w // 2), BF16),
        slot_outer_b=((1, 2, half, z.unit, w // 2), BF16), stage_outer_b=((1, z.unit, w // 2), BF16),
        slot_inner=((2, 2, half, z.rows, z.mine // 2), BF16), stage_inner=((2, z.rows, z.mine // 2), BF16),
        slot_qkv=((2, 2, half, z.rows, 3 * c // 2), BF16), stage_qkv=((2, z.rows, 3 * c // 2), BF16),
        slot_out=((1, 2, half, z.row, w // 1), BF16), stage_out=((1, z.row, w // 1), BF16),
        slot_vec=((1, 2, half, SLAB, 128 // 1), F32), stage_vec=((1, SLAB, 128 // 1), F32),
        fin_inner=((z.rows, z.mine), BF16), got_inner=((4, z.row, z.mine), BF16),
        fin_qkv=((z.rows, 3 * c), BF16), got_qkv=((4, z.row, 3 * c), BF16),
        fin_out=((z.row, w), BF16), got_out=((z.row, w), BF16),
        fin_vec=((SLAB, 128), F32), got_vec=((4, SLAB, 128), F32),
    )
    z.sems = 196
    z.groups, z.group_bytes = 7, 4 << 20
    fetched = dict(w_query=0, w_key=0, w_value=0, w_outer=0, w_out=0, tokens=0, w_inner=0, out_grad=0)
    z.fetched, z.held = tuple(fetched), "f_"
    for name in z.fetched:
        scratch[z.held + name] = (ins[name].shape, F32)
    sems = [pltpu.SemaphoreType.DMA((z.groups,)), pltpu.SemaphoreType.DMA((z.sems,)), pltpu.SemaphoreType.DMA((len(fetched),))]
    names = list(ins) + list(outs) + list(scratch) + list(dict(send_sem=0, recv_sem=0, load_sem=0))
    vmem = pl.BlockSpec(memory_space=pltpu.VMEM)
    parts = pl.pallas_call(
        functools.partial(layer_kernel, z, names),
        out_shape=[jax.ShapeDtypeStruct(*v) for v in outs.values()],
        in_specs=[
            pl.BlockSpec(memory_space=pltpu.SMEM)
            if v is valid_len
            else pl.BlockSpec(memory_space=pl.ANY)
            if k in fetched
            else vmem
            for k, v in ins.items()
        ],
        out_specs=[vmem] * len(outs),
        scratch_shapes=[pltpu.VMEM(*v) for v in scratch.values()]
        + sems,
        compiler_params=pltpu.CompilerParams(
            collective_id=0, has_side_effects=True, vmem_limit_bytes=67043328
        ),
        name="layer",
    )(*ins.values())
    row, big = z.row, jax.ShapeDtypeStruct((n, w), F32)
    mat = jax.ShapeDtypeStruct((row, w), F32)
    vec = jax.ShapeDtypeStruct((1, row), F32)
    shapes = [
        big, big, mat, vec, mat, mat, vec, mat, vec, vec, vec,
        jax.ShapeDtypeStruct((row, z.units), F32), jax.ShapeDtypeStruct((1, z.unit), F32),
        jax.ShapeDtypeStruct((z.unit, w), F32), vec, vec, vec,
    ]
    results = pl.pallas_call(
        functools.partial(finish_kernel, z),
        out_shape=shapes,
        in_specs=[vmem] * 7,
        out_specs=[vmem] * len(shapes),
        name="finish",
    )(*parts)
    results = list(results)
    for i in (0, 1):
        results[i] = results[i].reshape(tokens.shape)
    for i in range(2, 17):
        if results[i].shape[0] == 1:
            results[i] = results[i].reshape(results[i].shape[1])
    return tuple(results)


def body(
    tokens,
    valid_len,
    query_weight,
    query_bias,
    key_weight,
    value_weight,
    value_bias,
    output_weight,
    output_bias,
    attn_gain,
    attn_shift,
    inner_weight,
    inner_bias,
    outer_weight,
    outer_bias,
    final_gain,
    final_shift,
    out_grad,
):
    lowered = [
        piece.astype(jnp.bfloat16)
        for piece in (
            query_weight,
            query_bias,
            key_weight,
            value_weight,
            value_bias,
            output_weight,
            output_bias,
            attn_gain,
            attn_shift,
            inner_weight,
            inner_bias,
            outer_weight,
            outer_bias,
            final_gain,
            final_shift,
        )
    ]
    outputs = sequence_layer(tokens, valid_len, lowered, out_grad)
    return outputs


def solution(mesh):
    in_specs = (
        P("page", "seq", None),
        P("page"),
        P(("page", "seq"), None),
        P(("page", "seq")),
        P(("page", "seq"), None),
        P(("page", "seq"), None),
        P(("page", "seq")),
        P(("page", "seq"), None),
        P(("page", "seq")),
        P(("page", "seq")),
        P(("page", "seq")),
        P(("page", "seq"), None),
        P(("page", "seq")),
        P(("page", "seq"), None),
        P(("page", "seq")),
        P(("page", "seq")),
        P(("page", "seq")),
        P("page", "seq", None),
    )
    out_specs = (
        P("page", "seq", None),
        P("page", "seq", None),
        P(("page", "seq"), None),
        P(("page", "seq")),
        P(("page", "seq"), None),
        P(("page", "seq"), None),
        P(("page", "seq")),
        P(("page", "seq"), None),
        P(("page", "seq")),
        P(("page", "seq")),
        P(("page", "seq")),
        P(("page", "seq"), None),
        P(("page", "seq")),
        P(("page", "seq"), None),
        P(("page", "seq")),
        P(("page", "seq")),
        P(("page", "seq")),
    )

    def layer(*arrays):
        width, units = arrays[11].shape
        if supported(mesh, arrays[0].shape, width, units):
            z = Sizes(mesh, width, units, arrays[0].shape[1] // mesh.shape["seq"])

            def run(tokens, valid_len, *rest):
                return paged_layer(z, tokens, valid_len, rest[:-1], rest[-1])

            chosen = run
        else:
            chosen = body
        return jax.shard_map(
            chosen, mesh=mesh, in_specs=in_specs, out_specs=out_specs, check_vma=False
        )(*arrays)

    return layer
```

```python
import functools
import math
import types

import jax
import jax.numpy as jnp
from jax import lax
from jax.experimental import pallas as pl
from jax.experimental.pallas import tpu as pltpu
from jax.sharding import PartitionSpec as P

HEAD_DIM = 64


EPSILON = 1e-05
INV_ROOT_TWO = 1.0 / math.sqrt(2.0)
INV_ROOT_TWO_PI = 1.0 / math.sqrt(2.0 * math.pi)


def product(left, right):
    return jnp.dot(left, right, preferred_element_type=jnp.float32)


def product_tn(left, right):
    return lax.dot_general(
        left, right, (((0,), (0,)), ((), ())), preferred_element_type=jnp.float32
    )


def product_nt(left, right):
    return lax.dot_general(
        left, right, (((1,), (1,)), ((), ())), preferred_element_type=jnp.float32
    )


def norm_parts(values):
    center = values - jnp.mean(values, axis=-1, keepdims=True)
    inverse = lax.rsqrt(jnp.mean(center * center, axis=-1, keepdims=True) + EPSILON)
    return (center * inverse, inverse)


def norm_backward(grad_out, normed, inverse, gain):
    scaled = grad_out * gain
    return inverse * (
        scaled
        - jnp.mean(scaled, axis=-1, keepdims=True)
        - normed * jnp.mean(scaled * normed, axis=-1, keepdims=True)
    )


def gelu_parts(values):
    cumulative = 0.5 * (1.0 + lax.erf(values * INV_ROOT_TWO))
    return (
        values * cumulative,
        cumulative + values * jnp.exp(-0.5 * values * values) * INV_ROOT_TWO_PI,
    )


def sequence_layer(tokens, valid_len, lowered, out_grad):
    fetched = (
        lax.all_gather(lowered[0], ("page", "seq"), axis=0, tiled=True),
        lax.all_gather(lowered[1], ("page", "seq"), axis=0, tiled=True),
        lax.all_gather(lowered[2], ("page", "seq"), axis=0, tiled=True),
        lax.all_gather(lowered[3], ("page", "seq"), axis=0, tiled=True),
        lax.all_gather(lowered[4], ("page", "seq"), axis=0, tiled=True),
        lax.all_gather(lowered[5], ("page", "seq"), axis=0, tiled=True),
        lax.all_gather(lowered[6], ("page", "seq"), axis=0, tiled=True),
        lax.all_gather(lowered[7], ("page", "seq"), axis=0, tiled=True),
        lax.all_gather(lowered[8], ("page", "seq"), axis=0, tiled=True),
        lax.all_gather(lowered[9], ("page", "seq"), axis=0, tiled=True),
        lax.all_gather(lowered[10], ("page", "seq"), axis=0, tiled=True),
        lax.all_gather(lowered[11], ("page", "seq"), axis=0, tiled=True),
        lax.all_gather(lowered[12], ("page", "seq"), axis=0, tiled=True),
        lax.all_gather(lowered[13], ("page", "seq"), axis=0, tiled=True),
        lax.all_gather(lowered[14], ("page", "seq"), axis=0, tiled=True),
    )
    (
        w_query,
        b_query,
        w_key,
        w_value,
        b_value,
        w_out,
        b_out,
        g_attn,
        s_attn,
        w_inner,
        b_inner,
        w_outer,
        b_outer,
        g_final,
        s_final,
    ) = fetched
    f32 = jnp.float32
    bf16 = jnp.bfloat16
    scale = HEAD_DIM ** (-0.5)
    page_count, span_len, width = tokens.shape
    heads = width // HEAD_DIM
    row_count = page_count * span_len
    tok_rows = tokens.reshape(row_count, width)
    tok_low = tok_rows.astype(bf16)
    q_low = (product(tok_low, w_query) + b_query.astype(f32)).astype(bf16)
    k_low = product(tok_low, w_key).astype(bf16)
    v_low = (product(tok_low, w_value) + b_value.astype(f32)).astype(bf16)
    k_full, v_full = (
        lax.all_gather(k_low.reshape(page_count, span_len, width), "seq", axis=1, tiled=True),
        lax.all_gather(v_low.reshape(page_count, span_len, width), "seq", axis=1, tiled=True),
    )
    seq_len = k_full.shape[1]
    q_heads = q_low.reshape(page_count, span_len, heads, HEAD_DIM)
    k_heads = k_full.reshape(page_count, seq_len, heads, HEAD_DIM)
    v_heads = v_full.reshape(page_count, seq_len, heads, HEAD_DIM)
    key_mask = (lax.broadcasted_iota(jnp.int32, (page_count, seq_len), 1) < valid_len[:, None])[
        :, None, None, :
    ]

    def masked_scores():
        raw = jnp.einsum("pqhe,pkhe->phqk", q_heads, k_heads, preferred_element_type=f32) * scale
        return jnp.where(key_mask, raw, -1000000000.0)

    scores = masked_scores()
    top_score = jnp.max(scores, axis=-1, keepdims=True)
    log_total = top_score + jnp.log(jnp.sum(jnp.exp(scores - top_score), axis=-1, keepdims=True))
    probs_low = jnp.exp(scores - log_total).astype(bf16)
    context = jnp.einsum("phqk,pkhe->pqhe", probs_low, v_heads, preferred_element_type=f32)
    ctx_low = context.reshape(row_count, width).astype(bf16)
    attended = product(ctx_low, w_out) + b_out.astype(f32)
    norm_one, inv_one = norm_parts(tok_rows + attended)
    hidden = norm_one * g_attn.astype(f32) + s_attn.astype(f32)
    hid_low = hidden.astype(bf16)
    inner = product(hid_low, w_inner) + b_inner.astype(f32)
    active, slope = gelu_parts(inner)
    act_low = active.astype(bf16)
    outer = product(act_low, w_outer) + b_outer.astype(f32)
    norm_two, inv_two = norm_parts(hidden + outer)
    result = norm_two * g_final.astype(f32) + s_final.astype(f32)
    (
        w_query,
        b_query,
        w_key,
        w_value,
        b_value,
        w_out,
        b_out,
        g_attn,
        s_attn,
        w_inner,
        b_inner,
        w_outer,
        b_outer,
        g_final,
        s_final,
    ) = (
        lax.all_gather(lowered[0], ("page", "seq"), axis=0, tiled=True),
        lax.all_gather(lowered[1], ("page", "seq"), axis=0, tiled=True),
        lax.all_gather(lowered[2], ("page", "seq"), axis=0, tiled=True),
        lax.all_gather(lowered[3], ("page", "seq"), axis=0, tiled=True),
        lax.all_gather(lowered[4], ("page", "seq"), axis=0, tiled=True),
        lax.all_gather(lowered[5], ("page", "seq"), axis=0, tiled=True),
        lax.all_gather(lowered[6], ("page", "seq"), axis=0, tiled=True),
        lax.all_gather(lowered[7], ("page", "seq"), axis=0, tiled=True),
        lax.all_gather(lowered[8], ("page", "seq"), axis=0, tiled=True),
        lax.all_gather(lowered[9], ("page", "seq"), axis=0, tiled=True),
        lax.all_gather(lowered[10], ("page", "seq"), axis=0, tiled=True),
        lax.all_gather(lowered[11], ("page", "seq"), axis=0, tiled=True),
        lax.all_gather(lowered[12], ("page", "seq"), axis=0, tiled=True),
        lax.all_gather(lowered[13], ("page", "seq"), axis=0, tiled=True),
        lax.all_gather(lowered[14], ("page", "seq"), axis=0, tiled=True),
    )
    grad_rows = out_grad.reshape(row_count, width)
    grad_gfinal = jnp.sum(grad_rows * norm_two, axis=0)
    grad_sfinal = jnp.sum(grad_rows, axis=0)
    grad_sum = norm_backward(grad_rows, norm_two, inv_two, g_final.astype(f32))
    grad_f_low = grad_sum.astype(bf16)
    grad_bouter = jnp.sum(grad_f_low.astype(f32), axis=0)
    grad_wouter = product_tn(act_low, grad_f_low)
    grad_active = product_nt(grad_f_low, w_outer)
    grad_in_low = (grad_active * slope).astype(bf16)
    grad_binner = jnp.sum(grad_in_low.astype(f32), axis=0)
    grad_winner = product_tn(hid_low, grad_in_low)
    grad_hidden = grad_sum + product_nt(grad_in_low, w_inner)
    grad_gattn = jnp.sum(grad_hidden * norm_one, axis=0)
    grad_sattn = jnp.sum(grad_hidden, axis=0)
    grad_mixed = norm_backward(grad_hidden, norm_one, inv_one, g_attn.astype(f32))
    grad_att_low = grad_mixed.astype(bf16)
    grad_bout = jnp.sum(grad_att_low.astype(f32), axis=0)
    grad_wout = product_tn(ctx_low, grad_att_low)
    grad_ctx = (
        product_nt(grad_att_low, w_out).astype(bf16).reshape(page_count, span_len, heads, HEAD_DIM)
    )
    probs = jnp.exp(masked_scores() - log_total)
    probs_low = probs.astype(bf16)
    grad_probs = jnp.einsum("pqhe,pkhe->phqk", grad_ctx, v_heads, preferred_element_type=f32)
    grad_vfull = jnp.einsum("phqk,pqhe->pkhe", probs_low, grad_ctx, preferred_element_type=f32)
    grad_scores = (
        probs * (grad_probs - jnp.sum(grad_probs * probs, axis=-1, keepdims=True))
    ).astype(bf16)
    grad_q_low = (
        (jnp.einsum("phqk,pkhe->pqhe", grad_scores, k_heads, preferred_element_type=f32) * scale)
        .astype(bf16)
        .reshape(row_count, width)
    )
    grad_kfull = (
        jnp.einsum("phqk,pqhe->pkhe", grad_scores, q_heads, preferred_element_type=f32) * scale
    )
    grad_keys, grad_values = (
        lax.psum_scatter(
            grad_kfull.reshape(page_count, seq_len, width).astype(jnp.bfloat16),
            "seq",
            scatter_dimension=1,
            tiled=True,
        ).astype(jnp.float32),
        lax.psum_scatter(
            grad_vfull.reshape(page_count, seq_len, width).astype(jnp.bfloat16),
            "seq",
            scatter_dimension=1,
            tiled=True,
        ).astype(jnp.float32),
    )
    grad_k_low = grad_keys.reshape(row_count, width).astype(bf16)
    grad_v_low = grad_values.reshape(row_count, width).astype(bf16)
    grad_tokens = (
        grad_mixed
        + product_nt(grad_q_low, w_query)
        + product_nt(grad_k_low, w_key)
        + product_nt(grad_v_low, w_value)
    )
    grad_wquery = product_tn(tok_low, grad_q_low)
    grad_bquery = jnp.sum(grad_q_low.astype(f32), axis=0)
    grad_wkey = product_tn(tok_low, grad_k_low)
    grad_wvalue = product_tn(tok_low, grad_v_low)
    grad_bvalue = jnp.sum(grad_v_low.astype(f32), axis=0)
    owned = (
        lax.psum_scatter(grad_wquery, ("page", "seq"), scatter_dimension=0, tiled=True),
        lax.psum_scatter(grad_bquery, ("page", "seq"), scatter_dimension=0, tiled=True),
        lax.psum_scatter(grad_wkey, ("page", "seq"), scatter_dimension=0, tiled=True),
        lax.psum_scatter(grad_wvalue, ("page", "seq"), scatter_dimension=0, tiled=True),
        lax.psum_scatter(grad_bvalue, ("page", "seq"), scatter_dimension=0, tiled=True),
        lax.psum_scatter(grad_wout, ("page", "seq"), scatter_dimension=0, tiled=True),
        lax.psum_scatter(grad_bout, ("page", "seq"), scatter_dimension=0, tiled=True),
        lax.psum_scatter(grad_gattn, ("page", "seq"), scatter_dimension=0, tiled=True),
        lax.psum_scatter(grad_sattn, ("page", "seq"), scatter_dimension=0, tiled=True),
        lax.psum_scatter(grad_winner, ("page", "seq"), scatter_dimension=0, tiled=True),
        lax.psum_scatter(grad_binner, ("page", "seq"), scatter_dimension=0, tiled=True),
        lax.psum_scatter(grad_wouter, ("page", "seq"), scatter_dimension=0, tiled=True),
        lax.psum_scatter(grad_bouter, ("page", "seq"), scatter_dimension=0, tiled=True),
        lax.psum_scatter(grad_gfinal, ("page", "seq"), scatter_dimension=0, tiled=True),
        lax.psum_scatter(grad_sfinal, ("page", "seq"), scatter_dimension=0, tiled=True),
    )
    return (
        result.reshape(tokens.shape),
        grad_tokens.reshape(tokens.shape),
        owned[0],
        owned[1],
        owned[2],
        owned[3],
        owned[4],
        owned[5],
        owned[6],
        owned[7],
        owned[8],
        owned[9],
        owned[10],
        owned[11],
        owned[12],
        owned[13],
        owned[14],
    )


MESH = pl.DeviceIdType.MESH
BF16 = jnp.bfloat16
F32 = jnp.float32
VECTORS = 8
SLAB = 16
NEGATIVE = -1000000000.0


def dot_nn(left, right):
    return lax.dot_general(left, right, (((1,), (0,)), ((), ())), preferred_element_type=F32)


def dot_nt(left, right):
    return lax.dot_general(left, right, (((1,), (1,)), ((), ())), preferred_element_type=F32)


def dot_tn(left, right):
    return lax.dot_general(left, right, (((0,), (0,)), ((), ())), preferred_element_type=F32)


class Sizes:
    def __init__(self, mesh, width, units, span):
        self.pages = mesh.shape["page"]
        self.parts = mesh.shape["seq"]
        self.half = self.pages // 2
        self.width = width
        self.units = units
        self.span = span
        self.length = span * self.parts
        self.row = width // (self.pages * self.parts)
        self.rows = self.row * self.parts
        self.unit = units // (self.pages * self.parts)
        self.mine = self.unit * self.pages
        self.cols = width // self.parts
        self.heads = self.cols // HEAD_DIM
        self.pairs = self.cols // 128


def supported(mesh, token_shape, width, units):
    pages, parts = mesh.shape["page"], mesh.shape["seq"]
    return (
        parts == 4
        and pages % 2 == 0
        and pages >= 4
        and token_shape[0] == pages
        and token_shape[1] % (parts * 128) == 0
        and width % (pages * parts * 32) == 0
        and width // pages == 128
        and units % (pages * parts * 128) == 0
        and (width // parts) % 128 == 0
    )


def layer_kernel(z, names, *refs):
    r = types.SimpleNamespace(**dict(zip(names, refs)))
    send_sem, recv_sem, load_sem = r.send_sem, r.recv_sem, r.load_sem
    page = lax.axis_index("page")
    part = lax.axis_index("seq")
    counter = [0]

    def slots(count):
        first = counter[0]
        counter[0] += count
        return first

    odd = page % 2
    place = odd * (z.pages - 1 - page // 2) + (1 - odd) * (page // 2)

    def page_at(index):
        index = (index + z.pages) % z.pages
        late = index // z.half
        return (1 - late) * (2 * index) + late * (2 * z.pages - 1 - 2 * index)

    ring = [page] + [page_at(place + step) for step in range(1, z.pages)]
    peers = [part] + [
        ((part // 2 + j // 2) % 2) * 2 + (part % 2 + j % 2) % 2 for j in range(1, 4)
    ]

    def around(step):
        return ring[step % z.pages]

    def peer(j):
        return peers[j]

    rank = page * z.parts + part

    class Copy:
        def __init__(self, src, dst, index, device, group=None):
            self.args = src, dst, index, device
            self.group = group

        def made(self, group):
            src, dst, index, device = self.args
            return pltpu.make_async_remote_copy(
                src_ref=src,
                dst_ref=dst,
                send_sem=send_sem.at[group],
                recv_sem=recv_sem.at[index],
                device_id=device,
                device_id_type=MESH,
            )

        def start(self):
            group = self.group
            if group is None:
                src = self.args[0]
                size = math.prod(src.shape) * jnp.dtype(src.dtype).itemsize
                if groups[-1] + size > z.group_bytes:
                    groups.append(0)
                groups[-1] += size
                group = len(groups) - 1
            self.made(group).start()

        def wait_recv(self):
            self.made(0).wait_recv()

        def wait_send(self):
            self.made(self.group).wait_send()

    groups = [0]
    copy = Copy

    def block(ref, index, size):
        return ref.at[pl.ds(pl.multiple_of(index * size, size), size)]

    barrier = pltpu.get_barrier_semaphore()

    def greet(device):
        pl.semaphore_signal(barrier, inc=1, device_id=device, device_id_type=MESH)

    for j in (1, 2, 3):
        greet((page, peer(j)))
    greet((around(1), part))
    greet((around(-1), part))

    class Share:
        def __init__(self, ref, size, pieces=2):
            self.ref, self.size, self.pieces = ref, size, pieces
            self.first = slots(3 * pieces) - 1

        def copy(self, j, owner, k):
            height = self.size // self.pieces
            piece = block(self.ref, owner, self.size).at[pl.ds(k * height, height)]
            return copy(piece, piece, self.first + 3 * k + j, (page, peer(1 if j == 3 else j)))

        def start(self, k):
            self.copy(2, part, k).start()
            self.copy(1, part, k).start()

        def forward(self):
            for k in range(self.pieces):
                self.copy(2, peer(2), k).wait_recv()
                self.copy(3, peer(2), k).start()


        def wait(self, j):
            for k in range(self.pieces):
                self.copy(j, peer(j), k).wait_recv()

    class Combine:
        def __init__(self, refs, size, make, pieces=2):
            self.out, self.got, self.own = refs
            self.size, self.make, self.pieces = size, make, pieces
            self.height = size // pieces
            self.first = slots(3 * pieces) - 1

        def rows(self, j, k):
            at = pl.multiple_of(peer(j) * self.size + k * self.height, self.height)
            return pl.ds(at, self.height)

        def copy(self, j, k):
            return copy(
                self.out.at[self.rows(j, k)],
                self.got.at[j, pl.ds(k * self.height, self.height)],
                self.first + 3 * k + j,
                (page, peer(2 if j == 2 else 1)),
            )

        def term(self, j):
            value = self.make(pl.ds(pl.multiple_of(peer(j) * self.size, self.size), self.size), j)
            if j == 0:
                self.own[...] = value
                return
            for k in range(self.pieces):
                rows = slice(k * self.height, (k + 1) * self.height)
                mine = value[rows]
                if j == 2:
                    self.copy(3, k).wait_recv()
                    mine = mine + self.got[3, rows, :].astype(F32)
                self.out[self.rows(j, k), :] = mine.astype(BF16)
                self.copy(j, k).start()

        def finish(self, fn, after=None, step=32):
            for k in range(self.pieces):
                for j in (1, 2):
                    self.copy(j, k).wait_recv()

                def body(i, carry):
                    at = pl.multiple_of(k * self.height + i * step, step)
                    rows = pl.ds(at, step)
                    total = self.own[rows, :]
                    for j in (1, 2):
                        total = total + self.got[j, rows, :].astype(F32)
                    fn(rows, at, total)
                    return carry

                lax.fori_loop(0, self.height // step, body, 0)
                if after is not None:
                    after(k)

    def token_refs(phase):
        return r.part_out.at[phase], r.part_in.at[phase], r.part_own

    class Spread:
        def __init__(self, src, dst, size):
            self.src, self.dst, self.size, self.first = src, dst, size, slots(3) - 1

        def copy(self, j):
            return copy(
                block(self.src, peer(j), self.size),
                self.dst.at[j],
                self.first + j,
                (page, peer(j)),
            )

        def start(self):
            for j in (2, 3, 1):
                self.copy(j).start()

        def wait(self, j):
            self.copy(j).wait_recv()

    class Place:
        def __init__(self, src, dst, size, base):
            self.src, self.dst, self.size, self.base, self.first = src, dst, size, base, slots(3) - 1

        def copy(self, j, owner):
            return copy(
                block(self.src, peer(j), self.size),
                block(self.dst, self.base + owner, self.size),
                self.first + j,
                (page, peer(j)),
            )

        def start(self):
            for j in (2, 3, 1):
                self.copy(j, part).start()

        def wait(self):
            for j in (1, 2, 3):
                self.copy(j, peer(j)).wait_recv()

    class Gather:
        def __init__(self, ref, size, pieces=1):
            self.ref, self.size, self.pieces = ref, size, pieces
            self.first = slots(2 * z.half * pieces)

        def copy(self, t, d, k, step):
            height = self.size // self.pieces
            start = k * height
            if t == z.half - 1:
                height = height // 2
                start = start + d * height
            piece = block(self.ref, around(step), self.size).at[pl.ds(start, height)]
            return copy(
                piece,
                piece,
                self.first + (t * self.pieces + k) * 2 + d,
                (around(1 - 2 * d), part),
            )

        def wait(self, t, k, d):
            self.copy(t, d, k, -(1 - 2 * d) * (1 + t)).wait_recv()

        def step(self, t):
            for k in range(self.pieces):
                for d in (0, 1):
                    if t > 0:
                        self.wait(t - 1, k, d)
                    self.copy(t, d, k, -(1 - 2 * d) * t).start()


        def done(self):
            for k in range(self.pieces):
                for d in (0, 1):
                    self.wait(z.half - 1, k, d)

    class Reduce:
        def __init__(self, slot, stage, local, shape, kind, pieces=1):
            self.slot, self.stage, self.local = slot, stage, local
            self.size, self.kind, self.pieces = shape[0], kind, pieces
            self.wide = shape[1] // pieces
            self.first = slots(2 * z.half * pieces)

        def copy(self, t, d, k):
            h = self.size // 2
            if t == 0:
                src = self.stage.at[k, pl.ds(d * h, h)]
                dst = self.slot.at[k, d, 0, pl.ds(d * h, h)]
            else:
                src = self.slot.at[k, d, t - 1]
                dst = self.slot.at[k, d, t]
            return copy(
                src,
                dst,
                self.first + (t * self.pieces + k) * 2 + d,
                (around(1 - 2 * d), part),
            )


        def step(self, t):
            h = self.size // 2
            wide = self.wide
            if t == 0:
                term = self.local(around(z.half)).astype(self.kind)
                for k in range(self.pieces):
                    self.stage[k] = term[:, k * wide : (k + 1) * wide]
            else:
                terms = [
                    self.local(around((1 - 2 * d) * (z.half - t))) for d in (0, 1)
                ]
            for k in range(self.pieces):
                for d in (0, 1):
                    if t > 0:
                        term = terms[d][:, k * wide : (k + 1) * wide]
                        self.copy(t - 1, d, k).wait_recv()
                        held = self.slot.at[k, d, t - 1]
                        if t == 1:
                            near, far = pl.ds(d * h, h), pl.ds((1 - d) * h, h)
                            term_near = term[d * h : (d + 1) * h]
                            term_far = term[(1 - d) * h : (2 - d) * h]
                            held[near] = (held[near].astype(F32) + term_near).astype(self.kind)
                            held[far] = term_far.astype(self.kind)
                        else:
                            held[...] = (held[...].astype(F32) + term).astype(self.kind)
                    self.copy(t, d, k).start()

        def total(self, out):
            term = self.local(page)
            last = z.half - 1
            for k in range(self.pieces):
                for d in (0, 1):
                    self.copy(last, d, k).wait_recv()
                at = slice(k * self.wide, (k + 1) * self.wide)
                out[:, at] = (
                    term[:, at] + self.slot[k, 0, last].astype(F32) + self.slot[k, 1, last].astype(F32)
                ).astype(out.dtype)

    c, w, n = z.cols, z.width, z.span

    def fetch(i, name):
        return pltpu.make_async_copy(getattr(r, name), getattr(r, z.held + name), load_sem.at[i])

    for i, name in enumerate(z.fetched):
        fetch(i, name).start()
    hbm = r
    r = types.SimpleNamespace(**vars(hbm))
    for name in z.fetched:
        setattr(r, name, getattr(hbm, z.held + name))
    fetches = iter(range(len(z.fetched)))

    def arrive(count):
        for _ in range(count):
            i = next(fetches)
            pltpu.make_async_copy(
                getattr(hbm, z.fetched[i]), getattr(r, z.fetched[i]), load_sem.at[i]
            ).wait()

    arrive(3)
    for q in range(z.parts):
        rows = pl.ds(q * z.row, z.row)
        for i, weight in enumerate((r.w_query, r.w_key, r.w_value)):
            for k in range(z.pairs):
                r.cut_qkv[rows, (3 * k + i) * 128 : (3 * k + i + 1) * 128] = weight[
                    :, q * c + k * 128 : q * c + (k + 1) * 128
                ].astype(BF16)
    mine = pl.multiple_of(part * SLAB, SLAB)
    for i, small in enumerate(
        (r.b_query, r.b_value, r.b_out, r.g_attn, r.s_attn, r.b_outer, r.g_final, r.s_final)
    ):
        r.vec_raw[pl.ds(mine + i, 1), 0 : z.row] = small[...]
    at_page = pl.multiple_of(page * SLAB, SLAB)
    r.vec_all[pl.ds(at_page + VECTORS, 1), :] = r.b_inner[...]
    arrive(1)
    r.outer_w[pl.ds(pl.multiple_of(page * z.unit, z.unit), z.unit), :] = r.w_outer[...].astype(
        BF16
    )

    ring_qkv = Gather(r.qkv_w, z.rows, 2)
    ring_vec = Gather(r.vec_all, SLAB)
    ring_inner = Gather(r.inner_w, z.rows, 2)
    ring_out = Gather(r.out_w, z.rows)
    ring_outer = Gather(r.outer_w, z.unit, 2)
    cut_qkv = Place(r.cut_qkv, r.qkv_w, z.row, page * z.parts)
    cut_out = Place(r.cut_out, r.out_w, z.row, page * z.parts)
    cut_inner = Place(r.cut_inner, r.inner_w, z.row, page * z.parts)
    share_tok = Share(r.tok_all, n)

    class ShareVec:
        first = slots(3) - 1

        def copy(self, j, owner):
            piece = block(r.vec_raw, owner, SLAB).at[pl.ds(0, VECTORS)]
            return copy(piece, piece, self.first + j, (page, peer(j)))

    vec_share = ShareVec()
    pl.semaphore_wait(barrier, 5)
    cut_qkv.start()
    for j in (2, 3, 1):
        vec_share.copy(j, part).start()
    ring_outer.step(0)
    arrive(2)
    r.tok_all[pl.ds(pl.multiple_of(part * n, n), n), :] = r.tokens[...].astype(BF16)
    share_tok.start(0)
    share_tok.start(1)
    for q in range(z.parts):
        r.cut_out[pl.ds(q * z.row, z.row), :] = r.w_out[:, q * c : (q + 1) * c].astype(BF16)
    cut_out.start()
    arrive(1)
    for q in range(z.parts):
        rows = pl.ds(q * z.row, z.row)
        for g in range(z.pages):
            at = (z.parts * g + q) * z.unit
            r.cut_inner[rows, g * z.unit : (g + 1) * z.unit] = r.w_inner[
                :, at : at + z.unit
            ].astype(BF16)
    cut_inner.start()
    own_rows = pl.ds(pl.multiple_of(rank * z.row, z.row), z.row)
    cut_rows = pl.ds(pl.multiple_of(part * z.row, z.row), z.row)
    r.qkv_w[own_rows, :] = r.cut_qkv[cut_rows, :]
    r.out_w[own_rows, :] = r.cut_out[cut_rows, :]
    r.inner_w[own_rows, :] = r.cut_inner[cut_rows, :]

    cut_qkv.wait()
    ring_qkv.step(0)
    for j in (1, 2, 3):
        vec_share.copy(j, peer(j)).wait_recv()
    lane = lax.broadcasted_iota(jnp.int32, (VECTORS, 128), 1)
    total = jnp.zeros((VECTORS, 128), F32)
    for q in range(z.parts):
        tile = r.vec_raw[q * SLAB : q * SLAB + VECTORS, :]
        if q:
            tile = pltpu.roll(tile, q * z.row, 1)
        total = total + jnp.where(lane // z.row == q, tile, 0.0)
    r.vec_all[pl.ds(at_page, VECTORS), :] = total
    ring_vec.step(0)
    ring_qkv.step(1)
    ring_vec.step(1)
    cut_out.wait()
    ring_out.step(0)
    ring_qkv.step(2)
    ring_vec.step(2)
    ring_out.step(1)
    share_tok.forward()
    ring_qkv.step(3)
    ring_vec.step(3)
    ring_out.step(2)
    cut_inner.wait()
    ring_inner.step(0)
    ring_vec.done()

    for g in range(z.pages):
        tile = r.vec_all[g * SLAB : (g + 1) * SLAB, :].astype(BF16).astype(F32)
        r.vecs[:, g * 128 : (g + 1) * 128] = tile[0:VECTORS]
        r.b_mine[:, g * z.unit : (g + 1) * z.unit] = tile[VECTORS : VECTORS + 1]

    def vector(i):
        return r.vecs[i : i + 1, :]


    share_tok.wait(1)
    share_tok.wait(3)
    ring_qkv.done()

    def make_qkv(b, carry):
        rows = pl.ds(pl.multiple_of(b * n, n), n)
        out = dot_nn(r.tok_all[rows, :], r.qkv_w[...])
        for k in range(z.pairs):
            mine = pl.ds(pl.multiple_of(part * c + k * 128, 128), 128)
            for i, bias in enumerate((0, None, 1)):
                cols = slice((3 * k + i) * 128, (3 * k + i + 1) * 128)
                value = out[:, cols]
                if bias is not None:
                    value = value + r.vecs[bias : bias + 1, mine]
                r.qkv[rows, cols] = value.astype(BF16)
        return carry

    lax.fori_loop(0, z.parts, make_qkv, 0)
    ring_inner.step(1)
    ring_out.step(3)
    ring_outer.step(1)

    scale = HEAD_DIM ** (-0.5)
    first_head = lax.broadcasted_iota(jnp.int32, (n, 128), 1) < HEAD_DIM
    key_place = lax.broadcasted_iota(jnp.int32, (n, z.length), 1)
    valid = r.valid[0]

    def pair_cols(kind, pair):
        return pl.ds((3 * pair + kind) * 128, 128)

    def attend(pair):
        def body(b, carry):
            rows = pl.ds(pl.multiple_of(b * n, n), n)
            queries = r.qkv[rows, pair_cols(0, pair)]
            keys = r.qkv[:, pair_cols(1, pair)]
            values = r.qkv[:, pair_cols(2, pair)]
            outs = []
            for h in range(2):
                mine = first_head if h == 0 else ~first_head
                scores = dot_nt(jnp.where(mine, queries, jnp.zeros_like(queries)), keys) * scale
                scores = jnp.where(key_place < valid, scores, NEGATIVE)
                top = jnp.max(scores, axis=-1, keepdims=True)
                weight = jnp.exp(scores - top)
                probs = weight * (1.0 / jnp.sum(weight, axis=-1, keepdims=True))
                r.probs[2 * pair + h, rows, :] = probs
                outs.append(dot_nn(probs.astype(BF16), values))
            place_rows = pl.ds(
                pl.multiple_of((part * z.pairs + pair) * z.length + b * n, n), n
            )
            r.ctx_all[place_rows, :] = jnp.where(first_head, outs[0], outs[1]).astype(
                BF16
            )
            return carry

        lax.fori_loop(0, z.parts, body, 0)

    share_ctx = Share(r.ctx_all, z.pairs * z.length, z.pairs)
    for pair in range(z.pairs):
        attend(pair)
        share_ctx.start(pair)
    ring_inner.step(2)

    def project(j):
        term = None
        for k in range(z.pairs):
            rows = pl.ds(pl.multiple_of((peer(j) * z.pairs + k) * z.length, z.length), z.length)
            features = pl.ds(pl.multiple_of(peer(j) * c + k * 128, 128), 128)
            more = dot_nn(r.ctx_all[rows, :], r.out_w[features, :])
            term = more if term is None else term + more
        r.att_sum[...] = term if j == 0 else r.att_sum[...] + term

    ring_out.done()
    project(0)
    share_ctx.wait(1)
    project(1)
    share_ctx.forward()
    project(2)
    share_ctx.wait(3)
    project(3)
    r.att_cut[...] = r.att_sum[...].astype(BF16)
    move_att = Place(r.att_cut, r.att_got, n, 0)
    move_att.start()
    own_block = pl.ds(pl.multiple_of(part * n, n), n)
    r.att_got[own_block, :] = r.att_cut[own_block, :]

    def add_column_sum(i, values):
        r.sums[i : i + 1, :] += jnp.sum(values, axis=0, keepdims=True)

    r.sums[...] = jnp.zeros_like(r.sums)

    share_hid = Share(r.hid_all, n)

    def first_norm(rows, at, total):
        mixed = r.tokens[rows, :] + (total + vector(2))
        normed, inverse = norm_parts(mixed)
        hidden = normed * vector(3) + vector(4)
        r.norm_one[rows, :] = normed
        r.inv_one[rows, :] = inverse
        r.hidden[rows, :] = hidden
        r.hid_all[pl.ds(pl.multiple_of(part * n + at, 32), 32), :] = hidden.astype(BF16)

    ring_inner.step(3)
    move_att.wait()
    for k in range(2):

        def norm_rows(i, carry):
            at = pl.multiple_of(k * (n // 2) + i * 32, 32)
            total = jnp.concatenate(
                [
                    r.att_got[pl.ds(pl.multiple_of(q * n + at, 32), 32), :].astype(F32)
                    for q in range(z.parts)
                ],
                axis=1,
            )
            first_norm(pl.ds(at, 32), at, total)
            return carry

        lax.fori_loop(0, n // 64, norm_rows, 0)
        share_hid.start(k)
    ring_outer.step(2)
    ring_inner.done()

    tile = 256

    def make_inner(j):
        rows = pl.ds(pl.multiple_of(peer(j) * n, n), n)

        def columns(i, carry):
            cols = pl.ds(pl.multiple_of(i * tile, tile), tile)
            inner = dot_nn(r.hid_all[rows, :], r.inner_w[:, cols]) + r.b_mine[:, cols]
            active, slope = gelu_parts(inner)
            r.active[rows, cols] = active.astype(BF16)
            r.slope[rows, cols] = slope
            return carry

        lax.fori_loop(0, z.mine // tile, columns, 0)

    make_inner(0)
    share_hid.wait(1)
    make_inner(1)
    ring_outer.step(3)
    share_hid.forward()
    make_inner(2)
    share_hid.wait(3)
    make_inner(3)
    ring_outer.done()
    combine_two = Combine(token_refs(0), n, lambda rows, j: dot_nn(r.active[rows, :], r.outer_w[...]))
    for j in (3, 2, 1, 0):
        combine_two.term(j)
    share_gf = Share(r.gf_all, n)

    arrive(1)

    def second_norm(rows, at, total):
        outer = total + vector(5)
        normed, inverse = norm_parts(r.hidden[rows, :] + outer)
        r.o_out[rows, :] = normed * vector(6) + vector(7)
        grad = r.out_grad[rows, :]
        add_column_sum(6, grad * normed)
        add_column_sum(7, grad)
        grad_sum = norm_backward(grad, normed, inverse, vector(6))
        low = grad_sum.astype(BF16)
        add_column_sum(5, low.astype(F32))
        r.grad_sum[rows, :] = grad_sum
        r.gf_all[pl.ds(pl.multiple_of(part * n + at, 32), 32), :] = low

    combine_two.finish(second_norm, share_gf.start)

    def chunk_term(left, right, size):
        def local(g):
            cols = pl.ds(pl.multiple_of(g * size, size), size)
            return dot_tn(left[:, cols], right[...])

        return local

    reduce_outer_a = Reduce(
        r.slot_outer_a, r.stage_outer_a,
        chunk_term(r.active, r.gf_all.at[:, 0 : w // 2], z.unit), (z.unit, w // 2), BF16,
    )
    reduce_outer_b = Reduce(
        r.slot_outer_b, r.stage_outer_b,
        chunk_term(r.active, r.gf_all.at[:, w // 2 :], z.unit), (z.unit, w // 2), BF16,
    )
    reduce_inner = Reduce(
        r.slot_inner, r.stage_inner, chunk_term(r.hid_all, r.grad_inner, z.rows),
        (z.rows, z.mine), BF16, 2
    )
    def pair_term(k):
        def local(g):
            cols = pl.ds(pl.multiple_of(g * z.rows, z.rows), z.rows)
            return dot_tn(r.tok_all[:, cols], r.grad_qkv[:, 384 * k : 384 * (k + 1)])

        return local

    def out_term(g):
        rows = pl.ds(pl.multiple_of(g * z.length, z.length), z.length)
        return dot_tn(r.ctx_all[rows, :], r.ga_cols[...])

    reduce_pair = [
        Reduce(r.slot_pair.at[k], r.stage_pair.at[k], pair_term(k), (z.rows, 384), BF16)
        for k in range(z.pairs)
    ]
    reduce_out = Reduce(r.slot_out, r.stage_out, out_term, (z.rows, c), BF16)
    reduce_vec = Reduce(
        r.slot_vec, r.stage_vec,
        lambda g: r.term_vec[pl.ds(pl.multiple_of(g * SLAB, SLAB), SLAB), :], (SLAB, 128), F32,
    )

    r.b_sum[...] = jnp.zeros_like(r.b_sum)

    def make_grad_inner(j):
        rows = pl.ds(pl.multiple_of(peer(j) * n, n), n)

        def columns(i, carry):
            cols = pl.ds(pl.multiple_of(i * tile, tile), tile)
            grad = dot_nt(r.gf_all[rows, :], r.outer_w[cols, :]) * r.slope[rows, cols]
            low = grad.astype(BF16)
            r.grad_inner[rows, cols] = low
            r.b_sum[:, cols] += jnp.sum(low.astype(F32), axis=0, keepdims=True)
            return carry

        lax.fori_loop(0, z.mine // tile, columns, 0)

    make_grad_inner(0)
    share_gf.wait(1)
    make_grad_inner(1)
    share_gf.forward()
    make_grad_inner(2)
    share_gf.wait(3)
    reduce_outer_a.step(0)
    reduce_outer_b.step(0)
    make_grad_inner(3)
    combine_three = Combine(token_refs(1), n, lambda rows, j: dot_nt(r.grad_inner[rows, :], r.inner_w[...]))
    combine_three.term(3)
    combine_three.term(2)
    reduce_inner.step(0)
    reduce_outer_a.step(1)
    combine_three.term(1)
    combine_three.term(0)
    reduce_outer_b.step(1)
    reduce_inner.step(1)

    move_ga = Place(r.ga_cut, r.ga_cols, n, 0)

    def first_norm_back(rows, at, total):
        grad = r.grad_sum[rows, :] + total
        normed = r.norm_one[rows, :]
        add_column_sum(3, grad * normed)
        add_column_sum(4, grad)
        mixed = norm_backward(grad, normed, r.inv_one[rows, :], vector(3))
        low = mixed.astype(BF16)
        add_column_sum(2, low.astype(F32))
        r.grad_mixed[rows, :] = mixed
        for q in range(z.parts):
            r.ga_cut[pl.ds(pl.multiple_of(q * n + at, 32), 32), :] = low[:, q * c : (q + 1) * c]

    combine_three.finish(first_norm_back)
    move_ga.start()
    r.ga_cols[own_block, :] = r.ga_cut[own_block, :]
    reduce_outer_a.step(2)

    def grad_ctx_term(rows, j):
        return jnp.concatenate(
            [
                dot_nt(
                    r.ga_cols[...],
                    r.out_w[pl.ds(pl.multiple_of(peer(j) * c + k * 128, 128), 128), :],
                )
                for k in range(z.pairs)
            ],
            axis=0,
        )

    combine_ctx = Combine(
        (r.ctx_out, r.ctx_in, r.ctx_own), z.pairs * z.length, grad_ctx_term, z.pairs
    )
    move_ga.wait()
    combine_ctx.term(3)
    combine_ctx.term(2)
    combine_ctx.term(1)
    combine_ctx.term(0)
    reduce_out.step(0)
    reduce_inner.step(2)

    def keep_grad_ctx(rows, at, total):
        r.grad_ctx[rows, :] = total.astype(BF16)

    def attend_back(pair):
        r.grad_kv[...] = jnp.zeros_like(r.grad_kv)

        def body(b, carry):
            rows = pl.ds(pl.multiple_of(b * n, n), n)
            queries = r.qkv[rows, pair_cols(0, pair)]
            keys = r.qkv[:, pair_cols(1, pair)]
            values = r.qkv[:, pair_cols(2, pair)]
            grad = r.grad_ctx[pl.ds(pl.multiple_of(pair * z.length + b * n, n), n), :]
            outs = []
            for h in range(2):
                mine = first_head if h == 0 else ~first_head
                grad_mine = jnp.where(mine, grad, jnp.zeros_like(grad))
                query_mine = jnp.where(mine, queries, jnp.zeros_like(queries))
                probs = r.probs[2 * pair + h, rows, :]
                grad_probs = dot_nt(grad_mine, values)
                r.grad_kv[1] += dot_tn(probs.astype(BF16), grad_mine)
                inside = jnp.sum(grad_probs * probs, axis=-1, keepdims=True)
                grad_scores = (probs * (grad_probs - inside)).astype(BF16)
                outs.append(dot_nn(grad_scores, keys))
                r.grad_kv[0] += dot_tn(grad_scores, query_mine)
            r.grad_qkv[rows, pair_cols(0, pair)] = (
                jnp.where(first_head, outs[0], outs[1]) * scale
            ).astype(BF16)
            return carry

        lax.fori_loop(0, z.parts, body, 0)
        r.grad_qkv[:, pair_cols(1, pair)] = (r.grad_kv[0] * scale).astype(BF16)
        r.grad_qkv[:, pair_cols(2, pair)] = r.grad_kv[1].astype(BF16)

    def after_pair(pair):
        attend_back(pair)
        reduce_pair[pair].step(0)
        if pair == 0:
            reduce_outer_a.step(3)
            reduce_outer_b.step(2)
            reduce_out.step(1)

    combine_ctx.finish(keep_grad_ctx, after_pair, step=128)
    reduce_inner.step(3)
    reduce_out.step(2)

    for k in range(z.pairs):
        mine = pl.ds(pl.multiple_of(part * c + k * 128, 128), 128)
        for row, kind in ((0, 0), (1, 2)):
            r.sums[row : row + 1, mine] = jnp.sum(
                r.grad_qkv[:, pair_cols(kind, k)].astype(F32), axis=0, keepdims=True
            )
    r.term_vec[...] = jnp.zeros_like(r.term_vec)
    for g in range(z.pages):
        r.term_vec[g * SLAB : g * SLAB + VECTORS, :] = r.sums[:, g * 128 : (g + 1) * 128]
        r.term_vec[g * SLAB + VECTORS : g * SLAB + VECTORS + 1, :] = r.b_sum[
            :, g * z.unit : (g + 1) * z.unit
        ]
    reduce_vec.step(0)

    combine_four = Combine(token_refs(2), n, lambda rows, j: dot_nt(r.grad_qkv[rows, :], r.qkv_w[...]))
    combine_four.term(3)
    combine_four.term(2)
    reduce_vec.step(1)
    for pair in range(z.pairs):
        reduce_pair[pair].step(1)
    reduce_out.step(3)
    combine_four.term(1)
    combine_four.term(0)

    reduce_inner.total(r.fin_inner)
    fin_inner = Spread(r.fin_inner, r.got_inner, z.row)
    fin_inner.start()
    reduce_vec.step(2)
    for pair in range(z.pairs):
        reduce_pair[pair].step(2)

    def input_rows(rows, at, total):
        r.o_grad[rows, :] = r.grad_mixed[rows, :] + total

    combine_four.finish(input_rows)
    reduce_outer_a.total(r.o_outer.at[:, 0 : w // 2])
    reduce_vec.step(3)
    for pair in range(z.pairs):
        reduce_pair[pair].step(3)
    reduce_outer_b.step(3)
    reduce_out.total(r.fin_out)
    fin_out = Spread(r.fin_out, r.got_out, z.row)
    fin_out.start()
    reduce_vec.total(r.fin_vec)

    class VecAll:
        first = slots(3) - 1

        def copy(self, j):
            return copy(r.fin_vec, r.got_vec.at[j], self.first + j, (page, peer(j)))

    fin_vec = VecAll()
    for j in (2, 3, 1):
        fin_vec.copy(j).start()
    fin_pair = []
    for k in range(z.pairs):
        reduce_pair[k].total(r.fin_pair.at[k])
        fin_pair.append(Spread(r.fin_pair.at[k], r.got_pair.at[k], z.row))
        fin_pair[k].start()

    my_rows = pl.ds(pl.multiple_of(part * z.row, z.row), z.row)

    def deliver(spread, mine, got, out):
        for j in range(4):
            if j:
                spread.wait(j)
            value = got[j] if j else mine[my_rows, :]
            out[peer(j)] = value

    deliver(fin_inner, r.fin_inner, r.got_inner, r.o_inner)
    deliver(fin_out, r.fin_out, r.got_out, r.o_wout)
    summed = r.fin_vec[0:VECTORS, :]
    for j in (1, 2, 3):
        fin_vec.copy(j).wait_recv()
        summed = summed + r.got_vec[j, 0:VECTORS, :]
    r.o_vec[0:VECTORS, :] = pltpu.roll(summed, (128 - part * z.row) % 128, 1)
    r.o_vec[VECTORS:, :] = r.fin_vec[VECTORS:, :]
    reduce_outer_b.total(r.o_outer.at[:, w // 2 :])
    for k in range(z.pairs):
        deliver(fin_pair[k], r.fin_pair.at[k], r.got_pair.at[k], r.o_pair.at[k])

    for group, size in enumerate(groups):
        rows = r.measure.at[pl.ds(0, size // 512)]
        copy(rows, rows, 0, (page, part), group).wait_send()

    assert counter[0] == z.sems and len(groups) == z.groups, (counter, groups)


def finish_kernel(z, out, grad, outer, inner, pair, wout, vec, *outs):
    (o_out, o_grad, o_wq, o_bq, o_wk, o_wv, o_bv, o_wo, o_bo, o_ga, o_sa, o_wi, o_bi, o_wu, o_bu, o_gf, o_sf) = outs
    o_out[...] = out[...]
    o_grad[...] = grad[...]
    o_wu[...] = outer[...]
    c = z.cols
    for q in range(z.parts):
        o_wo[:, q * c : (q + 1) * c] = wout[q].astype(F32)
        for i, ref in enumerate((o_wq, o_wk, o_wv)):
            for k in range(z.pairs):
                ref[:, q * c + k * 128 : q * c + (k + 1) * 128] = pair[
                    k, q, :, i * 128 : (i + 1) * 128
                ].astype(F32)
        for g in range(z.pages):
            at = (z.parts * g + q) * z.unit
            o_wi[:, at : at + z.unit] = inner[q, :, g * z.unit : (g + 1) * z.unit].astype(F32)
    for i, ref in enumerate((o_bq, o_bv, o_bo, o_ga, o_sa, o_bu, o_gf, o_sf)):
        ref[...] = vec[i : i + 1, 0 : z.row]
    o_bi[...] = vec[VECTORS : VECTORS + 1, :]


def paged_layer(z, tokens, valid_len, params, out_grad):
    (
        w_query, b_query, w_key, w_value, b_value, w_out, b_out, g_attn, s_attn,
        w_inner, b_inner, w_outer, b_outer, g_final, s_final,
    ) = params
    flat = lambda v: v.reshape(1, v.shape[0])
    c, w, n, ln, half = z.cols, z.width, z.span, z.length, z.half
    ins = dict(
        valid=valid_len,
        tokens=tokens.reshape(n, w),
        out_grad=out_grad.reshape(n, w),
        w_query=w_query, w_key=w_key, w_value=w_value, w_out=w_out,
        w_inner=w_inner, w_outer=w_outer,
        b_query=flat(b_query), b_value=flat(b_value), b_out=flat(b_out),
        g_attn=flat(g_attn), s_attn=flat(s_attn), b_inner=flat(b_inner),
        b_outer=flat(b_outer), g_final=flat(g_final), s_final=flat(s_final),
    )
    outs = dict(
        o_out=((n, w), F32),
        o_grad=((n, w), F32),
        o_outer=((z.unit, w), F32),
        o_inner=((z.parts, z.row, z.mine), BF16),
        o_pair=((z.pairs, z.parts, z.row, 384), BF16),
        o_wout=((z.parts, z.row, c), BF16),
        o_vec=((SLAB, 128), F32),
    )
    scratch = dict(
        qkv_w=((w, 3 * c), BF16),
        out_w=((w, c), BF16),
        cut_out=((z.rows, c), BF16),
        inner_w=((w, z.mine), BF16),
        outer_w=((z.mine, w), BF16),
        vec_all=((z.pages * SLAB, 128), F32),
        vec_raw=((z.parts * SLAB, 128), F32),
        cut_qkv=((z.rows, 3 * c), BF16),
        cut_inner=((z.rows, z.mine), BF16),
        vecs=((VECTORS, w), F32),
        b_mine=((1, z.mine), F32),
        tok_all=((ln, w), BF16),
        hid_all=((ln, w), BF16),
        gf_all=((ln, w), BF16),
        ga_cut=((ln, c), BF16),
        ga_cols=((ln, c), BF16),
        att_sum=((ln, c), F32),
        att_cut=((ln, c), BF16),
        att_got=((ln, c), BF16),
        ctx_out=((w // 128 * ln, 128), BF16),
        ctx_in=((4, z.pairs * ln, 128), BF16),
        ctx_own=((z.pairs * ln, 128), F32),
        qkv=((ln, 3 * c), BF16),
        grad_qkv=((ln, 3 * c), BF16),
        probs=((z.heads, ln, ln), F32),
        measure=((8192, 128), F32),
        ctx_all=((w // 128 * ln, 128), BF16),
        grad_ctx=((z.pairs * ln, 128), BF16),
        grad_kv=((2, ln, 128), F32),
        part_out=((3, ln, w), BF16),
        part_in=((3, 4, n, w), BF16),
        part_own=((n, w), F32),
        norm_one=((n, w), F32),
        inv_one=((n, 1), F32),
        hidden=((n, w), F32),
        grad_sum=((n, w), F32),
        grad_mixed=((n, w), F32),
        active=((ln, z.mine), BF16),
        slope=((ln, z.mine), F32),
        grad_inner=((ln, z.mine), BF16),
        sums=((VECTORS, w), F32),
        b_sum=((1, z.mine), F32),
        term_vec=((z.pages * SLAB, 128), F32),
        slot_outer_a=((1, 2, half, z.unit, w // 2), BF16), stage_outer_a=((1, z.unit, w // 2), BF16),
        slot_outer_b=((1, 2, half, z.unit, w // 2), BF16), stage_outer_b=((1, z.unit, w // 2), BF16),
        slot_inner=((2, 2, half, z.rows, z.mine // 2), BF16), stage_inner=((2, z.rows, z.mine // 2), BF16),
        slot_pair=((z.pairs, 1, 2, half, z.rows, 384), BF16), stage_pair=((z.pairs, 1, z.rows, 384), BF16),
        slot_out=((1, 2, half, z.rows, c), BF16), stage_out=((1, z.rows, c), BF16),
        slot_vec=((1, 2, half, SLAB, 128 // 1), F32), stage_vec=((1, SLAB, 128 // 1), F32),
        fin_inner=((z.rows, z.mine), BF16), got_inner=((4, z.row, z.mine), BF16),
        fin_pair=((z.pairs, z.rows, 384), BF16), got_pair=((z.pairs, 4, z.row, 384), BF16),
        fin_out=((z.rows, c), BF16), got_out=((4, z.row, c), BF16),
        fin_vec=((SLAB, 128), F32), got_vec=((4, SLAB, 128), F32),
    )
    z.sems = 209
    z.groups, z.group_bytes = 5, 4 << 20
    fetched = dict(w_query=0, w_key=0, w_value=0, w_outer=0, w_out=0, tokens=0, w_inner=0, out_grad=0)
    z.fetched, z.held = tuple(fetched), "f_"
    for name in z.fetched:
        scratch[z.held + name] = (ins[name].shape, F32)
    sems = [pltpu.SemaphoreType.DMA((z.groups,)), pltpu.SemaphoreType.DMA((z.sems,)), pltpu.SemaphoreType.DMA((len(fetched),))]
    names = list(ins) + list(outs) + list(scratch) + list(dict(send_sem=0, recv_sem=0, load_sem=0))
    vmem = pl.BlockSpec(memory_space=pltpu.VMEM)
    parts = pl.pallas_call(
        functools.partial(layer_kernel, z, names),
        out_shape=[jax.ShapeDtypeStruct(*v) for v in outs.values()],
        in_specs=[
            pl.BlockSpec(memory_space=pltpu.SMEM)
            if v is valid_len
            else pl.BlockSpec(memory_space=pl.ANY)
            if k in fetched
            else vmem
            for k, v in ins.items()
        ],
        out_specs=[vmem] * len(outs),
        scratch_shapes=[pltpu.VMEM(*v) for v in scratch.values()]
        + sems,
        compiler_params=pltpu.CompilerParams(
            collective_id=0, has_side_effects=True, vmem_limit_bytes=67043328
        ),
        name="layer",
    )(*ins.values())
    row, big = z.row, jax.ShapeDtypeStruct((n, w), F32)
    mat = jax.ShapeDtypeStruct((row, w), F32)
    vec = jax.ShapeDtypeStruct((1, row), F32)
    shapes = [
        big, big, mat, vec, mat, mat, vec, mat, vec, vec, vec,
        jax.ShapeDtypeStruct((row, z.units), F32), jax.ShapeDtypeStruct((1, z.unit), F32),
        jax.ShapeDtypeStruct((z.unit, w), F32), vec, vec, vec,
    ]
    results = pl.pallas_call(
        functools.partial(finish_kernel, z),
        out_shape=shapes,
        in_specs=[vmem] * 7,
        out_specs=[vmem] * len(shapes),
        name="finish",
    )(*parts)
    results = list(results)
    for i in (0, 1):
        results[i] = results[i].reshape(tokens.shape)
    for i in range(2, 17):
        if results[i].shape[0] == 1:
            results[i] = results[i].reshape(results[i].shape[1])
    return tuple(results)


def body(
    tokens,
    valid_len,
    query_weight,
    query_bias,
    key_weight,
    value_weight,
    value_bias,
    output_weight,
    output_bias,
    attn_gain,
    attn_shift,
    inner_weight,
    inner_bias,
    outer_weight,
    outer_bias,
    final_gain,
    final_shift,
    out_grad,
):
    lowered = [
        piece.astype(jnp.bfloat16)
        for piece in (
            query_weight,
            query_bias,
            key_weight,
            value_weight,
            value_bias,
            output_weight,
            output_bias,
            attn_gain,
            attn_shift,
            inner_weight,
            inner_bias,
            outer_weight,
            outer_bias,
            final_gain,
            final_shift,
        )
    ]
    outputs = sequence_layer(tokens, valid_len, lowered, out_grad)
    return outputs


def solution(mesh):
    in_specs = (
        P("page", "seq", None),
        P("page"),
        P(("page", "seq"), None),
        P(("page", "seq")),
        P(("page", "seq"), None),
        P(("page", "seq"), None),
        P(("page", "seq")),
        P(("page", "seq"), None),
        P(("page", "seq")),
        P(("page", "seq")),
        P(("page", "seq")),
        P(("page", "seq"), None),
        P(("page", "seq")),
        P(("page", "seq"), None),
        P(("page", "seq")),
        P(("page", "seq")),
        P(("page", "seq")),
        P("page", "seq", None),
    )
    out_specs = (
        P("page", "seq", None),
        P("page", "seq", None),
        P(("page", "seq"), None),
        P(("page", "seq")),
        P(("page", "seq"), None),
        P(("page", "seq"), None),
        P(("page", "seq")),
        P(("page", "seq"), None),
        P(("page", "seq")),
        P(("page", "seq")),
        P(("page", "seq")),
        P(("page", "seq"), None),
        P(("page", "seq")),
        P(("page", "seq"), None),
        P(("page", "seq")),
        P(("page", "seq")),
        P(("page", "seq")),
    )

    def layer(*arrays):
        width, units = arrays[11].shape
        if supported(mesh, arrays[0].shape, width, units):
            z = Sizes(mesh, width, units, arrays[0].shape[1] // mesh.shape["seq"])

            def run(tokens, valid_len, *rest):
                return paged_layer(z, tokens, valid_len, rest[:-1], rest[-1])

            chosen = run
        else:
            chosen = body
        return jax.shard_map(
            chosen, mesh=mesh, in_specs=in_specs, out_specs=out_specs, check_vma=False
        )(*arrays)

    return layer
```

```python
import functools
import math
import types

import jax
import jax.numpy as jnp
from jax import lax
from jax.experimental import pallas as pl
from jax.experimental.pallas import tpu as pltpu
from jax.sharding import PartitionSpec as P

HEAD_DIM = 64


EPSILON = 1e-05
INV_ROOT_TWO = 1.0 / math.sqrt(2.0)
INV_ROOT_TWO_PI = 1.0 / math.sqrt(2.0 * math.pi)


def product(left, right):
    return jnp.dot(left, right, preferred_element_type=jnp.float32)


def product_tn(left, right):
    return lax.dot_general(
        left, right, (((0,), (0,)), ((), ())), preferred_element_type=jnp.float32
    )


def product_nt(left, right):
    return lax.dot_general(
        left, right, (((1,), (1,)), ((), ())), preferred_element_type=jnp.float32
    )


def norm_parts(values):
    center = values - jnp.mean(values, axis=-1, keepdims=True)
    inverse = lax.rsqrt(jnp.mean(center * center, axis=-1, keepdims=True) + EPSILON)
    return (center * inverse, inverse)


def norm_backward(grad_out, normed, inverse, gain):
    scaled = grad_out * gain
    return inverse * (
        scaled
        - jnp.mean(scaled, axis=-1, keepdims=True)
        - normed * jnp.mean(scaled * normed, axis=-1, keepdims=True)
    )


def gelu_parts(values):
    cumulative = 0.5 * (1.0 + lax.erf(values * INV_ROOT_TWO))
    return (
        values * cumulative,
        cumulative + values * jnp.exp(-0.5 * values * values) * INV_ROOT_TWO_PI,
    )


def sequence_layer(tokens, valid_len, lowered, out_grad):
    fetched = (
        lax.all_gather(lowered[0], ("page", "seq"), axis=0, tiled=True),
        lax.all_gather(lowered[1], ("page", "seq"), axis=0, tiled=True),
        lax.all_gather(lowered[2], ("page", "seq"), axis=0, tiled=True),
        lax.all_gather(lowered[3], ("page", "seq"), axis=0, tiled=True),
        lax.all_gather(lowered[4], ("page", "seq"), axis=0, tiled=True),
        lax.all_gather(lowered[5], ("page", "seq"), axis=0, tiled=True),
        lax.all_gather(lowered[6], ("page", "seq"), axis=0, tiled=True),
        lax.all_gather(lowered[7], ("page", "seq"), axis=0, tiled=True),
        lax.all_gather(lowered[8], ("page", "seq"), axis=0, tiled=True),
        lax.all_gather(lowered[9], ("page", "seq"), axis=0, tiled=True),
        lax.all_gather(lowered[10], ("page", "seq"), axis=0, tiled=True),
        lax.all_gather(lowered[11], ("page", "seq"), axis=0, tiled=True),
        lax.all_gather(lowered[12], ("page", "seq"), axis=0, tiled=True),
        lax.all_gather(lowered[13], ("page", "seq"), axis=0, tiled=True),
        lax.all_gather(lowered[14], ("page", "seq"), axis=0, tiled=True),
    )
    (
        w_query,
        b_query,
        w_key,
        w_value,
        b_value,
        w_out,
        b_out,
        g_attn,
        s_attn,
        w_inner,
        b_inner,
        w_outer,
        b_outer,
        g_final,
        s_final,
    ) = fetched
    f32 = jnp.float32
    bf16 = jnp.bfloat16
    scale = HEAD_DIM ** (-0.5)
    page_count, span_len, width = tokens.shape
    heads = width // HEAD_DIM
    row_count = page_count * span_len
    tok_rows = tokens.reshape(row_count, width)
    tok_low = tok_rows.astype(bf16)
    q_low = (product(tok_low, w_query) + b_query.astype(f32)).astype(bf16)
    k_low = product(tok_low, w_key).astype(bf16)
    v_low = (product(tok_low, w_value) + b_value.astype(f32)).astype(bf16)
    k_full, v_full = (
        lax.all_gather(k_low.reshape(page_count, span_len, width), "seq", axis=1, tiled=True),
        lax.all_gather(v_low.reshape(page_count, span_len, width), "seq", axis=1, tiled=True),
    )
    seq_len = k_full.shape[1]
    q_heads = q_low.reshape(page_count, span_len, heads, HEAD_DIM)
    k_heads = k_full.reshape(page_count, seq_len, heads, HEAD_DIM)
    v_heads = v_full.reshape(page_count, seq_len, heads, HEAD_DIM)
    key_mask = (lax.broadcasted_iota(jnp.int32, (page_count, seq_len), 1) < valid_len[:, None])[
        :, None, None, :
    ]

    def masked_scores():
        raw = jnp.einsum("pqhe,pkhe->phqk", q_heads, k_heads, preferred_element_type=f32) * scale
        return jnp.where(key_mask, raw, -1000000000.0)

    scores = masked_scores()
    top_score = jnp.max(scores, axis=-1, keepdims=True)
    log_total = top_score + jnp.log(jnp.sum(jnp.exp(scores - top_score), axis=-1, keepdims=True))
    probs_low = jnp.exp(scores - log_total).astype(bf16)
    context = jnp.einsum("phqk,pkhe->pqhe", probs_low, v_heads, preferred_element_type=f32)
    ctx_low = context.reshape(row_count, width).astype(bf16)
    attended = product(ctx_low, w_out) + b_out.astype(f32)
    norm_one, inv_one = norm_parts(tok_rows + attended)
    hidden = norm_one * g_attn.astype(f32) + s_attn.astype(f32)
    hid_low = hidden.astype(bf16)
    inner = product(hid_low, w_inner) + b_inner.astype(f32)
    active, slope = gelu_parts(inner)
    act_low = active.astype(bf16)
    outer = product(act_low, w_outer) + b_outer.astype(f32)
    norm_two, inv_two = norm_parts(hidden + outer)
    result = norm_two * g_final.astype(f32) + s_final.astype(f32)
    (
        w_query,
        b_query,
        w_key,
        w_value,
        b_value,
        w_out,
        b_out,
        g_attn,
        s_attn,
        w_inner,
        b_inner,
        w_outer,
        b_outer,
        g_final,
        s_final,
    ) = (
        lax.all_gather(lowered[0], ("page", "seq"), axis=0, tiled=True),
        lax.all_gather(lowered[1], ("page", "seq"), axis=0, tiled=True),
        lax.all_gather(lowered[2], ("page", "seq"), axis=0, tiled=True),
        lax.all_gather(lowered[3], ("page", "seq"), axis=0, tiled=True),
        lax.all_gather(lowered[4], ("page", "seq"), axis=0, tiled=True),
        lax.all_gather(lowered[5], ("page", "seq"), axis=0, tiled=True),
        lax.all_gather(lowered[6], ("page", "seq"), axis=0, tiled=True),
        lax.all_gather(lowered[7], ("page", "seq"), axis=0, tiled=True),
        lax.all_gather(lowered[8], ("page", "seq"), axis=0, tiled=True),
        lax.all_gather(lowered[9], ("page", "seq"), axis=0, tiled=True),
        lax.all_gather(lowered[10], ("page", "seq"), axis=0, tiled=True),
        lax.all_gather(lowered[11], ("page", "seq"), axis=0, tiled=True),
        lax.all_gather(lowered[12], ("page", "seq"), axis=0, tiled=True),
        lax.all_gather(lowered[13], ("page", "seq"), axis=0, tiled=True),
        lax.all_gather(lowered[14], ("page", "seq"), axis=0, tiled=True),
    )
    grad_rows = out_grad.reshape(row_count, width)
    grad_gfinal = jnp.sum(grad_rows * norm_two, axis=0)
    grad_sfinal = jnp.sum(grad_rows, axis=0)
    grad_sum = norm_backward(grad_rows, norm_two, inv_two, g_final.astype(f32))
    grad_f_low = grad_sum.astype(bf16)
    grad_bouter = jnp.sum(grad_f_low.astype(f32), axis=0)
    grad_wouter = product_tn(act_low, grad_f_low)
    grad_active = product_nt(grad_f_low, w_outer)
    grad_in_low = (grad_active * slope).astype(bf16)
    grad_binner = jnp.sum(grad_in_low.astype(f32), axis=0)
    grad_winner = product_tn(hid_low, grad_in_low)
    grad_hidden = grad_sum + product_nt(grad_in_low, w_inner)
    grad_gattn = jnp.sum(grad_hidden * norm_one, axis=0)
    grad_sattn = jnp.sum(grad_hidden, axis=0)
    grad_mixed = norm_backward(grad_hidden, norm_one, inv_one, g_attn.astype(f32))
    grad_att_low = grad_mixed.astype(bf16)
    grad_bout = jnp.sum(grad_att_low.astype(f32), axis=0)
    grad_wout = product_tn(ctx_low, grad_att_low)
    grad_ctx = (
        product_nt(grad_att_low, w_out).astype(bf16).reshape(page_count, span_len, heads, HEAD_DIM)
    )
    probs = jnp.exp(masked_scores() - log_total)
    probs_low = probs.astype(bf16)
    grad_probs = jnp.einsum("pqhe,pkhe->phqk", grad_ctx, v_heads, preferred_element_type=f32)
    grad_vfull = jnp.einsum("phqk,pqhe->pkhe", probs_low, grad_ctx, preferred_element_type=f32)
    grad_scores = (
        probs * (grad_probs - jnp.sum(grad_probs * probs, axis=-1, keepdims=True))
    ).astype(bf16)
    grad_q_low = (
        (jnp.einsum("phqk,pkhe->pqhe", grad_scores, k_heads, preferred_element_type=f32) * scale)
        .astype(bf16)
        .reshape(row_count, width)
    )
    grad_kfull = (
        jnp.einsum("phqk,pqhe->pkhe", grad_scores, q_heads, preferred_element_type=f32) * scale
    )
    grad_keys, grad_values = (
        lax.psum_scatter(
            grad_kfull.reshape(page_count, seq_len, width).astype(jnp.bfloat16),
            "seq",
            scatter_dimension=1,
            tiled=True,
        ).astype(jnp.float32),
        lax.psum_scatter(
            grad_vfull.reshape(page_count, seq_len, width).astype(jnp.bfloat16),
            "seq",
            scatter_dimension=1,
            tiled=True,
        ).astype(jnp.float32),
    )
    grad_k_low = grad_keys.reshape(row_count, width).astype(bf16)
    grad_v_low = grad_values.reshape(row_count, width).astype(bf16)
    grad_tokens = (
        grad_mixed
        + product_nt(grad_q_low, w_query)
        + product_nt(grad_k_low, w_key)
        + product_nt(grad_v_low, w_value)
    )
    grad_wquery = product_tn(tok_low, grad_q_low)
    grad_bquery = jnp.sum(grad_q_low.astype(f32), axis=0)
    grad_wkey = product_tn(tok_low, grad_k_low)
    grad_wvalue = product_tn(tok_low, grad_v_low)
    grad_bvalue = jnp.sum(grad_v_low.astype(f32), axis=0)
    owned = (
        lax.psum_scatter(grad_wquery, ("page", "seq"), scatter_dimension=0, tiled=True),
        lax.psum_scatter(grad_bquery, ("page", "seq"), scatter_dimension=0, tiled=True),
        lax.psum_scatter(grad_wkey, ("page", "seq"), scatter_dimension=0, tiled=True),
        lax.psum_scatter(grad_wvalue, ("page", "seq"), scatter_dimension=0, tiled=True),
        lax.psum_scatter(grad_bvalue, ("page", "seq"), scatter_dimension=0, tiled=True),
        lax.psum_scatter(grad_wout, ("page", "seq"), scatter_dimension=0, tiled=True),
        lax.psum_scatter(grad_bout, ("page", "seq"), scatter_dimension=0, tiled=True),
        lax.psum_scatter(grad_gattn, ("page", "seq"), scatter_dimension=0, tiled=True),
        lax.psum_scatter(grad_sattn, ("page", "seq"), scatter_dimension=0, tiled=True),
        lax.psum_scatter(grad_winner, ("page", "seq"), scatter_dimension=0, tiled=True),
        lax.psum_scatter(grad_binner, ("page", "seq"), scatter_dimension=0, tiled=True),
        lax.psum_scatter(grad_wouter, ("page", "seq"), scatter_dimension=0, tiled=True),
        lax.psum_scatter(grad_bouter, ("page", "seq"), scatter_dimension=0, tiled=True),
        lax.psum_scatter(grad_gfinal, ("page", "seq"), scatter_dimension=0, tiled=True),
        lax.psum_scatter(grad_sfinal, ("page", "seq"), scatter_dimension=0, tiled=True),
    )
    return (
        result.reshape(tokens.shape),
        grad_tokens.reshape(tokens.shape),
        owned[0],
        owned[1],
        owned[2],
        owned[3],
        owned[4],
        owned[5],
        owned[6],
        owned[7],
        owned[8],
        owned[9],
        owned[10],
        owned[11],
        owned[12],
        owned[13],
        owned[14],
    )


MESH = pl.DeviceIdType.MESH
BF16 = jnp.bfloat16
F32 = jnp.float32
VECTORS = 8
SLAB = 16
NEGATIVE = -1000000000.0


def dot_nn(left, right):
    return lax.dot_general(left, right, (((1,), (0,)), ((), ())), preferred_element_type=F32)


def dot_nt(left, right):
    return lax.dot_general(left, right, (((1,), (1,)), ((), ())), preferred_element_type=F32)


def dot_tn(left, right):
    return lax.dot_general(left, right, (((0,), (0,)), ((), ())), preferred_element_type=F32)


class Sizes:
    def __init__(self, mesh, width, units, span):
        self.pages = mesh.shape["page"]
        self.parts = mesh.shape["seq"]
        self.half = self.pages // 2
        self.width = width
        self.units = units
        self.span = span
        self.length = span * self.parts
        self.row = width // (self.pages * self.parts)
        self.rows = self.row * self.parts
        self.unit = units // (self.pages * self.parts)
        self.mine = self.unit * self.pages
        self.cols = width // self.parts
        self.heads = self.cols // HEAD_DIM
        self.pairs = self.cols // 128


def supported(mesh, token_shape, width, units):
    pages, parts = mesh.shape["page"], mesh.shape["seq"]
    return (
        parts == 4
        and pages % 2 == 0
        and pages >= 4
        and token_shape[0] == pages
        and token_shape[1] % (parts * 128) == 0
        and width % (pages * parts * 32) == 0
        and width // pages == 128
        and units % (pages * parts * 128) == 0
        and (width // parts) % 128 == 0
    )


def layer_kernel(z, names, *refs):
    r = types.SimpleNamespace(**dict(zip(names, refs)))
    send_sem, recv_sem, load_sem = r.send_sem, r.recv_sem, r.load_sem
    page = lax.axis_index("page")
    part = lax.axis_index("seq")
    counter = [0]

    def slots(count):
        first = counter[0]
        counter[0] += count
        return first

    odd = page % 2
    place = odd * (z.pages - 1 - page // 2) + (1 - odd) * (page // 2)

    def page_at(index):
        index = (index + z.pages) % z.pages
        late = index // z.half
        return (1 - late) * (2 * index) + late * (2 * z.pages - 1 - 2 * index)

    ring = [page] + [page_at(place + step) for step in range(1, z.pages)]
    peers = [part] + [
        ((part // 2 + j // 2) % 2) * 2 + (part % 2 + j % 2) % 2 for j in range(1, 4)
    ]

    def around(step):
        return ring[step % z.pages]

    def peer(j):
        return peers[j]

    rank = page * z.parts + part

    class Copy:
        def __init__(self, src, dst, index, device, group=None):
            self.args = src, dst, index, device
            self.group = group

        def made(self, group):
            src, dst, index, device = self.args
            return pltpu.make_async_remote_copy(
                src_ref=src,
                dst_ref=dst,
                send_sem=send_sem.at[group],
                recv_sem=recv_sem.at[index],
                device_id=device,
                device_id_type=MESH,
            )

        def start(self):
            group = self.group
            if group is None:
                size = self.size()
                if groups[-1] + size > z.group_bytes:
                    groups.append(0)
                groups[-1] += size
                group = len(groups) - 1
            self.made(group).start()

        def wait_recv(self):
            self.made(0).wait_recv()

        def size(self):
            src = self.args[0]
            return math.prod(src.shape) * jnp.dtype(src.dtype).itemsize

        def wait_bytes(self, size):
            rows = r.measure.at[pl.ds(0, size // 512)]
            Copy(rows, rows, *self.args[2:]).wait_recv()

        def wait_send(self):
            self.made(self.group).wait_send()

    groups = [0]
    copy = Copy

    def block(ref, index, size):
        return ref.at[pl.ds(pl.multiple_of(index * size, size), size)]

    barrier = pltpu.get_barrier_semaphore()

    def greet(device):
        pl.semaphore_signal(barrier, inc=1, device_id=device, device_id_type=MESH)

    for j in (1, 2, 3):
        greet((page, peer(j)))
    greet((around(1), part))
    greet((around(-1), part))

    class Share:
        def __init__(self, ref, size, pieces=2):
            self.ref, self.size, self.pieces = ref, size, pieces
            self.first = slots(2 + pieces)

        def copy(self, j, owner, k):
            height = self.size // self.pieces
            piece = block(self.ref, owner, self.size).at[pl.ds(k * height, height)]
            index = self.first + (2 + k if j == 2 else j // 2)
            return copy(piece, piece, index, (page, peer(1 if j == 3 else j)))

        def start(self, k):
            self.copy(2, part, k).start()
            self.copy(1, part, k).start()

        def forward(self):
            for k in range(self.pieces):
                self.copy(2, peer(2), k).wait_recv()
                self.copy(3, peer(2), k).start()


        def wait(self, j):
            arrival = self.copy(j, peer(j), 0)
            arrival.wait_bytes(self.pieces * arrival.size())

    class Combine:
        def __init__(self, refs, size, make, pieces=2):
            self.out, self.got, self.own = refs
            self.size, self.make, self.pieces = size, make, pieces
            self.height = size // pieces
            self.first = slots(2 * pieces)

        def rows(self, j, k):
            at = pl.multiple_of(peer(j) * self.size + k * self.height, self.height)
            return pl.ds(at, self.height)

        def copy(self, j, k):
            return copy(
                self.out.at[self.rows(j, k)],
                self.got.at[j, pl.ds(k * self.height, self.height)],
                self.first + 2 * k + j // 3,
                (page, peer(2 if j == 2 else 1)),
            )

        def term(self, j):
            value = self.make(pl.ds(pl.multiple_of(peer(j) * self.size, self.size), self.size), j)
            if j == 0:
                self.own[...] = value
                return
            for k in range(self.pieces):
                rows = slice(k * self.height, (k + 1) * self.height)
                mine = value[rows]
                if j == 2:
                    self.copy(3, k).wait_recv()
                    mine = mine + self.got[3, rows, :].astype(F32)
                self.out[self.rows(j, k), :] = mine.astype(BF16)
                self.copy(j, k).start()

        def finish(self, fn, after=None, step=32):
            for k in range(self.pieces):
                arrival = self.copy(1, k)
                arrival.wait_bytes(2 * arrival.size())

                def body(i, carry):
                    at = pl.multiple_of(k * self.height + i * step, step)
                    rows = pl.ds(at, step)
                    total = self.own[rows, :]
                    for j in (1, 2):
                        total = total + self.got[j, rows, :].astype(F32)
                    fn(rows, at, total)
                    return carry

                lax.fori_loop(0, self.height // step, body, 0)
                if after is not None:
                    after(k)

    def token_refs(phase):
        return r.part_out.at[phase], r.part_in.at[phase], r.part_own

    class Spread:
        def __init__(self, src, dst, size):
            self.src, self.dst, self.size, self.first = src, dst, size, slots(1)

        def copy(self, j):
            return copy(
                block(self.src, peer(j), self.size),
                self.dst.at[j],
                self.first,
                (page, peer(j)),
            )

        def start(self):
            for j in (2, 3, 1):
                self.copy(j).start()

        def wait(self):
            arrival = self.copy(1)
            arrival.wait_bytes(3 * arrival.size())

    class Place:
        def __init__(self, src, dst, size, base):
            self.src, self.dst, self.size, self.base, self.first = src, dst, size, base, slots(1)

        def copy(self, j, owner):
            return copy(
                block(self.src, peer(j), self.size),
                block(self.dst, self.base + owner, self.size),
                self.first,
                (page, peer(j)),
            )

        def start(self):
            for j in (2, 3, 1):
                self.copy(j, part).start()

        def wait(self):
            arrival = self.copy(1, peer(1))
            arrival.wait_bytes(3 * arrival.size())

    class Gather:
        def __init__(self, ref, size, pieces=1):
            self.ref, self.size, self.pieces = ref, size, pieces
            self.first = slots(z.half * pieces)

        def copy(self, t, d, k, step):
            height = self.size // self.pieces
            start = k * height
            if t == z.half - 1:
                height = height // 2
                start = start + d * height
            piece = block(self.ref, around(step), self.size).at[pl.ds(start, height)]
            return copy(
                piece,
                piece,
                self.first + t * self.pieces + k,
                (around(1 - 2 * d), part),
            )

        def wait(self, t, k):
            both = 2 * self.copy(t, 0, k, 0).size()
            self.copy(t, 0, k, 0).wait_bytes(both)

        def step(self, t, pieces=None):
            for k in pieces or range(self.pieces):
                if t > 0:
                    self.wait(t - 1, k)
                for d in (0, 1):
                    self.copy(t, d, k, -(1 - 2 * d) * t).start()


        def done(self):
            for k in range(self.pieces):
                self.wait(z.half - 1, k)

    class Reduce:
        def __init__(self, slot, stage, local, shape, kind, pieces=1):
            self.slot, self.stage, self.local = slot, stage, local
            self.size, self.kind, self.pieces = shape[0], kind, pieces
            self.wide = shape[1] // pieces
            self.first = slots(z.half * pieces)

        def copy(self, t, d, k):
            h = self.size // 2
            if t == 0:
                src = self.stage.at[k, pl.ds(d * h, h)]
                dst = self.slot.at[k, d, 0, pl.ds(d * h, h)]
            else:
                src = self.slot.at[k, d, t - 1]
                dst = self.slot.at[k, d, t]
            return copy(
                src,
                dst,
                self.first + t * self.pieces + k,
                (around(1 - 2 * d), part),
            )


        def step(self, t):
            h = self.size // 2
            wide = self.wide
            if t == 0:
                term = self.local(around(z.half)).astype(self.kind)
                for k in range(self.pieces):
                    self.stage[k] = term[:, k * wide : (k + 1) * wide]
            else:
                terms = [
                    self.local(around((1 - 2 * d) * (z.half - t))) for d in (0, 1)
                ]
            for k in range(self.pieces):
                if t > 0:
                    self.wait(t - 1, k)
                for d in (0, 1):
                    if t > 0:
                        term = terms[d][:, k * wide : (k + 1) * wide]
                        held = self.slot.at[k, d, t - 1]
                        if t == 1:
                            near, far = pl.ds(d * h, h), pl.ds((1 - d) * h, h)
                            term_near = term[d * h : (d + 1) * h]
                            term_far = term[(1 - d) * h : (2 - d) * h]
                            held[near] = (held[near].astype(F32) + term_near).astype(self.kind)
                            held[far] = term_far.astype(self.kind)
                        else:
                            held[...] = (held[...].astype(F32) + term).astype(self.kind)
                    self.copy(t, d, k).start()

        def wait(self, t, k):
            arrival = self.copy(t, 0, k)
            arrival.wait_bytes(2 * arrival.size())

        def total(self, out):
            term = self.local(page)
            last = z.half - 1
            for k in range(self.pieces):
                self.wait(last, k)
                at = slice(k * self.wide, (k + 1) * self.wide)
                out[:, at] = (
                    term[:, at] + self.slot[k, 0, last].astype(F32) + self.slot[k, 1, last].astype(F32)
                ).astype(out.dtype)

    c, w, n = z.cols, z.width, z.span

    def fetch(i, name):
        return pltpu.make_async_copy(getattr(r, name), getattr(r, z.held + name), load_sem.at[i])

    for i, name in enumerate(z.fetched):
        fetch(i, name).start()
    hbm = r
    r = types.SimpleNamespace(**vars(hbm))
    for name in z.fetched:
        setattr(r, name, getattr(hbm, z.held + name))
    fetches = iter(range(len(z.fetched)))

    def arrive(count):
        for _ in range(count):
            i = next(fetches)
            pltpu.make_async_copy(
                getattr(hbm, z.fetched[i]), getattr(r, z.fetched[i]), load_sem.at[i]
            ).wait()

    arrive(3)
    for q in range(z.parts):
        rows = pl.ds(q * z.row, z.row)
        for i, weight in enumerate((r.w_query, r.w_key, r.w_value)):
            for k in range(z.pairs):
                r.cut_qkv[rows, (3 * k + i) * 128 : (3 * k + i + 1) * 128] = weight[
                    :, q * c + k * 128 : q * c + (k + 1) * 128
                ].astype(BF16)
    mine = pl.multiple_of(part * SLAB, SLAB)
    for i, small in enumerate(
        (r.b_query, r.b_value, r.b_out, r.g_attn, r.s_attn, r.b_outer, r.g_final, r.s_final)
    ):
        r.vec_raw[pl.ds(mine + i, 1), 0 : z.row] = small[...]
    at_page = pl.multiple_of(page * SLAB, SLAB)
    r.vec_all[pl.ds(at_page + VECTORS, 1), :] = r.b_inner[...]
    arrive(1)
    r.outer_w[pl.ds(pl.multiple_of(page * z.unit, z.unit), z.unit), :] = r.w_outer[...].astype(
        BF16
    )

    ring_qkv = Gather(r.qkv_w, z.rows, 2)
    ring_vec = Gather(r.vec_all, SLAB)
    ring_inner = Gather(r.inner_w, z.rows, 2)
    ring_out = Gather(r.out_w, z.rows)
    ring_outer = Gather(r.outer_w, z.unit, 2)
    cut_qkv = Place(r.cut_qkv, r.qkv_w, z.row, page * z.parts)
    cut_out = Place(r.cut_out, r.out_w, z.row, page * z.parts)
    cut_inner = Place(r.cut_inner, r.inner_w, z.row, page * z.parts)
    share_tok = Share(r.tok_all, n)

    class ShareVec:
        first = slots(1)

        def copy(self, j, owner):
            piece = block(r.vec_raw, owner, SLAB).at[pl.ds(0, VECTORS)]
            return copy(piece, piece, self.first, (page, peer(j)))

    vec_share = ShareVec()
    pl.semaphore_wait(barrier, 5)
    cut_qkv.start()
    for j in (2, 3, 1):
        vec_share.copy(j, part).start()
    ring_outer.step(0)
    arrive(2)
    r.tok_all[pl.ds(pl.multiple_of(part * n, n), n), :] = r.tokens[...].astype(BF16)
    share_tok.start(0)
    share_tok.start(1)
    for q in range(z.parts):
        r.cut_out[pl.ds(q * z.row, z.row), :] = r.w_out[:, q * c : (q + 1) * c].astype(BF16)
    cut_out.start()
    arrive(1)
    for q in range(z.parts):
        rows = pl.ds(q * z.row, z.row)
        for g in range(z.pages):
            at = (z.parts * g + q) * z.unit
            r.cut_inner[rows, g * z.unit : (g + 1) * z.unit] = r.w_inner[
                :, at : at + z.unit
            ].astype(BF16)
    cut_inner.start()
    own_rows = pl.ds(pl.multiple_of(rank * z.row, z.row), z.row)
    cut_rows = pl.ds(pl.multiple_of(part * z.row, z.row), z.row)
    r.qkv_w[own_rows, :] = r.cut_qkv[cut_rows, :]
    r.out_w[own_rows, :] = r.cut_out[cut_rows, :]
    r.inner_w[own_rows, :] = r.cut_inner[cut_rows, :]

    cut_qkv.wait()
    ring_qkv.step(0)
    arrival = vec_share.copy(1, peer(1))
    arrival.wait_bytes(3 * arrival.size())
    lane = lax.broadcasted_iota(jnp.int32, (VECTORS, 128), 1)
    total = jnp.zeros((VECTORS, 128), F32)
    for q in range(z.parts):
        tile = r.vec_raw[q * SLAB : q * SLAB + VECTORS, :]
        if q:
            tile = pltpu.roll(tile, q * z.row, 1)
        total = total + jnp.where(lane // z.row == q, tile, 0.0)
    r.vec_all[pl.ds(at_page, VECTORS), :] = total
    ring_vec.step(0)
    ring_qkv.step(1)
    ring_vec.step(1)
    cut_out.wait()
    ring_out.step(0)
    ring_qkv.step(2)
    ring_vec.step(2)
    ring_out.step(1)
    share_tok.forward()
    ring_qkv.step(3)
    ring_vec.step(3)
    ring_out.step(2)
    cut_inner.wait()
    ring_inner.step(0)
    ring_vec.done()

    for g in range(z.pages):
        tile = r.vec_all[g * SLAB : (g + 1) * SLAB, :].astype(BF16).astype(F32)
        r.vecs[:, g * 128 : (g + 1) * 128] = tile[0:VECTORS]
        r.b_mine[:, g * z.unit : (g + 1) * z.unit] = tile[VECTORS : VECTORS + 1]

    def vector(i):
        return r.vecs[i : i + 1, :]


    share_tok.wait(1)
    share_tok.wait(3)
    ring_qkv.done()

    def make_qkv(b, carry):
        rows = pl.ds(pl.multiple_of(b * n, n), n)
        out = dot_nn(r.tok_all[rows, :], r.qkv_w[...])
        for k in range(z.pairs):
            mine = pl.ds(pl.multiple_of(part * c + k * 128, 128), 128)
            for i, bias in enumerate((0, None, 1)):
                cols = slice((3 * k + i) * 128, (3 * k + i + 1) * 128)
                value = out[:, cols]
                if bias is not None:
                    value = value + r.vecs[bias : bias + 1, mine]
                r.qkv[rows, cols] = value.astype(BF16)
        return carry

    lax.fori_loop(0, z.parts, make_qkv, 0)
    ring_inner.step(1)
    ring_out.step(3)
    ring_outer.step(1)

    scale = HEAD_DIM ** (-0.5)
    first_head = lax.broadcasted_iota(jnp.int32, (n, 128), 1) < HEAD_DIM
    key_place = lax.broadcasted_iota(jnp.int32, (n, z.length), 1)
    valid = r.valid[0]

    def pair_cols(kind, pair):
        return pl.ds((3 * pair + kind) * 128, 128)

    def attend(pair):
        def body(b, carry):
            rows = pl.ds(pl.multiple_of(b * n, n), n)
            queries = r.qkv[rows, pair_cols(0, pair)]
            keys = r.qkv[:, pair_cols(1, pair)]
            values = r.qkv[:, pair_cols(2, pair)]
            outs = []
            for h in range(2):
                mine = first_head if h == 0 else ~first_head
                scores = dot_nt(jnp.where(mine, queries, jnp.zeros_like(queries)), keys) * scale
                scores = jnp.where(key_place < valid, scores, NEGATIVE)
                top = jnp.max(scores, axis=-1, keepdims=True)
                weight = jnp.exp(scores - top)
                probs = weight * (1.0 / jnp.sum(weight, axis=-1, keepdims=True))
                r.probs[2 * pair + h, rows, :] = probs
                outs.append(dot_nn(probs.astype(BF16), values))
            place_rows = pl.ds(
                pl.multiple_of((part * z.pairs + pair) * z.length + b * n, n), n
            )
            r.ctx_all[place_rows, :] = jnp.where(first_head, outs[0], outs[1]).astype(
                BF16
            )
            return carry

        lax.fori_loop(0, z.parts, body, 0)

    share_ctx = Share(r.ctx_all, z.pairs * z.length, z.pairs)
    for pair in range(z.pairs):
        attend(pair)
        share_ctx.start(pair)
    ring_inner.step(2)
    ring_outer.step(2, (0,))

    def project(j):
        term = None
        for k in range(z.pairs):
            rows = pl.ds(pl.multiple_of((peer(j) * z.pairs + k) * z.length, z.length), z.length)
            features = pl.ds(pl.multiple_of(peer(j) * c + k * 128, 128), 128)
            more = dot_nn(r.ctx_all[rows, :], r.out_w[features, :])
            term = more if term is None else term + more
        r.att_sum[...] = term if j == 0 else r.att_sum[...] + term

    ring_out.done()
    project(0)
    share_ctx.wait(1)
    project(1)
    share_ctx.forward()
    project(2)
    share_ctx.wait(3)
    project(3)
    r.att_cut[...] = r.att_sum[...].astype(BF16)
    move_att = Place(r.att_cut, r.att_got, n, 0)
    move_att.start()
    own_block = pl.ds(pl.multiple_of(part * n, n), n)
    r.att_got[own_block, :] = r.att_cut[own_block, :]

    def add_column_sum(i, values):
        r.sums[i : i + 1, :] += jnp.sum(values, axis=0, keepdims=True)

    r.sums[...] = jnp.zeros_like(r.sums)

    share_hid = Share(r.hid_all, n)

    def first_norm(rows, at, total):
        mixed = r.tokens[rows, :] + (total + vector(2))
        normed, inverse = norm_parts(mixed)
        hidden = normed * vector(3) + vector(4)
        r.norm_one[rows, :] = normed
        r.inv_one[rows, :] = inverse
        r.hidden[rows, :] = hidden
        r.hid_all[pl.ds(pl.multiple_of(part * n + at, 32), 32), :] = hidden.astype(BF16)

    ring_inner.step(3)
    ring_outer.step(2, (1,))
    move_att.wait()
    for k in range(2):

        def norm_rows(i, carry):
            at = pl.multiple_of(k * (n // 2) + i * 32, 32)
            total = jnp.concatenate(
                [
                    r.att_got[pl.ds(pl.multiple_of(q * n + at, 32), 32), :].astype(F32)
                    for q in range(z.parts)
                ],
                axis=1,
            )
            first_norm(pl.ds(at, 32), at, total)
            return carry

        lax.fori_loop(0, n // 64, norm_rows, 0)
        share_hid.start(k)
    ring_inner.done()

    tile = 256

    def make_inner(j):
        rows = pl.ds(pl.multiple_of(peer(j) * n, n), n)

        def columns(i, carry):
            cols = pl.ds(pl.multiple_of(i * tile, tile), tile)
            inner = dot_nn(r.hid_all[rows, :], r.inner_w[:, cols]) + r.b_mine[:, cols]
            active, slope = gelu_parts(inner)
            r.active[rows, cols] = active.astype(BF16)
            r.slope[rows, cols] = slope
            return carry

        lax.fori_loop(0, z.mine // tile, columns, 0)

    make_inner(0)
    share_hid.wait(1)
    make_inner(1)
    ring_outer.step(3)
    share_hid.forward()
    make_inner(2)
    share_hid.wait(3)
    make_inner(3)
    ring_outer.done()
    combine_two = Combine(token_refs(0), n, lambda rows, j: dot_nn(r.active[rows, :], r.outer_w[...]))
    for j in (3, 2, 1, 0):
        combine_two.term(j)
    share_gf = Share(r.gf_all, n)

    arrive(1)

    def second_norm(rows, at, total):
        outer = total + vector(5)
        normed, inverse = norm_parts(r.hidden[rows, :] + outer)
        r.v_out[rows, :] = normed * vector(6) + vector(7)
        grad = r.out_grad[rows, :]
        add_column_sum(6, grad * normed)
        add_column_sum(7, grad)
        grad_sum = norm_backward(grad, normed, inverse, vector(6))
        low = grad_sum.astype(BF16)
        add_column_sum(5, low.astype(F32))
        r.grad_sum[rows, :] = grad_sum
        r.gf_all[pl.ds(pl.multiple_of(part * n + at, 32), 32), :] = low

    combine_two.finish(second_norm, share_gf.start)

    def leave_early(i, src, dst):
        return pltpu.make_async_copy(src, dst, load_sem.at[len(z.fetched) + i])

    leave_early(0, r.v_out, r.o_out).start()

    def chunk_term(left, right, size):
        def local(g):
            cols = pl.ds(pl.multiple_of(g * size, size), size)
            return dot_tn(left[:, cols], right[...])

        return local

    reduce_outer_a = Reduce(
        r.slot_outer_a, r.stage_outer_a,
        chunk_term(r.active, r.gf_all.at[:, 0 : w // 2], z.unit), (z.unit, w // 2), BF16,
    )
    reduce_outer_b = Reduce(
        r.slot_outer_b, r.stage_outer_b,
        chunk_term(r.active, r.gf_all.at[:, w // 2 :], z.unit), (z.unit, w // 2), BF16,
    )
    reduce_inner = Reduce(
        r.slot_inner, r.stage_inner, chunk_term(r.hid_all, r.grad_inner, z.rows),
        (z.rows, z.mine), BF16, 2
    )
    def pair_term(k):
        def local(g):
            cols = pl.ds(pl.multiple_of(g * z.rows, z.rows), z.rows)
            return dot_tn(r.tok_all[:, cols], r.grad_qkv[:, 384 * k : 384 * (k + 1)])

        return local

    def out_term(g):
        rows = pl.ds(pl.multiple_of(g * z.length, z.length), z.length)
        return dot_tn(r.ctx_all[rows, :], r.ga_cols[...])

    reduce_pair = [
        Reduce(r.slot_pair.at[k], r.stage_pair.at[k], pair_term(k), (z.rows, 384), BF16)
        for k in range(z.pairs)
    ]
    reduce_out = Reduce(r.slot_out, r.stage_out, out_term, (z.rows, c), BF16)
    reduce_vec = Reduce(
        r.slot_vec, r.stage_vec,
        lambda g: r.term_vec[pl.ds(pl.multiple_of(g * SLAB, SLAB), SLAB), :], (SLAB, 128), F32,
    )

    r.b_sum[...] = jnp.zeros_like(r.b_sum)

    def make_grad_inner(j):
        rows = pl.ds(pl.multiple_of(peer(j) * n, n), n)

        def columns(i, carry):
            cols = pl.ds(pl.multiple_of(i * tile, tile), tile)
            grad = dot_nt(r.gf_all[rows, :], r.outer_w[cols, :]) * r.slope[rows, cols]
            low = grad.astype(BF16)
            r.grad_inner[rows, cols] = low
            r.b_sum[:, cols] += jnp.sum(low.astype(F32), axis=0, keepdims=True)
            return carry

        lax.fori_loop(0, z.mine // tile, columns, 0)

    make_grad_inner(0)
    share_gf.wait(1)
    make_grad_inner(1)
    share_gf.forward()
    make_grad_inner(2)
    share_gf.wait(3)
    reduce_outer_a.step(0)
    reduce_outer_b.step(0)
    make_grad_inner(3)
    combine_three = Combine(token_refs(1), n, lambda rows, j: dot_nt(r.grad_inner[rows, :], r.inner_w[...]))
    combine_three.term(3)
    combine_three.term(2)
    reduce_inner.step(0)
    reduce_outer_a.step(1)
    combine_three.term(1)
    combine_three.term(0)
    reduce_outer_b.step(1)
    reduce_inner.step(1)

    move_ga = Place(r.ga_cut, r.ga_cols, n, 0)

    def first_norm_back(rows, at, total):
        grad = r.grad_sum[rows, :] + total
        normed = r.norm_one[rows, :]
        add_column_sum(3, grad * normed)
        add_column_sum(4, grad)
        mixed = norm_backward(grad, normed, r.inv_one[rows, :], vector(3))
        low = mixed.astype(BF16)
        add_column_sum(2, low.astype(F32))
        r.grad_mixed[rows, :] = mixed
        for q in range(z.parts):
            r.ga_cut[pl.ds(pl.multiple_of(q * n + at, 32), 32), :] = low[:, q * c : (q + 1) * c]

    combine_three.finish(first_norm_back)
    move_ga.start()
    r.ga_cols[own_block, :] = r.ga_cut[own_block, :]
    reduce_outer_a.step(2)

    def grad_ctx_term(rows, j):
        return jnp.concatenate(
            [
                dot_nt(
                    r.ga_cols[...],
                    r.out_w[pl.ds(pl.multiple_of(peer(j) * c + k * 128, 128), 128), :],
                )
                for k in range(z.pairs)
            ],
            axis=0,
        )

    combine_ctx = Combine(
        (r.ctx_out, r.ctx_in, r.ctx_own), z.pairs * z.length, grad_ctx_term, z.pairs
    )
    move_ga.wait()
    combine_ctx.term(3)
    combine_ctx.term(2)
    combine_ctx.term(1)
    combine_ctx.term(0)
    reduce_out.step(0)
    reduce_inner.step(2)

    def keep_grad_ctx(rows, at, total):
        r.grad_ctx[rows, :] = total.astype(BF16)

    def attend_back(pair):
        r.grad_kv[...] = jnp.zeros_like(r.grad_kv)

        def body(b, carry):
            rows = pl.ds(pl.multiple_of(b * n, n), n)
            queries = r.qkv[rows, pair_cols(0, pair)]
            keys = r.qkv[:, pair_cols(1, pair)]
            values = r.qkv[:, pair_cols(2, pair)]
            grad = r.grad_ctx[pl.ds(pl.multiple_of(pair * z.length + b * n, n), n), :]
            outs = []
            for h in range(2):
                mine = first_head if h == 0 else ~first_head
                grad_mine = jnp.where(mine, grad, jnp.zeros_like(grad))
                query_mine = jnp.where(mine, queries, jnp.zeros_like(queries))
                probs = r.probs[2 * pair + h, rows, :]
                grad_probs = dot_nt(grad_mine, values)
                r.grad_kv[1] += dot_tn(probs.astype(BF16), grad_mine)
                inside = jnp.sum(grad_probs * probs, axis=-1, keepdims=True)
                grad_scores = (probs * (grad_probs - inside)).astype(BF16)
                outs.append(dot_nn(grad_scores, keys))
                r.grad_kv[0] += dot_tn(grad_scores, query_mine)
            r.grad_qkv[rows, pair_cols(0, pair)] = (
                jnp.where(first_head, outs[0], outs[1]) * scale
            ).astype(BF16)
            return carry

        lax.fori_loop(0, z.parts, body, 0)
        r.grad_qkv[:, pair_cols(1, pair)] = (r.grad_kv[0] * scale).astype(BF16)
        r.grad_qkv[:, pair_cols(2, pair)] = r.grad_kv[1].astype(BF16)

    def after_pair(pair):
        attend_back(pair)
        reduce_pair[pair].step(0)
        if pair == 0:
            reduce_outer_a.step(3)
            reduce_outer_b.step(2)
            reduce_out.step(1)

    combine_ctx.finish(keep_grad_ctx, after_pair, step=128)
    reduce_inner.step(3)
    reduce_out.step(2)

    for k in range(z.pairs):
        mine = pl.ds(pl.multiple_of(part * c + k * 128, 128), 128)
        for row, kind in ((0, 0), (1, 2)):
            r.sums[row : row + 1, mine] = jnp.sum(
                r.grad_qkv[:, pair_cols(kind, k)].astype(F32), axis=0, keepdims=True
            )
    r.term_vec[...] = jnp.zeros_like(r.term_vec)
    for g in range(z.pages):
        r.term_vec[g * SLAB : g * SLAB + VECTORS, :] = r.sums[:, g * 128 : (g + 1) * 128]
        r.term_vec[g * SLAB + VECTORS : g * SLAB + VECTORS + 1, :] = r.b_sum[
            :, g * z.unit : (g + 1) * z.unit
        ]
    reduce_vec.step(0)

    combine_four = Combine(token_refs(2), n, lambda rows, j: dot_nt(r.grad_qkv[rows, :], r.qkv_w[...]))
    combine_four.term(3)
    combine_four.term(2)
    for pair in range(z.pairs):
        reduce_pair[pair].step(1)
    reduce_vec.step(1)
    reduce_out.step(3)
    combine_four.term(1)
    combine_four.term(0)

    reduce_inner.total(r.fin_inner)
    fin_inner = Spread(r.fin_inner, r.got_inner, z.row)
    fin_inner.start()
    for pair in range(z.pairs):
        reduce_pair[pair].step(2)
    reduce_vec.step(2)

    def input_rows(rows, at, total):
        r.v_grad[rows, :] = r.grad_mixed[rows, :] + total

    combine_four.finish(input_rows)
    leave_early(1, r.v_grad, r.o_grad).start()
    reduce_outer_a.total(r.o_outer.at[:, 0 : w // 2])
    for pair in range(z.pairs):
        reduce_pair[pair].step(3)
    reduce_vec.step(3)
    reduce_outer_b.step(3)
    reduce_out.total(r.fin_out)
    fin_out = Spread(r.fin_out, r.got_out, z.row)
    fin_out.start()
    fin_pair = []
    for k in range(z.pairs):
        reduce_pair[k].total(r.fin_pair.at[k])
        fin_pair.append(Spread(r.fin_pair.at[k], r.got_pair.at[k], z.row))
        fin_pair[k].start()
    reduce_vec.total(r.fin_vec)

    class VecAll:
        first = slots(1)

        def copy(self, j):
            return copy(r.fin_vec, r.got_vec.at[j], self.first, (page, peer(j)))

    fin_vec = VecAll()
    for j in (2, 3, 1):
        fin_vec.copy(j).start()

    my_rows = pl.ds(pl.multiple_of(part * z.row, z.row), z.row)

    def deliver(spread, mine, got, out):
        spread.wait()
        for j in range(4):
            value = got[j] if j else mine[my_rows, :]
            out[peer(j)] = value

    deliver(fin_inner, r.fin_inner, r.got_inner, r.o_inner)
    deliver(fin_out, r.fin_out, r.got_out, r.o_wout)
    arrival = fin_vec.copy(1)
    arrival.wait_bytes(3 * arrival.size())
    summed = r.fin_vec[0:VECTORS, :]
    for j in (1, 2, 3):
        summed = summed + r.got_vec[j, 0:VECTORS, :]
    r.o_vec[0:VECTORS, :] = pltpu.roll(summed, (128 - part * z.row) % 128, 1)
    r.o_vec[VECTORS:, :] = r.fin_vec[VECTORS:, :]
    reduce_outer_b.total(r.o_outer.at[:, w // 2 :])
    for k in range(z.pairs):
        deliver(fin_pair[k], r.fin_pair.at[k], r.got_pair.at[k], r.o_pair.at[k])

    leave_early(0, r.v_out, r.o_out).wait()
    leave_early(1, r.v_grad, r.o_grad).wait()
    for group, size in enumerate(groups):
        rows = r.measure.at[pl.ds(0, size // 512)]
        copy(rows, rows, 0, (page, part), group).wait_send()

    assert counter[0] == z.sems and len(groups) == z.groups, (counter, groups)


def finish_kernel(z, out, grad, outer, inner, pair, wout, vec, *outs):
    (o_out, o_grad, o_wq, o_bq, o_wk, o_wv, o_bv, o_wo, o_bo, o_ga, o_sa, o_wi, o_bi, o_wu, o_bu, o_gf, o_sf) = outs
    o_out[...] = out[...]
    o_grad[...] = grad[...]
    o_wu[...] = outer[...]
    c = z.cols
    for q in range(z.parts):
        o_wo[:, q * c : (q + 1) * c] = wout[q].astype(F32)
        for i, ref in enumerate((o_wq, o_wk, o_wv)):
            for k in range(z.pairs):
                ref[:, q * c + k * 128 : q * c + (k + 1) * 128] = pair[
                    k, q, :, i * 128 : (i + 1) * 128
                ].astype(F32)
        for g in range(z.pages):
            at = (z.parts * g + q) * z.unit
            o_wi[:, at : at + z.unit] = inner[q, :, g * z.unit : (g + 1) * z.unit].astype(F32)
    for i, ref in enumerate((o_bq, o_bv, o_bo, o_ga, o_sa, o_bu, o_gf, o_sf)):
        ref[...] = vec[i : i + 1, 0 : z.row]
    o_bi[...] = vec[VECTORS : VECTORS + 1, :]


def paged_layer(z, tokens, valid_len, params, out_grad):
    (
        w_query, b_query, w_key, w_value, b_value, w_out, b_out, g_attn, s_attn,
        w_inner, b_inner, w_outer, b_outer, g_final, s_final,
    ) = params
    flat = lambda v: v.reshape(1, v.shape[0])
    c, w, n, ln, half = z.cols, z.width, z.span, z.length, z.half
    ins = dict(
        valid=valid_len,
        tokens=tokens.reshape(n, w),
        out_grad=out_grad.reshape(n, w),
        w_query=w_query, w_key=w_key, w_value=w_value, w_out=w_out,
        w_inner=w_inner, w_outer=w_outer,
        b_query=flat(b_query), b_value=flat(b_value), b_out=flat(b_out),
        g_attn=flat(g_attn), s_attn=flat(s_attn), b_inner=flat(b_inner),
        b_outer=flat(b_outer), g_final=flat(g_final), s_final=flat(s_final),
    )
    outs = dict(
        o_out=((n, w), F32),
        o_grad=((n, w), F32),
        o_outer=((z.unit, w), F32),
        o_inner=((z.parts, z.row, z.mine), BF16),
        o_pair=((z.pairs, z.parts, z.row, 384), BF16),
        o_wout=((z.parts, z.row, c), BF16),
        o_vec=((SLAB, 128), F32),
    )
    scratch = dict(
        qkv_w=((w, 3 * c), BF16),
        out_w=((w, c), BF16),
        cut_out=((z.rows, c), BF16),
        inner_w=((w, z.mine), BF16),
        outer_w=((z.mine, w), BF16),
        vec_all=((z.pages * SLAB, 128), F32),
        vec_raw=((z.parts * SLAB, 128), F32),
        cut_qkv=((z.rows, 3 * c), BF16),
        cut_inner=((z.rows, z.mine), BF16),
        vecs=((VECTORS, w), F32),
        b_mine=((1, z.mine), F32),
        tok_all=((ln, w), BF16),
        hid_all=((ln, w), BF16),
        gf_all=((ln, w), BF16),
        ga_cut=((ln, c), BF16),
        ga_cols=((ln, c), BF16),
        att_sum=((ln, c), F32),
        att_cut=((ln, c), BF16),
        att_got=((ln, c), BF16),
        ctx_out=((w // 128 * ln, 128), BF16),
        ctx_in=((4, z.pairs * ln, 128), BF16),
        ctx_own=((z.pairs * ln, 128), F32),
        qkv=((ln, 3 * c), BF16),
        grad_qkv=((ln, 3 * c), BF16),
        probs=((z.heads, ln, ln), F32),
        measure=((8192, 128), F32),
        ctx_all=((w // 128 * ln, 128), BF16),
        grad_ctx=((z.pairs * ln, 128), BF16),
        grad_kv=((2, ln, 128), F32),
        part_out=((3, ln, w), BF16),
        part_in=((3, 4, n, w), BF16),
        part_own=((n, w), F32),
        norm_one=((n, w), F32),
        v_out=((n, w), F32),
        v_grad=((n, w), F32),
        inv_one=((n, 1), F32),
        hidden=((n, w), F32),
        grad_sum=((n, w), F32),
        grad_mixed=((n, w), F32),
        active=((ln, z.mine), BF16),
        slope=((ln, z.mine), F32),
        grad_inner=((ln, z.mine), BF16),
        sums=((VECTORS, w), F32),
        b_sum=((1, z.mine), F32),
        term_vec=((z.pages * SLAB, 128), F32),
        slot_outer_a=((1, 2, half, z.unit, w // 2), BF16), stage_outer_a=((1, z.unit, w // 2), BF16),
        slot_outer_b=((1, 2, half, z.unit, w // 2), BF16), stage_outer_b=((1, z.unit, w // 2), BF16),
        slot_inner=((2, 2, half, z.rows, z.mine // 2), BF16), stage_inner=((2, z.rows, z.mine // 2), BF16),
        slot_pair=((z.pairs, 1, 2, half, z.rows, 384), BF16), stage_pair=((z.pairs, 1, z.rows, 384), BF16),
        slot_out=((1, 2, half, z.rows, c), BF16), stage_out=((1, z.rows, c), BF16),
        slot_vec=((1, 2, half, SLAB, 128 // 1), F32), stage_vec=((1, SLAB, 128 // 1), F32),
        fin_inner=((z.rows, z.mine), BF16), got_inner=((4, z.row, z.mine), BF16),
        fin_pair=((z.pairs, z.rows, 384), BF16), got_pair=((z.pairs, 4, z.row, 384), BF16),
        fin_out=((z.rows, c), BF16), got_out=((4, z.row, c), BF16),
        fin_vec=((SLAB, 128), F32), got_vec=((4, SLAB, 128), F32),
    )
    z.sems = 107
    z.groups, z.group_bytes = 5, 4 << 20
    fetched = dict(w_query=0, w_key=0, w_value=0, w_outer=0, w_out=0, tokens=0, w_inner=0, out_grad=0)
    z.fetched, z.held = tuple(fetched), "f_"
    for name in z.fetched:
        scratch[z.held + name] = (ins[name].shape, F32)
    sems = [pltpu.SemaphoreType.DMA((z.groups,)), pltpu.SemaphoreType.DMA((z.sems,)), pltpu.SemaphoreType.DMA((len(fetched) + 2,))]
    names = list(ins) + list(outs) + list(scratch) + list(dict(send_sem=0, recv_sem=0, load_sem=0))
    vmem = pl.BlockSpec(memory_space=pltpu.VMEM)
    parts = pl.pallas_call(
        functools.partial(layer_kernel, z, names),
        out_shape=[jax.ShapeDtypeStruct(*v) for v in outs.values()],
        in_specs=[
            pl.BlockSpec(memory_space=pltpu.SMEM)
            if v is valid_len
            else pl.BlockSpec(memory_space=pl.ANY)
            if k in fetched
            else vmem
            for k, v in ins.items()
        ],
        out_specs=[pl.BlockSpec(memory_space=pl.ANY)] * 2 + [vmem] * (len(outs) - 2),
        scratch_shapes=[pltpu.VMEM(*v) for v in scratch.values()]
        + sems,
        compiler_params=pltpu.CompilerParams(
            collective_id=0, has_side_effects=True, vmem_limit_bytes=67043328
        ),
        name="layer",
    )(*ins.values())
    row, big = z.row, jax.ShapeDtypeStruct((n, w), F32)
    mat = jax.ShapeDtypeStruct((row, w), F32)
    vec = jax.ShapeDtypeStruct((1, row), F32)
    shapes = [
        big, big, mat, vec, mat, mat, vec, mat, vec, vec, vec,
        jax.ShapeDtypeStruct((row, z.units), F32), jax.ShapeDtypeStruct((1, z.unit), F32),
        jax.ShapeDtypeStruct((z.unit, w), F32), vec, vec, vec,
    ]
    results = pl.pallas_call(
        functools.partial(finish_kernel, z),
        out_shape=shapes,
        in_specs=[vmem] * 7,
        out_specs=[vmem] * len(shapes),
        name="finish",
    )(*parts)
    results = list(results)
    for i in (0, 1):
        results[i] = results[i].reshape(tokens.shape)
    for i in range(2, 17):
        if results[i].shape[0] == 1:
            results[i] = results[i].reshape(results[i].shape[1])
    return tuple(results)


def body(
    tokens,
    valid_len,
    query_weight,
    query_bias,
    key_weight,
    value_weight,
    value_bias,
    output_weight,
    output_bias,
    attn_gain,
    attn_shift,
    inner_weight,
    inner_bias,
    outer_weight,
    outer_bias,
    final_gain,
    final_shift,
    out_grad,
):
    lowered = [
        piece.astype(jnp.bfloat16)
        for piece in (
            query_weight,
            query_bias,
            key_weight,
            value_weight,
            value_bias,
            output_weight,
            output_bias,
            attn_gain,
            attn_shift,
            inner_weight,
            inner_bias,
            outer_weight,
            outer_bias,
            final_gain,
            final_shift,
        )
    ]
    outputs = sequence_layer(tokens, valid_len, lowered, out_grad)
    return outputs


def solution(mesh):
    in_specs = (
        P("page", "seq", None),
        P("page"),
        P(("page", "seq"), None),
        P(("page", "seq")),
        P(("page", "seq"), None),
        P(("page", "seq"), None),
        P(("page", "seq")),
        P(("page", "seq"), None),
        P(("page", "seq")),
        P(("page", "seq")),
        P(("page", "seq")),
        P(("page", "seq"), None),
        P(("page", "seq")),
        P(("page", "seq"), None),
        P(("page", "seq")),
        P(("page", "seq")),
        P(("page", "seq")),
        P("page", "seq", None),
    )
    out_specs = (
        P("page", "seq", None),
        P("page", "seq", None),
        P(("page", "seq"), None),
        P(("page", "seq")),
        P(("page", "seq"), None),
        P(("page", "seq"), None),
        P(("page", "seq")),
        P(("page", "seq"), None),
        P(("page", "seq")),
        P(("page", "seq")),
        P(("page", "seq")),
        P(("page", "seq"), None),
        P(("page", "seq")),
        P(("page", "seq"), None),
        P(("page", "seq")),
        P(("page", "seq")),
        P(("page", "seq")),
    )

    def layer(*arrays):
        width, units = arrays[11].shape
        if supported(mesh, arrays[0].shape, width, units):
            z = Sizes(mesh, width, units, arrays[0].shape[1] // mesh.shape["seq"])

            def run(tokens, valid_len, *rest):
                return paged_layer(z, tokens, valid_len, rest[:-1], rest[-1])

            chosen = run
        else:
            chosen = body
        return jax.shard_map(
            chosen, mesh=mesh, in_specs=in_specs, out_specs=out_specs, check_vma=False
        )(*arrays)

    return layer
```

```python
import functools
import math
import types

import jax
import jax.numpy as jnp
from jax import lax
from jax.experimental import pallas as pl
from jax.experimental.pallas import tpu as pltpu
from jax.sharding import PartitionSpec as P

HEAD_DIM = 64


EPSILON = 1e-05
INV_ROOT_TWO = 1.0 / math.sqrt(2.0)
INV_ROOT_TWO_PI = 1.0 / math.sqrt(2.0 * math.pi)


def product(left, right):
    return jnp.dot(left, right, preferred_element_type=jnp.float32)


def product_tn(left, right):
    return lax.dot_general(
        left, right, (((0,), (0,)), ((), ())), preferred_element_type=jnp.float32
    )


def product_nt(left, right):
    return lax.dot_general(
        left, right, (((1,), (1,)), ((), ())), preferred_element_type=jnp.float32
    )


def norm_parts(values):
    center = values - jnp.mean(values, axis=-1, keepdims=True)
    inverse = lax.rsqrt(jnp.mean(center * center, axis=-1, keepdims=True) + EPSILON)
    return (center * inverse, inverse)


def norm_backward(grad_out, normed, inverse, gain):
    scaled = grad_out * gain
    return inverse * (
        scaled
        - jnp.mean(scaled, axis=-1, keepdims=True)
        - normed * jnp.mean(scaled * normed, axis=-1, keepdims=True)
    )


def gelu_parts(values):
    cumulative = 0.5 * (1.0 + lax.erf(values * INV_ROOT_TWO))
    return (
        values * cumulative,
        cumulative + values * jnp.exp(-0.5 * values * values) * INV_ROOT_TWO_PI,
    )


def sequence_layer(tokens, valid_len, lowered, out_grad):
    fetched = (
        lax.all_gather(lowered[0], ("page", "seq"), axis=0, tiled=True),
        lax.all_gather(lowered[1], ("page", "seq"), axis=0, tiled=True),
        lax.all_gather(lowered[2], ("page", "seq"), axis=0, tiled=True),
        lax.all_gather(lowered[3], ("page", "seq"), axis=0, tiled=True),
        lax.all_gather(lowered[4], ("page", "seq"), axis=0, tiled=True),
        lax.all_gather(lowered[5], ("page", "seq"), axis=0, tiled=True),
        lax.all_gather(lowered[6], ("page", "seq"), axis=0, tiled=True),
        lax.all_gather(lowered[7], ("page", "seq"), axis=0, tiled=True),
        lax.all_gather(lowered[8], ("page", "seq"), axis=0, tiled=True),
        lax.all_gather(lowered[9], ("page", "seq"), axis=0, tiled=True),
        lax.all_gather(lowered[10], ("page", "seq"), axis=0, tiled=True),
        lax.all_gather(lowered[11], ("page", "seq"), axis=0, tiled=True),
        lax.all_gather(lowered[12], ("page", "seq"), axis=0, tiled=True),
        lax.all_gather(lowered[13], ("page", "seq"), axis=0, tiled=True),
        lax.all_gather(lowered[14], ("page", "seq"), axis=0, tiled=True),
    )
    (
        w_query,
        b_query,
        w_key,
        w_value,
        b_value,
        w_out,
        b_out,
        g_attn,
        s_attn,
        w_inner,
        b_inner,
        w_outer,
        b_outer,
        g_final,
        s_final,
    ) = fetched
    f32 = jnp.float32
    bf16 = jnp.bfloat16
    scale = HEAD_DIM ** (-0.5)
    page_count, span_len, width = tokens.shape
    heads = width // HEAD_DIM
    row_count = page_count * span_len
    tok_rows = tokens.reshape(row_count, width)
    tok_low = tok_rows.astype(bf16)
    q_low = (product(tok_low, w_query) + b_query.astype(f32)).astype(bf16)
    k_low = product(tok_low, w_key).astype(bf16)
    v_low = (product(tok_low, w_value) + b_value.astype(f32)).astype(bf16)
    k_full, v_full = (
        lax.all_gather(k_low.reshape(page_count, span_len, width), "seq", axis=1, tiled=True),
        lax.all_gather(v_low.reshape(page_count, span_len, width), "seq", axis=1, tiled=True),
    )
    seq_len = k_full.shape[1]
    q_heads = q_low.reshape(page_count, span_len, heads, HEAD_DIM)
    k_heads = k_full.reshape(page_count, seq_len, heads, HEAD_DIM)
    v_heads = v_full.reshape(page_count, seq_len, heads, HEAD_DIM)
    key_mask = (lax.broadcasted_iota(jnp.int32, (page_count, seq_len), 1) < valid_len[:, None])[
        :, None, None, :
    ]

    def masked_scores():
        raw = jnp.einsum("pqhe,pkhe->phqk", q_heads, k_heads, preferred_element_type=f32) * scale
        return jnp.where(key_mask, raw, -1000000000.0)

    scores = masked_scores()
    top_score = jnp.max(scores, axis=-1, keepdims=True)
    log_total = top_score + jnp.log(jnp.sum(jnp.exp(scores - top_score), axis=-1, keepdims=True))
    probs_low = jnp.exp(scores - log_total).astype(bf16)
    context = jnp.einsum("phqk,pkhe->pqhe", probs_low, v_heads, preferred_element_type=f32)
    ctx_low = context.reshape(row_count, width).astype(bf16)
    attended = product(ctx_low, w_out) + b_out.astype(f32)
    norm_one, inv_one = norm_parts(tok_rows + attended)
    hidden = norm_one * g_attn.astype(f32) + s_attn.astype(f32)
    hid_low = hidden.astype(bf16)
    inner = product(hid_low, w_inner) + b_inner.astype(f32)
    active, slope = gelu_parts(inner)
    act_low = active.astype(bf16)
    outer = product(act_low, w_outer) + b_outer.astype(f32)
    norm_two, inv_two = norm_parts(hidden + outer)
    result = norm_two * g_final.astype(f32) + s_final.astype(f32)
    (
        w_query,
        b_query,
        w_key,
        w_value,
        b_value,
        w_out,
        b_out,
        g_attn,
        s_attn,
        w_inner,
        b_inner,
        w_outer,
        b_outer,
        g_final,
        s_final,
    ) = (
        lax.all_gather(lowered[0], ("page", "seq"), axis=0, tiled=True),
        lax.all_gather(lowered[1], ("page", "seq"), axis=0, tiled=True),
        lax.all_gather(lowered[2], ("page", "seq"), axis=0, tiled=True),
        lax.all_gather(lowered[3], ("page", "seq"), axis=0, tiled=True),
        lax.all_gather(lowered[4], ("page", "seq"), axis=0, tiled=True),
        lax.all_gather(lowered[5], ("page", "seq"), axis=0, tiled=True),
        lax.all_gather(lowered[6], ("page", "seq"), axis=0, tiled=True),
        lax.all_gather(lowered[7], ("page", "seq"), axis=0, tiled=True),
        lax.all_gather(lowered[8], ("page", "seq"), axis=0, tiled=True),
        lax.all_gather(lowered[9], ("page", "seq"), axis=0, tiled=True),
        lax.all_gather(lowered[10], ("page", "seq"), axis=0, tiled=True),
        lax.all_gather(lowered[11], ("page", "seq"), axis=0, tiled=True),
        lax.all_gather(lowered[12], ("page", "seq"), axis=0, tiled=True),
        lax.all_gather(lowered[13], ("page", "seq"), axis=0, tiled=True),
        lax.all_gather(lowered[14], ("page", "seq"), axis=0, tiled=True),
    )
    grad_rows = out_grad.reshape(row_count, width)
    grad_gfinal = jnp.sum(grad_rows * norm_two, axis=0)
    grad_sfinal = jnp.sum(grad_rows, axis=0)
    grad_sum = norm_backward(grad_rows, norm_two, inv_two, g_final.astype(f32))
    grad_f_low = grad_sum.astype(bf16)
    grad_bouter = jnp.sum(grad_f_low.astype(f32), axis=0)
    grad_wouter = product_tn(act_low, grad_f_low)
    grad_active = product_nt(grad_f_low, w_outer)
    grad_in_low = (grad_active * slope).astype(bf16)
    grad_binner = jnp.sum(grad_in_low.astype(f32), axis=0)
    grad_winner = product_tn(hid_low, grad_in_low)
    grad_hidden = grad_sum + product_nt(grad_in_low, w_inner)
    grad_gattn = jnp.sum(grad_hidden * norm_one, axis=0)
    grad_sattn = jnp.sum(grad_hidden, axis=0)
    grad_mixed = norm_backward(grad_hidden, norm_one, inv_one, g_attn.astype(f32))
    grad_att_low = grad_mixed.astype(bf16)
    grad_bout = jnp.sum(grad_att_low.astype(f32), axis=0)
    grad_wout = product_tn(ctx_low, grad_att_low)
    grad_ctx = (
        product_nt(grad_att_low, w_out).astype(bf16).reshape(page_count, span_len, heads, HEAD_DIM)
    )
    probs = jnp.exp(masked_scores() - log_total)
    probs_low = probs.astype(bf16)
    grad_probs = jnp.einsum("pqhe,pkhe->phqk", grad_ctx, v_heads, preferred_element_type=f32)
    grad_vfull = jnp.einsum("phqk,pqhe->pkhe", probs_low, grad_ctx, preferred_element_type=f32)
    grad_scores = (
        probs * (grad_probs - jnp.sum(grad_probs * probs, axis=-1, keepdims=True))
    ).astype(bf16)
    grad_q_low = (
        (jnp.einsum("phqk,pkhe->pqhe", grad_scores, k_heads, preferred_element_type=f32) * scale)
        .astype(bf16)
        .reshape(row_count, width)
    )
    grad_kfull = (
        jnp.einsum("phqk,pqhe->pkhe", grad_scores, q_heads, preferred_element_type=f32) * scale
    )
    grad_keys, grad_values = (
        lax.psum_scatter(
            grad_kfull.reshape(page_count, seq_len, width).astype(jnp.bfloat16),
            "seq",
            scatter_dimension=1,
            tiled=True,
        ).astype(jnp.float32),
        lax.psum_scatter(
            grad_vfull.reshape(page_count, seq_len, width).astype(jnp.bfloat16),
            "seq",
            scatter_dimension=1,
            tiled=True,
        ).astype(jnp.float32),
    )
    grad_k_low = grad_keys.reshape(row_count, width).astype(bf16)
    grad_v_low = grad_values.reshape(row_count, width).astype(bf16)
    grad_tokens = (
        grad_mixed
        + product_nt(grad_q_low, w_query)
        + product_nt(grad_k_low, w_key)
        + product_nt(grad_v_low, w_value)
    )
    grad_wquery = product_tn(tok_low, grad_q_low)
    grad_bquery = jnp.sum(grad_q_low.astype(f32), axis=0)
    grad_wkey = product_tn(tok_low, grad_k_low)
    grad_wvalue = product_tn(tok_low, grad_v_low)
    grad_bvalue = jnp.sum(grad_v_low.astype(f32), axis=0)
    owned = (
        lax.psum_scatter(grad_wquery, ("page", "seq"), scatter_dimension=0, tiled=True),
        lax.psum_scatter(grad_bquery, ("page", "seq"), scatter_dimension=0, tiled=True),
        lax.psum_scatter(grad_wkey, ("page", "seq"), scatter_dimension=0, tiled=True),
        lax.psum_scatter(grad_wvalue, ("page", "seq"), scatter_dimension=0, tiled=True),
        lax.psum_scatter(grad_bvalue, ("page", "seq"), scatter_dimension=0, tiled=True),
        lax.psum_scatter(grad_wout, ("page", "seq"), scatter_dimension=0, tiled=True),
        lax.psum_scatter(grad_bout, ("page", "seq"), scatter_dimension=0, tiled=True),
        lax.psum_scatter(grad_gattn, ("page", "seq"), scatter_dimension=0, tiled=True),
        lax.psum_scatter(grad_sattn, ("page", "seq"), scatter_dimension=0, tiled=True),
        lax.psum_scatter(grad_winner, ("page", "seq"), scatter_dimension=0, tiled=True),
        lax.psum_scatter(grad_binner, ("page", "seq"), scatter_dimension=0, tiled=True),
        lax.psum_scatter(grad_wouter, ("page", "seq"), scatter_dimension=0, tiled=True),
        lax.psum_scatter(grad_bouter, ("page", "seq"), scatter_dimension=0, tiled=True),
        lax.psum_scatter(grad_gfinal, ("page", "seq"), scatter_dimension=0, tiled=True),
        lax.psum_scatter(grad_sfinal, ("page", "seq"), scatter_dimension=0, tiled=True),
    )
    return (
        result.reshape(tokens.shape),
        grad_tokens.reshape(tokens.shape),
        owned[0],
        owned[1],
        owned[2],
        owned[3],
        owned[4],
        owned[5],
        owned[6],
        owned[7],
        owned[8],
        owned[9],
        owned[10],
        owned[11],
        owned[12],
        owned[13],
        owned[14],
    )


MESH = pl.DeviceIdType.MESH
BF16 = jnp.bfloat16
F32 = jnp.float32
VECTORS = 8
SLAB = 16
NEGATIVE = -1000000000.0


def dot_nn(left, right):
    return lax.dot_general(left, right, (((1,), (0,)), ((), ())), preferred_element_type=F32)


def dot_nt(left, right):
    return lax.dot_general(left, right, (((1,), (1,)), ((), ())), preferred_element_type=F32)


def dot_tn(left, right):
    return lax.dot_general(left, right, (((0,), (0,)), ((), ())), preferred_element_type=F32)


class Sizes:
    def __init__(self, mesh, width, units, span):
        self.pages = mesh.shape["page"]
        self.parts = mesh.shape["seq"]
        self.half = self.pages // 2
        self.width = width
        self.units = units
        self.span = span
        self.length = span * self.parts
        self.row = width // (self.pages * self.parts)
        self.rows = self.row * self.parts
        self.unit = units // (self.pages * self.parts)
        self.mine = self.unit * self.pages
        self.cols = width // self.parts
        self.heads = self.cols // HEAD_DIM
        self.pairs = self.cols // 128


def supported(mesh, token_shape, width, units):
    pages, parts = mesh.shape["page"], mesh.shape["seq"]
    return (
        parts == 4
        and pages % 2 == 0
        and pages >= 4
        and token_shape[0] == pages
        and token_shape[1] % (parts * 128) == 0
        and width % (pages * parts * 32) == 0
        and width // pages == 128
        and units % (pages * parts * 128) == 0
        and (width // parts) % 128 == 0
    )


def layer_kernel(z, names, *refs):
    r = types.SimpleNamespace(**dict(zip(names, refs)))
    send_sem, recv_sem, load_sem = r.send_sem, r.recv_sem, r.load_sem
    page = lax.axis_index("page")
    part = lax.axis_index("seq")
    counter = [0]

    def slots(count):
        first = counter[0]
        counter[0] += count
        return first

    odd = page % 2
    place = odd * (z.pages - 1 - page // 2) + (1 - odd) * (page // 2)

    def page_at(index):
        index = (index + z.pages) % z.pages
        late = index // z.half
        return (1 - late) * (2 * index) + late * (2 * z.pages - 1 - 2 * index)

    ring = [page] + [page_at(place + step) for step in range(1, z.pages)]
    peers = [part] + [
        ((part // 2 + j // 2) % 2) * 2 + (part % 2 + j % 2) % 2 for j in range(1, 4)
    ]

    def around(step):
        return ring[step % z.pages]

    def peer(j):
        return peers[j]

    rank = page * z.parts + part

    class Copy:
        def __init__(self, src, dst, index, device, group=None):
            self.args = src, dst, index, device
            self.group = group

        def made(self, group):
            src, dst, index, device = self.args
            return pltpu.make_async_remote_copy(
                src_ref=src,
                dst_ref=dst,
                send_sem=send_sem.at[group],
                recv_sem=recv_sem.at[index],
                device_id=device,
                device_id_type=MESH,
            )

        def start(self):
            group = self.group
            if group is None:
                size = self.size()
                if groups[-1] + size > z.group_bytes:
                    groups.append(0)
                groups[-1] += size
                group = len(groups) - 1
            self.made(group).start()

        def wait_recv(self):
            self.made(0).wait_recv()

        def size(self):
            src = self.args[0]
            return math.prod(src.shape) * jnp.dtype(src.dtype).itemsize

        def wait_bytes(self, size):
            rows = r.measure.at[pl.ds(0, size // 512)]
            Copy(rows, rows, *self.args[2:]).wait_recv()

        def wait_send(self):
            self.made(self.group).wait_send()

    groups = [0]
    copy = Copy

    def block(ref, index, size):
        return ref.at[pl.ds(pl.multiple_of(index * size, size), size)]

    barrier = pltpu.get_barrier_semaphore()

    def greet(device):
        pl.semaphore_signal(barrier, inc=1, device_id=device, device_id_type=MESH)

    for j in (1, 2, 3):
        greet((page, peer(j)))
    greet((around(1), part))
    greet((around(-1), part))

    class Share:
        def __init__(self, ref, size, pieces=2):
            self.ref, self.size, self.pieces = ref, size, pieces
            self.first = slots(2 + pieces)

        def copy(self, j, owner, k):
            height = self.size // self.pieces
            piece = block(self.ref, owner, self.size).at[pl.ds(k * height, height)]
            index = self.first + (2 + k if j == 2 else j // 2)
            return copy(piece, piece, index, (page, peer(1 if j == 3 else j)))

        def start(self, k):
            self.copy(2, part, k).start()
            self.copy(1, part, k).start()

        def forward(self):
            for k in range(self.pieces):
                self.copy(2, peer(2), k).wait_recv()
                self.copy(3, peer(2), k).start()


        def wait(self, j):
            arrival = self.copy(j, peer(j), 0)
            arrival.wait_bytes(self.pieces * arrival.size())

    class Combine:
        def __init__(self, refs, size, make, pieces=2):
            self.out, self.got, self.own = refs
            self.size, self.make, self.pieces = size, make, pieces
            self.height = size // pieces
            self.first = slots(2 * pieces)

        def rows(self, j, k):
            at = pl.multiple_of(peer(j) * self.size + k * self.height, self.height)
            return pl.ds(at, self.height)

        def copy(self, j, k):
            return copy(
                self.out.at[self.rows(j, k)],
                self.got.at[j, pl.ds(k * self.height, self.height)],
                self.first + 2 * k + j // 3,
                (page, peer(2 if j == 2 else 1)),
            )

        def term(self, j):
            value = self.make(pl.ds(pl.multiple_of(peer(j) * self.size, self.size), self.size), j)
            if j == 0:
                self.own[...] = value
                return
            for k in range(self.pieces):
                rows = slice(k * self.height, (k + 1) * self.height)
                mine = value[rows]
                if j == 2:
                    self.copy(3, k).wait_recv()
                    mine = mine + self.got[3, rows, :].astype(F32)
                self.out[self.rows(j, k), :] = mine.astype(BF16)
                self.copy(j, k).start()

        def finish(self, fn, after=None, step=32):
            for k in range(self.pieces):
                arrival = self.copy(1, k)
                arrival.wait_bytes(2 * arrival.size())

                def body(i, carry):
                    at = pl.multiple_of(k * self.height + i * step, step)
                    rows = pl.ds(at, step)
                    total = self.own[rows, :]
                    for j in (1, 2):
                        total = total + self.got[j, rows, :].astype(F32)
                    fn(rows, at, total)
                    return carry

                lax.fori_loop(0, self.height // step, body, 0)
                if after is not None:
                    after(k)

    def token_refs(phase):
        return r.part_out.at[phase], r.part_in.at[phase], r.part_own

    class Spread:
        def __init__(self, src, dst, size):
            self.src, self.dst, self.size, self.first = src, dst, size, slots(1)

        def copy(self, j):
            return copy(
                block(self.src, peer(j), self.size),
                self.dst.at[j],
                self.first,
                (page, peer(j)),
            )

        def start(self):
            for j in (2, 3, 1):
                self.copy(j).start()

        def wait(self):
            arrival = self.copy(1)
            arrival.wait_bytes(3 * arrival.size())

    class Place:
        def __init__(self, src, dst, size, base):
            self.src, self.dst, self.size, self.base, self.first = src, dst, size, base, slots(1)

        def copy(self, j, owner):
            return copy(
                block(self.src, peer(j), self.size),
                block(self.dst, self.base + owner, self.size),
                self.first,
                (page, peer(j)),
            )

        def start(self):
            for j in (2, 3, 1):
                self.copy(j, part).start()

        def wait(self):
            arrival = self.copy(1, peer(1))
            arrival.wait_bytes(3 * arrival.size())

    class Gather:
        def __init__(self, ref, size, pieces=1):
            self.ref, self.size, self.pieces = ref, size, pieces
            self.first = slots(z.half * pieces)

        def copy(self, t, d, k, step):
            height = self.size // self.pieces
            start = k * height
            if t == z.half - 1:
                height = height // 2
                start = start + d * height
            piece = block(self.ref, around(step), self.size).at[pl.ds(start, height)]
            return copy(
                piece,
                piece,
                self.first + t * self.pieces + k,
                (around(1 - 2 * d), part),
            )

        def wait(self, t, k):
            both = 2 * self.copy(t, 0, k, 0).size()
            self.copy(t, 0, k, 0).wait_bytes(both)

        def step(self, t, pieces=None):
            for k in pieces or range(self.pieces):
                if t > 0:
                    self.wait(t - 1, k)
                for d in (0, 1):
                    self.copy(t, d, k, -(1 - 2 * d) * t).start()


        def done(self):
            for k in range(self.pieces):
                self.wait(z.half - 1, k)

    class Reduce:
        def __init__(self, slot, stage, local, shape, kind, pieces=1):
            self.slot, self.stage, self.local = slot, stage, local
            self.size, self.kind, self.pieces = shape[0], kind, pieces
            self.wide = shape[1] // pieces
            self.first = slots(z.half * pieces)

        def copy(self, t, d, k):
            h = self.size // 2
            if t == 0:
                src = self.stage.at[k, pl.ds(d * h, h)]
                dst = self.slot.at[k, d, 0, pl.ds(d * h, h)]
            else:
                src = self.slot.at[k, d, t - 1]
                dst = self.slot.at[k, d, t]
            return copy(
                src,
                dst,
                self.first + t * self.pieces + k,
                (around(1 - 2 * d), part),
            )


        def step(self, t):
            h = self.size // 2
            wide = self.wide
            if t == 0:
                term = self.local(around(z.half)).astype(self.kind)
                for k in range(self.pieces):
                    self.stage[k] = term[:, k * wide : (k + 1) * wide]
            else:
                terms = [
                    self.local(around((1 - 2 * d) * (z.half - t))) for d in (0, 1)
                ]
            for k in range(self.pieces):
                if t > 0:
                    self.wait(t - 1, k)
                for d in (0, 1):
                    if t > 0:
                        term = terms[d][:, k * wide : (k + 1) * wide]
                        held = self.slot.at[k, d, t - 1]
                        if t == 1:
                            near, far = pl.ds(d * h, h), pl.ds((1 - d) * h, h)
                            term_near = term[d * h : (d + 1) * h]
                            term_far = term[(1 - d) * h : (2 - d) * h]
                            held[near] = (held[near].astype(F32) + term_near).astype(self.kind)
                            held[far] = term_far.astype(self.kind)
                        else:
                            held[...] = (held[...].astype(F32) + term).astype(self.kind)
                    self.copy(t, d, k).start()

        def wait(self, t, k):
            arrival = self.copy(t, 0, k)
            arrival.wait_bytes(2 * arrival.size())

        def total(self, out):
            term = self.local(page)
            last = z.half - 1
            for k in range(self.pieces):
                self.wait(last, k)
                at = slice(k * self.wide, (k + 1) * self.wide)
                out[:, at] = (
                    term[:, at] + self.slot[k, 0, last].astype(F32) + self.slot[k, 1, last].astype(F32)
                ).astype(out.dtype)

    c, w, n = z.cols, z.width, z.span

    def fetch(i, name):
        return pltpu.make_async_copy(getattr(r, name), getattr(r, z.held + name), load_sem.at[i])

    for i, name in enumerate(z.fetched):
        fetch(i, name).start()
    hbm = r
    r = types.SimpleNamespace(**vars(hbm))
    for name in z.fetched:
        setattr(r, name, getattr(hbm, z.held + name))
    fetches = iter(range(len(z.fetched)))

    def arrive(count):
        for _ in range(count):
            i = next(fetches)
            pltpu.make_async_copy(
                getattr(hbm, z.fetched[i]), getattr(r, z.fetched[i]), load_sem.at[i]
            ).wait()

    arrive(3)
    for q in range(z.parts):
        rows = pl.ds(q * z.row, z.row)
        for i, weight in enumerate((r.w_query, r.w_key, r.w_value)):
            for k in range(z.pairs):
                r.cut_qkv[rows, (3 * k + i) * 128 : (3 * k + i + 1) * 128] = weight[
                    :, q * c + k * 128 : q * c + (k + 1) * 128
                ].astype(BF16)
    arrive(9)
    mine = pl.multiple_of(part * SLAB, SLAB)
    for i, small in enumerate(
        (r.b_query, r.b_value, r.b_out, r.g_attn, r.s_attn, r.b_outer, r.g_final, r.s_final)
    ):
        r.vec_raw[pl.ds(mine + i, 1), 0 : z.row] = small[...]
    at_page = pl.multiple_of(page * SLAB, SLAB)
    r.vec_all[pl.ds(at_page + VECTORS, 1), :] = r.b_inner[...]
    arrive(1)
    r.outer_w[pl.ds(pl.multiple_of(page * z.unit, z.unit), z.unit), :] = r.w_outer[...].astype(
        BF16
    )

    ring_qkv = Gather(r.qkv_w, z.rows, 2)
    ring_vec = Gather(r.vec_all, SLAB)
    ring_inner = Gather(r.inner_w, z.rows, 2)
    ring_out = Gather(r.out_w, z.rows)
    ring_outer = Gather(r.outer_w, z.unit, 2)
    cut_qkv = Place(r.cut_qkv, r.qkv_w, z.row, page * z.parts)
    cut_out = Place(r.cut_out, r.out_w, z.row, page * z.parts)
    cut_inner = Place(r.cut_inner, r.inner_w, z.row, page * z.parts)
    share_tok = Share(r.tok_all, n)

    class ShareVec:
        first = slots(1)

        def copy(self, j, owner):
            piece = block(r.vec_raw, owner, SLAB).at[pl.ds(0, VECTORS)]
            return copy(piece, piece, self.first, (page, peer(j)))

    vec_share = ShareVec()
    pl.semaphore_wait(barrier, 5)
    cut_qkv.start()
    for j in (2, 3, 1):
        vec_share.copy(j, part).start()
    ring_outer.step(0)
    arrive(2)
    r.tok_all[pl.ds(pl.multiple_of(part * n, n), n), :] = r.tokens[...].astype(BF16)
    share_tok.start(0)
    share_tok.start(1)
    for q in range(z.parts):
        r.cut_out[pl.ds(q * z.row, z.row), :] = r.w_out[:, q * c : (q + 1) * c].astype(BF16)
    cut_out.start()
    arrive(1)
    for q in range(z.parts):
        rows = pl.ds(q * z.row, z.row)
        for g in range(z.pages):
            at = (z.parts * g + q) * z.unit
            r.cut_inner[rows, g * z.unit : (g + 1) * z.unit] = r.w_inner[
                :, at : at + z.unit
            ].astype(BF16)
    cut_inner.start()
    own_rows = pl.ds(pl.multiple_of(rank * z.row, z.row), z.row)
    cut_rows = pl.ds(pl.multiple_of(part * z.row, z.row), z.row)
    r.qkv_w[own_rows, :] = r.cut_qkv[cut_rows, :]
    r.out_w[own_rows, :] = r.cut_out[cut_rows, :]
    r.inner_w[own_rows, :] = r.cut_inner[cut_rows, :]

    cut_qkv.wait()
    ring_qkv.step(0)
    arrival = vec_share.copy(1, peer(1))
    arrival.wait_bytes(3 * arrival.size())
    lane = lax.broadcasted_iota(jnp.int32, (VECTORS, 128), 1)
    total = jnp.zeros((VECTORS, 128), F32)
    for q in range(z.parts):
        tile = r.vec_raw[q * SLAB : q * SLAB + VECTORS, :]
        if q:
            tile = pltpu.roll(tile, q * z.row, 1)
        total = total + jnp.where(lane // z.row == q, tile, 0.0)
    r.vec_all[pl.ds(at_page, VECTORS), :] = total
    ring_vec.step(0)
    ring_qkv.step(1)
    ring_vec.step(1)
    cut_out.wait()
    ring_out.step(0)
    ring_qkv.step(2)
    ring_vec.step(2)
    ring_out.step(1)
    share_tok.forward()
    ring_qkv.step(3)
    ring_vec.step(3)
    ring_out.step(2)
    cut_inner.wait()
    ring_inner.step(0)
    ring_vec.done()

    for g in range(z.pages):
        tile = r.vec_all[g * SLAB : (g + 1) * SLAB, :].astype(BF16).astype(F32)
        r.vecs[:, g * 128 : (g + 1) * 128] = tile[0:VECTORS]
        r.b_mine[:, g * z.unit : (g + 1) * z.unit] = tile[VECTORS : VECTORS + 1]

    def vector(i):
        return r.vecs[i : i + 1, :]


    share_tok.wait(1)
    share_tok.wait(3)
    ring_qkv.done()

    def make_qkv(b, carry):
        rows = pl.ds(pl.multiple_of(b * n, n), n)
        out = dot_nn(r.tok_all[rows, :], r.qkv_w[...])
        for k in range(z.pairs):
            mine = pl.ds(pl.multiple_of(part * c + k * 128, 128), 128)
            for i, bias in enumerate((0, None, 1)):
                cols = slice((3 * k + i) * 128, (3 * k + i + 1) * 128)
                value = out[:, cols]
                if bias is not None:
                    value = value + r.vecs[bias : bias + 1, mine]
                r.qkv[rows, cols] = value.astype(BF16)
        return carry

    lax.fori_loop(0, z.parts, make_qkv, 0)
    ring_inner.step(1)
    ring_out.step(3)
    ring_outer.step(1)

    scale = HEAD_DIM ** (-0.5)
    first_head = lax.broadcasted_iota(jnp.int32, (n, 128), 1) < HEAD_DIM
    key_place = lax.broadcasted_iota(jnp.int32, (n, z.length), 1)
    pltpu.make_async_copy(hbm.valid, r.valid, load_sem.at[len(z.fetched) - 1]).wait()
    valid = r.valid[0]

    def pair_cols(kind, pair):
        return pl.ds((3 * pair + kind) * 128, 128)

    def attend(pair):
        def body(b, carry):
            rows = pl.ds(pl.multiple_of(b * n, n), n)
            queries = r.qkv[rows, pair_cols(0, pair)]
            keys = r.qkv[:, pair_cols(1, pair)]
            values = r.qkv[:, pair_cols(2, pair)]
            outs = []
            for h in range(2):
                mine = first_head if h == 0 else ~first_head
                scores = dot_nt(jnp.where(mine, queries, jnp.zeros_like(queries)), keys) * scale
                scores = jnp.where(key_place < valid, scores, NEGATIVE)
                top = jnp.max(scores, axis=-1, keepdims=True)
                weight = jnp.exp(scores - top)
                probs = weight * (1.0 / jnp.sum(weight, axis=-1, keepdims=True))
                r.probs[2 * pair + h, rows, :] = probs
                outs.append(dot_nn(probs.astype(BF16), values))
            place_rows = pl.ds(
                pl.multiple_of((part * z.pairs + pair) * z.length + b * n, n), n
            )
            r.ctx_all[place_rows, :] = jnp.where(first_head, outs[0], outs[1]).astype(
                BF16
            )
            return carry

        lax.fori_loop(0, z.parts, body, 0)

    share_ctx = Share(r.ctx_all, z.pairs * z.length, z.pairs)
    for pair in range(z.pairs):
        attend(pair)
        share_ctx.start(pair)
    ring_inner.step(2)
    ring_outer.step(2, (0,))

    def project(j):
        term = None
        for k in range(z.pairs):
            rows = pl.ds(pl.multiple_of((peer(j) * z.pairs + k) * z.length, z.length), z.length)
            features = pl.ds(pl.multiple_of(peer(j) * c + k * 128, 128), 128)
            more = dot_nn(r.ctx_all[rows, :], r.out_w[features, :])
            term = more if term is None else term + more
        r.att_sum[...] = term if j == 0 else r.att_sum[...] + term

    ring_out.done()
    project(0)
    share_ctx.wait(1)
    project(1)
    share_ctx.forward()
    project(2)
    share_ctx.wait(3)
    project(3)
    r.att_cut[...] = r.att_sum[...].astype(BF16)
    move_att = Place(r.att_cut, r.att_got, n, 0)
    move_att.start()
    own_block = pl.ds(pl.multiple_of(part * n, n), n)
    r.att_got[own_block, :] = r.att_cut[own_block, :]

    def add_column_sum(i, values):
        r.sums[i : i + 1, :] += jnp.sum(values, axis=0, keepdims=True)

    r.sums[...] = jnp.zeros_like(r.sums)

    share_hid = Share(r.hid_all, n)

    def first_norm(rows, at, total):
        mixed = r.tokens[rows, :] + (total + vector(2))
        normed, inverse = norm_parts(mixed)
        hidden = normed * vector(3) + vector(4)
        r.norm_one[rows, :] = normed
        r.inv_one[rows, :] = inverse
        r.hidden[rows, :] = hidden
        r.hid_all[pl.ds(pl.multiple_of(part * n + at, 32), 32), :] = hidden.astype(BF16)

    ring_inner.step(3)
    ring_outer.step(2, (1,))
    move_att.wait()
    for k in range(2):

        def norm_rows(i, carry):
            at = pl.multiple_of(k * (n // 2) + i * 32, 32)
            total = jnp.concatenate(
                [
                    r.att_got[pl.ds(pl.multiple_of(q * n + at, 32), 32), :].astype(F32)
                    for q in range(z.parts)
                ],
                axis=1,
            )
            first_norm(pl.ds(at, 32), at, total)
            return carry

        lax.fori_loop(0, n // 64, norm_rows, 0)
        share_hid.start(k)
    ring_inner.done()

    tile = 256

    def make_inner(j):
        rows = pl.ds(pl.multiple_of(peer(j) * n, n), n)

        def columns(i, carry):
            cols = pl.ds(pl.multiple_of(i * tile, tile), tile)
            inner = dot_nn(r.hid_all[rows, :], r.inner_w[:, cols]) + r.b_mine[:, cols]
            active, slope = gelu_parts(inner)
            r.active[rows, cols] = active.astype(BF16)
            r.slope[rows, cols] = slope
            return carry

        lax.fori_loop(0, z.mine // tile, columns, 0)

    make_inner(0)
    share_hid.wait(1)
    make_inner(1)
    ring_outer.step(3)
    share_hid.forward()
    make_inner(2)
    share_hid.wait(3)
    make_inner(3)
    ring_outer.done()
    combine_two = Combine(token_refs(0), n, lambda rows, j: dot_nn(r.active[rows, :], r.outer_w[...]))
    for j in (3, 2, 1, 0):
        combine_two.term(j)
    share_gf = Share(r.gf_all, n)

    arrive(1)

    def second_norm(rows, at, total):
        outer = total + vector(5)
        normed, inverse = norm_parts(r.hidden[rows, :] + outer)
        r.v_out[rows, :] = normed * vector(6) + vector(7)
        grad = r.out_grad[rows, :]
        add_column_sum(6, grad * normed)
        add_column_sum(7, grad)
        grad_sum = norm_backward(grad, normed, inverse, vector(6))
        low = grad_sum.astype(BF16)
        add_column_sum(5, low.astype(F32))
        r.grad_sum[rows, :] = grad_sum
        r.gf_all[pl.ds(pl.multiple_of(part * n + at, 32), 32), :] = low

    combine_two.finish(second_norm, share_gf.start)

    def leave_early(i, src, dst):
        return pltpu.make_async_copy(src, dst, load_sem.at[len(z.fetched) + i])

    leave_early(0, r.v_out, r.o_out).start()

    def chunk_term(left, right, size):
        def local(g):
            cols = pl.ds(pl.multiple_of(g * size, size), size)
            return dot_tn(left[:, cols], right[...])

        return local

    reduce_outer_a = Reduce(
        r.slot_outer_a, r.stage_outer_a,
        chunk_term(r.active, r.gf_all.at[:, 0 : w // 2], z.unit), (z.unit, w // 2), BF16,
    )
    reduce_outer_b = Reduce(
        r.slot_outer_b, r.stage_outer_b,
        chunk_term(r.active, r.gf_all.at[:, w // 2 :], z.unit), (z.unit, w // 2), BF16,
    )
    reduce_inner = Reduce(
        r.slot_inner, r.stage_inner, chunk_term(r.hid_all, r.grad_inner, z.rows),
        (z.rows, z.mine), BF16, 2
    )
    def pair_term(k):
        def local(g):
            cols = pl.ds(pl.multiple_of(g * z.rows, z.rows), z.rows)
            return dot_tn(r.tok_all[:, cols], r.grad_qkv[:, 384 * k : 384 * (k + 1)])

        return local

    def out_term(g):
        rows = pl.ds(pl.multiple_of(g * z.length, z.length), z.length)
        return dot_tn(r.ctx_all[rows, :], r.ga_cols[...])

    reduce_pair = [
        Reduce(r.slot_pair.at[k], r.stage_pair.at[k], pair_term(k), (z.rows, 384), BF16)
        for k in range(z.pairs)
    ]
    reduce_out = Reduce(r.slot_out, r.stage_out, out_term, (z.rows, c), BF16)
    reduce_vec = Reduce(
        r.slot_vec, r.stage_vec,
        lambda g: r.term_vec[pl.ds(pl.multiple_of(g * SLAB, SLAB), SLAB), :], (SLAB, 128), F32,
    )

    r.b_sum[...] = jnp.zeros_like(r.b_sum)

    def make_grad_inner(j):
        rows = pl.ds(pl.multiple_of(peer(j) * n, n), n)

        def columns(i, carry):
            cols = pl.ds(pl.multiple_of(i * tile, tile), tile)
            grad = dot_nt(r.gf_all[rows, :], r.outer_w[cols, :]) * r.slope[rows, cols]
            low = grad.astype(BF16)
            r.grad_inner[rows, cols] = low
            r.b_sum[:, cols] += jnp.sum(low.astype(F32), axis=0, keepdims=True)
            return carry

        lax.fori_loop(0, z.mine // tile, columns, 0)

    make_grad_inner(0)
    share_gf.wait(1)
    make_grad_inner(1)
    share_gf.forward()
    make_grad_inner(2)
    share_gf.wait(3)
    reduce_outer_a.step(0)
    reduce_outer_b.step(0)
    make_grad_inner(3)
    combine_three = Combine(token_refs(1), n, lambda rows, j: dot_nt(r.grad_inner[rows, :], r.inner_w[...]))
    combine_three.term(3)
    combine_three.term(2)
    reduce_inner.step(0)
    reduce_outer_a.step(1)
    combine_three.term(1)
    combine_three.term(0)
    reduce_inner.step(1)
    reduce_outer_b.step(1)

    move_ga = Place(r.ga_cut, r.ga_cols, n, 0)

    def first_norm_back(rows, at, total):
        grad = r.grad_sum[rows, :] + total
        normed = r.norm_one[rows, :]
        add_column_sum(3, grad * normed)
        add_column_sum(4, grad)
        mixed = norm_backward(grad, normed, r.inv_one[rows, :], vector(3))
        low = mixed.astype(BF16)
        add_column_sum(2, low.astype(F32))
        r.grad_mixed[rows, :] = mixed
        for q in range(z.parts):
            r.ga_cut[pl.ds(pl.multiple_of(q * n + at, 32), 32), :] = low[:, q * c : (q + 1) * c]

    combine_three.finish(first_norm_back)
    move_ga.start()
    r.ga_cols[own_block, :] = r.ga_cut[own_block, :]
    reduce_outer_a.step(2)

    def grad_ctx_term(rows, j):
        return jnp.concatenate(
            [
                dot_nt(
                    r.ga_cols[...],
                    r.out_w[pl.ds(pl.multiple_of(peer(j) * c + k * 128, 128), 128), :],
                )
                for k in range(z.pairs)
            ],
            axis=0,
        )

    combine_ctx = Combine(
        (r.ctx_out, r.ctx_in, r.ctx_own), z.pairs * z.length, grad_ctx_term, z.pairs
    )
    move_ga.wait()
    combine_ctx.term(3)
    combine_ctx.term(2)
    combine_ctx.term(1)
    combine_ctx.term(0)
    reduce_out.step(0)
    reduce_inner.step(2)

    def keep_grad_ctx(rows, at, total):
        r.grad_ctx[rows, :] = total.astype(BF16)

    def attend_back(pair):
        r.grad_kv[...] = jnp.zeros_like(r.grad_kv)

        def body(b, carry):
            rows = pl.ds(pl.multiple_of(b * n, n), n)
            queries = r.qkv[rows, pair_cols(0, pair)]
            keys = r.qkv[:, pair_cols(1, pair)]
            values = r.qkv[:, pair_cols(2, pair)]
            grad = r.grad_ctx[pl.ds(pl.multiple_of(pair * z.length + b * n, n), n), :]
            outs = []
            for h in range(2):
                mine = first_head if h == 0 else ~first_head
                grad_mine = jnp.where(mine, grad, jnp.zeros_like(grad))
                query_mine = jnp.where(mine, queries, jnp.zeros_like(queries))
                probs = r.probs[2 * pair + h, rows, :]
                grad_probs = dot_nt(grad_mine, values)
                r.grad_kv[1] += dot_tn(probs.astype(BF16), grad_mine)
                inside = jnp.sum(grad_probs * probs, axis=-1, keepdims=True)
                grad_scores = (probs * (grad_probs - inside)).astype(BF16)
                outs.append(dot_nn(grad_scores, keys))
                r.grad_kv[0] += dot_tn(grad_scores, query_mine)
            r.grad_qkv[rows, pair_cols(0, pair)] = (
                jnp.where(first_head, outs[0], outs[1]) * scale
            ).astype(BF16)
            return carry

        lax.fori_loop(0, z.parts, body, 0)
        r.grad_qkv[:, pair_cols(1, pair)] = (r.grad_kv[0] * scale).astype(BF16)
        r.grad_qkv[:, pair_cols(2, pair)] = r.grad_kv[1].astype(BF16)

    def after_pair(pair):
        attend_back(pair)
        reduce_pair[pair].step(0)
        if pair == 0:
            reduce_outer_a.step(3)
            reduce_outer_b.step(2)
            reduce_out.step(1)

    combine_ctx.finish(keep_grad_ctx, after_pair, step=128)
    reduce_inner.step(3)

    for k in range(z.pairs):
        mine = pl.ds(pl.multiple_of(part * c + k * 128, 128), 128)
        for row, kind in ((0, 0), (1, 2)):
            r.sums[row : row + 1, mine] = jnp.sum(
                r.grad_qkv[:, pair_cols(kind, k)].astype(F32), axis=0, keepdims=True
            )
    r.term_vec[...] = jnp.zeros_like(r.term_vec)
    for g in range(z.pages):
        r.term_vec[g * SLAB : g * SLAB + VECTORS, :] = r.sums[:, g * 128 : (g + 1) * 128]
        r.term_vec[g * SLAB + VECTORS : g * SLAB + VECTORS + 1, :] = r.b_sum[
            :, g * z.unit : (g + 1) * z.unit
        ]
    reduce_vec.step(0)

    combine_four = Combine(token_refs(2), n, lambda rows, j: dot_nt(r.grad_qkv[rows, :], r.qkv_w[...]))
    combine_four.term(3)
    combine_four.term(2)
    for pair in range(z.pairs):
        reduce_pair[pair].step(1)
    reduce_vec.step(1)
    reduce_out.step(2)
    combine_four.term(1)
    combine_four.term(0)

    reduce_inner.total(r.fin_inner)
    fin_inner = Spread(r.fin_inner, r.got_inner, z.row)
    fin_inner.start()
    for pair in range(z.pairs):
        reduce_pair[pair].step(2)
    reduce_vec.step(2)
    reduce_out.step(3)

    def input_rows(rows, at, total):
        r.v_grad[rows, :] = r.grad_mixed[rows, :] + total

    reduce_outer_a.total(r.o_outer.at[:, 0 : w // 2])
    for pair in range(z.pairs):
        reduce_pair[pair].step(3)
    reduce_vec.step(3)
    reduce_outer_b.step(3)
    combine_four.finish(input_rows)
    leave_early(1, r.v_grad, r.o_grad).start()
    reduce_out.total(r.fin_out)
    fin_out = Spread(r.fin_out, r.got_out, z.row)
    fin_out.start()
    fin_pair = []
    for k in range(z.pairs):
        reduce_pair[k].total(r.fin_pair.at[k])
        fin_pair.append(Spread(r.fin_pair.at[k], r.got_pair.at[k], z.row))
        fin_pair[k].start()
    reduce_vec.total(r.fin_vec)

    class VecAll:
        first = slots(1)

        def copy(self, j):
            return copy(r.fin_vec, r.got_vec.at[j], self.first, (page, peer(j)))

    fin_vec = VecAll()
    for j in (2, 3, 1):
        fin_vec.copy(j).start()

    my_rows = pl.ds(pl.multiple_of(part * z.row, z.row), z.row)

    def deliver(spread, mine, got, out):
        spread.wait()
        for j in range(4):
            value = got[j] if j else mine[my_rows, :]
            out[peer(j)] = value

    deliver(fin_inner, r.fin_inner, r.got_inner, r.o_inner)
    deliver(fin_out, r.fin_out, r.got_out, r.o_wout)
    arrival = fin_vec.copy(1)
    arrival.wait_bytes(3 * arrival.size())
    summed = r.fin_vec[0:VECTORS, :]
    for j in (1, 2, 3):
        summed = summed + r.got_vec[j, 0:VECTORS, :]
    r.o_vec[0:VECTORS, :] = pltpu.roll(summed, (128 - part * z.row) % 128, 1)
    r.o_vec[VECTORS:, :] = r.fin_vec[VECTORS:, :]
    reduce_outer_b.total(r.o_outer.at[:, w // 2 :])
    for k in range(z.pairs):
        deliver(fin_pair[k], r.fin_pair.at[k], r.got_pair.at[k], r.o_pair.at[k])

    leave_early(0, r.v_out, r.o_out).wait()
    leave_early(1, r.v_grad, r.o_grad).wait()
    for group, size in enumerate(groups):
        rows = r.measure.at[pl.ds(0, size // 512)]
        copy(rows, rows, 0, (page, part), group).wait_send()

    assert counter[0] == z.sems and len(groups) == z.groups, (counter, groups)


def finish_kernel(z, out, grad, outer, inner, pair, wout, vec, *outs):
    (o_out, o_grad, o_wq, o_bq, o_wk, o_wv, o_bv, o_wo, o_bo, o_ga, o_sa, o_wi, o_bi, o_wu, o_bu, o_gf, o_sf) = outs
    o_out[...] = out[...]
    o_grad[...] = grad[...]
    o_wu[...] = outer[...]
    c = z.cols
    for q in range(z.parts):
        o_wo[:, q * c : (q + 1) * c] = wout[q].astype(F32)
        for i, ref in enumerate((o_wq, o_wk, o_wv)):
            for k in range(z.pairs):
                ref[:, q * c + k * 128 : q * c + (k + 1) * 128] = pair[
                    k, q, :, i * 128 : (i + 1) * 128
                ].astype(F32)
        for g in range(z.pages):
            at = (z.parts * g + q) * z.unit
            o_wi[:, at : at + z.unit] = inner[q, :, g * z.unit : (g + 1) * z.unit].astype(F32)
    for i, ref in enumerate((o_bq, o_bv, o_bo, o_ga, o_sa, o_bu, o_gf, o_sf)):
        ref[...] = vec[i : i + 1, 0 : z.row]
    o_bi[...] = vec[VECTORS : VECTORS + 1, :]


def paged_layer(z, tokens, valid_len, params, out_grad):
    (
        w_query, b_query, w_key, w_value, b_value, w_out, b_out, g_attn, s_attn,
        w_inner, b_inner, w_outer, b_outer, g_final, s_final,
    ) = params
    flat = lambda v: v.reshape(1, v.shape[0])
    c, w, n, ln, half = z.cols, z.width, z.span, z.length, z.half
    ins = dict(
        valid=valid_len,
        tokens=tokens.reshape(n, w),
        out_grad=out_grad.reshape(n, w),
        w_query=w_query, w_key=w_key, w_value=w_value, w_out=w_out,
        w_inner=w_inner, w_outer=w_outer,
        b_query=flat(b_query), b_value=flat(b_value), b_out=flat(b_out),
        g_attn=flat(g_attn), s_attn=flat(s_attn), b_inner=flat(b_inner),
        b_outer=flat(b_outer), g_final=flat(g_final), s_final=flat(s_final),
    )
    outs = dict(
        o_out=((n, w), F32),
        o_grad=((n, w), F32),
        o_outer=((z.unit, w), F32),
        o_inner=((z.parts, z.row, z.mine), BF16),
        o_pair=((z.pairs, z.parts, z.row, 384), BF16),
        o_wout=((z.parts, z.row, c), BF16),
        o_vec=((SLAB, 128), F32),
    )
    scratch = dict(
        qkv_w=((w, 3 * c), BF16),
        out_w=((w, c), BF16),
        cut_out=((z.rows, c), BF16),
        inner_w=((w, z.mine), BF16),
        outer_w=((z.mine, w), BF16),
        vec_all=((z.pages * SLAB, 128), F32),
        vec_raw=((z.parts * SLAB, 128), F32),
        cut_qkv=((z.rows, 3 * c), BF16),
        cut_inner=((z.rows, z.mine), BF16),
        vecs=((VECTORS, w), F32),
        b_mine=((1, z.mine), F32),
        tok_all=((ln, w), BF16),
        hid_all=((ln, w), BF16),
        gf_all=((ln, w), BF16),
        ga_cut=((ln, c), BF16),
        ga_cols=((ln, c), BF16),
        att_sum=((ln, c), F32),
        att_cut=((ln, c), BF16),
        att_got=((ln, c), BF16),
        ctx_out=((w // 128 * ln, 128), BF16),
        ctx_in=((4, z.pairs * ln, 128), BF16),
        ctx_own=((z.pairs * ln, 128), F32),
        qkv=((ln, 3 * c), BF16),
        grad_qkv=((ln, 3 * c), BF16),
        probs=((z.heads, ln, ln), F32),
        measure=((8192, 128), F32),
        ctx_all=((w // 128 * ln, 128), BF16),
        grad_ctx=((z.pairs * ln, 128), BF16),
        grad_kv=((2, ln, 128), F32),
        part_out=((3, ln, w), BF16),
        part_in=((3, 4, n, w), BF16),
        part_own=((n, w), F32),
        norm_one=((n, w), F32),
        v_out=((n, w), F32),
        v_grad=((n, w), F32),
        inv_one=((n, 1), F32),
        hidden=((n, w), F32),
        grad_sum=((n, w), F32),
        grad_mixed=((n, w), F32),
        active=((ln, z.mine), BF16),
        slope=((ln, z.mine), F32),
        grad_inner=((ln, z.mine), BF16),
        sums=((VECTORS, w), F32),
        b_sum=((1, z.mine), F32),
        term_vec=((z.pages * SLAB, 128), F32),
        slot_outer_a=((1, 2, half, z.unit, w // 2), BF16), stage_outer_a=((1, z.unit, w // 2), BF16),
        slot_outer_b=((1, 2, half, z.unit, w // 2), BF16), stage_outer_b=((1, z.unit, w // 2), BF16),
        slot_inner=((2, 2, half, z.rows, z.mine // 2), BF16), stage_inner=((2, z.rows, z.mine // 2), BF16),
        slot_pair=((z.pairs, 1, 2, half, z.rows, 384), BF16), stage_pair=((z.pairs, 1, z.rows, 384), BF16),
        slot_out=((1, 2, half, z.rows, c), BF16), stage_out=((1, z.rows, c), BF16),
        slot_vec=((1, 2, half, SLAB, 128 // 1), F32), stage_vec=((1, SLAB, 128 // 1), F32),
        fin_inner=((z.rows, z.mine), BF16), got_inner=((4, z.row, z.mine), BF16),
        fin_pair=((z.pairs, z.rows, 384), BF16), got_pair=((z.pairs, 4, z.row, 384), BF16),
        fin_out=((z.rows, c), BF16), got_out=((4, z.row, c), BF16),
        fin_vec=((SLAB, 128), F32), got_vec=((4, SLAB, 128), F32),
    )
    z.sems = 107
    z.groups, z.group_bytes = 5, 4 << 20
    fetched = dict(
        w_query=0, w_key=0, w_value=0, b_query=0, b_value=0, b_out=0, g_attn=0, s_attn=0, b_outer=0,
        g_final=0, s_final=0, b_inner=0, w_outer=0, w_out=0, tokens=0, w_inner=0, out_grad=0, valid=0)
    z.fetched, z.held = tuple(fetched), "f_"
    for name in z.fetched:
        scratch[z.held + name] = (ins[name].shape, ins[name].dtype)
    sems = [pltpu.SemaphoreType.DMA((v,)) for v in (z.groups, z.sems, len(fetched) + 2)]
    names = list(ins) + list(outs) + list(scratch) + list(dict(send_sem=0, recv_sem=0, load_sem=0))
    vmem = pl.BlockSpec(memory_space=pltpu.VMEM)
    parts = pl.pallas_call(
        functools.partial(layer_kernel, z, names),
        out_shape=[jax.ShapeDtypeStruct(*v) for v in outs.values()],
        in_specs=[
            pl.BlockSpec(memory_space=pl.ANY)
            if k in fetched
            else vmem
            for k, v in ins.items()
        ],
        out_specs=[pl.BlockSpec(memory_space=pl.ANY)] * 2 + [vmem] * (len(outs) - 2),
        scratch_shapes=[
            (pltpu.SMEM if v[1] == jnp.int32 else pltpu.VMEM)(*v) for v in scratch.values()
        ]
        + sems,
        compiler_params=pltpu.CompilerParams(
            collective_id=0, has_side_effects=True, vmem_limit_bytes=67043328
        ),
        name="layer",
    )(*ins.values())
    row, big = z.row, jax.ShapeDtypeStruct((n, w), F32)
    mat = jax.ShapeDtypeStruct((row, w), F32)
    vec = jax.ShapeDtypeStruct((1, row), F32)
    shapes = [
        big, big, mat, vec, mat, mat, vec, mat, vec, vec, vec,
        jax.ShapeDtypeStruct((row, z.units), F32), jax.ShapeDtypeStruct((1, z.unit), F32),
        jax.ShapeDtypeStruct((z.unit, w), F32), vec, vec, vec,
    ]
    steps = 2

    def rows_of(rows, width):
        return pl.BlockSpec((rows // steps, width), lambda i: (i, 0))

    results = pl.pallas_call(
        functools.partial(finish_kernel, z),
        out_shape=shapes,
        grid=(steps,),
        in_specs=[
            rows_of(n, w), rows_of(n, w), rows_of(z.unit, w),
            pl.BlockSpec((z.parts, row // steps, z.mine), lambda i: (0, i, 0)),
            pl.BlockSpec((z.pairs, z.parts, row // steps, 384), lambda i: (0, 0, i, 0)),
            pl.BlockSpec((z.parts, row // steps, c), lambda i: (0, i, 0)),
            pl.BlockSpec((SLAB, 128), lambda i: (0, 0)),
        ],
        out_specs=[
            rows_of(v.shape[0], v.shape[1])
            if v.shape[0] > 1
            else pl.BlockSpec(v.shape, lambda i: (0, 0))
            for v in shapes
        ],
        name="finish",
    )(*parts)
    results = list(results)
    for i in (0, 1):
        results[i] = results[i].reshape(tokens.shape)
    for i in range(2, 17):
        if results[i].shape[0] == 1:
            results[i] = results[i].reshape(results[i].shape[1])
    return tuple(results)


def body(
    tokens,
    valid_len,
    query_weight,
    query_bias,
    key_weight,
    value_weight,
    value_bias,
    output_weight,
    output_bias,
    attn_gain,
    attn_shift,
    inner_weight,
    inner_bias,
    outer_weight,
    outer_bias,
    final_gain,
    final_shift,
    out_grad,
):
    lowered = [
        piece.astype(jnp.bfloat16)
        for piece in (
            query_weight,
            query_bias,
            key_weight,
            value_weight,
            value_bias,
            output_weight,
            output_bias,
            attn_gain,
            attn_shift,
            inner_weight,
            inner_bias,
            outer_weight,
            outer_bias,
            final_gain,
            final_shift,
        )
    ]
    outputs = sequence_layer(tokens, valid_len, lowered, out_grad)
    return outputs


def solution(mesh):
    in_specs = (
        P("page", "seq", None),
        P("page"),
        P(("page", "seq"), None),
        P(("page", "seq")),
        P(("page", "seq"), None),
        P(("page", "seq"), None),
        P(("page", "seq")),
        P(("page", "seq"), None),
        P(("page", "seq")),
        P(("page", "seq")),
        P(("page", "seq")),
        P(("page", "seq"), None),
        P(("page", "seq")),
        P(("page", "seq"), None),
        P(("page", "seq")),
        P(("page", "seq")),
        P(("page", "seq")),
        P("page", "seq", None),
    )
    out_specs = (
        P("page", "seq", None),
        P("page", "seq", None),
        P(("page", "seq"), None),
        P(("page", "seq")),
        P(("page", "seq"), None),
        P(("page", "seq"), None),
        P(("page", "seq")),
        P(("page", "seq"), None),
        P(("page", "seq")),
        P(("page", "seq")),
        P(("page", "seq")),
        P(("page", "seq"), None),
        P(("page", "seq")),
        P(("page", "seq"), None),
        P(("page", "seq")),
        P(("page", "seq")),
        P(("page", "seq")),
    )

    def layer(*arrays):
        width, units = arrays[11].shape
        if supported(mesh, arrays[0].shape, width, units):
            z = Sizes(mesh, width, units, arrays[0].shape[1] // mesh.shape["seq"])

            def run(tokens, valid_len, *rest):
                return paged_layer(z, tokens, valid_len, rest[:-1], rest[-1])

            chosen = run
        else:
            chosen = body
        return jax.shard_map(
            chosen, mesh=mesh, in_specs=in_specs, out_specs=out_specs, check_vma=False
        )(*arrays)

    return layer
```

```python
import functools
import math
import types

import jax
import jax.numpy as jnp
from jax import lax
from jax.experimental import pallas as pl
from jax.experimental.pallas import tpu as pltpu
from jax.sharding import PartitionSpec as P

HEAD_DIM = 64


EPSILON = 1e-05
INV_ROOT_TWO = 1.0 / math.sqrt(2.0)
INV_ROOT_TWO_PI = 1.0 / math.sqrt(2.0 * math.pi)


def product(left, right):
    return jnp.dot(left, right, preferred_element_type=jnp.float32)


def product_tn(left, right):
    return lax.dot_general(
        left, right, (((0,), (0,)), ((), ())), preferred_element_type=jnp.float32
    )


def product_nt(left, right):
    return lax.dot_general(
        left, right, (((1,), (1,)), ((), ())), preferred_element_type=jnp.float32
    )


def norm_parts(values):
    center = values - jnp.mean(values, axis=-1, keepdims=True)
    inverse = lax.rsqrt(jnp.mean(center * center, axis=-1, keepdims=True) + EPSILON)
    return (center * inverse, inverse)


def norm_backward(grad_out, normed, inverse, gain):
    scaled = grad_out * gain
    return inverse * (
        scaled
        - jnp.mean(scaled, axis=-1, keepdims=True)
        - normed * jnp.mean(scaled * normed, axis=-1, keepdims=True)
    )


def gelu_parts(values):
    cumulative = 0.5 * (1.0 + lax.erf(values * INV_ROOT_TWO))
    return (
        values * cumulative,
        cumulative + values * jnp.exp(-0.5 * values * values) * INV_ROOT_TWO_PI,
    )


def sequence_layer(tokens, valid_len, lowered, out_grad):
    fetched = (
        lax.all_gather(lowered[0], ("page", "seq"), axis=0, tiled=True),
        lax.all_gather(lowered[1], ("page", "seq"), axis=0, tiled=True),
        lax.all_gather(lowered[2], ("page", "seq"), axis=0, tiled=True),
        lax.all_gather(lowered[3], ("page", "seq"), axis=0, tiled=True),
        lax.all_gather(lowered[4], ("page", "seq"), axis=0, tiled=True),
        lax.all_gather(lowered[5], ("page", "seq"), axis=0, tiled=True),
        lax.all_gather(lowered[6], ("page", "seq"), axis=0, tiled=True),
        lax.all_gather(lowered[7], ("page", "seq"), axis=0, tiled=True),
        lax.all_gather(lowered[8], ("page", "seq"), axis=0, tiled=True),
        lax.all_gather(lowered[9], ("page", "seq"), axis=0, tiled=True),
        lax.all_gather(lowered[10], ("page", "seq"), axis=0, tiled=True),
        lax.all_gather(lowered[11], ("page", "seq"), axis=0, tiled=True),
        lax.all_gather(lowered[12], ("page", "seq"), axis=0, tiled=True),
        lax.all_gather(lowered[13], ("page", "seq"), axis=0, tiled=True),
        lax.all_gather(lowered[14], ("page", "seq"), axis=0, tiled=True),
    )
    (
        w_query,
        b_query,
        w_key,
        w_value,
        b_value,
        w_out,
        b_out,
        g_attn,
        s_attn,
        w_inner,
        b_inner,
        w_outer,
        b_outer,
        g_final,
        s_final,
    ) = fetched
    f32 = jnp.float32
    bf16 = jnp.bfloat16
    scale = HEAD_DIM ** (-0.5)
    page_count, span_len, width = tokens.shape
    heads = width // HEAD_DIM
    row_count = page_count * span_len
    tok_rows = tokens.reshape(row_count, width)
    tok_low = tok_rows.astype(bf16)
    q_low = (product(tok_low, w_query) + b_query.astype(f32)).astype(bf16)
    k_low = product(tok_low, w_key).astype(bf16)
    v_low = (product(tok_low, w_value) + b_value.astype(f32)).astype(bf16)
    k_full, v_full = (
        lax.all_gather(k_low.reshape(page_count, span_len, width), "seq", axis=1, tiled=True),
        lax.all_gather(v_low.reshape(page_count, span_len, width), "seq", axis=1, tiled=True),
    )
    seq_len = k_full.shape[1]
    q_heads = q_low.reshape(page_count, span_len, heads, HEAD_DIM)
    k_heads = k_full.reshape(page_count, seq_len, heads, HEAD_DIM)
    v_heads = v_full.reshape(page_count, seq_len, heads, HEAD_DIM)
    key_mask = (lax.broadcasted_iota(jnp.int32, (page_count, seq_len), 1) < valid_len[:, None])[
        :, None, None, :
    ]

    def masked_scores():
        raw = jnp.einsum("pqhe,pkhe->phqk", q_heads, k_heads, preferred_element_type=f32) * scale
        return jnp.where(key_mask, raw, -1000000000.0)

    scores = masked_scores()
    top_score = jnp.max(scores, axis=-1, keepdims=True)
    log_total = top_score + jnp.log(jnp.sum(jnp.exp(scores - top_score), axis=-1, keepdims=True))
    probs_low = jnp.exp(scores - log_total).astype(bf16)
    context = jnp.einsum("phqk,pkhe->pqhe", probs_low, v_heads, preferred_element_type=f32)
    ctx_low = context.reshape(row_count, width).astype(bf16)
    attended = product(ctx_low, w_out) + b_out.astype(f32)
    norm_one, inv_one = norm_parts(tok_rows + attended)
    hidden = norm_one * g_attn.astype(f32) + s_attn.astype(f32)
    hid_low = hidden.astype(bf16)
    inner = product(hid_low, w_inner) + b_inner.astype(f32)
    active, slope = gelu_parts(inner)
    act_low = active.astype(bf16)
    outer = product(act_low, w_outer) + b_outer.astype(f32)
    norm_two, inv_two = norm_parts(hidden + outer)
    result = norm_two * g_final.astype(f32) + s_final.astype(f32)
    (
        w_query,
        b_query,
        w_key,
        w_value,
        b_value,
        w_out,
        b_out,
        g_attn,
        s_attn,
        w_inner,
        b_inner,
        w_outer,
        b_outer,
        g_final,
        s_final,
    ) = (
        lax.all_gather(lowered[0], ("page", "seq"), axis=0, tiled=True),
        lax.all_gather(lowered[1], ("page", "seq"), axis=0, tiled=True),
        lax.all_gather(lowered[2], ("page", "seq"), axis=0, tiled=True),
        lax.all_gather(lowered[3], ("page", "seq"), axis=0, tiled=True),
        lax.all_gather(lowered[4], ("page", "seq"), axis=0, tiled=True),
        lax.all_gather(lowered[5], ("page", "seq"), axis=0, tiled=True),
        lax.all_gather(lowered[6], ("page", "seq"), axis=0, tiled=True),
        lax.all_gather(lowered[7], ("page", "seq"), axis=0, tiled=True),
        lax.all_gather(lowered[8], ("page", "seq"), axis=0, tiled=True),
        lax.all_gather(lowered[9], ("page", "seq"), axis=0, tiled=True),
        lax.all_gather(lowered[10], ("page", "seq"), axis=0, tiled=True),
        lax.all_gather(lowered[11], ("page", "seq"), axis=0, tiled=True),
        lax.all_gather(lowered[12], ("page", "seq"), axis=0, tiled=True),
        lax.all_gather(lowered[13], ("page", "seq"), axis=0, tiled=True),
        lax.all_gather(lowered[14], ("page", "seq"), axis=0, tiled=True),
    )
    grad_rows = out_grad.reshape(row_count, width)
    grad_gfinal = jnp.sum(grad_rows * norm_two, axis=0)
    grad_sfinal = jnp.sum(grad_rows, axis=0)
    grad_sum = norm_backward(grad_rows, norm_two, inv_two, g_final.astype(f32))
    grad_f_low = grad_sum.astype(bf16)
    grad_bouter = jnp.sum(grad_f_low.astype(f32), axis=0)
    grad_wouter = product_tn(act_low, grad_f_low)
    grad_active = product_nt(grad_f_low, w_outer)
    grad_in_low = (grad_active * slope).astype(bf16)
    grad_binner = jnp.sum(grad_in_low.astype(f32), axis=0)
    grad_winner = product_tn(hid_low, grad_in_low)
    grad_hidden = grad_sum + product_nt(grad_in_low, w_inner)
    grad_gattn = jnp.sum(grad_hidden * norm_one, axis=0)
    grad_sattn = jnp.sum(grad_hidden, axis=0)
    grad_mixed = norm_backward(grad_hidden, norm_one, inv_one, g_attn.astype(f32))
    grad_att_low = grad_mixed.astype(bf16)
    grad_bout = jnp.sum(grad_att_low.astype(f32), axis=0)
    grad_wout = product_tn(ctx_low, grad_att_low)
    grad_ctx = (
        product_nt(grad_att_low, w_out).astype(bf16).reshape(page_count, span_len, heads, HEAD_DIM)
    )
    probs = jnp.exp(masked_scores() - log_total)
    probs_low = probs.astype(bf16)
    grad_probs = jnp.einsum("pqhe,pkhe->phqk", grad_ctx, v_heads, preferred_element_type=f32)
    grad_vfull = jnp.einsum("phqk,pqhe->pkhe", probs_low, grad_ctx, preferred_element_type=f32)
    grad_scores = (
        probs * (grad_probs - jnp.sum(grad_probs * probs, axis=-1, keepdims=True))
    ).astype(bf16)
    grad_q_low = (
        (jnp.einsum("phqk,pkhe->pqhe", grad_scores, k_heads, preferred_element_type=f32) * scale)
        .astype(bf16)
        .reshape(row_count, width)
    )
    grad_kfull = (
        jnp.einsum("phqk,pqhe->pkhe", grad_scores, q_heads, preferred_element_type=f32) * scale
    )
    grad_keys, grad_values = (
        lax.psum_scatter(
            grad_kfull.reshape(page_count, seq_len, width).astype(jnp.bfloat16),
            "seq",
            scatter_dimension=1,
            tiled=True,
        ).astype(jnp.float32),
        lax.psum_scatter(
            grad_vfull.reshape(page_count, seq_len, width).astype(jnp.bfloat16),
            "seq",
            scatter_dimension=1,
            tiled=True,
        ).astype(jnp.float32),
    )
    grad_k_low = grad_keys.reshape(row_count, width).astype(bf16)
    grad_v_low = grad_values.reshape(row_count, width).astype(bf16)
    grad_tokens = (
        grad_mixed
        + product_nt(grad_q_low, w_query)
        + product_nt(grad_k_low, w_key)
        + product_nt(grad_v_low, w_value)
    )
    grad_wquery = product_tn(tok_low, grad_q_low)
    grad_bquery = jnp.sum(grad_q_low.astype(f32), axis=0)
    grad_wkey = product_tn(tok_low, grad_k_low)
    grad_wvalue = product_tn(tok_low, grad_v_low)
    grad_bvalue = jnp.sum(grad_v_low.astype(f32), axis=0)
    owned = (
        lax.psum_scatter(grad_wquery, ("page", "seq"), scatter_dimension=0, tiled=True),
        lax.psum_scatter(grad_bquery, ("page", "seq"), scatter_dimension=0, tiled=True),
        lax.psum_scatter(grad_wkey, ("page", "seq"), scatter_dimension=0, tiled=True),
        lax.psum_scatter(grad_wvalue, ("page", "seq"), scatter_dimension=0, tiled=True),
        lax.psum_scatter(grad_bvalue, ("page", "seq"), scatter_dimension=0, tiled=True),
        lax.psum_scatter(grad_wout, ("page", "seq"), scatter_dimension=0, tiled=True),
        lax.psum_scatter(grad_bout, ("page", "seq"), scatter_dimension=0, tiled=True),
        lax.psum_scatter(grad_gattn, ("page", "seq"), scatter_dimension=0, tiled=True),
        lax.psum_scatter(grad_sattn, ("page", "seq"), scatter_dimension=0, tiled=True),
        lax.psum_scatter(grad_winner, ("page", "seq"), scatter_dimension=0, tiled=True),
        lax.psum_scatter(grad_binner, ("page", "seq"), scatter_dimension=0, tiled=True),
        lax.psum_scatter(grad_wouter, ("page", "seq"), scatter_dimension=0, tiled=True),
        lax.psum_scatter(grad_bouter, ("page", "seq"), scatter_dimension=0, tiled=True),
        lax.psum_scatter(grad_gfinal, ("page", "seq"), scatter_dimension=0, tiled=True),
        lax.psum_scatter(grad_sfinal, ("page", "seq"), scatter_dimension=0, tiled=True),
    )
    return (
        result.reshape(tokens.shape),
        grad_tokens.reshape(tokens.shape),
        owned[0],
        owned[1],
        owned[2],
        owned[3],
        owned[4],
        owned[5],
        owned[6],
        owned[7],
        owned[8],
        owned[9],
        owned[10],
        owned[11],
        owned[12],
        owned[13],
        owned[14],
    )


MESH = pl.DeviceIdType.MESH
BF16 = jnp.bfloat16
F32 = jnp.float32
VECTORS = 8
SLAB = 16
NEGATIVE = -1000000000.0


def dot_nn(left, right):
    return lax.dot_general(left, right, (((1,), (0,)), ((), ())), preferred_element_type=F32)


def dot_nt(left, right):
    return lax.dot_general(left, right, (((1,), (1,)), ((), ())), preferred_element_type=F32)


def dot_tn(left, right):
    return lax.dot_general(left, right, (((0,), (0,)), ((), ())), preferred_element_type=F32)


class Sizes:
    def __init__(self, mesh, width, units, span):
        self.pages = mesh.shape["page"]
        self.parts = mesh.shape["seq"]
        self.half = self.pages // 2
        self.width = width
        self.units = units
        self.span = span
        self.length = span * self.parts
        self.row = width // (self.pages * self.parts)
        self.rows = self.row * self.parts
        self.unit = units // (self.pages * self.parts)
        self.mine = self.unit * self.pages
        self.cols = width // self.parts
        self.heads = self.cols // HEAD_DIM
        self.pairs = self.cols // 128


def supported(mesh, token_shape, width, units):
    pages, parts = mesh.shape["page"], mesh.shape["seq"]
    return (
        parts == 4
        and pages % 2 == 0
        and pages >= 4
        and token_shape[0] == pages
        and token_shape[1] % (parts * 128) == 0
        and width % (pages * parts * 32) == 0
        and width // pages == 128
        and units % (pages * parts * 128) == 0
        and (width // parts) % 128 == 0
    )


def layer_kernel(z, names, *refs):
    r = types.SimpleNamespace(**dict(zip(names, refs)))
    send_sem, recv_sem, load_sem = r.send_sem, r.recv_sem, r.load_sem
    page = lax.axis_index("page")
    part = lax.axis_index("seq")
    counter = [0]

    def slots(count):
        first = counter[0]
        counter[0] += count
        return first

    odd = page % 2
    place = odd * (z.pages - 1 - page // 2) + (1 - odd) * (page // 2)

    def page_at(index):
        index = (index + z.pages) % z.pages
        late = index // z.half
        return (1 - late) * (2 * index) + late * (2 * z.pages - 1 - 2 * index)

    ring = [page] + [page_at(place + step) for step in range(1, z.pages)]
    peers = [part] + [
        ((part // 2 + j // 2) % 2) * 2 + (part % 2 + j % 2) % 2 for j in range(1, 4)
    ]

    def around(step):
        return ring[step % z.pages]

    def peer(j):
        return peers[j]

    rank = page * z.parts + part

    class Copy:
        def __init__(self, src, dst, index, device, group=None):
            self.args = src, dst, index, device
            self.group = group

        def made(self, group):
            src, dst, index, device = self.args
            return pltpu.make_async_remote_copy(
                src_ref=src,
                dst_ref=dst,
                send_sem=send_sem.at[group],
                recv_sem=recv_sem.at[index],
                device_id=device,
                device_id_type=MESH,
            )

        def start(self):
            group = self.group
            if group is None:
                size = self.size()
                if groups[-1] + size > z.group_bytes:
                    groups.append(0)
                groups[-1] += size
                group = len(groups) - 1
            self.made(group).start()

        def wait_recv(self):
            self.made(0).wait_recv()

        def size(self):
            src = self.args[0]
            return math.prod(src.shape) * jnp.dtype(src.dtype).itemsize

        def wait_bytes(self, size):
            rows = r.measure.at[pl.ds(0, size // 512)]
            Copy(rows, rows, *self.args[2:]).wait_recv()

        def wait_send(self):
            self.made(self.group).wait_send()

    groups = [0]
    copy = Copy

    def block(ref, index, size):
        return ref.at[pl.ds(pl.multiple_of(index * size, size), size)]

    barrier = pltpu.get_barrier_semaphore()

    def greet(device):
        pl.semaphore_signal(barrier, inc=1, device_id=device, device_id_type=MESH)

    for j in (1, 2, 3):
        greet((page, peer(j)))
    greet((around(1), part))
    greet((around(-1), part))

    class Share:
        def __init__(self, ref, size, pieces=2):
            self.ref, self.size, self.pieces = ref, size, pieces
            self.first = slots(2 + pieces)

        def copy(self, j, owner, k):
            height = self.size // self.pieces
            piece = block(self.ref, owner, self.size).at[pl.ds(k * height, height)]
            index = self.first + (2 + k if j == 2 else j // 2)
            return copy(piece, piece, index, (page, peer(1 if j == 3 else j)))

        def start(self, k):
            self.copy(2, part, k).start()
            self.copy(1, part, k).start()

        def forward(self):
            for k in range(self.pieces):
                self.copy(2, peer(2), k).wait_recv()
                self.copy(3, peer(2), k).start()


        def wait(self, j):
            arrival = self.copy(j, peer(j), 0)
            arrival.wait_bytes(self.pieces * arrival.size())

    class Combine:
        def __init__(self, refs, size, make, pieces=2):
            self.out, self.got, self.own = refs
            self.size, self.make, self.pieces = size, make, pieces
            self.height = size // pieces
            self.first = slots(2 * pieces)

        def rows(self, j, k):
            at = pl.multiple_of(peer(j) * self.size + k * self.height, self.height)
            return pl.ds(at, self.height)

        def copy(self, j, k):
            return copy(
                self.out.at[self.rows(j, k)],
                self.got.at[j, pl.ds(k * self.height, self.height)],
                self.first + 2 * k + j // 3,
                (page, peer(2 if j == 2 else 1)),
            )

        def term(self, j):
            value = self.make(pl.ds(pl.multiple_of(peer(j) * self.size, self.size), self.size), j)
            if j == 0:
                self.own[...] = value
                return
            for k in range(self.pieces):
                rows = slice(k * self.height, (k + 1) * self.height)
                mine = value[rows]
                if j == 2:
                    self.copy(3, k).wait_recv()
                    mine = mine + self.got[3, rows, :].astype(F32)
                self.out[self.rows(j, k), :] = mine.astype(BF16)
                self.copy(j, k).start()

        def finish(self, fn, after=None, step=32):
            for k in range(self.pieces):
                arrival = self.copy(1, k)
                arrival.wait_bytes(2 * arrival.size())

                def body(i, carry):
                    at = pl.multiple_of(k * self.height + i * step, step)
                    rows = pl.ds(at, step)
                    total = self.own[rows, :]
                    for j in (1, 2):
                        total = total + self.got[j, rows, :].astype(F32)
                    fn(rows, at, total)
                    return carry

                lax.fori_loop(0, self.height // step, body, 0)
                if after is not None:
                    after(k)

    def token_refs(phase):
        return r.part_out.at[phase], r.part_in.at[phase], r.part_own

    class Spread:
        def __init__(self, src, dst, size):
            self.src, self.dst, self.size, self.first = src, dst, size, slots(1)

        def copy(self, j):
            return copy(
                block(self.src, peer(j), self.size),
                self.dst.at[j],
                self.first,
                (page, peer(j)),
            )

        def start(self):
            for j in (2, 3, 1):
                self.copy(j).start()

        def wait(self):
            arrival = self.copy(1)
            arrival.wait_bytes(3 * arrival.size())

    class Place:
        def __init__(self, src, dst, size, base):
            self.src, self.dst, self.size, self.base, self.first = src, dst, size, base, slots(1)

        def copy(self, j, owner):
            return copy(
                block(self.src, peer(j), self.size),
                block(self.dst, self.base + owner, self.size),
                self.first,
                (page, peer(j)),
            )

        def start(self):
            for j in (2, 3, 1):
                self.copy(j, part).start()

        def wait(self):
            arrival = self.copy(1, peer(1))
            arrival.wait_bytes(3 * arrival.size())

    class Gather:
        def __init__(self, ref, size, pieces=1):
            self.ref, self.size, self.pieces = ref, size, pieces
            self.first = slots(z.half * pieces)

        def copy(self, t, d, k, step):
            height = self.size // self.pieces
            start = k * height
            if t == z.half - 1:
                height = height // 2
                start = start + d * height
            piece = block(self.ref, around(step), self.size).at[pl.ds(start, height)]
            return copy(
                piece,
                piece,
                self.first + t * self.pieces + k,
                (around(1 - 2 * d), part),
            )

        def wait(self, t, k):
            both = 2 * self.copy(t, 0, k, 0).size()
            self.copy(t, 0, k, 0).wait_bytes(both)

        def step(self, t, pieces=None):
            for k in pieces or range(self.pieces):
                if t > 0:
                    self.wait(t - 1, k)
                for d in (0, 1):
                    self.copy(t, d, k, -(1 - 2 * d) * t).start()


        def done(self):
            for k in range(self.pieces):
                self.wait(z.half - 1, k)

    class Reduce:
        def __init__(self, slot, stage, local, shape, kind, pieces=1):
            self.slot, self.stage, self.local = slot, stage, local
            self.size, self.kind, self.pieces = shape[0], kind, pieces
            self.wide = shape[1] // pieces
            self.first = slots(z.half * pieces)

        def copy(self, t, d, k):
            h = self.size // 2
            if t == 0:
                src = self.stage.at[k, pl.ds(d * h, h)]
                dst = self.slot.at[k, d, 0, pl.ds(d * h, h)]
            else:
                src = self.slot.at[k, d, t - 1]
                dst = self.slot.at[k, d, t]
            return copy(
                src,
                dst,
                self.first + t * self.pieces + k,
                (around(1 - 2 * d), part),
            )


        def step(self, t):
            h = self.size // 2
            wide = self.wide
            if t == 0:
                term = self.local(around(z.half)).astype(self.kind)
                for k in range(self.pieces):
                    self.stage[k] = term[:, k * wide : (k + 1) * wide]
            else:
                terms = [
                    self.local(around((1 - 2 * d) * (z.half - t))) for d in (0, 1)
                ]
            for k in range(self.pieces):
                if t > 0:
                    self.wait(t - 1, k)
                for d in (0, 1):
                    if t > 0:
                        term = terms[d][:, k * wide : (k + 1) * wide]
                        held = self.slot.at[k, d, t - 1]
                        if t == 1:
                            near, far = pl.ds(d * h, h), pl.ds((1 - d) * h, h)
                            term_near = term[d * h : (d + 1) * h]
                            term_far = term[(1 - d) * h : (2 - d) * h]
                            held[near] = (held[near].astype(F32) + term_near).astype(self.kind)
                            held[far] = term_far.astype(self.kind)
                        else:
                            held[...] = (held[...].astype(F32) + term).astype(self.kind)
                    self.copy(t, d, k).start()

        def wait(self, t, k):
            arrival = self.copy(t, 0, k)
            arrival.wait_bytes(2 * arrival.size())

        def total(self, out):
            term = self.local(page)
            last = z.half - 1
            for k in range(self.pieces):
                self.wait(last, k)
                at = slice(k * self.wide, (k + 1) * self.wide)
                out[:, at] = (
                    term[:, at] + self.slot[k, 0, last].astype(F32) + self.slot[k, 1, last].astype(F32)
                ).astype(out.dtype)

    c, w, n = z.cols, z.width, z.span

    def fetch(i, name):
        return pltpu.make_async_copy(getattr(r, name), getattr(r, z.held + name), load_sem.at[i])

    for i, name in enumerate(z.fetched):
        fetch(i, name).start()
    hbm = r
    r = types.SimpleNamespace(**vars(hbm))
    for name in z.fetched:
        setattr(r, name, getattr(hbm, z.held + name))
    fetches = iter(range(len(z.fetched)))

    def arrive(count):
        for _ in range(count):
            i = next(fetches)
            pltpu.make_async_copy(
                getattr(hbm, z.fetched[i]), getattr(r, z.fetched[i]), load_sem.at[i]
            ).wait()

    arrive(3)
    for q in range(z.parts):
        rows = pl.ds(q * z.row, z.row)
        for i, weight in enumerate((r.w_query, r.w_key, r.w_value)):
            for k in range(z.pairs):
                r.cut_qkv[rows, (3 * k + i) * 128 : (3 * k + i + 1) * 128] = weight[
                    :, q * c + k * 128 : q * c + (k + 1) * 128
                ].astype(BF16)
    arrive(9)
    mine = pl.multiple_of(part * SLAB, SLAB)
    for i, small in enumerate(
        (r.b_query, r.b_value, r.b_out, r.g_attn, r.s_attn, r.b_outer, r.g_final, r.s_final)
    ):
        r.vec_raw[pl.ds(mine + i, 1), 0 : z.row] = small[...]
    at_page = pl.multiple_of(page * SLAB, SLAB)
    r.vec_all[pl.ds(at_page + VECTORS, 1), :] = r.b_inner[...]
    arrive(1)
    r.outer_w[pl.ds(pl.multiple_of(page * z.unit, z.unit), z.unit), :] = r.w_outer[...].astype(
        BF16
    )

    ring_qkv = Gather(r.qkv_w, z.rows, 2)
    ring_vec = Gather(r.vec_all, SLAB)
    ring_inner = Gather(r.inner_w, z.rows, 2)
    ring_out = Gather(r.out_w, z.rows)
    ring_outer = Gather(r.outer_w, z.unit, 2)
    cut_qkv = Place(r.cut_qkv, r.qkv_w, z.row, page * z.parts)
    cut_out = Place(r.cut_out, r.out_w, z.row, page * z.parts)
    cut_inner = Place(r.cut_inner, r.inner_w, z.row, page * z.parts)
    share_tok = Share(r.tok_all, n)

    class ShareVec:
        first = slots(1)

        def copy(self, j, owner):
            piece = block(r.vec_raw, owner, SLAB).at[pl.ds(0, VECTORS)]
            return copy(piece, piece, self.first, (page, peer(j)))

    vec_share = ShareVec()
    pl.semaphore_wait(barrier, 5)
    cut_qkv.start()
    for j in (2, 3, 1):
        vec_share.copy(j, part).start()
    ring_outer.step(0)
    arrive(2)
    r.tok_all[pl.ds(pl.multiple_of(part * n, n), n), :] = r.tokens[...].astype(BF16)
    share_tok.start(0)
    share_tok.start(1)
    for q in range(z.parts):
        r.cut_out[pl.ds(q * z.row, z.row), :] = r.w_out[:, q * c : (q + 1) * c].astype(BF16)
    cut_out.start()
    arrive(1)
    for q in range(z.parts):
        rows = pl.ds(q * z.row, z.row)
        for g in range(z.pages):
            at = (z.parts * g + q) * z.unit
            r.cut_inner[rows, g * z.unit : (g + 1) * z.unit] = r.w_inner[
                :, at : at + z.unit
            ].astype(BF16)
    cut_inner.start()
    own_rows = pl.ds(pl.multiple_of(rank * z.row, z.row), z.row)
    cut_rows = pl.ds(pl.multiple_of(part * z.row, z.row), z.row)
    r.qkv_w[own_rows, :] = r.cut_qkv[cut_rows, :]
    r.out_w[own_rows, :] = r.cut_out[cut_rows, :]
    r.inner_w[own_rows, :] = r.cut_inner[cut_rows, :]

    cut_qkv.wait()
    ring_qkv.step(0)
    arrival = vec_share.copy(1, peer(1))
    arrival.wait_bytes(3 * arrival.size())
    lane = lax.broadcasted_iota(jnp.int32, (VECTORS, 128), 1)
    total = jnp.zeros((VECTORS, 128), F32)
    for q in range(z.parts):
        tile = r.vec_raw[q * SLAB : q * SLAB + VECTORS, :]
        if q:
            tile = pltpu.roll(tile, q * z.row, 1)
        total = total + jnp.where(lane // z.row == q, tile, 0.0)
    r.vec_all[pl.ds(at_page, VECTORS), :] = total
    ring_vec.step(0)
    ring_qkv.step(1)
    ring_vec.step(1)
    cut_out.wait()
    ring_out.step(0)
    ring_qkv.step(2)
    ring_vec.step(2)
    ring_out.step(1)
    share_tok.forward()
    ring_qkv.step(3)
    ring_vec.step(3)
    ring_out.step(2)
    cut_inner.wait()
    ring_inner.step(0)
    ring_vec.done()

    for g in range(z.pages):
        tile = r.vec_all[g * SLAB : (g + 1) * SLAB, :].astype(BF16).astype(F32)
        r.vecs[:, g * 128 : (g + 1) * 128] = tile[0:VECTORS]
        r.b_mine[:, g * z.unit : (g + 1) * z.unit] = tile[VECTORS : VECTORS + 1]

    def vector(i):
        return r.vecs[i : i + 1, :]


    share_tok.wait(1)
    share_tok.wait(3)
    ring_qkv.done()

    def make_qkv(b, carry):
        rows = pl.ds(pl.multiple_of(b * n, n), n)
        out = dot_nn(r.tok_all[rows, :], r.qkv_w[...])
        for k in range(z.pairs):
            mine = pl.ds(pl.multiple_of(part * c + k * 128, 128), 128)
            for i, bias in enumerate((0, None, 1)):
                cols = slice((3 * k + i) * 128, (3 * k + i + 1) * 128)
                value = out[:, cols]
                if bias is not None:
                    value = value + r.vecs[bias : bias + 1, mine]
                r.qkv[rows, cols] = value.astype(BF16)
        return carry

    lax.fori_loop(0, z.parts, make_qkv, 0)
    ring_inner.step(1)
    ring_out.step(3)
    ring_outer.step(1)

    scale = HEAD_DIM ** (-0.5)
    first_head = lax.broadcasted_iota(jnp.int32, (n, 128), 1) < HEAD_DIM
    key_place = lax.broadcasted_iota(jnp.int32, (n, z.length), 1)
    pltpu.make_async_copy(hbm.valid, r.valid, load_sem.at[len(z.fetched) - 1]).wait()
    valid = r.valid[0]

    def pair_cols(kind, pair):
        return pl.ds((3 * pair + kind) * 128, 128)

    def attend(pair):
        def body(b, carry):
            rows = pl.ds(pl.multiple_of(b * n, n), n)
            queries = r.qkv[rows, pair_cols(0, pair)]
            keys = r.qkv[:, pair_cols(1, pair)]
            values = r.qkv[:, pair_cols(2, pair)]
            outs = []
            for h in range(2):
                mine = first_head if h == 0 else ~first_head
                scores = dot_nt(jnp.where(mine, queries, jnp.zeros_like(queries)), keys) * scale
                scores = jnp.where(key_place < valid, scores, NEGATIVE)
                top = jnp.max(scores, axis=-1, keepdims=True)
                weight = jnp.exp(scores - top)
                probs = weight * (1.0 / jnp.sum(weight, axis=-1, keepdims=True))
                r.probs[2 * pair + h, rows, :] = probs
                outs.append(dot_nn(probs.astype(BF16), values))
            place_rows = pl.ds(
                pl.multiple_of((part * z.pairs + pair) * z.length + b * n, n), n
            )
            r.ctx_all[place_rows, :] = jnp.where(first_head, outs[0], outs[1]).astype(
                BF16
            )
            return carry

        lax.fori_loop(0, z.parts, body, 0)

    share_ctx = Share(r.ctx_all, z.pairs * z.length, z.pairs)
    for pair in range(z.pairs):
        attend(pair)
        share_ctx.start(pair)
    ring_inner.step(2)
    ring_outer.step(2, (0,))

    def project(j):
        term = None
        for k in range(z.pairs):
            rows = pl.ds(pl.multiple_of((peer(j) * z.pairs + k) * z.length, z.length), z.length)
            features = pl.ds(pl.multiple_of(peer(j) * c + k * 128, 128), 128)
            more = dot_nn(r.ctx_all[rows, :], r.out_w[features, :])
            term = more if term is None else term + more
        r.att_sum[...] = term if j == 0 else r.att_sum[...] + term

    ring_out.done()
    project(0)
    share_ctx.wait(1)
    project(1)
    share_ctx.forward()
    project(2)
    share_ctx.wait(3)
    project(3)
    r.att_cut[...] = r.att_sum[...].astype(BF16)
    move_att = Place(r.att_cut, r.att_got, n, 0)
    move_att.start()
    own_block = pl.ds(pl.multiple_of(part * n, n), n)
    r.att_got[own_block, :] = r.att_cut[own_block, :]

    def add_column_sum(i, values):
        r.sums[i : i + 1, :] += jnp.sum(values, axis=0, keepdims=True)

    r.sums[...] = jnp.zeros_like(r.sums)

    share_hid = Share(r.hid_all, n)

    def first_norm(rows, at, total):
        mixed = r.tokens[rows, :] + (total + vector(2))
        normed, inverse = norm_parts(mixed)
        hidden = normed * vector(3) + vector(4)
        r.norm_one[rows, :] = normed
        r.inv_one[rows, :] = inverse
        r.hidden[rows, :] = hidden
        r.hid_all[pl.ds(pl.multiple_of(part * n + at, 32), 32), :] = hidden.astype(BF16)

    ring_inner.step(3)
    ring_outer.step(2, (1,))
    move_att.wait()
    for k in range(2):

        def norm_rows(i, carry):
            at = pl.multiple_of(k * (n // 2) + i * 32, 32)
            total = jnp.concatenate(
                [
                    r.att_got[pl.ds(pl.multiple_of(q * n + at, 32), 32), :].astype(F32)
                    for q in range(z.parts)
                ],
                axis=1,
            )
            first_norm(pl.ds(at, 32), at, total)
            return carry

        lax.fori_loop(0, n // 64, norm_rows, 0)
        share_hid.start(k)
    ring_inner.done()

    tile = 512

    def make_inner(j):
        chip = (part // 2 + j) % 2
        rows = pl.ds(pl.multiple_of(chip * 2 * n, 2 * n), 2 * n)

        def columns(i, carry):
            cols = pl.ds(pl.multiple_of(i * tile, tile), tile)
            inner = dot_nn(r.hid_all[rows, :], r.inner_w[:, cols]) + r.b_mine[:, cols]
            active, slope = gelu_parts(inner)
            r.active[rows, cols] = active.astype(BF16)
            r.slope[rows, cols] = slope
            return carry

        lax.fori_loop(0, z.mine // tile, columns, 0)

    share_hid.wait(1)
    make_inner(0)
    ring_outer.step(3)
    share_hid.forward()
    share_hid.wait(3)
    make_inner(1)
    ring_outer.done()
    combine_two = Combine(token_refs(0), n, lambda rows, j: dot_nn(r.active[rows, :], r.outer_w[...]), 4)
    for j in (3, 2, 1, 0):
        combine_two.term(j)
    share_gf = Share(r.gf_all, n, 4)

    arrive(1)

    def second_norm(rows, at, total):
        outer = total + vector(5)
        normed, inverse = norm_parts(r.hidden[rows, :] + outer)
        r.v_out[rows, :] = normed * vector(6) + vector(7)
        grad = r.out_grad[rows, :]
        add_column_sum(6, grad * normed)
        add_column_sum(7, grad)
        grad_sum = norm_backward(grad, normed, inverse, vector(6))
        low = grad_sum.astype(BF16)
        add_column_sum(5, low.astype(F32))
        r.grad_sum[rows, :] = grad_sum
        r.gf_all[pl.ds(pl.multiple_of(part * n + at, 32), 32), :] = low

    combine_two.finish(second_norm, share_gf.start)

    def leave_early(i, src, dst):
        return pltpu.make_async_copy(src, dst, load_sem.at[len(z.fetched) + i])

    leave_early(0, r.v_out, r.o_out).start()

    def chunk_term(left, right, size):
        def local(g):
            cols = pl.ds(pl.multiple_of(g * size, size), size)
            return dot_tn(left[:, cols], right[...])

        return local

    reduce_outer_a = Reduce(
        r.slot_outer_a, r.stage_outer_a,
        chunk_term(r.active, r.gf_all.at[:, 0 : w // 2], z.unit), (z.unit, w // 2), BF16,
    )
    reduce_outer_b = Reduce(
        r.slot_outer_b, r.stage_outer_b,
        chunk_term(r.active, r.gf_all.at[:, w // 2 :], z.unit), (z.unit, w // 2), BF16,
    )
    reduce_inner = Reduce(
        r.slot_inner, r.stage_inner, chunk_term(r.hid_all, r.grad_inner, z.rows),
        (z.rows, z.mine), BF16, 2
    )
    def pair_term(k):
        def local(g):
            cols = pl.ds(pl.multiple_of(g * z.rows, z.rows), z.rows)
            return dot_tn(r.tok_all[:, cols], r.grad_qkv[:, 384 * k : 384 * (k + 1)])

        return local

    def out_term(g):
        rows = pl.ds(pl.multiple_of(g * z.length, z.length), z.length)
        return dot_tn(r.ctx_all[rows, :], r.ga_cols[...])

    reduce_pair = [
        Reduce(r.slot_pair.at[k], r.stage_pair.at[k], pair_term(k), (z.rows, 384), BF16, 3)
        for k in range(z.pairs)
    ]
    reduce_out = Reduce(r.slot_out, r.stage_out, out_term, (z.rows, c), BF16)
    reduce_vec = Reduce(
        r.slot_vec, r.stage_vec,
        lambda g: r.term_vec[pl.ds(pl.multiple_of(g * SLAB, SLAB), SLAB), :], (SLAB, 128), F32,
    )

    r.b_sum[...] = jnp.zeros_like(r.b_sum)

    def make_grad_inner(j):
        chip = (part // 2 + j) % 2
        rows = pl.ds(pl.multiple_of(chip * 2 * n, 2 * n), 2 * n)

        def columns(i, carry):
            cols = pl.ds(pl.multiple_of(i * tile, tile), tile)
            grad = dot_nt(r.gf_all[rows, :], r.outer_w[cols, :]) * r.slope[rows, cols]
            low = grad.astype(BF16)
            r.grad_inner[rows, cols] = low
            r.b_sum[:, cols] += jnp.sum(low.astype(F32), axis=0, keepdims=True)
            return carry

        lax.fori_loop(0, z.mine // tile, columns, 0)

    share_gf.wait(1)
    make_grad_inner(0)
    share_gf.forward()
    share_gf.wait(3)
    reduce_outer_a.step(0)
    reduce_outer_b.step(0)
    make_grad_inner(1)
    combine_three = Combine(token_refs(1), n, lambda rows, j: dot_nt(r.grad_inner[rows, :], r.inner_w[...]))
    combine_three.term(3)
    combine_three.term(2)
    reduce_inner.step(0)
    reduce_outer_a.step(1)
    combine_three.term(1)
    combine_three.term(0)
    reduce_inner.step(1)
    reduce_outer_b.step(1)

    move_ga = Place(r.ga_cut, r.ga_cols, n, 0)

    def first_norm_back(rows, at, total):
        grad = r.grad_sum[rows, :] + total
        normed = r.norm_one[rows, :]
        add_column_sum(3, grad * normed)
        add_column_sum(4, grad)
        mixed = norm_backward(grad, normed, r.inv_one[rows, :], vector(3))
        low = mixed.astype(BF16)
        add_column_sum(2, low.astype(F32))
        r.grad_mixed[rows, :] = mixed
        for q in range(z.parts):
            r.ga_cut[pl.ds(pl.multiple_of(q * n + at, 32), 32), :] = low[:, q * c : (q + 1) * c]

    combine_three.finish(first_norm_back)
    move_ga.start()
    r.ga_cols[own_block, :] = r.ga_cut[own_block, :]
    reduce_outer_a.step(2)

    def grad_ctx_term(rows, j):
        return jnp.concatenate(
            [
                dot_nt(
                    r.ga_cols[...],
                    r.out_w[pl.ds(pl.multiple_of(peer(j) * c + k * 128, 128), 128), :],
                )
                for k in range(z.pairs)
            ],
            axis=0,
        )

    combine_ctx = Combine(
        (r.ctx_out, r.ctx_in, r.ctx_own), z.pairs * z.length, grad_ctx_term, z.pairs
    )
    move_ga.wait()
    combine_ctx.term(3)
    combine_ctx.term(2)
    combine_ctx.term(1)
    combine_ctx.term(0)
    reduce_out.step(0)
    reduce_inner.step(2)

    def keep_grad_ctx(rows, at, total):
        r.grad_ctx[rows, :] = total.astype(BF16)

    def attend_back(pair):
        r.grad_kv[...] = jnp.zeros_like(r.grad_kv)

        def body(b, carry):
            rows = pl.ds(pl.multiple_of(b * n, n), n)
            queries = r.qkv[rows, pair_cols(0, pair)]
            keys = r.qkv[:, pair_cols(1, pair)]
            values = r.qkv[:, pair_cols(2, pair)]
            grad = r.grad_ctx[pl.ds(pl.multiple_of(pair * z.length + b * n, n), n), :]
            outs = []
            for h in range(2):
                mine = first_head if h == 0 else ~first_head
                grad_mine = jnp.where(mine, grad, jnp.zeros_like(grad))
                query_mine = jnp.where(mine, queries, jnp.zeros_like(queries))
                probs = r.probs[2 * pair + h, rows, :]
                grad_probs = dot_nt(grad_mine, values)
                r.grad_kv[1] += dot_tn(probs.astype(BF16), grad_mine)
                inside = jnp.sum(grad_probs * probs, axis=-1, keepdims=True)
                grad_scores = (probs * (grad_probs - inside)).astype(BF16)
                outs.append(dot_nn(grad_scores, keys))
                r.grad_kv[0] += dot_tn(grad_scores, query_mine)
            r.grad_qkv[rows, pair_cols(0, pair)] = (
                jnp.where(first_head, outs[0], outs[1]) * scale
            ).astype(BF16)
            return carry

        lax.fori_loop(0, z.parts, body, 0)
        r.grad_qkv[:, pair_cols(1, pair)] = (r.grad_kv[0] * scale).astype(BF16)
        r.grad_qkv[:, pair_cols(2, pair)] = r.grad_kv[1].astype(BF16)

    def after_pair(pair):
        attend_back(pair)
        reduce_pair[pair].step(0)
        if pair == 0:
            reduce_outer_a.step(3)
            reduce_outer_b.step(2)
            reduce_out.step(1)

    combine_ctx.finish(keep_grad_ctx, after_pair, step=128)
    reduce_inner.step(3)

    for k in range(z.pairs):
        mine = pl.ds(pl.multiple_of(part * c + k * 128, 128), 128)
        for row, kind in ((0, 0), (1, 2)):
            r.sums[row : row + 1, mine] = jnp.sum(
                r.grad_qkv[:, pair_cols(kind, k)].astype(F32), axis=0, keepdims=True
            )
    r.term_vec[...] = jnp.zeros_like(r.term_vec)
    for g in range(z.pages):
        r.term_vec[g * SLAB : g * SLAB + VECTORS, :] = r.sums[:, g * 128 : (g + 1) * 128]
        r.term_vec[g * SLAB + VECTORS : g * SLAB + VECTORS + 1, :] = r.b_sum[
            :, g * z.unit : (g + 1) * z.unit
        ]
    reduce_vec.step(0)

    combine_four = Combine(token_refs(2), n, lambda rows, j: dot_nt(r.grad_qkv[rows, :], r.qkv_w[...]))
    combine_four.term(3)
    combine_four.term(2)
    for pair in range(z.pairs):
        reduce_pair[pair].step(1)
    reduce_vec.step(1)
    reduce_out.step(2)
    combine_four.term(1)
    combine_four.term(0)

    reduce_inner.total(r.fin_inner)
    fin_inner = Spread(r.fin_inner, r.got_inner, z.row)
    fin_inner.start()
    for pair in range(z.pairs):
        reduce_pair[pair].step(2)
    reduce_vec.step(2)
    reduce_out.step(3)

    def input_rows(rows, at, total):
        r.v_grad[rows, :] = r.grad_mixed[rows, :] + total

    reduce_outer_a.total(r.o_outer.at[:, 0 : w // 2])
    for pair in range(z.pairs):
        reduce_pair[pair].step(3)
    reduce_vec.step(3)
    reduce_outer_b.step(3)
    combine_four.finish(input_rows)
    leave_early(1, r.v_grad, r.o_grad).start()
    reduce_out.total(r.fin_out)
    fin_out = Spread(r.fin_out, r.got_out, z.row)
    fin_out.start()
    fin_pair = []
    for k in range(z.pairs):
        reduce_pair[k].total(r.fin_pair.at[k])
        fin_pair.append(Spread(r.fin_pair.at[k], r.got_pair.at[k], z.row))
        fin_pair[k].start()
    reduce_vec.total(r.fin_vec)

    class VecAll:
        first = slots(1)

        def copy(self, j):
            return copy(r.fin_vec, r.got_vec.at[j], self.first, (page, peer(j)))

    fin_vec = VecAll()
    for j in (2, 3, 1):
        fin_vec.copy(j).start()

    my_rows = pl.ds(pl.multiple_of(part * z.row, z.row), z.row)

    def deliver(spread, mine, got, out):
        spread.wait()
        for j in range(4):
            value = got[j] if j else mine[my_rows, :]
            out[peer(j)] = value

    deliver(fin_inner, r.fin_inner, r.got_inner, r.o_inner)
    deliver(fin_out, r.fin_out, r.got_out, r.o_wout)
    arrival = fin_vec.copy(1)
    arrival.wait_bytes(3 * arrival.size())
    summed = r.fin_vec[0:VECTORS, :]
    for j in (1, 2, 3):
        summed = summed + r.got_vec[j, 0:VECTORS, :]
    r.o_vec[0:VECTORS, :] = pltpu.roll(summed, (128 - part * z.row) % 128, 1)
    r.o_vec[VECTORS:, :] = r.fin_vec[VECTORS:, :]
    reduce_outer_b.total(r.o_outer.at[:, w // 2 :])
    for k in range(z.pairs):
        deliver(fin_pair[k], r.fin_pair.at[k], r.got_pair.at[k], r.o_pair.at[k])

    leave_early(0, r.v_out, r.o_out).wait()
    leave_early(1, r.v_grad, r.o_grad).wait()
    for group, size in enumerate(groups):
        rows = r.measure.at[pl.ds(0, size // 512)]
        copy(rows, rows, 0, (page, part), group).wait_send()

    assert counter[0] == z.sems and len(groups) == z.groups, (counter, groups)


def finish_kernel(z, out, grad, outer, inner, pair, wout, vec, *outs):
    (o_out, o_grad, o_wq, o_bq, o_wk, o_wv, o_bv, o_wo, o_bo, o_ga, o_sa, o_wi, o_bi, o_wu, o_bu, o_gf, o_sf) = outs
    o_out[...] = out[...]
    o_grad[...] = grad[...]
    o_wu[...] = outer[...]
    c = z.cols
    for q in range(z.parts):
        o_wo[:, q * c : (q + 1) * c] = wout[q].astype(F32)
        for i, ref in enumerate((o_wq, o_wk, o_wv)):
            for k in range(z.pairs):
                ref[:, q * c + k * 128 : q * c + (k + 1) * 128] = pair[
                    k, q, :, i * 128 : (i + 1) * 128
                ].astype(F32)
        for g in range(z.pages):
            at = (z.parts * g + q) * z.unit
            o_wi[:, at : at + z.unit] = inner[q, :, g * z.unit : (g + 1) * z.unit].astype(F32)
    for i, ref in enumerate((o_bq, o_bv, o_bo, o_ga, o_sa, o_bu, o_gf, o_sf)):
        ref[...] = vec[i : i + 1, 0 : z.row]
    o_bi[...] = vec[VECTORS : VECTORS + 1, :]


def paged_layer(z, tokens, valid_len, params, out_grad):
    (
        w_query, b_query, w_key, w_value, b_value, w_out, b_out, g_attn, s_attn,
        w_inner, b_inner, w_outer, b_outer, g_final, s_final,
    ) = params
    flat = lambda v: v.reshape(1, v.shape[0])
    c, w, n, ln, half = z.cols, z.width, z.span, z.length, z.half
    ins = dict(
        valid=valid_len,
        tokens=tokens.reshape(n, w),
        out_grad=out_grad.reshape(n, w),
        w_query=w_query, w_key=w_key, w_value=w_value, w_out=w_out,
        w_inner=w_inner, w_outer=w_outer,
        b_query=flat(b_query), b_value=flat(b_value), b_out=flat(b_out),
        g_attn=flat(g_attn), s_attn=flat(s_attn), b_inner=flat(b_inner),
        b_outer=flat(b_outer), g_final=flat(g_final), s_final=flat(s_final),
    )
    outs = dict(
        o_out=((n, w), F32),
        o_grad=((n, w), F32),
        o_outer=((z.unit, w), F32),
        o_inner=((z.parts, z.row, z.mine), BF16),
        o_pair=((z.pairs, z.parts, z.row, 384), BF16),
        o_wout=((z.parts, z.row, c), BF16),
        o_vec=((SLAB, 128), F32),
    )
    scratch = dict(
        qkv_w=((w, 3 * c), BF16),
        out_w=((w, c), BF16),
        cut_out=((z.rows, c), BF16),
        inner_w=((w, z.mine), BF16),
        outer_w=((z.mine, w), BF16),
        vec_all=((z.pages * SLAB, 128), F32),
        vec_raw=((z.parts * SLAB, 128), F32),
        cut_qkv=((z.rows, 3 * c), BF16),
        cut_inner=((z.rows, z.mine), BF16),
        vecs=((VECTORS, w), F32),
        b_mine=((1, z.mine), F32),
        tok_all=((ln, w), BF16),
        hid_all=((ln, w), BF16),
        gf_all=((ln, w), BF16),
        ga_cut=((ln, c), BF16),
        ga_cols=((ln, c), BF16),
        att_sum=((ln, c), F32),
        att_cut=((ln, c), BF16),
        att_got=((ln, c), BF16),
        ctx_out=((w // 128 * ln, 128), BF16),
        ctx_in=((4, z.pairs * ln, 128), BF16),
        ctx_own=((z.pairs * ln, 128), F32),
        qkv=((ln, 3 * c), BF16),
        grad_qkv=((ln, 3 * c), BF16),
        probs=((z.heads, ln, ln), F32),
        measure=((8192, 128), F32),
        ctx_all=((w // 128 * ln, 128), BF16),
        grad_ctx=((z.pairs * ln, 128), BF16),
        grad_kv=((2, ln, 128), F32),
        part_out=((3, ln, w), BF16),
        part_in=((3, 4, n, w), BF16),
        part_own=((n, w), F32),
        norm_one=((n, w), F32),
        v_out=((n, w), F32),
        v_grad=((n, w), F32),
        inv_one=((n, 1), F32),
        hidden=((n, w), F32),
        grad_sum=((n, w), F32),
        grad_mixed=((n, w), F32),
        active=((ln, z.mine), BF16),
        slope=((ln, z.mine), F32),
        grad_inner=((ln, z.mine), BF16),
        sums=((VECTORS, w), F32),
        b_sum=((1, z.mine), F32),
        term_vec=((z.pages * SLAB, 128), F32),
        slot_outer_a=((1, 2, half, z.unit, w // 2), BF16), stage_outer_a=((1, z.unit, w // 2), BF16),
        slot_outer_b=((1, 2, half, z.unit, w // 2), BF16), stage_outer_b=((1, z.unit, w // 2), BF16),
        slot_inner=((2, 2, half, z.rows, z.mine // 2), BF16), stage_inner=((2, z.rows, z.mine // 2), BF16),
        slot_pair=((z.pairs, 3, 2, half, z.rows, 128), BF16), stage_pair=((z.pairs, 3, z.rows, 128), BF16),
        slot_out=((1, 2, half, z.rows, c), BF16), stage_out=((1, z.rows, c), BF16),
        slot_vec=((1, 2, half, SLAB, 128 // 1), F32), stage_vec=((1, SLAB, 128 // 1), F32),
        fin_inner=((z.rows, z.mine), BF16), got_inner=((4, z.row, z.mine), BF16),
        fin_pair=((z.pairs, z.rows, 384), BF16), got_pair=((z.pairs, 4, z.row, 384), BF16),
        fin_out=((z.rows, c), BF16), got_out=((4, z.row, c), BF16),
        fin_vec=((SLAB, 128), F32), got_vec=((4, SLAB, 128), F32),
    )
    z.sems = 129
    z.groups, z.group_bytes = 5, 4 << 20
    fetched = dict(
        w_query=0, w_key=0, w_value=0, b_query=0, b_value=0, b_out=0, g_attn=0, s_attn=0, b_outer=0,
        g_final=0, s_final=0, b_inner=0, w_outer=0, w_out=0, tokens=0, w_inner=0, out_grad=0, valid=0)
    z.fetched, z.held = tuple(fetched), "f_"
    for name in z.fetched:
        scratch[z.held + name] = (ins[name].shape, ins[name].dtype)
    sems = [pltpu.SemaphoreType.DMA((v,)) for v in (z.groups, z.sems, len(fetched) + 2)]
    names = list(ins) + list(outs) + list(scratch) + list(dict(send_sem=0, recv_sem=0, load_sem=0))
    vmem = pl.BlockSpec(memory_space=pltpu.VMEM)
    parts = pl.pallas_call(
        functools.partial(layer_kernel, z, names),
        out_shape=[jax.ShapeDtypeStruct(*v) for v in outs.values()],
        in_specs=[
            pl.BlockSpec(memory_space=pl.ANY)
            if k in fetched
            else vmem
            for k, v in ins.items()
        ],
        out_specs=[pl.BlockSpec(memory_space=pl.ANY)] * 2 + [vmem] * (len(outs) - 2),
        scratch_shapes=[
            (pltpu.SMEM if v[1] == jnp.int32 else pltpu.VMEM)(*v) for v in scratch.values()
        ]
        + sems,
        compiler_params=pltpu.CompilerParams(
            collective_id=0, has_side_effects=True, vmem_limit_bytes=67043328
        ),
        name="layer",
    )(*ins.values())
    row, big = z.row, jax.ShapeDtypeStruct((n, w), F32)
    mat = jax.ShapeDtypeStruct((row, w), F32)
    vec = jax.ShapeDtypeStruct((1, row), F32)
    shapes = [
        big, big, mat, vec, mat, mat, vec, mat, vec, vec, vec,
        jax.ShapeDtypeStruct((row, z.units), F32), jax.ShapeDtypeStruct((1, z.unit), F32),
        jax.ShapeDtypeStruct((z.unit, w), F32), vec, vec, vec,
    ]
    steps = 2

    def rows_of(rows, width):
        return pl.BlockSpec((rows // steps, width), lambda i: (i, 0))

    results = pl.pallas_call(
        functools.partial(finish_kernel, z),
        out_shape=shapes,
        grid=(steps,),
        in_specs=[
            rows_of(n, w), rows_of(n, w), rows_of(z.unit, w),
            pl.BlockSpec((z.parts, row // steps, z.mine), lambda i: (0, i, 0)),
            pl.BlockSpec((z.pairs, z.parts, row // steps, 384), lambda i: (0, 0, i, 0)),
            pl.BlockSpec((z.parts, row // steps, c), lambda i: (0, i, 0)),
            pl.BlockSpec((SLAB, 128), lambda i: (0, 0)),
        ],
        out_specs=[
            rows_of(v.shape[0], v.shape[1])
            if v.shape[0] > 1
            else pl.BlockSpec(v.shape, lambda i: (0, 0))
            for v in shapes
        ],
        name="finish",
    )(*parts)
    results = list(results)
    for i in (0, 1):
        results[i] = results[i].reshape(tokens.shape)
    for i in range(2, 17):
        if results[i].shape[0] == 1:
            results[i] = results[i].reshape(results[i].shape[1])
    return tuple(results)


def body(
    tokens,
    valid_len,
    query_weight,
    query_bias,
    key_weight,
    value_weight,
    value_bias,
    output_weight,
    output_bias,
    attn_gain,
    attn_shift,
    inner_weight,
    inner_bias,
    outer_weight,
    outer_bias,
    final_gain,
    final_shift,
    out_grad,
):
    lowered = [
        piece.astype(jnp.bfloat16)
        for piece in (
            query_weight,
            query_bias,
            key_weight,
            value_weight,
            value_bias,
            output_weight,
            output_bias,
            attn_gain,
            attn_shift,
            inner_weight,
            inner_bias,
            outer_weight,
            outer_bias,
            final_gain,
            final_shift,
        )
    ]
    outputs = sequence_layer(tokens, valid_len, lowered, out_grad)
    return outputs


def solution(mesh):
    in_specs = (
        P("page", "seq", None),
        P("page"),
        P(("page", "seq"), None),
        P(("page", "seq")),
        P(("page", "seq"), None),
        P(("page", "seq"), None),
        P(("page", "seq")),
        P(("page", "seq"), None),
        P(("page", "seq")),
        P(("page", "seq")),
        P(("page", "seq")),
        P(("page", "seq"), None),
        P(("page", "seq")),
        P(("page", "seq"), None),
        P(("page", "seq")),
        P(("page", "seq")),
        P(("page", "seq")),
        P("page", "seq", None),
    )
    out_specs = (
        P("page", "seq", None),
        P("page", "seq", None),
        P(("page", "seq"), None),
        P(("page", "seq")),
        P(("page", "seq"), None),
        P(("page", "seq"), None),
        P(("page", "seq")),
        P(("page", "seq"), None),
        P(("page", "seq")),
        P(("page", "seq")),
        P(("page", "seq")),
        P(("page", "seq"), None),
        P(("page", "seq")),
        P(("page", "seq"), None),
        P(("page", "seq")),
        P(("page", "seq")),
        P(("page", "seq")),
    )

    def layer(*arrays):
        width, units = arrays[11].shape
        if supported(mesh, arrays[0].shape, width, units):
            z = Sizes(mesh, width, units, arrays[0].shape[1] // mesh.shape["seq"])

            def run(tokens, valid_len, *rest):
                return paged_layer(z, tokens, valid_len, rest[:-1], rest[-1])

            chosen = run
        else:
            chosen = body
        return jax.shard_map(
            chosen, mesh=mesh, in_specs=in_specs, out_specs=out_specs, check_vma=False
        )(*arrays)

    return layer
```

```python
import functools
import math
import types

import jax
import jax.numpy as jnp
from jax import lax
from jax.experimental import pallas as pl
from jax.experimental.pallas import tpu as pltpu
from jax.sharding import PartitionSpec as P

HEAD_DIM = 64


EPSILON = 1e-05
INV_ROOT_TWO = 1.0 / math.sqrt(2.0)
INV_ROOT_TWO_PI = 1.0 / math.sqrt(2.0 * math.pi)


def product(left, right):
    return jnp.dot(left, right, preferred_element_type=jnp.float32)


def product_tn(left, right):
    return lax.dot_general(
        left, right, (((0,), (0,)), ((), ())), preferred_element_type=jnp.float32
    )


def product_nt(left, right):
    return lax.dot_general(
        left, right, (((1,), (1,)), ((), ())), preferred_element_type=jnp.float32
    )


def norm_parts(values):
    center = values - jnp.mean(values, axis=-1, keepdims=True)
    inverse = lax.rsqrt(jnp.mean(center * center, axis=-1, keepdims=True) + EPSILON)
    return (center * inverse, inverse)


def norm_backward(grad_out, normed, inverse, gain):
    scaled = grad_out * gain
    return inverse * (
        scaled
        - jnp.mean(scaled, axis=-1, keepdims=True)
        - normed * jnp.mean(scaled * normed, axis=-1, keepdims=True)
    )


def gelu_parts(values):
    cumulative = 0.5 * (1.0 + lax.erf(values * INV_ROOT_TWO))
    return (
        values * cumulative,
        cumulative + values * jnp.exp(-0.5 * values * values) * INV_ROOT_TWO_PI,
    )


def sequence_layer(tokens, valid_len, lowered, out_grad):
    fetched = (
        lax.all_gather(lowered[0], ("page", "seq"), axis=0, tiled=True),
        lax.all_gather(lowered[1], ("page", "seq"), axis=0, tiled=True),
        lax.all_gather(lowered[2], ("page", "seq"), axis=0, tiled=True),
        lax.all_gather(lowered[3], ("page", "seq"), axis=0, tiled=True),
        lax.all_gather(lowered[4], ("page", "seq"), axis=0, tiled=True),
        lax.all_gather(lowered[5], ("page", "seq"), axis=0, tiled=True),
        lax.all_gather(lowered[6], ("page", "seq"), axis=0, tiled=True),
        lax.all_gather(lowered[7], ("page", "seq"), axis=0, tiled=True),
        lax.all_gather(lowered[8], ("page", "seq"), axis=0, tiled=True),
        lax.all_gather(lowered[9], ("page", "seq"), axis=0, tiled=True),
        lax.all_gather(lowered[10], ("page", "seq"), axis=0, tiled=True),
        lax.all_gather(lowered[11], ("page", "seq"), axis=0, tiled=True),
        lax.all_gather(lowered[12], ("page", "seq"), axis=0, tiled=True),
        lax.all_gather(lowered[13], ("page", "seq"), axis=0, tiled=True),
        lax.all_gather(lowered[14], ("page", "seq"), axis=0, tiled=True),
    )
    (
        w_query,
        b_query,
        w_key,
        w_value,
        b_value,
        w_out,
        b_out,
        g_attn,
        s_attn,
        w_inner,
        b_inner,
        w_outer,
        b_outer,
        g_final,
        s_final,
    ) = fetched
    f32 = jnp.float32
    bf16 = jnp.bfloat16
    scale = HEAD_DIM ** (-0.5)
    page_count, span_len, width = tokens.shape
    heads = width // HEAD_DIM
    row_count = page_count * span_len
    tok_rows = tokens.reshape(row_count, width)
    tok_low = tok_rows.astype(bf16)
    q_low = (product(tok_low, w_query) + b_query.astype(f32)).astype(bf16)
    k_low = product(tok_low, w_key).astype(bf16)
    v_low = (product(tok_low, w_value) + b_value.astype(f32)).astype(bf16)
    k_full, v_full = (
        lax.all_gather(k_low.reshape(page_count, span_len, width), "seq", axis=1, tiled=True),
        lax.all_gather(v_low.reshape(page_count, span_len, width), "seq", axis=1, tiled=True),
    )
    seq_len = k_full.shape[1]
    q_heads = q_low.reshape(page_count, span_len, heads, HEAD_DIM)
    k_heads = k_full.reshape(page_count, seq_len, heads, HEAD_DIM)
    v_heads = v_full.reshape(page_count, seq_len, heads, HEAD_DIM)
    key_mask = (lax.broadcasted_iota(jnp.int32, (page_count, seq_len), 1) < valid_len[:, None])[
        :, None, None, :
    ]

    def masked_scores():
        raw = jnp.einsum("pqhe,pkhe->phqk", q_heads, k_heads, preferred_element_type=f32) * scale
        return jnp.where(key_mask, raw, -1000000000.0)

    scores = masked_scores()
    top_score = jnp.max(scores, axis=-1, keepdims=True)
    log_total = top_score + jnp.log(jnp.sum(jnp.exp(scores - top_score), axis=-1, keepdims=True))
    probs_low = jnp.exp(scores - log_total).astype(bf16)
    context = jnp.einsum("phqk,pkhe->pqhe", probs_low, v_heads, preferred_element_type=f32)
    ctx_low = context.reshape(row_count, width).astype(bf16)
    attended = product(ctx_low, w_out) + b_out.astype(f32)
    norm_one, inv_one = norm_parts(tok_rows + attended)
    hidden = norm_one * g_attn.astype(f32) + s_attn.astype(f32)
    hid_low = hidden.astype(bf16)
    inner = product(hid_low, w_inner) + b_inner.astype(f32)
    active, slope = gelu_parts(inner)
    act_low = active.astype(bf16)
    outer = product(act_low, w_outer) + b_outer.astype(f32)
    norm_two, inv_two = norm_parts(hidden + outer)
    result = norm_two * g_final.astype(f32) + s_final.astype(f32)
    (
        w_query,
        b_query,
        w_key,
        w_value,
        b_value,
        w_out,
        b_out,
        g_attn,
        s_attn,
        w_inner,
        b_inner,
        w_outer,
        b_outer,
        g_final,
        s_final,
    ) = (
        lax.all_gather(lowered[0], ("page", "seq"), axis=0, tiled=True),
        lax.all_gather(lowered[1], ("page", "seq"), axis=0, tiled=True),
        lax.all_gather(lowered[2], ("page", "seq"), axis=0, tiled=True),
        lax.all_gather(lowered[3], ("page", "seq"), axis=0, tiled=True),
        lax.all_gather(lowered[4], ("page", "seq"), axis=0, tiled=True),
        lax.all_gather(lowered[5], ("page", "seq"), axis=0, tiled=True),
        lax.all_gather(lowered[6], ("page", "seq"), axis=0, tiled=True),
        lax.all_gather(lowered[7], ("page", "seq"), axis=0, tiled=True),
        lax.all_gather(lowered[8], ("page", "seq"), axis=0, tiled=True),
        lax.all_gather(lowered[9], ("page", "seq"), axis=0, tiled=True),
        lax.all_gather(lowered[10], ("page", "seq"), axis=0, tiled=True),
        lax.all_gather(lowered[11], ("page", "seq"), axis=0, tiled=True),
        lax.all_gather(lowered[12], ("page", "seq"), axis=0, tiled=True),
        lax.all_gather(lowered[13], ("page", "seq"), axis=0, tiled=True),
        lax.all_gather(lowered[14], ("page", "seq"), axis=0, tiled=True),
    )
    grad_rows = out_grad.reshape(row_count, width)
    grad_gfinal = jnp.sum(grad_rows * norm_two, axis=0)
    grad_sfinal = jnp.sum(grad_rows, axis=0)
    grad_sum = norm_backward(grad_rows, norm_two, inv_two, g_final.astype(f32))
    grad_f_low = grad_sum.astype(bf16)
    grad_bouter = jnp.sum(grad_f_low.astype(f32), axis=0)
    grad_wouter = product_tn(act_low, grad_f_low)
    grad_active = product_nt(grad_f_low, w_outer)
    grad_in_low = (grad_active * slope).astype(bf16)
    grad_binner = jnp.sum(grad_in_low.astype(f32), axis=0)
    grad_winner = product_tn(hid_low, grad_in_low)
    grad_hidden = grad_sum + product_nt(grad_in_low, w_inner)
    grad_gattn = jnp.sum(grad_hidden * norm_one, axis=0)
    grad_sattn = jnp.sum(grad_hidden, axis=0)
    grad_mixed = norm_backward(grad_hidden, norm_one, inv_one, g_attn.astype(f32))
    grad_att_low = grad_mixed.astype(bf16)
    grad_bout = jnp.sum(grad_att_low.astype(f32), axis=0)
    grad_wout = product_tn(ctx_low, grad_att_low)
    grad_ctx = (
        product_nt(grad_att_low, w_out).astype(bf16).reshape(page_count, span_len, heads, HEAD_DIM)
    )
    probs = jnp.exp(masked_scores() - log_total)
    probs_low = probs.astype(bf16)
    grad_probs = jnp.einsum("pqhe,pkhe->phqk", grad_ctx, v_heads, preferred_element_type=f32)
    grad_vfull = jnp.einsum("phqk,pqhe->pkhe", probs_low, grad_ctx, preferred_element_type=f32)
    grad_scores = (
        probs * (grad_probs - jnp.sum(grad_probs * probs, axis=-1, keepdims=True))
    ).astype(bf16)
    grad_q_low = (
        (jnp.einsum("phqk,pkhe->pqhe", grad_scores, k_heads, preferred_element_type=f32) * scale)
        .astype(bf16)
        .reshape(row_count, width)
    )
    grad_kfull = (
        jnp.einsum("phqk,pqhe->pkhe", grad_scores, q_heads, preferred_element_type=f32) * scale
    )
    grad_keys, grad_values = (
        lax.psum_scatter(
            grad_kfull.reshape(page_count, seq_len, width).astype(jnp.bfloat16),
            "seq",
            scatter_dimension=1,
            tiled=True,
        ).astype(jnp.float32),
        lax.psum_scatter(
            grad_vfull.reshape(page_count, seq_len, width).astype(jnp.bfloat16),
            "seq",
            scatter_dimension=1,
            tiled=True,
        ).astype(jnp.float32),
    )
    grad_k_low = grad_keys.reshape(row_count, width).astype(bf16)
    grad_v_low = grad_values.reshape(row_count, width).astype(bf16)
    grad_tokens = (
        grad_mixed
        + product_nt(grad_q_low, w_query)
        + product_nt(grad_k_low, w_key)
        + product_nt(grad_v_low, w_value)
    )
    grad_wquery = product_tn(tok_low, grad_q_low)
    grad_bquery = jnp.sum(grad_q_low.astype(f32), axis=0)
    grad_wkey = product_tn(tok_low, grad_k_low)
    grad_wvalue = product_tn(tok_low, grad_v_low)
    grad_bvalue = jnp.sum(grad_v_low.astype(f32), axis=0)
    owned = (
        lax.psum_scatter(grad_wquery, ("page", "seq"), scatter_dimension=0, tiled=True),
        lax.psum_scatter(grad_bquery, ("page", "seq"), scatter_dimension=0, tiled=True),
        lax.psum_scatter(grad_wkey, ("page", "seq"), scatter_dimension=0, tiled=True),
        lax.psum_scatter(grad_wvalue, ("page", "seq"), scatter_dimension=0, tiled=True),
        lax.psum_scatter(grad_bvalue, ("page", "seq"), scatter_dimension=0, tiled=True),
        lax.psum_scatter(grad_wout, ("page", "seq"), scatter_dimension=0, tiled=True),
        lax.psum_scatter(grad_bout, ("page", "seq"), scatter_dimension=0, tiled=True),
        lax.psum_scatter(grad_gattn, ("page", "seq"), scatter_dimension=0, tiled=True),
        lax.psum_scatter(grad_sattn, ("page", "seq"), scatter_dimension=0, tiled=True),
        lax.psum_scatter(grad_winner, ("page", "seq"), scatter_dimension=0, tiled=True),
        lax.psum_scatter(grad_binner, ("page", "seq"), scatter_dimension=0, tiled=True),
        lax.psum_scatter(grad_wouter, ("page", "seq"), scatter_dimension=0, tiled=True),
        lax.psum_scatter(grad_bouter, ("page", "seq"), scatter_dimension=0, tiled=True),
        lax.psum_scatter(grad_gfinal, ("page", "seq"), scatter_dimension=0, tiled=True),
        lax.psum_scatter(grad_sfinal, ("page", "seq"), scatter_dimension=0, tiled=True),
    )
    return (
        result.reshape(tokens.shape),
        grad_tokens.reshape(tokens.shape),
        owned[0],
        owned[1],
        owned[2],
        owned[3],
        owned[4],
        owned[5],
        owned[6],
        owned[7],
        owned[8],
        owned[9],
        owned[10],
        owned[11],
        owned[12],
        owned[13],
        owned[14],
    )


MESH = pl.DeviceIdType.MESH
BF16 = jnp.bfloat16
F32 = jnp.float32
VECTORS = 8
SLAB = 16
NEGATIVE = -1000000000.0


def dot_nn(left, right):
    return lax.dot_general(left, right, (((1,), (0,)), ((), ())), preferred_element_type=F32)


def dot_nt(left, right):
    return lax.dot_general(left, right, (((1,), (1,)), ((), ())), preferred_element_type=F32)


def dot_tn(left, right):
    return lax.dot_general(left, right, (((0,), (0,)), ((), ())), preferred_element_type=F32)


class Sizes:
    def __init__(self, mesh, width, units, span):
        self.pages = mesh.shape["page"]
        self.parts = mesh.shape["seq"]
        self.half = self.pages // 2
        self.width = width
        self.units = units
        self.span = span
        self.length = span * self.parts
        self.row = width // (self.pages * self.parts)
        self.rows = self.row * self.parts
        self.unit = units // (self.pages * self.parts)
        self.mine = self.unit * self.pages
        self.cols = width // self.parts
        self.heads = self.cols // HEAD_DIM
        self.pairs = self.cols // 128


def supported(mesh, token_shape, width, units):
    pages, parts = mesh.shape["page"], mesh.shape["seq"]
    return (
        parts == 4
        and pages % 2 == 0
        and pages >= 4
        and token_shape[0] == pages
        and token_shape[1] % (parts * 128) == 0
        and width % (pages * parts * 32) == 0
        and width // pages == 128
        and units % (pages * parts * 128) == 0
        and (width // parts) % 128 == 0
    )


def layer_kernel(z, names, *refs):
    r = types.SimpleNamespace(**dict(zip(names, refs)))
    send_sem, recv_sem, load_sem = r.send_sem, r.recv_sem, r.load_sem
    page = lax.axis_index("page")
    part = lax.axis_index("seq")
    counter = [0]

    def slots(count):
        first = counter[0]
        counter[0] += count
        return first

    odd = page % 2
    place = odd * (z.pages - 1 - page // 2) + (1 - odd) * (page // 2)

    def page_at(index):
        index = (index + z.pages) % z.pages
        late = index // z.half
        return (1 - late) * (2 * index) + late * (2 * z.pages - 1 - 2 * index)

    ring = [page] + [page_at(place + step) for step in range(1, z.pages)]
    peers = [part] + [
        ((part // 2 + j // 2) % 2) * 2 + (part % 2 + j % 2) % 2 for j in range(1, 4)
    ]

    def around(step):
        return ring[step % z.pages]

    def peer(j):
        return peers[j]

    rank = page * z.parts + part

    class Copy:
        def __init__(self, src, dst, index, device, group=None):
            self.args = src, dst, index, device
            self.group = group

        def made(self, group):
            src, dst, index, device = self.args
            return pltpu.make_async_remote_copy(
                src_ref=src,
                dst_ref=dst,
                send_sem=send_sem.at[group],
                recv_sem=recv_sem.at[index],
                device_id=device,
                device_id_type=MESH,
            )

        def start(self):
            group = self.group
            if group is None:
                size = self.size()
                if groups[-1] + size > z.group_bytes:
                    groups.append(0)
                groups[-1] += size
                group = len(groups) - 1
            self.made(group).start()

        def wait_recv(self):
            self.made(0).wait_recv()

        def size(self):
            src = self.args[0]
            return math.prod(src.shape) * jnp.dtype(src.dtype).itemsize

        def wait_bytes(self, size):
            rows = r.measure.at[pl.ds(0, size // 512)]
            Copy(rows, rows, *self.args[2:]).wait_recv()

        def wait_send(self):
            self.made(self.group).wait_send()

    groups = [0]
    copy = Copy

    def block(ref, index, size):
        return ref.at[pl.ds(pl.multiple_of(index * size, size), size)]

    barrier = pltpu.get_barrier_semaphore()

    def greet(device):
        pl.semaphore_signal(barrier, inc=1, device_id=device, device_id_type=MESH)

    for j in (1, 2, 3):
        greet((page, peer(j)))
    greet((around(1), part))
    greet((around(-1), part))

    class Share:
        def __init__(self, ref, size, pieces=2):
            self.ref, self.size, self.pieces = ref, size, pieces
            self.first = slots(2 + pieces)

        def copy(self, j, owner, k):
            height = self.size // self.pieces
            piece = block(self.ref, owner, self.size).at[pl.ds(k * height, height)]
            index = self.first + (2 + k if j == 2 else j // 2)
            return copy(piece, piece, index, (page, peer(1 if j == 3 else j)))

        def start(self, k):
            self.copy(2, part, k).start()
            self.copy(1, part, k).start()

        def forward(self):
            for k in range(self.pieces):
                self.copy(2, peer(2), k).wait_recv()
                self.copy(3, peer(2), k).start()


        def wait(self, j):
            arrival = self.copy(j, peer(j), 0)
            arrival.wait_bytes(self.pieces * arrival.size())

    class Combine:
        def __init__(self, refs, size, make, pieces=2, wide=None):
            self.wide = wide
            self.out, self.got, self.own = refs
            self.size, self.make, self.pieces = size, make, pieces
            self.height = size // pieces
            self.first = slots(2 * pieces)

        def rows(self, j, k):
            at = pl.multiple_of(peer(j) * self.size + k * self.height, self.height)
            return pl.ds(at, self.height)

        def copy(self, j, k):
            return copy(
                self.out.at[self.rows(j, k)],
                self.got.at[j, pl.ds(k * self.height, self.height)],
                self.first + 2 * k + j // 3,
                (page, peer(2 if j == 2 else 1)),
            )

        def term(self, j):
            if self.wide is None:
                at = pl.multiple_of(peer(j) * self.size, self.size)
                value = self.make(pl.ds(at, self.size), j)
            else:
                if j in (1, 3):
                    chip = (part // 2 + j // 2) % 2
                    at = pl.multiple_of(chip * 2 * self.size, 2 * self.size)
                    self.wide[...] = self.make(pl.ds(at, 2 * self.size), j)
                at = pl.multiple_of((peer(j) % 2) * self.size, self.size)
                value = self.wide[pl.ds(at, self.size), :]
            if j == 0:
                self.own[...] = value
                return
            for k in range(self.pieces):
                rows = slice(k * self.height, (k + 1) * self.height)
                mine = value[rows]
                if j == 2:
                    self.copy(3, k).wait_recv()
                    mine = mine + self.got[3, rows, :].astype(F32)
                self.out[self.rows(j, k), :] = mine.astype(BF16)
                self.copy(j, k).start()

        def finish(self, fn, after=None, step=32):
            for k in range(self.pieces):
                arrival = self.copy(1, k)
                arrival.wait_bytes(2 * arrival.size())

                def body(i, carry):
                    at = pl.multiple_of(k * self.height + i * step, step)
                    rows = pl.ds(at, step)
                    total = self.own[rows, :]
                    for j in (1, 2):
                        total = total + self.got[j, rows, :].astype(F32)
                    fn(rows, at, total)
                    return carry

                lax.fori_loop(0, self.height // step, body, 0)
                if after is not None:
                    after(k)

    def token_refs(phase):
        return r.part_out.at[phase], r.part_in.at[phase], r.part_own

    class Spread:
        def __init__(self, src, dst, size):
            self.src, self.dst, self.size, self.first = src, dst, size, slots(1)

        def copy(self, j):
            return copy(
                block(self.src, peer(j), self.size),
                self.dst.at[j],
                self.first,
                (page, peer(j)),
            )

        def start(self):
            for j in (2, 3, 1):
                self.copy(j).start()

        def wait(self):
            arrival = self.copy(1)
            arrival.wait_bytes(3 * arrival.size())

    class Place:
        def __init__(self, src, dst, size, base):
            self.src, self.dst, self.size, self.base, self.first = src, dst, size, base, slots(1)

        def copy(self, j, owner):
            return copy(
                block(self.src, peer(j), self.size),
                block(self.dst, self.base + owner, self.size),
                self.first,
                (page, peer(j)),
            )

        def start(self):
            for j in (2, 3, 1):
                self.copy(j, part).start()

        def wait(self):
            arrival = self.copy(1, peer(1))
            arrival.wait_bytes(3 * arrival.size())

    class Gather:
        def __init__(self, ref, size, pieces=1):
            self.ref, self.size, self.pieces = ref, size, pieces
            self.first = slots(z.half * pieces)

        def copy(self, t, d, k, step):
            height = self.size // self.pieces
            start = k * height
            if t == z.half - 1:
                height = height // 2
                start = start + d * height
            piece = block(self.ref, around(step), self.size).at[pl.ds(start, height)]
            return copy(
                piece,
                piece,
                self.first + t * self.pieces + k,
                (around(1 - 2 * d), part),
            )

        def wait(self, t, k):
            both = 2 * self.copy(t, 0, k, 0).size()
            self.copy(t, 0, k, 0).wait_bytes(both)

        def step(self, t, pieces=None):
            for k in pieces or range(self.pieces):
                if t > 0:
                    self.wait(t - 1, k)
                for d in (0, 1):
                    self.copy(t, d, k, -(1 - 2 * d) * t).start()


        def done(self):
            for k in range(self.pieces):
                self.wait(z.half - 1, k)

    class Reduce:
        def __init__(self, slot, stage, local, shape, kind, pieces=1):
            self.slot, self.stage, self.local = slot, stage, local
            self.size, self.kind, self.pieces = shape[0], kind, pieces
            self.wide = shape[1] // pieces
            self.first = slots(z.half * pieces)

        def copy(self, t, d, k):
            h = self.size // 2
            if t == 0:
                src = self.stage.at[k, pl.ds(d * h, h)]
                dst = self.slot.at[k, d, 0, pl.ds(d * h, h)]
            else:
                src = self.slot.at[k, d, t - 1]
                dst = self.slot.at[k, d, t]
            return copy(
                src,
                dst,
                self.first + t * self.pieces + k,
                (around(1 - 2 * d), part),
            )


        def step(self, t):
            h = self.size // 2
            wide = self.wide
            if t == 0:
                term = self.local(around(z.half)).astype(self.kind)
                for k in range(self.pieces):
                    self.stage[k] = term[:, k * wide : (k + 1) * wide]
            else:
                terms = [
                    self.local(around((1 - 2 * d) * (z.half - t))) for d in (0, 1)
                ]
            for k in range(self.pieces):
                if t > 0:
                    self.wait(t - 1, k)
                for d in (0, 1):
                    if t > 0:
                        term = terms[d][:, k * wide : (k + 1) * wide]
                        held = self.slot.at[k, d, t - 1]
                        if t == 1:
                            near, far = pl.ds(d * h, h), pl.ds((1 - d) * h, h)
                            term_near = term[d * h : (d + 1) * h]
                            term_far = term[(1 - d) * h : (2 - d) * h]
                            held[near] = (held[near].astype(F32) + term_near).astype(self.kind)
                            held[far] = term_far.astype(self.kind)
                        else:
                            held[...] = (held[...].astype(F32) + term).astype(self.kind)
                    self.copy(t, d, k).start()

        def wait(self, t, k):
            arrival = self.copy(t, 0, k)
            arrival.wait_bytes(2 * arrival.size())

        def total(self, out):
            term = self.local(page)
            last = z.half - 1
            for k in range(self.pieces):
                self.wait(last, k)
                at = slice(k * self.wide, (k + 1) * self.wide)
                out[:, at] = (
                    term[:, at] + self.slot[k, 0, last].astype(F32) + self.slot[k, 1, last].astype(F32)
                ).astype(out.dtype)

    c, w, n = z.cols, z.width, z.span

    def fetch(i, name):
        return pltpu.make_async_copy(getattr(r, name), getattr(r, z.held + name), load_sem.at[i])

    for i, name in enumerate(z.fetched):
        fetch(i, name).start()
    hbm = r
    r = types.SimpleNamespace(**vars(hbm))
    for name in z.fetched:
        setattr(r, name, getattr(hbm, z.held + name))
    fetches = iter(range(len(z.fetched)))

    def arrive(count):
        for _ in range(count):
            i = next(fetches)
            pltpu.make_async_copy(
                getattr(hbm, z.fetched[i]), getattr(r, z.fetched[i]), load_sem.at[i]
            ).wait()

    arrive(3)
    for q in range(z.parts):
        rows = pl.ds(q * z.row, z.row)
        for i, weight in enumerate((r.w_query, r.w_key, r.w_value)):
            for k in range(z.pairs):
                r.cut_qkv[rows, (3 * k + i) * 128 : (3 * k + i + 1) * 128] = weight[
                    :, q * c + k * 128 : q * c + (k + 1) * 128
                ].astype(BF16)
    arrive(9)
    mine = pl.multiple_of(part * SLAB, SLAB)
    for i, small in enumerate(
        (r.b_query, r.b_value, r.b_out, r.g_attn, r.s_attn, r.b_outer, r.g_final, r.s_final)
    ):
        r.vec_raw[pl.ds(mine + i, 1), 0 : z.row] = small[...]
    at_page = pl.multiple_of(page * SLAB, SLAB)
    r.vec_all[pl.ds(at_page + VECTORS, 1), :] = r.b_inner[...]
    arrive(1)
    r.outer_w[pl.ds(pl.multiple_of(page * z.unit, z.unit), z.unit), :] = r.w_outer[...].astype(
        BF16
    )

    ring_qkv = Gather(r.qkv_w, z.rows, 2)
    ring_vec = Gather(r.vec_all, SLAB)
    ring_inner = Gather(r.inner_w, z.rows, 2)
    ring_out = Gather(r.out_w, z.rows)
    ring_outer = Gather(r.outer_w, z.unit, 2)
    cut_qkv = Place(r.cut_qkv, r.qkv_w, z.row, page * z.parts)
    cut_out = Place(r.cut_out, r.out_w, z.row, page * z.parts)
    cut_inner = Place(r.cut_inner, r.inner_w, z.row, page * z.parts)
    share_tok = Share(r.tok_all, n)

    class ShareVec:
        first = slots(1)

        def copy(self, j, owner):
            piece = block(r.vec_raw, owner, SLAB).at[pl.ds(0, VECTORS)]
            return copy(piece, piece, self.first, (page, peer(j)))

    vec_share = ShareVec()
    pl.semaphore_wait(barrier, 5)
    cut_qkv.start()
    for j in (2, 3, 1):
        vec_share.copy(j, part).start()
    ring_outer.step(0)
    arrive(2)
    r.tok_all[pl.ds(pl.multiple_of(part * n, n), n), :] = r.tokens[...].astype(BF16)
    share_tok.start(0)
    share_tok.start(1)
    for q in range(z.parts):
        r.cut_out[pl.ds(q * z.row, z.row), :] = r.w_out[:, q * c : (q + 1) * c].astype(BF16)
    cut_out.start()
    arrive(1)
    for q in range(z.parts):
        rows = pl.ds(q * z.row, z.row)
        for g in range(z.pages):
            at = (z.parts * g + q) * z.unit
            r.cut_inner[rows, g * z.unit : (g + 1) * z.unit] = r.w_inner[
                :, at : at + z.unit
            ].astype(BF16)
    cut_inner.start()
    own_rows = pl.ds(pl.multiple_of(rank * z.row, z.row), z.row)
    cut_rows = pl.ds(pl.multiple_of(part * z.row, z.row), z.row)
    r.qkv_w[own_rows, :] = r.cut_qkv[cut_rows, :]
    r.out_w[own_rows, :] = r.cut_out[cut_rows, :]
    r.inner_w[own_rows, :] = r.cut_inner[cut_rows, :]

    cut_qkv.wait()
    ring_qkv.step(0)
    arrival = vec_share.copy(1, peer(1))
    arrival.wait_bytes(3 * arrival.size())
    lane = lax.broadcasted_iota(jnp.int32, (VECTORS, 128), 1)
    total = jnp.zeros((VECTORS, 128), F32)
    for q in range(z.parts):
        tile = r.vec_raw[q * SLAB : q * SLAB + VECTORS, :]
        if q:
            tile = pltpu.roll(tile, q * z.row, 1)
        total = total + jnp.where(lane // z.row == q, tile, 0.0)
    r.vec_all[pl.ds(at_page, VECTORS), :] = total
    ring_vec.step(0)
    ring_qkv.step(1)
    ring_vec.step(1)
    cut_out.wait()
    ring_out.step(0)
    ring_qkv.step(2)
    ring_vec.step(2)
    ring_out.step(1)
    share_tok.forward()
    ring_qkv.step(3)
    ring_vec.step(3)
    ring_out.step(2)
    cut_inner.wait()
    ring_inner.step(0)
    ring_vec.done()

    for g in range(z.pages):
        tile = r.vec_all[g * SLAB : (g + 1) * SLAB, :].astype(BF16).astype(F32)
        r.vecs[:, g * 128 : (g + 1) * 128] = tile[0:VECTORS]
        r.b_mine[:, g * z.unit : (g + 1) * z.unit] = tile[VECTORS : VECTORS + 1]

    def vector(i):
        return r.vecs[i : i + 1, :]


    share_tok.wait(1)
    share_tok.wait(3)
    ring_qkv.done()

    def make_qkv(b, carry):
        rows = pl.ds(pl.multiple_of(b * n, n), n)
        out = dot_nn(r.tok_all[rows, :], r.qkv_w[...])
        for k in range(z.pairs):
            mine = pl.ds(pl.multiple_of(part * c + k * 128, 128), 128)
            for i, bias in enumerate((0, None, 1)):
                cols = slice((3 * k + i) * 128, (3 * k + i + 1) * 128)
                value = out[:, cols]
                if bias is not None:
                    value = value + r.vecs[bias : bias + 1, mine]
                r.qkv[rows, cols] = value.astype(BF16)
        return carry

    lax.fori_loop(0, z.parts, make_qkv, 0)
    ring_inner.step(1)
    ring_out.step(3)
    ring_outer.step(1)

    scale = HEAD_DIM ** (-0.5)
    first_head = lax.broadcasted_iota(jnp.int32, (n, 128), 1) < HEAD_DIM
    key_place = lax.broadcasted_iota(jnp.int32, (n, z.length), 1)
    pltpu.make_async_copy(hbm.valid, r.valid, load_sem.at[len(z.fetched) - 1]).wait()
    valid = r.valid[0]

    def pair_cols(kind, pair):
        return pl.ds((3 * pair + kind) * 128, 128)

    def attend(pair):
        def body(b, carry):
            rows = pl.ds(pl.multiple_of(b * n, n), n)
            queries = r.qkv[rows, pair_cols(0, pair)]
            keys = r.qkv[:, pair_cols(1, pair)]
            values = r.qkv[:, pair_cols(2, pair)]
            outs = []
            for h in range(2):
                mine = first_head if h == 0 else ~first_head
                scores = dot_nt(jnp.where(mine, queries, jnp.zeros_like(queries)), keys) * scale
                scores = jnp.where(key_place < valid, scores, NEGATIVE)
                top = jnp.max(scores, axis=-1, keepdims=True)
                weight = jnp.exp(scores - top)
                probs = weight * (1.0 / jnp.sum(weight, axis=-1, keepdims=True))
                r.probs[2 * pair + h, rows, :] = probs
                outs.append(dot_nn(probs.astype(BF16), values))
            place_rows = pl.ds(
                pl.multiple_of((part * z.pairs + pair) * z.length + b * n, n), n
            )
            r.ctx_all[place_rows, :] = jnp.where(first_head, outs[0], outs[1]).astype(
                BF16
            )
            return carry

        lax.fori_loop(0, z.parts, body, 0)

    share_ctx = Share(r.ctx_all, z.pairs * z.length, z.pairs)
    for pair in range(z.pairs):
        attend(pair)
        share_ctx.start(pair)
    ring_inner.step(2)
    ring_outer.step(2, (0,))

    def project(j):
        term = None
        for k in range(z.pairs):
            rows = pl.ds(pl.multiple_of((peer(j) * z.pairs + k) * z.length, z.length), z.length)
            features = pl.ds(pl.multiple_of(peer(j) * c + k * 128, 128), 128)
            more = dot_nn(r.ctx_all[rows, :], r.out_w[features, :])
            term = more if term is None else term + more
        r.att_sum[...] = term if j == 0 else r.att_sum[...] + term

    ring_out.done()
    project(0)
    share_ctx.wait(1)
    project(1)
    share_ctx.forward()
    project(2)
    share_ctx.wait(3)
    project(3)
    r.att_cut[...] = r.att_sum[...].astype(BF16)
    move_att = Place(r.att_cut, r.att_got, n, 0)
    move_att.start()
    own_block = pl.ds(pl.multiple_of(part * n, n), n)
    r.att_got[own_block, :] = r.att_cut[own_block, :]

    def add_column_sum(i, values):
        r.sums[i : i + 1, :] += jnp.sum(values, axis=0, keepdims=True)

    r.sums[...] = jnp.zeros_like(r.sums)

    share_hid = Share(r.hid_all, n)

    def first_norm(rows, at, total):
        mixed = r.tokens[rows, :] + (total + vector(2))
        normed, inverse = norm_parts(mixed)
        hidden = normed * vector(3) + vector(4)
        r.norm_one[rows, :] = normed
        r.inv_one[rows, :] = inverse
        r.hidden[rows, :] = hidden
        r.hid_all[pl.ds(pl.multiple_of(part * n + at, 32), 32), :] = hidden.astype(BF16)

    ring_inner.step(3)
    ring_outer.step(2, (1,))
    move_att.wait()
    for k in range(2):

        def norm_rows(i, carry):
            at = pl.multiple_of(k * (n // 2) + i * 32, 32)
            total = jnp.concatenate(
                [
                    r.att_got[pl.ds(pl.multiple_of(q * n + at, 32), 32), :].astype(F32)
                    for q in range(z.parts)
                ],
                axis=1,
            )
            first_norm(pl.ds(at, 32), at, total)
            return carry

        lax.fori_loop(0, n // 64, norm_rows, 0)
        share_hid.start(k)
    ring_inner.done()

    tile = 512

    def make_inner(j):
        chip = (part // 2 + j) % 2
        rows = pl.ds(pl.multiple_of(chip * 2 * n, 2 * n), 2 * n)

        def columns(i, carry):
            cols = pl.ds(pl.multiple_of(i * tile, tile), tile)
            inner = dot_nn(r.hid_all[rows, :], r.inner_w[:, cols]) + r.b_mine[:, cols]
            active, slope = gelu_parts(inner)
            r.active[rows, cols] = active.astype(BF16)
            r.slope[rows, cols] = slope
            return carry

        lax.fori_loop(0, z.mine // tile, columns, 0)

    share_hid.wait(1)
    make_inner(0)
    ring_outer.step(3)
    share_hid.forward()
    share_hid.wait(3)
    make_inner(1)
    ring_outer.done()
    combine_two = Combine(token_refs(0), n, lambda rows, j: dot_nn(r.active[rows, :], r.outer_w[...]), 4, r.wide)
    for j in (3, 2, 1, 0):
        combine_two.term(j)
    share_gf = Share(r.gf_all, n, 4)

    arrive(1)

    def second_norm(rows, at, total):
        outer = total + vector(5)
        normed, inverse = norm_parts(r.hidden[rows, :] + outer)
        r.v_out[rows, :] = normed * vector(6) + vector(7)
        grad = r.out_grad[rows, :]
        add_column_sum(6, grad * normed)
        add_column_sum(7, grad)
        grad_sum = norm_backward(grad, normed, inverse, vector(6))
        low = grad_sum.astype(BF16)
        add_column_sum(5, low.astype(F32))
        r.grad_sum[rows, :] = grad_sum
        r.gf_all[pl.ds(pl.multiple_of(part * n + at, 32), 32), :] = low

    combine_two.finish(second_norm, share_gf.start)

    def leave_early(i, src, dst):
        return pltpu.make_async_copy(src, dst, load_sem.at[len(z.fetched) + i])

    leave_early(0, r.v_out, r.o_out).start()

    def chunk_term(left, right, size):
        def local(g):
            cols = pl.ds(pl.multiple_of(g * size, size), size)
            return dot_tn(left[:, cols], right[...])

        return local

    reduce_outer_a = Reduce(
        r.slot_outer_a, r.stage_outer_a,
        chunk_term(r.active, r.gf_all.at[:, 0 : w // 2], z.unit), (z.unit, w // 2), BF16,
    )
    reduce_outer_b = Reduce(
        r.slot_outer_b, r.stage_outer_b,
        chunk_term(r.active, r.gf_all.at[:, w // 2 :], z.unit), (z.unit, w // 2), BF16,
    )
    reduce_inner = Reduce(
        r.slot_inner, r.stage_inner, chunk_term(r.hid_all, r.grad_inner, z.rows),
        (z.rows, z.mine), BF16, 2
    )
    def pair_term(k):
        def local(g):
            cols = pl.ds(pl.multiple_of(g * z.rows, z.rows), z.rows)
            return dot_tn(r.tok_all[:, cols], r.grad_qkv[:, 384 * k : 384 * (k + 1)])

        return local

    def out_term(g):
        rows = pl.ds(pl.multiple_of(g * z.length, z.length), z.length)
        return dot_tn(r.ctx_all[rows, :], r.ga_cols[...])

    reduce_pair = [
        Reduce(r.slot_pair.at[k], r.stage_pair.at[k], pair_term(k), (z.rows, 384), BF16, 3)
        for k in range(z.pairs)
    ]
    reduce_out = Reduce(r.slot_out, r.stage_out, out_term, (z.rows, c), BF16)
    reduce_vec = Reduce(
        r.slot_vec, r.stage_vec,
        lambda g: r.term_vec[pl.ds(pl.multiple_of(g * SLAB, SLAB), SLAB), :], (SLAB, 128), F32,
    )

    r.b_sum[...] = jnp.zeros_like(r.b_sum)

    def make_grad_inner(j):
        chip = (part // 2 + j) % 2
        rows = pl.ds(pl.multiple_of(chip * 2 * n, 2 * n), 2 * n)

        def columns(i, carry):
            cols = pl.ds(pl.multiple_of(i * tile, tile), tile)
            grad = dot_nt(r.gf_all[rows, :], r.outer_w[cols, :]) * r.slope[rows, cols]
            low = grad.astype(BF16)
            r.grad_inner[rows, cols] = low
            r.b_sum[:, cols] += jnp.sum(low.astype(F32), axis=0, keepdims=True)
            return carry

        lax.fori_loop(0, z.mine // tile, columns, 0)

    share_gf.wait(1)
    make_grad_inner(0)
    share_gf.forward()
    share_gf.wait(3)
    reduce_outer_a.step(0)
    reduce_outer_b.step(0)
    make_grad_inner(1)
    combine_three = Combine(
        token_refs(1), n, lambda rows, j: dot_nt(r.grad_inner[rows, :], r.inner_w[...]), wide=r.wide
    )
    combine_three.term(3)
    combine_three.term(2)
    reduce_inner.step(0)
    reduce_outer_a.step(1)
    combine_three.term(1)
    combine_three.term(0)
    reduce_inner.step(1)
    reduce_outer_b.step(1)

    move_ga = Place(r.ga_cut, r.ga_cols, n, 0)

    def first_norm_back(rows, at, total):
        grad = r.grad_sum[rows, :] + total
        normed = r.norm_one[rows, :]
        add_column_sum(3, grad * normed)
        add_column_sum(4, grad)
        mixed = norm_backward(grad, normed, r.inv_one[rows, :], vector(3))
        low = mixed.astype(BF16)
        add_column_sum(2, low.astype(F32))
        r.grad_mixed[rows, :] = mixed
        for q in range(z.parts):
            r.ga_cut[pl.ds(pl.multiple_of(q * n + at, 32), 32), :] = low[:, q * c : (q + 1) * c]

    combine_three.finish(first_norm_back)
    move_ga.start()
    r.ga_cols[own_block, :] = r.ga_cut[own_block, :]
    reduce_outer_a.step(2)

    def grad_ctx_term(rows, j):
        return jnp.concatenate(
            [
                dot_nt(
                    r.ga_cols[...],
                    r.out_w[pl.ds(pl.multiple_of(peer(j) * c + k * 128, 128), 128), :],
                )
                for k in range(z.pairs)
            ],
            axis=0,
        )

    combine_ctx = Combine(
        (r.ctx_out, r.ctx_in, r.ctx_own), z.pairs * z.length, grad_ctx_term, z.pairs
    )
    move_ga.wait()
    combine_ctx.term(3)
    combine_ctx.term(2)
    combine_ctx.term(1)
    combine_ctx.term(0)
    reduce_out.step(0)
    reduce_inner.step(2)

    def keep_grad_ctx(rows, at, total):
        r.grad_ctx[rows, :] = total.astype(BF16)

    def attend_back(pair):
        r.grad_kv[...] = jnp.zeros_like(r.grad_kv)

        def body(b, carry):
            rows = pl.ds(pl.multiple_of(b * n, n), n)
            queries = r.qkv[rows, pair_cols(0, pair)]
            keys = r.qkv[:, pair_cols(1, pair)]
            values = r.qkv[:, pair_cols(2, pair)]
            grad = r.grad_ctx[pl.ds(pl.multiple_of(pair * z.length + b * n, n), n), :]
            outs = []
            for h in range(2):
                mine = first_head if h == 0 else ~first_head
                grad_mine = jnp.where(mine, grad, jnp.zeros_like(grad))
                query_mine = jnp.where(mine, queries, jnp.zeros_like(queries))
                probs = r.probs[2 * pair + h, rows, :]
                grad_probs = dot_nt(grad_mine, values)
                r.grad_kv[1] += dot_tn(probs.astype(BF16), grad_mine)
                inside = jnp.sum(grad_probs * probs, axis=-1, keepdims=True)
                grad_scores = (probs * (grad_probs - inside)).astype(BF16)
                outs.append(dot_nn(grad_scores, keys))
                r.grad_kv[0] += dot_tn(grad_scores, query_mine)
            r.grad_qkv[rows, pair_cols(0, pair)] = (
                jnp.where(first_head, outs[0], outs[1]) * scale
            ).astype(BF16)
            return carry

        lax.fori_loop(0, z.parts, body, 0)
        r.grad_qkv[:, pair_cols(1, pair)] = (r.grad_kv[0] * scale).astype(BF16)
        r.grad_qkv[:, pair_cols(2, pair)] = r.grad_kv[1].astype(BF16)

    def after_pair(pair):
        attend_back(pair)
        reduce_pair[pair].step(0)
        if pair == 0:
            reduce_outer_a.step(3)
            reduce_outer_b.step(2)
            reduce_out.step(1)

    combine_ctx.finish(keep_grad_ctx, after_pair, step=128)
    reduce_inner.step(3)

    for k in range(z.pairs):
        mine = pl.ds(pl.multiple_of(part * c + k * 128, 128), 128)
        for row, kind in ((0, 0), (1, 2)):
            r.sums[row : row + 1, mine] = jnp.sum(
                r.grad_qkv[:, pair_cols(kind, k)].astype(F32), axis=0, keepdims=True
            )
    r.term_vec[...] = jnp.zeros_like(r.term_vec)
    for g in range(z.pages):
        r.term_vec[g * SLAB : g * SLAB + VECTORS, :] = r.sums[:, g * 128 : (g + 1) * 128]
        r.term_vec[g * SLAB + VECTORS : g * SLAB + VECTORS + 1, :] = r.b_sum[
            :, g * z.unit : (g + 1) * z.unit
        ]
    reduce_vec.step(0)

    combine_four = Combine(token_refs(2), n, lambda rows, j: dot_nt(r.grad_qkv[rows, :], r.qkv_w[...]))
    combine_four.term(3)
    combine_four.term(2)
    for pair in range(z.pairs):
        reduce_pair[pair].step(1)
    reduce_vec.step(1)
    reduce_out.step(2)
    combine_four.term(1)
    combine_four.term(0)

    reduce_inner.total(r.fin_inner)
    fin_inner = Spread(r.fin_inner, r.got_inner, z.row)
    fin_inner.start()
    for pair in range(z.pairs):
        reduce_pair[pair].step(2)
    reduce_vec.step(2)
    reduce_out.step(3)

    def input_rows(rows, at, total):
        r.v_grad[rows, :] = r.grad_mixed[rows, :] + total

    reduce_outer_a.total(r.o_outer.at[:, 0 : w // 2])
    for pair in range(z.pairs):
        reduce_pair[pair].step(3)
    reduce_vec.step(3)
    reduce_outer_b.step(3)
    combine_four.finish(input_rows)
    leave_early(1, r.v_grad, r.o_grad).start()
    reduce_out.total(r.fin_out)
    fin_out = Spread(r.fin_out, r.got_out, z.row)
    fin_out.start()
    fin_pair = []
    for k in range(z.pairs):
        reduce_pair[k].total(r.fin_pair.at[k])
        fin_pair.append(Spread(r.fin_pair.at[k], r.got_pair.at[k], z.row))
        fin_pair[k].start()
    reduce_vec.total(r.fin_vec)

    class VecAll:
        first = slots(1)

        def copy(self, j):
            return copy(r.fin_vec, r.got_vec.at[j], self.first, (page, peer(j)))

    fin_vec = VecAll()
    for j in (2, 3, 1):
        fin_vec.copy(j).start()

    my_rows = pl.ds(pl.multiple_of(part * z.row, z.row), z.row)

    def deliver(spread, mine, got, out):
        spread.wait()
        for j in range(4):
            value = got[j] if j else mine[my_rows, :]
            out[peer(j)] = value

    deliver(fin_inner, r.fin_inner, r.got_inner, r.o_inner)
    deliver(fin_out, r.fin_out, r.got_out, r.o_wout)
    arrival = fin_vec.copy(1)
    arrival.wait_bytes(3 * arrival.size())
    summed = r.fin_vec[0:VECTORS, :]
    for j in (1, 2, 3):
        summed = summed + r.got_vec[j, 0:VECTORS, :]
    r.o_vec[0:VECTORS, :] = pltpu.roll(summed, (128 - part * z.row) % 128, 1)
    r.o_vec[VECTORS:, :] = r.fin_vec[VECTORS:, :]
    reduce_outer_b.total(r.o_outer.at[:, w // 2 :])
    for k in range(z.pairs):
        deliver(fin_pair[k], r.fin_pair.at[k], r.got_pair.at[k], r.o_pair.at[k])

    leave_early(0, r.v_out, r.o_out).wait()
    leave_early(1, r.v_grad, r.o_grad).wait()
    for group, size in enumerate(groups):
        rows = r.measure.at[pl.ds(0, size // 512)]
        copy(rows, rows, 0, (page, part), group).wait_send()

    assert counter[0] == z.sems and len(groups) == z.groups, (counter, groups)


def finish_kernel(z, out, grad, outer, inner, pair, wout, vec, *outs):
    (o_out, o_grad, o_wq, o_bq, o_wk, o_wv, o_bv, o_wo, o_bo, o_ga, o_sa, o_wi, o_bi, o_wu, o_bu, o_gf, o_sf) = outs
    o_out[...] = out[...]
    o_grad[...] = grad[...]
    o_wu[...] = outer[...]
    c = z.cols
    for q in range(z.parts):
        o_wo[:, q * c : (q + 1) * c] = wout[q].astype(F32)
        for i, ref in enumerate((o_wq, o_wk, o_wv)):
            for k in range(z.pairs):
                ref[:, q * c + k * 128 : q * c + (k + 1) * 128] = pair[
                    k, q, :, i * 128 : (i + 1) * 128
                ].astype(F32)
        for g in range(z.pages):
            at = (z.parts * g + q) * z.unit
            o_wi[:, at : at + z.unit] = inner[q, :, g * z.unit : (g + 1) * z.unit].astype(F32)
    for i, ref in enumerate((o_bq, o_bv, o_bo, o_ga, o_sa, o_bu, o_gf, o_sf)):
        ref[...] = vec[i : i + 1, 0 : z.row]
    o_bi[...] = vec[VECTORS : VECTORS + 1, :]


def paged_layer(z, tokens, valid_len, params, out_grad):
    (
        w_query, b_query, w_key, w_value, b_value, w_out, b_out, g_attn, s_attn,
        w_inner, b_inner, w_outer, b_outer, g_final, s_final,
    ) = params
    flat = lambda v: v.reshape(1, v.shape[0])
    c, w, n, ln, half = z.cols, z.width, z.span, z.length, z.half
    ins = dict(
        valid=valid_len,
        tokens=tokens.reshape(n, w),
        out_grad=out_grad.reshape(n, w),
        w_query=w_query, w_key=w_key, w_value=w_value, w_out=w_out,
        w_inner=w_inner, w_outer=w_outer,
        b_query=flat(b_query), b_value=flat(b_value), b_out=flat(b_out),
        g_attn=flat(g_attn), s_attn=flat(s_attn), b_inner=flat(b_inner),
        b_outer=flat(b_outer), g_final=flat(g_final), s_final=flat(s_final),
    )
    outs = dict(
        o_out=((n, w), F32),
        o_grad=((n, w), F32),
        o_outer=((z.unit, w), F32),
        o_inner=((z.parts, z.row, z.mine), BF16),
        o_pair=((z.pairs, z.parts, z.row, 384), BF16),
        o_wout=((z.parts, z.row, c), BF16),
        o_vec=((SLAB, 128), F32),
    )
    scratch = dict(
        qkv_w=((w, 3 * c), BF16),
        out_w=((w, c), BF16),
        cut_out=((z.rows, c), BF16),
        inner_w=((w, z.mine), BF16),
        outer_w=((z.mine, w), BF16),
        vec_all=((z.pages * SLAB, 128), F32),
        vec_raw=((z.parts * SLAB, 128), F32),
        cut_qkv=((z.rows, 3 * c), BF16),
        cut_inner=((z.rows, z.mine), BF16),
        vecs=((VECTORS, w), F32),
        b_mine=((1, z.mine), F32),
        tok_all=((ln, w), BF16),
        hid_all=((ln, w), BF16),
        gf_all=((ln, w), BF16),
        ga_cut=((ln, c), BF16),
        ga_cols=((ln, c), BF16),
        att_sum=((ln, c), F32),
        att_cut=((ln, c), BF16),
        att_got=((ln, c), BF16),
        ctx_out=((w // 128 * ln, 128), BF16),
        ctx_in=((4, z.pairs * ln, 128), BF16),
        ctx_own=((z.pairs * ln, 128), F32),
        qkv=((ln, 3 * c), BF16),
        grad_qkv=((ln, 3 * c), BF16),
        probs=((z.heads, ln, ln), F32),
        measure=((8192, 128), F32),
        ctx_all=((w // 128 * ln, 128), BF16),
        grad_ctx=((z.pairs * ln, 128), BF16),
        grad_kv=((2, ln, 128), F32),
        part_out=((3, ln, w), BF16),
        part_in=((3, 4, n, w), BF16),
        part_own=((n, w), F32),
        wide=((2 * n, w), F32),
        norm_one=((n, w), F32),
        v_out=((n, w), F32),
        v_grad=((n, w), F32),
        inv_one=((n, 1), F32),
        hidden=((n, w), F32),
        grad_sum=((n, w), F32),
        grad_mixed=((n, w), F32),
        active=((ln, z.mine), BF16),
        slope=((ln, z.mine), F32),
        grad_inner=((ln, z.mine), BF16),
        sums=((VECTORS, w), F32),
        b_sum=((1, z.mine), F32),
        term_vec=((z.pages * SLAB, 128), F32),
        slot_outer_a=((1, 2, half, z.unit, w // 2), BF16), stage_outer_a=((1, z.unit, w // 2), BF16),
        slot_outer_b=((1, 2, half, z.unit, w // 2), BF16), stage_outer_b=((1, z.unit, w // 2), BF16),
        slot_inner=((2, 2, half, z.rows, z.mine // 2), BF16), stage_inner=((2, z.rows, z.mine // 2), BF16),
        slot_pair=((z.pairs, 3, 2, half, z.rows, 128), BF16), stage_pair=((z.pairs, 3, z.rows, 128), BF16),
        slot_out=((1, 2, half, z.rows, c), BF16), stage_out=((1, z.rows, c), BF16),
        slot_vec=((1, 2, half, SLAB, 128 // 1), F32), stage_vec=((1, SLAB, 128 // 1), F32),
        fin_inner=((z.rows, z.mine), BF16), got_inner=((4, z.row, z.mine), BF16),
        fin_pair=((z.pairs, z.rows, 384), BF16), got_pair=((z.pairs, 4, z.row, 384), BF16),
        fin_out=((z.rows, c), BF16), got_out=((4, z.row, c), BF16),
        fin_vec=((SLAB, 128), F32), got_vec=((4, SLAB, 128), F32),
    )
    z.sems = 129
    z.groups, z.group_bytes = 5, 4 << 20
    fetched = dict(
        w_query=0, w_key=0, w_value=0, b_query=0, b_value=0, b_out=0, g_attn=0, s_attn=0, b_outer=0,
        g_final=0, s_final=0, b_inner=0, w_outer=0, w_out=0, tokens=0, w_inner=0, out_grad=0, valid=0)
    z.fetched, z.held = tuple(fetched), "f_"
    for name in z.fetched:
        scratch[z.held + name] = (ins[name].shape, ins[name].dtype)
    sems = [pltpu.SemaphoreType.DMA((v,)) for v in (z.groups, z.sems, len(fetched) + 2)]
    names = list(ins) + list(outs) + list(scratch) + list(dict(send_sem=0, recv_sem=0, load_sem=0))
    vmem = pl.BlockSpec(memory_space=pltpu.VMEM)
    parts = pl.pallas_call(
        functools.partial(layer_kernel, z, names),
        out_shape=[jax.ShapeDtypeStruct(*v) for v in outs.values()],
        in_specs=[
            pl.BlockSpec(memory_space=pl.ANY)
            if k in fetched
            else vmem
            for k, v in ins.items()
        ],
        out_specs=[pl.BlockSpec(memory_space=pl.ANY)] * 2 + [vmem] * (len(outs) - 2),
        scratch_shapes=[
            (pltpu.SMEM if v[1] == jnp.int32 else pltpu.VMEM)(*v) for v in scratch.values()
        ]
        + sems,
        compiler_params=pltpu.CompilerParams(
            collective_id=0, has_side_effects=True, vmem_limit_bytes=67043328
        ),
        name="layer",
    )(*ins.values())
    row, big = z.row, jax.ShapeDtypeStruct((n, w), F32)
    mat = jax.ShapeDtypeStruct((row, w), F32)
    vec = jax.ShapeDtypeStruct((1, row), F32)
    shapes = [
        big, big, mat, vec, mat, mat, vec, mat, vec, vec, vec,
        jax.ShapeDtypeStruct((row, z.units), F32), jax.ShapeDtypeStruct((1, z.unit), F32),
        jax.ShapeDtypeStruct((z.unit, w), F32), vec, vec, vec,
    ]
    steps = 2

    def rows_of(rows, width):
        return pl.BlockSpec((rows // steps, width), lambda i: (i, 0))

    results = pl.pallas_call(
        functools.partial(finish_kernel, z),
        out_shape=shapes,
        grid=(steps,),
        in_specs=[
            rows_of(n, w), rows_of(n, w), rows_of(z.unit, w),
            pl.BlockSpec((z.parts, row // steps, z.mine), lambda i: (0, i, 0)),
            pl.BlockSpec((z.pairs, z.parts, row // steps, 384), lambda i: (0, 0, i, 0)),
            pl.BlockSpec((z.parts, row // steps, c), lambda i: (0, i, 0)),
            pl.BlockSpec((SLAB, 128), lambda i: (0, 0)),
        ],
        out_specs=[
            rows_of(v.shape[0], v.shape[1])
            if v.shape[0] > 1
            else pl.BlockSpec(v.shape, lambda i: (0, 0))
            for v in shapes
        ],
        name="finish",
    )(*parts)
    results = list(results)
    for i in (0, 1):
        results[i] = results[i].reshape(tokens.shape)
    for i in range(2, 17):
        if results[i].shape[0] == 1:
            results[i] = results[i].reshape(results[i].shape[1])
    return tuple(results)


def body(
    tokens,
    valid_len,
    query_weight,
    query_bias,
    key_weight,
    value_weight,
    value_bias,
    output_weight,
    output_bias,
    attn_gain,
    attn_shift,
    inner_weight,
    inner_bias,
    outer_weight,
    outer_bias,
    final_gain,
    final_shift,
    out_grad,
):
    lowered = [
        piece.astype(jnp.bfloat16)
        for piece in (
            query_weight,
            query_bias,
            key_weight,
            value_weight,
            value_bias,
            output_weight,
            output_bias,
            attn_gain,
            attn_shift,
            inner_weight,
            inner_bias,
            outer_weight,
            outer_bias,
            final_gain,
            final_shift,
        )
    ]
    outputs = sequence_layer(tokens, valid_len, lowered, out_grad)
    return outputs


def solution(mesh):
    in_specs = (
        P("page", "seq", None),
        P("page"),
        P(("page", "seq"), None),
        P(("page", "seq")),
        P(("page", "seq"), None),
        P(("page", "seq"), None),
        P(("page", "seq")),
        P(("page", "seq"), None),
        P(("page", "seq")),
        P(("page", "seq")),
        P(("page", "seq")),
        P(("page", "seq"), None),
        P(("page", "seq")),
        P(("page", "seq"), None),
        P(("page", "seq")),
        P(("page", "seq")),
        P(("page", "seq")),
        P("page", "seq", None),
    )
    out_specs = (
        P("page", "seq", None),
        P("page", "seq", None),
        P(("page", "seq"), None),
        P(("page", "seq")),
        P(("page", "seq"), None),
        P(("page", "seq"), None),
        P(("page", "seq")),
        P(("page", "seq"), None),
        P(("page", "seq")),
        P(("page", "seq")),
        P(("page", "seq")),
        P(("page", "seq"), None),
        P(("page", "seq")),
        P(("page", "seq"), None),
        P(("page", "seq")),
        P(("page", "seq")),
        P(("page", "seq")),
    )

    def layer(*arrays):
        width, units = arrays[11].shape
        if supported(mesh, arrays[0].shape, width, units):
            z = Sizes(mesh, width, units, arrays[0].shape[1] // mesh.shape["seq"])

            def run(tokens, valid_len, *rest):
                return paged_layer(z, tokens, valid_len, rest[:-1], rest[-1])

            chosen = run
        else:
            chosen = body
        return jax.shard_map(
            chosen, mesh=mesh, in_specs=in_specs, out_specs=out_specs, check_vma=False
        )(*arrays)

    return layer
```
